32 devices in a mesh: dp: 4 (over y, x), tensor: 8 (over z, core).
Axes of the slice: x: 2, y: 2, z: 4, core: 2. Of those that a mesh axis runs over, the one named last changes fastest.
Arguments:
- tokens: bfloat16 [8, 2048, 1024], P('dp', 'tensor'), may hold values from -6 to 6
- cotangent: bfloat16 [8, 2048, 1024], P('dp', 'tensor'), may hold values from -6 to 6
- lengths: int32 [8, 12], P('dp'), may hold values from 1 to 256, 1536 in all within a row
- parents: int32 [8, 13], P('dp'), may hold values from 0 to 4, as said below
- first_gain: float32 [1024], replicated, may hold values from 0.25 to 1.75
- first_shift: float32 [1024], replicated, may hold values from -1 to 1
- in_weight: bfloat16 [1024, 3, 1024], P(None, None, 'tensor'), may hold values from -0.1875 to 0.1875
- out_weight: bfloat16 [1024, 1024], P('tensor'), may hold values from -0.1875 to 0.1875
- second_gain: float32 [1024], replicated, may hold values from 0.25 to 1.75
- second_shift: float32 [1024], replicated, may hold values from -1 to 1
- third_gain: float32 [1024], replicated, may hold values from 0.25 to 1.75
- third_shift: float32 [1024], replicated, may hold values from -1 to 1
- up_weight: bfloat16 [1024, 4096], P(None, 'tensor'), may hold values from -0.1875 to 0.1875
- down_weight: bfloat16 [4096, 1024], P('tensor'), may hold values from -0.09375 to 0.09375
- fourth_gain: float32 [1024], replicated, may hold values from 0.25 to 1.75
- fourth_shift: float32 [1024], replicated, may hold values from -1 to 1
Outputs:
- output: bfloat16 [8, 2048, 1024], P('dp', 'tensor')
- tokens_gradient: bfloat16 [8, 2048, 1024], P('dp', 'tensor')
- first_gain_gradient: float32 [1024], replicated
- first_shift_gradient: float32 [1024], replicated
- in_weight_gradient: float32 [1024, 3, 1024], P(None, None, 'tensor')
- out_weight_gradient: float32 [1024, 1024], P('tensor')
- second_gain_gradient: float32 [1024], replicated
- second_shift_gradient: float32 [1024], replicated
- third_gain_gradient: float32 [1024], replicated
- third_shift_gradient: float32 [1024], replicated
- up_weight_gradient: float32 [1024, 4096], P(None, 'tensor')
- down_weight_gradient: float32 [4096, 1024], P('tensor')
- fourth_gain_gradient: float32 [1024], replicated
- fourth_shift_gradient: float32 [1024], replicated
The draws below stay inside these ranges and needn't reach their ends.
Inputs may be any that keep to these rules, and one draw needn't show every extreme that they name: lengths of a tree's branches and leaves, summing to 1536. `parents`: segment 0 is the trunk (its own entry 0); segments 1 to 4 are branches with parent 0; segments 5 to 12 are leaves, two on each branch.
All inputs are finite; a program needn't handle non-finite values.
Results may differ from the reference program's by a relative error of at most 0.019.
Values may be sent and summed in bfloat16 or wider, within the bound.
A program may use at most 192 MiB of HBM per device.

```python
import math
import jax
import jax.numpy as jnp
import numpy as np
from jax import lax

D = 1024
HEADS = 16
HEAD_DIM = 64
FF = 4096
TRUNK = 512
REST = 1536
SEG_MOST = 256
SEGMENTS = 13
TREE = 2048
TREES = 8
QBLOCK = 512


def draw_parents(key, part):

    def one_tree(tree_key):
        order = jax.random.permutation(tree_key, 8)
        leaves = (1 + order // 2).astype(jnp.int32)
        return jnp.concatenate([jnp.zeros((5,), jnp.int32), leaves])
    tree_keys = jax.random.split(jax.random.fold_in(key, 7), TREES)
    return jax.vmap(one_tree)(tree_keys)


def block_scale(key, shape, pieces, smallest, largest):
    level = 1.0
    for dim, parts in pieces:
        steps = jax.random.uniform(jax.random.fold_in(jax.random.fold_in(key, 6), dim), (parts,), jnp.float32, smallest / len(pieces), largest / len(pieces))
        level = level * jnp.repeat(jnp.exp(steps), shape[dim] // parts).reshape((-1,) + (1,) * (len(shape) - 1 - dim))
    return level


def split_up(amount, total, bound, skew):
    loads = [(1 << 20) // math.isqrt(standing ** skew) + 1 for standing in range(2, amount + 1)]
    spare, given = total - bound - (amount - 1), [1] * (amount - 1)
    while spare > 0:
        movable = [i for i in range(amount - 1) if given[i] < bound]
        mass, remaining = sum([loads[i] for i in movable]), spare
        for i in movable:
            extra = min(bound - given[i], max(1, remaining * loads[i] // mass), spare)
            given[i] = given[i] + extra
            spare = spare - extra
    return np.array([bound] + given)


def uneven(rng, number_of, total, reach, slope):
    if number_of == 2:
        one = jax.random.randint(rng, (), max(1, total - reach), min(reach, total - 1) + 1)
        return jnp.stack([one, total - one])
    sizes = jnp.asarray(split_up(number_of, total, reach, slope), jnp.int32)
    twos = (number_of - 1) // 2
    giver, receiver = sizes[1:1 + 2 * twos:2], sizes[2:2 + 2 * twos:2]
    margin = jnp.minimum(giver - 1, reach - receiver)
    passed = jax.random.randint(jax.random.fold_in(rng, 1), (twos,), 0, 1 << 20) % (margin + 1)
    sizes = sizes.at[1:1 + 2 * twos:2].set(giver - passed).at[2:2 + 2 * twos:2].set(receiver + passed)
    return sizes[jax.random.permutation(jax.random.fold_in(rng, 2), number_of)]


def noise(rng, dims, scale, limit, pieces=(), held_as=jnp.bfloat16):
    drawn = scale * jax.random.normal(rng, dims, jnp.float32)
    if pieces:
        drawn = drawn * block_scale(rng, dims, pieces, -0.22, 0.18)
    return jnp.clip(drawn, -limit, limit).astype(held_as)


def setup_inputs(seed: int = 0) -> dict:
    splits = jax.random.split(jax.random.key(seed), 17)
    return {
        "tokens": noise(splits[0], (TREES, TREE, D), 1.0, 6.0, ((0, 4), (1, 8))),
        "cotangent": noise(splits[1], (TREES, TREE, D), 1.0, 6.0, ((0, 4), (1, 8))),
        "lengths": jax.vmap(lambda own: uneven(own, SEGMENTS - 1, REST, SEG_MOST, 1))(jax.random.split(splits[2], TREES)).reshape((TREES, SEGMENTS - 1)).astype(jnp.int32),
        "parents": draw_parents(jax.random.fold_in(splits[16], 71), 0),
        "first_gain": jnp.clip(1.0 + 0.15 * jax.random.normal(splits[4], (D,), jnp.float32), 0.25, 1.75),
        "first_shift": noise(splits[5], (D,), 0.2, 1.0, (), jnp.float32),
        "in_weight": noise(splits[6], (D, 3, D), D ** -0.5, 0.1875, ((2, 8),)),
        "out_weight": noise(splits[7], (D, D), D ** -0.5, 0.1875, ((0, 8),)),
        "second_gain": jnp.clip(1.0 + 0.15 * jax.random.normal(splits[8], (D,), jnp.float32), 0.25, 1.75),
        "second_shift": noise(splits[9], (D,), 0.2, 1.0, (), jnp.float32),
        "third_gain": jnp.clip(1.0 + 0.15 * jax.random.normal(splits[10], (D,), jnp.float32), 0.25, 1.75),
        "third_shift": noise(splits[11], (D,), 0.2, 1.0, (), jnp.float32),
        "up_weight": noise(splits[12], (D, FF), D ** -0.5, 0.1875, ((1, 8),)),
        "down_weight": noise(splits[13], (FF, D), FF ** -0.5, 0.09375, ((0, 8),)),
        "fourth_gain": jnp.clip(1.0 + 0.15 * jax.random.normal(splits[14], (D,), jnp.float32), 0.25, 1.75),
        "fourth_shift": noise(splits[15], (D,), 0.2, 1.0, (), jnp.float32),
    }


rope_base = 10000.0
norm_eps = 1e-05
masked_score = -1e+30
highest = lax.Precision.HIGHEST

@jax.custom_vjp
def low(v):
    return lax.optimization_barrier(v.astype(jnp.bfloat16)).astype(jnp.float32)

@jax.custom_vjp
def low_back(v):
    return v

def low_keep(v):
    return (low(v), None)

def low_pass(kept, grad):
    return (grad,)

def back_keep(v):
    return (v, None)

def back_low(kept, grad):
    return (low(grad),)
low.defvjp(low_keep, low_pass)
low_back.defvjp(back_keep, back_low)

def layer_norm(values, gain, shift):
    average = lax.optimization_barrier(jnp.mean(values, axis=-1, keepdims=True))
    centered = values - average
    spread = lax.optimization_barrier(jnp.mean(centered * centered, axis=-1, keepdims=True))
    return centered * lax.rsqrt(spread + norm_eps) * gain + shift

def gelu_tanh(values):
    return 0.5 * values * (1.0 + jnp.tanh(0.7978845608028654 * (values + 0.044715 * values * values * values)))

def rotate(block, position):
    half = block.shape[-1] // 2
    inverse = rope_base ** (-jnp.arange(half, dtype=jnp.float32) * 2.0 / block.shape[-1])
    angle = position.astype(jnp.float32)[:, None] * inverse[None, :]
    cosine = jnp.cos(angle)[:, None, :]
    sine = jnp.sin(angle)[:, None, :]
    former = block[..., :half]
    latter = block[..., half:]
    return jnp.concatenate([former * cosine - latter * sine, former * sine + latter * cosine], axis=-1)

def tree_layout(tree_lengths, tree_parents):
    seg_sizes = jnp.concatenate([jnp.full((1,), TRUNK, jnp.int32), tree_lengths.astype(jnp.int32)])
    ends = jnp.cumsum(seg_sizes).astype(jnp.int32)
    starts = ends - seg_sizes
    places = jnp.arange(TREE, dtype=jnp.int32)
    labels = jnp.arange(SEGMENTS, dtype=jnp.int32)
    segment = lax.optimization_barrier(jnp.sum((places[:, None] >= ends[None, :]).astype(jnp.int32), axis=1)).astype(jnp.int32)
    own_hot = (segment[:, None] == labels[None, :]).astype(jnp.int32)
    parent = lax.optimization_barrier(jnp.sum(own_hot * tree_parents[None, :], axis=1)).astype(jnp.int32)
    parent_hot = (parent[:, None] == labels[None, :]).astype(jnp.int32)
    grandparent = lax.optimization_barrier(jnp.sum(parent_hot * tree_parents[None, :], axis=1)).astype(jnp.int32)
    parent_size = lax.optimization_barrier(jnp.sum(parent_hot * seg_sizes[None, :], axis=1)).astype(jnp.int32)
    depth_start = jnp.where(segment > 0, TRUNK, 0).astype(jnp.int32) + jnp.where(parent > 0, parent_size, 0).astype(jnp.int32)
    position = (places - lax.optimization_barrier(jnp.sum(own_hot * starts[None, :], axis=1)) + depth_start).astype(jnp.int32)
    return (segment, parent, grandparent, position)

def visible(first, segment, parent, grandparent):
    rows = first + jnp.arange(QBLOCK, dtype=jnp.int32)
    row_segment = lax.dynamic_slice_in_dim(segment, first, QBLOCK, 0)
    row_parent = lax.dynamic_slice_in_dim(parent, first, QBLOCK, 0)
    row_grand = lax.dynamic_slice_in_dim(grandparent, first, QBLOCK, 0)
    columns = jnp.arange(TREE, dtype=jnp.int32)
    same_path = (segment[None, :] == row_segment[:, None]) | (segment[None, :] == row_parent[:, None]) | (segment[None, :] == row_grand[:, None])
    return same_path & (columns[None, :] <= rows[:, None])

def attention(query, keys, values, segment, parent, grandparent):
    scale = HEAD_DIM ** (-0.5)

    def block_scores(index, query, keys, values):
        first = (index * QBLOCK).astype(jnp.int32)
        rows = lax.dynamic_slice_in_dim(query, first, QBLOCK, 0)
        allowed = visible(first, segment, parent, grandparent)
        raw = low_back(jnp.einsum('qhd,khd->hqk', rows, keys, precision=highest))
        scores = jnp.where(allowed[None], raw * scale, masked_score)
        top = lax.optimization_barrier(jnp.max(scores, axis=-1, keepdims=True))
        exponent = jnp.exp(scores - top)
        weights = low(exponent / lax.optimization_barrier(jnp.sum(exponent, axis=-1, keepdims=True)))
        return jnp.einsum('hqk,khd->qhd', weights, values, precision=highest)
    checked = jax.checkpoint(block_scores)
    blocks = lax.map(lambda index: checked(index, query, keys, values), jnp.arange(TREE // QBLOCK, dtype=jnp.int32))
    return blocks.reshape(TREE, query.shape[1], query.shape[2])

def tree_forward(rows, weights, layout):
    first_gain, first_shift, in_weight, out_weight, second_gain, second_shift, third_gain, third_shift, up_weight, down_weight, fourth_gain, fourth_shift = weights
    segment, parent, grandparent, position = layout
    normed = low(layer_norm(rows, first_gain, first_shift))
    mixed = low_back(jnp.dot(normed, in_weight.reshape(D, 3 * D), precision=highest))
    mixed = mixed.reshape(TREE, 3, HEADS, HEAD_DIM)
    query = low(rotate(mixed[:, 0], position))
    keys = low(rotate(mixed[:, 1], position))
    values = low(mixed[:, 2])
    attended = attention(query, keys, values, segment, parent, grandparent)
    attended = low(low_back(attended)).reshape(TREE, D)
    branch = low_back(jnp.dot(attended, out_weight, precision=highest))
    hidden = rows + layer_norm(branch, second_gain, second_shift)
    feed_in = low(layer_norm(hidden, third_gain, third_shift))
    upper = low_back(jnp.dot(feed_in, up_weight, precision=highest))
    active = low(gelu_tanh(upper))
    feed_out = low_back(jnp.dot(active, down_weight, precision=highest))
    return hidden + layer_norm(feed_out, fourth_gain, fourth_shift)

def reference(tokens, cotangent, lengths, parents, first_gain, first_shift, in_weight, out_weight, second_gain, second_shift, third_gain, third_shift, up_weight, down_weight, fourth_gain, fourth_shift):
    params = tuple((array.astype(jnp.float32) for array in (first_gain, first_shift, in_weight, out_weight, second_gain, second_shift, third_gain, third_shift, up_weight, down_weight, fourth_gain, fourth_shift)))

    def one_tree(sums, inputs):
        rows, back_rows, tree_lengths, tree_parents = inputs
        layout = tree_layout(tree_lengths, tree_parents)

        def forward(rows_in, weights):
            return tree_forward(rows_in, weights, layout)
        result, pullback = jax.vjp(forward, rows.astype(jnp.float32), params)
        back_in, back_weights = pullback(back_rows.astype(jnp.float32))
        sums = jax.tree.map(lambda total, part: total + part, sums, back_weights)
        return (sums, (result.astype(jnp.bfloat16), back_in.astype(jnp.bfloat16)))
    zeros = jax.tree.map(jnp.zeros_like, params)
    sums, (outputs, back_tokens) = lax.scan(one_tree, zeros, (tokens, cotangent, lengths, parents))
    return (outputs, back_tokens, sums[0], sums[1], sums[2], sums[3], sums[4], sums[5], sums[6], sums[7], sums[8], sums[9], sums[10], sums[11])
```

```python
import functools
import jax
import jax.numpy as jnp
from jax import lax
from jax.experimental import pallas as pl
from jax.experimental.pallas import tpu as pltpu
from jax.sharding import PartitionSpec as P

HEAD_DIM = 64
LANES = 128
VROWS = 80
BLOCK = 256
TRUNK = 512
SEGMENTS = 13

rope_base = 10000.0
norm_eps = 1e-05
masked_score = -1e30
f32, bf16 = jnp.float32, jnp.bfloat16
NN = (((1,), (0,)), ((), ()))
NT = (((1,), (1,)), ((), ()))
TN = (((0,), (0,)), ((), ()))
MESH = pl.DeviceIdType.MESH
VMEM = pl.BlockSpec(memory_space=pltpu.VMEM)


def dot(a, b, dims=NN):
    return lax.dot_general(a, b, dims, preferred_element_type=f32)


def lane_of(shape):
    return lax.broadcasted_iota(jnp.int32, shape, len(shape) - 1)


def row_of(shape):
    return lax.broadcasted_iota(jnp.int32, shape, len(shape) - 2)


def span(i, n):
    return pl.ds(pl.multiple_of(i * n, n), n)


def split3(v):
    hi = v.astype(bf16).astype(f32)
    mid = (v - hi).astype(bf16).astype(f32)
    return hi, mid, v - hi - mid


def layer_norm(values, gain, shift):
    average = jnp.mean(values, axis=-1, keepdims=True)
    centered = values - average
    spread = jnp.mean(centered * centered, axis=-1, keepdims=True)
    return centered * lax.rsqrt(spread + norm_eps) * gain + shift


def tree_layout(tree_lengths, tree_parents, rows):
    seg_sizes = jnp.concatenate([jnp.full((1,), TRUNK, jnp.int32), tree_lengths])
    ends = jnp.cumsum(seg_sizes)
    starts = ends - seg_sizes
    places = jnp.arange(rows, dtype=jnp.int32)
    labels = jnp.arange(SEGMENTS, dtype=jnp.int32)
    segment = jnp.sum((places[:, None] >= ends[None, :]).astype(jnp.int32), axis=1)
    own_hot = (segment[:, None] == labels[None, :]).astype(jnp.int32)
    parent = jnp.sum(own_hot * tree_parents[None, :], axis=1)
    parent_hot = (parent[:, None] == labels[None, :]).astype(jnp.int32)
    grandparent = jnp.sum(parent_hot * tree_parents[None, :], axis=1)
    parent_size = jnp.sum(parent_hot * seg_sizes[None, :], axis=1)
    depth_start = jnp.where(segment > 0, TRUNK, 0).astype(jnp.int32) + jnp.where(
        parent > 0, parent_size, 0
    )
    position = places - jnp.sum(own_hot * starts[None, :], axis=1) + depth_start
    return (segment, parent, grandparent, position)


def tables(tree_lengths, tree_parents, rows):
    segment, parent, grand, position = tree_layout(tree_lengths, tree_parents, rows)
    lane = jnp.arange(LANES, dtype=jnp.int32)
    half = HEAD_DIM // 2
    inverse = rope_base ** (-(lane % half).astype(f32) * 2.0 / HEAD_DIM)
    angle = position.astype(f32)[:, None] * inverse[None, :]
    cosine = jnp.cos(angle)
    sine = jnp.where((lane % HEAD_DIM) < half, -1.0, 1.0)[None, :] * jnp.sin(angle)
    label = (lane - HEAD_DIM)[None, :]
    own = segment[:, None] == label
    path = own | (parent[:, None] == label) | (grand[:, None] == label)
    hidden = (label >= 0) & (label < SEGMENTS) & ~path
    queries = jnp.where(hidden, masked_score, 0.0).astype(f32)
    ones = (label >= 16) & (label < 19)
    keys = jnp.where(own | ones, 1.0, 0.0).astype(f32)
    return cosine, sine, queries, keys
def barrier(partners):
    semaphore = pltpu.get_barrier_semaphore()
    for partner in partners:
        pl.semaphore_signal(semaphore, inc=1, device_id=partner, device_id_type=MESH)
    pl.semaphore_wait(semaphore, len(partners))


def send(source, target, send_sem, recv_sem, device):
    copy = pltpu.make_async_remote_copy(
        src_ref=source,
        dst_ref=target,
        send_sem=send_sem,
        recv_sem=recv_sem,
        device_id=device,
        device_id_type=MESH,
    )
    copy.start()
    return copy


def gather_kernel(n_d, n_t, x_ref, w_ref, o_ref, u_ref, rs, ss, rb, sb, rw, sw, rp, sp):
    d, t = lax.axis_index("dp"), lax.axis_index("tensor")
    trees, rows, _ = x_ref.shape
    chips = n_t // 2
    group = n_t // trees
    chip, core = t // 2, lax.rem(t, 2)
    other = 2 * chip + 1 - core
    near = group // 2
    tree = t // group
    line = [lax.rem(chip + k, chips) for k in range(1, chips)]
    planes = [lax.rem(d + k, n_d) for k in range(1, n_d)]
    owners = [(j * group + t // trees) for j in range(trees)]
    givers = [lax.rem(t, group) * trees + i for i in range(trees)]
    barrier([(d, lax.rem(t + k, n_t)) for k in range(1, n_t)] + [(p, t) for p in planes])
    part = w_ref.shape[1] // n_d

    copies = []
    mine = w_ref.at[:, span(d, part), :]
    for j in range(trees):
        slot = u_ref.at[lax.rem(t, trees), :, span(d, part), :]

        @pl.when(owners[j] != t)
        def _():
            send(mine, slot, sw.at[j], rw.at[lax.rem(t, trees)], (d, owners[j]))

        @pl.when(owners[j] == t)
        def _():
            u_ref[lax.rem(t, trees), :, span(d, part), :] = w_ref[:, span(d, part), :]

    def block(c, k):
        return o_ref.at[span(2 * c + k, rows)]

    for k, c in enumerate(line):
        copies.append(send(x_ref.at[c // near], block(chip, core), ss.at[k], rs.at[k], (d, 2 * c + core)))
    o_ref[span(t, rows), :] = x_ref[tree]
    copies.append(send(x_ref.at[tree], block(chip, core), sb.at[chips - 1], rb.at[chips - 1], (d, other)))
    for i in range(trees):
        slot = u_ref.at[i, :, span(d, part), :]

        @pl.when(givers[i] != t)
        def _():
            pltpu.make_async_remote_copy(
                src_ref=mine, dst_ref=slot, send_sem=sw.at[0], recv_sem=rw.at[i],
                device_id=(d, givers[i]), device_id_type=MESH,
            ).wait_recv()

    mine_all = u_ref.at[:, :, span(d, part), :]
    for k, p in enumerate(planes):
        copies.append(send(mine_all, mine_all, sp.at[k], rp.at[k], (p, t)))
    for k in range(chips - 1):
        source = lax.rem(chip + chips - 1 - k, chips)
        copies[k].wait_recv()
        copies.append(send(block(source, core), block(source, core), sb.at[k], rb.at[k], (d, other)))
    for j in range(trees):

        @pl.when(owners[j] != t)
        def _():
            pltpu.make_async_remote_copy(
                src_ref=mine, dst_ref=mine, send_sem=sw.at[j], recv_sem=rw.at[0],
                device_id=(d, owners[j]), device_id_type=MESH,
            ).wait_send()

    for i, copy in enumerate(copies):
        if i < chips - 1:
            copy.wait_send()
        else:
            copy.wait()


def gather_tree(n_d, n_t, normed, weight):
    trees, rows, wide = normed.shape
    chips = n_t // 2
    dma = pltpu.SemaphoreType.DMA
    return pl.pallas_call(
        functools.partial(gather_kernel, n_d, n_t),
        in_specs=[VMEM] * 2,
        out_specs=[VMEM] * 2,
        out_shape=[
            jax.ShapeDtypeStruct((n_t * rows, wide), bf16),
            jax.ShapeDtypeStruct((trees,) + weight.shape, bf16),
        ],
        scratch_shapes=[
            dma((chips - 1,)), dma((chips - 1,)), dma((chips,)), dma((chips,)),
            dma((trees,)), dma((trees,)), dma((n_d - 1,)), dma((n_d - 1,)),
        ],
        compiler_params=pltpu.CompilerParams(collective_id=0, has_side_effects=True),
        name="gather_tree",
    )(normed, weight)


def heads_kernel(n_t, trees, back, x_ref, o_ref, ss, rs):
    d, t = lax.axis_index("dp"), lax.axis_index("tensor")
    group = n_t // trees
    others = [lax.rem(t + k, n_t) for k in range(1, n_t)]
    barrier([(d, o) for o in others])
    if back:
        rows, width = x_ref.shape[1], x_ref.shape[2] // group
        cut = lambda o: x_ref.at[o // group, :, span(lax.rem(o, group), width)]
        place = o_ref.at[span(t, rows), :]
    else:
        rows, width = o_ref.shape[1], x_ref.shape[1]
        cut = lambda o: x_ref.at[span(o, rows), :]
        place = o_ref.at[t // group, :, span(lax.rem(t, group), width)]
    copies = [
        send(cut(o), place, ss.at[k], rs.at[k], (d, o)) for k, o in enumerate(others)
    ]
    place[...] = cut(t)[...]
    for copy in copies:
        copy.wait()


def exchange_heads(n_t, trees, x, back):
    if back:
        _, rows, wide = x.shape
        shape = (n_t * rows, wide * trees // n_t)
    else:
        shape = (trees, x.shape[0] // n_t, x.shape[1] * (n_t // trees))
    dma = pltpu.SemaphoreType.DMA
    return pl.pallas_call(
        functools.partial(heads_kernel, n_t, trees, back),
        in_specs=[VMEM],
        out_specs=VMEM,
        out_shape=jax.ShapeDtypeStruct(shape, bf16),
        scratch_shapes=[dma((n_t - 1,)), dma((n_t - 1,))],
        compiler_params=pltpu.CompilerParams(collective_id=2 if back else 1, has_side_effects=True),
        name="heads_back" if back else "heads_out",
    )(x)


def reduce_kernel(n_t, x_ref, o_ref, side, out, land, ss, rs, sb, rb):
    d, t = lax.axis_index("dp"), lax.axis_index("tensor")
    trees, rows, _ = o_ref.shape
    chips = n_t // 2
    near = chips // trees
    chip, core = t // 2, lax.rem(t, 2)
    other = 2 * chip + 1 - core
    line = [lax.rem(chip + k, chips) for k in range(1, chips)]
    barrier([(d, other)] + [(d, 2 * c + core) for c in line])
    pairs = []
    for k, c in enumerate(line + [chip]):
        theirs = x_ref.at[span(2 * c + 1 - core, rows), :]
        pairs.append(send(theirs, side.at[k], sb.at[k], rb.at[k], (d, other)))
    copies = []
    for k, c in enumerate(line):
        pairs[k].wait_recv()
        out[k] = (x_ref[span(2 * c + core, rows), :].astype(f32) + side[k].astype(f32)).astype(bf16)
        copies.append(send(out.at[k], land.at[k], ss.at[k], rs.at[k], (d, 2 * c + core)))
    pairs[chips - 1].wait_recv()
    o_ref[...] = jnp.zeros_like(o_ref)
    o_ref[chip // near] = x_ref[span(t, rows), :].astype(f32) + side[chips - 1].astype(f32)
    for k in range(chips - 1):
        copies[k].wait_recv()
        source = lax.rem(chip + chips - 1 - k, chips)
        o_ref[source // near] += land[k].astype(f32)
    for copy in pairs + copies:
        copy.wait_send()


def reduce_tree(n_t, trees, x):
    rows, wide = x.shape[0] // n_t, x.shape[1]
    chips = n_t // 2
    dma = pltpu.SemaphoreType.DMA
    return pl.pallas_call(
        functools.partial(reduce_kernel, n_t),
        in_specs=[VMEM],
        out_specs=VMEM,
        out_shape=jax.ShapeDtypeStruct((trees, rows, wide), f32),
        scratch_shapes=[
            pltpu.VMEM((chips, rows, wide), bf16),
            pltpu.VMEM((chips - 1, rows, wide), bf16),
            pltpu.VMEM((chips - 1, rows, wide), bf16),
            dma((chips - 1,)), dma((chips - 1,)), dma((chips,)), dma((chips,)),
        ],
        compiler_params=pltpu.CompilerParams(collective_id=3, has_side_effects=True),
        name="reduce_tree",
    )(x)
def qkv_kernel(x_ref, w_ref, cos_ref, sin_ref, mq_ref, mk_ref, q_ref, k_ref, v_ref, kt_ref, vt_ref):
    x = x_ref[...]
    heads = q_ref.shape[0]
    cosine, sine = cos_ref[...], sin_ref[...]
    mq, mk = mq_ref[...], mk_ref[...]
    lane = lane_of(cosine.shape)
    low = lax.rem(lane, HEAD_DIM) < HEAD_DIM // 2
    first = lane < HEAD_DIM
    mv = jnp.where((lane >= HEAD_DIM) & (lane < HEAD_DIM + 3), 1.0, 0.0)
    tail = jnp.where(row_of((VROWS - HEAD_DIM, x.shape[0])) == 0, 1.0, 0.0).astype(bf16)

    def both(slab):
        return slab, pltpu.roll(slab, HEAD_DIM, 1)

    def rotate(slab):
        partner = jnp.where(
            low, pltpu.roll(slab, LANES - HEAD_DIM // 2, 1), pltpu.roll(slab, HEAD_DIM // 2, 1)
        )
        return slab * cosine + partner * sine

    q_all, k_all, v_all = (dot(x, w_ref[i]) for i in range(3))
    for h in range(0, heads, 2):
        cols = slice(h * HEAD_DIM, (h + 2) * HEAD_DIM)
        for g, slab in enumerate(both(rotate(q_all[:, cols]) * HEAD_DIM**-0.5)):
            q_ref[h + g] = jnp.where(first, slab, mq).astype(bf16)
        keys = rotate(k_all[:, cols])
        for g, slab in enumerate(both(keys)):
            k_ref[h + g] = jnp.where(first, slab, mk).astype(bf16)
        flat = keys.T.astype(bf16)
        for g, slab in enumerate(both(v_all[:, cols])):
            v_ref[h + g] = jnp.where(first, slab, mv).astype(bf16)
        flat_v = v_all[:, cols].T.astype(bf16)
        for g in range(2):
            part = slice(g * HEAD_DIM, (g + 1) * HEAD_DIM)
            kt_ref[h + g] = flat[part]
            vt_ref[h + g, :HEAD_DIM] = flat_v[part]
            vt_ref[h + g, HEAD_DIM:] = tail


def project(x, w, cosine, sine, mq, mk):
    rows, wide = x.shape
    heads = w.shape[2] // HEAD_DIM
    table = pl.BlockSpec((BLOCK, LANES), lambda i: (i, 0))
    slab = pl.BlockSpec((heads, BLOCK, LANES), lambda i: (0, i, 0))
    shape = jax.ShapeDtypeStruct((heads, rows, LANES), bf16)
    return pl.pallas_call(
        qkv_kernel,
        grid=(rows // BLOCK,),
        in_specs=[
            pl.BlockSpec((BLOCK, wide), lambda i: (i, 0)),
            pl.BlockSpec(w.shape, lambda i: (0, 0, 0)),
            table, table, table, table,
        ],
        out_specs=[
            slab, slab, slab,
            pl.BlockSpec((heads, HEAD_DIM, BLOCK), lambda i: (0, 0, i)),
            pl.BlockSpec((heads, VROWS, BLOCK), lambda i: (0, 0, i)),
        ],
        out_shape=[
            shape, shape, shape,
            jax.ShapeDtypeStruct((heads, HEAD_DIM, rows), bf16),
            jax.ShapeDtypeStruct((heads, VROWS, rows), bf16),
        ],
        name="project",
    )(x, w, cosine, sine, mq, mk)


def fwd_kernel(q_ref, k_ref, vt_ref, o_ref, qb_ref):
    qi = pl.program_id(1)
    heads = q_ref.shape[0]
    row, col = row_of((BLOCK, BLOCK)), lane_of((BLOCK, BLOCK))
    qs = [q_ref[h] for h in range(heads)]

    def scores(h, j):
        return dot(k_ref[h, span(j, BLOCK), :], qs[h], NT)

    state = []
    for h in range(heads):
        s = jnp.where(row <= col, scores(h, qi), masked_score)
        m = jnp.max(s, axis=0, keepdims=True)
        p = jnp.exp(s - m)
        state.append((m, dot(vt_ref[h, :, span(qi, BLOCK)], p.astype(bf16))))

    def step(j, carry):
        out = []
        for h in range(heads):
            m, acc = carry[h]
            s = scores(h, j)
            top = jnp.maximum(m, jnp.max(s, axis=0, keepdims=True))
            p = jnp.exp(s - top)
            acc = acc * jnp.exp(m - top) + dot(vt_ref[h, :, span(j, BLOCK)], p.astype(bf16))
            out.append((top, acc))
        return tuple(out)

    state = lax.fori_loop(0, qi, step, tuple(state))
    r = row_of((LANES, BLOCK))
    for h in range(0, heads, 2):
        outs = []
        for g in (h, h + 1):
            m, acc = state[g]
            total = acc[HEAD_DIM : HEAD_DIM + 1]
            outs.append(acc[:HEAD_DIM] / total)
            a, b, c = split3(-(m + jnp.log(total)))
            extra = jnp.where(r == 80, a, jnp.where(r == 81, b, jnp.where(r == 82, c, 0.0))).T
            qb_ref[g] = qs[g] + extra.astype(bf16)
        o_ref[:, h * HEAD_DIM : (h + 2) * HEAD_DIM] = jnp.concatenate(outs, axis=0).T.astype(bf16)


def attend(q, k, vt):
    heads, rows, _ = q.shape
    together = min(4, heads)
    slab = pl.BlockSpec((together, rows, LANES), lambda h, i: (h, 0, 0))
    block = pl.BlockSpec((together, BLOCK, LANES), lambda h, i: (h, i, 0))
    return pl.pallas_call(
        fwd_kernel,
        grid=(heads // together, rows // BLOCK),
        in_specs=[block, slab, pl.BlockSpec((together, VROWS, rows), lambda h, i: (h, 0, 0))],
        out_specs=[pl.BlockSpec((BLOCK, together * HEAD_DIM), lambda h, i: (i, h)), block],
        out_shape=[
            jax.ShapeDtypeStruct((rows, heads * HEAD_DIM), bf16),
            jax.ShapeDtypeStruct(q.shape, bf16),
        ],
        name="attend",
    )(q, k, vt)


def bwd_kernel(q_ref, k_ref, v_ref, kt_ref, d_ref, o_ref, cos_ref, sin_ref, m_ref, sums, wide):
    j = pl.program_id(0)
    heads, rows, _ = q_ref.shape
    nq = rows // BLOCK
    row, col = row_of((BLOCK, BLOCK)), lane_of((BLOCK, BLOCK))
    lane = lane_of((BLOCK, LANES))
    first = lane < HEAD_DIM

    @pl.when(j == 0)
    def _():
        sums[...] = jnp.zeros_like(sums)

        def widen(i, _):
            at = span(i, BLOCK)
            for h in range(0, heads, 2):
                cols = slice(h * HEAD_DIM, (h + 2) * HEAD_DIM)
                slab = d_ref[at, cols].astype(f32)
                prod = slab * o_ref[at, cols].astype(f32)
                for g, (s, mine) in enumerate(((slab, first), (pltpu.roll(slab, HEAD_DIM, 1), ~first))):
                    inner = -jnp.sum(jnp.where(mine, prod, 0.0), axis=1, keepdims=True)
                    a, b, c = split3(inner)
                    n = HEAD_DIM
                    tail = jnp.where(lane == n, a, jnp.where(lane == n + 1, b, jnp.where(lane == n + 2, c, 0.0)))
                    wide[h + g, at, :] = jnp.where(first, s, tail).astype(bf16)
            return 0

        lax.fori_loop(0, nq, widen, 0)

    ks = [k_ref[h] for h in range(heads)]
    vs = [v_ref[h] for h in range(heads)]
    kts = [kt_ref[h] for h in range(heads)]

    def pair(h, i, mask):
        at = span(i, BLOCK)
        q = q_ref[h, at, :]
        d = wide[h, at, :]
        s = dot(ks[h], q, NT)
        if mask:
            s = jnp.where(row <= col, s, masked_score)
        p = jnp.exp(s)
        back = (p * dot(vs[h], d, NT)).astype(bf16)
        sums[h, :, at] += dot(kts[h], back)
        return dot(back, q), dot(p.astype(bf16), d)

    def step(i, carry):
        out = []
        for h in range(heads):
            dk, dv = pair(h, i, False)
            out.append((carry[h][0] + dk, carry[h][1] + dv))
        return tuple(out)

    state = tuple(pair(h, j, True) for h in range(heads))
    state = lax.fori_loop(j + 1, nq, step, state)

    def join(a, b):
        return jnp.where(first, a, pltpu.roll(b, HEAD_DIM, 1))

    cosine, sine = cos_ref[...], sin_ref[...]
    low = lax.rem(lane, HEAD_DIM) < HEAD_DIM // 2

    def unrotate(slab):
        partner = jnp.where(
            low, pltpu.roll(slab, LANES - HEAD_DIM // 2, 1), pltpu.roll(slab, HEAD_DIM // 2, 1)
        )
        return slab * cosine - partner * sine

    at = span(j, BLOCK)
    total = heads * HEAD_DIM
    for h in range(0, heads, 2):
        dq = jnp.concatenate([sums[h, :, at], sums[h + 1, :, at]], axis=0).T * HEAD_DIM**-0.5
        dk = join(state[h][0], state[h + 1][0])
        dv = join(state[h][1], state[h + 1][1])
        for n, part in enumerate((unrotate(dq), unrotate(dk), dv)):
            begin = n * total + h * HEAD_DIM
            m_ref[:, begin : begin + 2 * HEAD_DIM] = part.astype(bf16)


def attend_back(q, k, v, kt, d, o, cosine, sine):
    heads, rows, _ = q.shape
    whole = lambda a: pl.BlockSpec(a.shape, lambda j: (0,) * a.ndim)
    block = pl.BlockSpec((heads, BLOCK, LANES), lambda j: (0, j, 0))
    table = pl.BlockSpec((BLOCK, LANES), lambda j: (j, 0))
    return pl.pallas_call(
        bwd_kernel,
        grid=(rows // BLOCK,),
        in_specs=[
            whole(q), block, block,
            pl.BlockSpec((heads, HEAD_DIM, BLOCK), lambda j: (0, 0, j)),
            whole(d), whole(o), table, table,
        ],
        out_specs=pl.BlockSpec((BLOCK, 3 * heads * HEAD_DIM), lambda j: (j, 0)),
        out_shape=jax.ShapeDtypeStruct((rows, 3 * heads * HEAD_DIM), bf16),
        scratch_shapes=[
            pltpu.VMEM((heads, HEAD_DIM, rows), f32),
            pltpu.VMEM((heads, rows, LANES), bf16),
        ],
        name="attend_back",
    )(q, k, v, kt, d, o, cosine, sine)


def ln_parts(v):
    centered = v - jnp.mean(v, axis=-1, keepdims=True)
    r = lax.rsqrt(jnp.mean(centered * centered, axis=-1, keepdims=True) + norm_eps)
    return centered * r, r


def ln_back(e, n, r, gain):
    f = e * gain
    return r * (f - jnp.mean(f, axis=-1, keepdims=True) - n * jnp.mean(f * n, axis=-1, keepdims=True))


def feed_kernel(
    att_ref, x_ref, cot_ref, ow_ref, par_ref, up_ref, down_ref,
    out_ref, hid_ref, ba_ref, upg_ref, downg_ref, outg_ref, vec_ref,
    hidden, branch, acc, feed_in, back_feed, active, slope,
):
    phase, n = pl.program_id(0), pl.program_id(1)
    last = pl.num_programs(1) - 1
    par = lambda i: par_ref[i : i + 1]
    total = lambda v: jnp.sum(v, axis=0, keepdims=True)

    @pl.when((phase == 0) & (n == 0))
    def _():
        b = dot(att_ref[...], ow_ref[...])
        branch[...] = b
        h = x_ref[...].astype(f32) + ln_parts(b)[0] * par(0) + par(1)
        hidden[...] = h
        feed_in[...] = (ln_parts(h)[0] * par(2) + par(3)).astype(bf16)
        acc[...] = jnp.zeros_like(acc)

    up = up_ref[...].reshape(feed_in.shape[1], -1)
    down = down_ref[...].reshape(-1, feed_in.shape[1])

    @pl.when(phase == 0)
    def _():
        u = dot(feed_in[...], up)
        t = jnp.tanh(0.7978845608028654 * (u + 0.044715 * u * u * u))
        half = 0.5 * (1.0 + t)
        a = (u * half).astype(bf16)
        active[n] = a
        slope[n] = half + 0.5 * u * (1.0 - t * t) * (
            0.7978845608028654 * (1.0 + 3 * 0.044715 * u * u)
        )
        acc[...] += dot(a, down)

    @pl.when((phase == 1) & (n == 0))
    def _():
        e = cot_ref[...].astype(f32)
        norm, r = ln_parts(acc[...])
        out_ref[...] = (hidden[...] + norm * par(4) + par(5)).astype(bf16)
        vec_ref[4:5] = total(e * norm)
        vec_ref[5:6] = total(e)
        back_feed[...] = ln_back(e, norm, r, par(4)).astype(bf16)
        acc[...] = jnp.zeros_like(acc)

    @pl.when(phase == 1)
    def _():
        b = back_feed[...]
        upper = (dot(b, down, NT) * slope[n]).astype(bf16)
        acc[...] += dot(upper, up, NT)
        downg_ref[0] = dot(active[n], b, TN).astype(bf16)
        upg_ref[0] = dot(feed_in[...], upper, TN).astype(bf16)

    @pl.when((phase == 1) & (n == last))
    def _():
        e = acc[...]
        norm, r = ln_parts(hidden[...])
        vec_ref[2:3] = total(e * norm)
        vec_ref[3:4] = total(e)
        h = cot_ref[...].astype(f32) + ln_back(e, norm, r, par(2))
        hid_ref[...] = h
        norm, r = ln_parts(branch[...])
        vec_ref[0:1] = total(h * norm)
        vec_ref[1:2] = total(h)
        b = ln_back(h, norm, r, par(0)).astype(bf16)
        ba_ref[...] = dot(b, ow_ref[...], NT).astype(bf16)
        outg_ref[...] = dot(att_ref[...], b, TN).astype(bf16)


def feed(att, x, cot, ow, par, up, down):
    rows, wide = att.shape
    n_d, n_t, _, width = up.shape
    one = lambda a: pl.BlockSpec(a.shape, lambda p, n: (0,) * len(a.shape), pipeline_mode=pl.Buffered(1))
    sds = jax.ShapeDtypeStruct
    outs = [
        sds((rows, wide), bf16), sds((rows, wide), f32), sds((rows, wide), bf16),
        sds((n_t, wide, width), bf16), sds((n_t, width, wide), bf16), sds((wide, wide), bf16),
        sds((8, wide), f32),
    ]
    chunk = lambda a: pl.BlockSpec((1,) + a.shape[1:], lambda p, n: (p * n, 0, 0))
    weight = lambda a: pl.BlockSpec((a.shape[0], 1) + a.shape[2:], lambda p, n: (0, n, 0, 0))
    return pl.pallas_call(
        feed_kernel,
        grid=(2, n_t),
        in_specs=[one(a) for a in (att, x, cot, ow, par)] + [weight(up), weight(down)],
        out_specs=[one(o) for o in outs[:3]] + [chunk(outs[3]), chunk(outs[4])] + [one(o) for o in outs[5:]],
        out_shape=outs,
        scratch_shapes=[
            pltpu.VMEM((rows, wide), f32), pltpu.VMEM((rows, wide), f32), pltpu.VMEM((rows, wide), f32),
            pltpu.VMEM((rows, wide), bf16), pltpu.VMEM((rows, wide), bf16),
            pltpu.VMEM((n_t, rows, width), bf16), pltpu.VMEM((n_t, rows, width), f32),
        ],
        compiler_params=pltpu.CompilerParams(vmem_limit_bytes=64 << 20),
        name="feed",
    )(att, x, cot, ow, par, up, down)
def shards(
    n_d, n_t,
    tokens, cotangent, lengths, parents, first_gain, first_shift, in_weight, out_weight,
    second_gain, second_shift, third_gain, third_shift, up_weight, down_weight, fourth_gain, fourth_shift,
):
    trees, rows, wide = tokens.shape
    group = n_t // trees
    d, t = lax.axis_index("dp"), lax.axis_index("tensor")
    tree = t // group
    width = out_weight.shape[0]

    def part(w):
        return lax.dynamic_slice_in_dim(w, d * (w.shape[0] // n_d), w.shape[0] // n_d, 0)

    def everyone(w):
        full = lax.all_gather(part(w), ("dp", "tensor"), axis=0, tiled=False)
        return full.reshape((n_d, n_t) + full.shape[1:])

    out_all, up_all, down_all = everyone(out_weight), everyone(up_weight), everyone(down_weight)
    out_all = out_all.transpose(1, 0, 2, 3).reshape(-1, wide)

    mine = lambda a: lax.dynamic_index_in_dim(a, tree, 0, keepdims=False)
    cosine, sine, mq, mk = tables(mine(lengths), mine(parents), n_t * rows)

    x = tokens.astype(f32)
    normed, first_back = jax.vjp(layer_norm, x, first_gain, first_shift)
    gathered, w = gather_tree(n_d, n_t, normed.astype(bf16), in_weight.transpose(1, 0, 2))
    w = w.transpose(1, 2, 0, 3).reshape(3, wide, -1)
    q, k, v, kt, vt = project(gathered, w, cosine, sine, mq, mk)
    attended, qb = attend(q, k, vt)
    att = exchange_heads(n_t, trees, attended, False)
    par = jnp.stack(
        [second_gain, second_shift, third_gain, third_shift, fourth_gain, fourth_shift, first_gain, first_shift]
    )
    flat = lambda a: a.reshape(trees * rows, a.shape[-1])
    output, back_hidden, back_att, up_g, down_g, out_g, vec = feed(
        flat(att), flat(tokens), flat(cotangent), out_all, par, up_all, down_all
    )
    d_heads = exchange_heads(n_t, trees, back_att.reshape(trees, rows, wide), True)
    back_mixed = attend_back(qb, k, v, kt, d_heads, attended, cosine, sine)
    w_flat = w.transpose(1, 0, 2).reshape(wide, -1)
    partial = lax.dot_general(back_mixed, w_flat, NT, preferred_element_type=f32).astype(bf16)
    in_part = lax.dot_general(gathered, back_mixed, TN, preferred_element_type=f32)
    back_normed = reduce_tree(n_t, trees, partial)
    back_x, first_gain_back, first_shift_back = first_back(back_normed)
    back_tokens = (back_hidden.reshape(x.shape) + back_x).astype(bf16)

    in_part = in_part.astype(bf16).reshape(wide, 3, trees, width).transpose(2, 0, 1, 3)
    own = lax.rem(t, group) * trees
    spread = jnp.zeros((n_t, wide, 3, width), bf16)
    spread = lax.dynamic_update_slice(spread, in_part, (own, 0, 0, 0))

    def collect(g):
        mine = lax.psum_scatter(g, "tensor", scatter_dimension=0, tiled=False)
        return lax.psum(mine, "dp").astype(f32)

    vec = jnp.concatenate([vec[:6], first_gain_back[None], first_shift_back[None]])
    vec = lax.psum(vec, ("dp", "tensor"))
    return (
        output.reshape(tokens.shape),
        back_tokens,
        vec[6], vec[7],
        collect(spread),
        collect(out_g.reshape(n_t, width, wide)),
        vec[0], vec[1], vec[2], vec[3],
        collect(up_g),
        collect(down_g),
        vec[4], vec[5],
    )


def solution(mesh):
    in_specs = (
        P("dp", "tensor", None), P("dp", "tensor", None), P("dp", None), P("dp", None),
        P(), P(), P(None, None, "tensor"), P("tensor", None), P(), P(), P(), P(),
        P(None, "tensor"), P("tensor", None), P(), P(),
    )
    out_specs = (
        P("dp", "tensor", None), P("dp", "tensor", None), P(), P(), P(None, None, "tensor"),
        P("tensor", None), P(), P(), P(), P(), P(None, "tensor"), P("tensor", None), P(), P(),
    )
    run = functools.partial(shards, mesh.shape["dp"], mesh.shape["tensor"])
    return jax.shard_map(run, mesh=mesh, in_specs=in_specs, out_specs=out_specs, check_vma=False)
```

```python
import functools
import jax
import jax.numpy as jnp
from jax import lax
from jax.experimental import pallas as pl
from jax.experimental.pallas import tpu as pltpu
from jax.sharding import PartitionSpec as P

HEAD_DIM = 64
LANES = 128
VROWS = 80
BLOCK = 256
TRUNK = 512
SEGMENTS = 13

rope_base = 10000.0
norm_eps = 1e-05
masked_score = -1e30
f32, bf16 = jnp.float32, jnp.bfloat16
NN = (((1,), (0,)), ((), ()))
NT = (((1,), (1,)), ((), ()))
TN = (((0,), (0,)), ((), ()))
MESH = pl.DeviceIdType.MESH
VMEM = pl.BlockSpec(memory_space=pltpu.VMEM)


def dot(a, b, dims=NN):
    return lax.dot_general(a, b, dims, preferred_element_type=f32)


def lane_of(shape):
    return lax.broadcasted_iota(jnp.int32, shape, len(shape) - 1)


def row_of(shape):
    return lax.broadcasted_iota(jnp.int32, shape, len(shape) - 2)


def span(i, n):
    return pl.ds(pl.multiple_of(i * n, n), n)


def split3(v):
    hi = v.astype(bf16).astype(f32)
    mid = (v - hi).astype(bf16).astype(f32)
    return hi, mid, v - hi - mid


def layer_norm(values, gain, shift):
    average = jnp.mean(values, axis=-1, keepdims=True)
    centered = values - average
    spread = jnp.mean(centered * centered, axis=-1, keepdims=True)
    return centered * lax.rsqrt(spread + norm_eps) * gain + shift


def tree_layout(tree_lengths, tree_parents, rows):
    seg_sizes = jnp.concatenate([jnp.full((1,), TRUNK, jnp.int32), tree_lengths])
    ends = jnp.cumsum(seg_sizes)
    starts = ends - seg_sizes
    places = jnp.arange(rows, dtype=jnp.int32)
    labels = jnp.arange(SEGMENTS, dtype=jnp.int32)
    segment = jnp.sum((places[:, None] >= ends[None, :]).astype(jnp.int32), axis=1)
    own_hot = (segment[:, None] == labels[None, :]).astype(jnp.int32)
    parent = jnp.sum(own_hot * tree_parents[None, :], axis=1)
    parent_hot = (parent[:, None] == labels[None, :]).astype(jnp.int32)
    grandparent = jnp.sum(parent_hot * tree_parents[None, :], axis=1)
    parent_size = jnp.sum(parent_hot * seg_sizes[None, :], axis=1)
    depth_start = jnp.where(segment > 0, TRUNK, 0).astype(jnp.int32) + jnp.where(
        parent > 0, parent_size, 0
    )
    position = places - jnp.sum(own_hot * starts[None, :], axis=1) + depth_start
    return (segment, parent, grandparent, position)


def tables(tree_lengths, tree_parents, rows):
    segment, parent, grand, position = tree_layout(tree_lengths, tree_parents, rows)
    lane = jnp.arange(LANES, dtype=jnp.int32)
    half = HEAD_DIM // 2
    inverse = rope_base ** (-(lane % half).astype(f32) * 2.0 / HEAD_DIM)
    angle = position.astype(f32)[:, None] * inverse[None, :]
    cosine = jnp.cos(angle)
    sine = jnp.where((lane % HEAD_DIM) < half, -1.0, 1.0)[None, :] * jnp.sin(angle)
    label = (lane - HEAD_DIM)[None, :]
    own = segment[:, None] == label
    path = own | (parent[:, None] == label) | (grand[:, None] == label)
    hidden = (label >= 0) & (label < SEGMENTS) & ~path
    queries = jnp.where(hidden, masked_score, 0.0).astype(f32)
    ones = (label >= 16) & (label < 19)
    keys = jnp.where(own | ones, 1.0, 0.0).astype(f32)
    return cosine, sine, queries, keys
def barrier(partners):
    semaphore = pltpu.get_barrier_semaphore()
    for partner in partners:
        pl.semaphore_signal(semaphore, inc=1, device_id=partner, device_id_type=MESH)
    pl.semaphore_wait(semaphore, len(partners))


def send(source, target, send_sem, recv_sem, device):
    copy = pltpu.make_async_remote_copy(
        src_ref=source,
        dst_ref=target,
        send_sem=send_sem,
        recv_sem=recv_sem,
        device_id=device,
        device_id_type=MESH,
    )
    copy.start()
    return copy


def gather_kernel(n_d, n_t, x_ref, w_ref, o_ref, u_ref, rs, ss, rb, sb, rw, sw, rp, sp):
    d, t = lax.axis_index("dp"), lax.axis_index("tensor")
    trees, rows, _ = x_ref.shape
    chips = n_t // 2
    group = n_t // trees
    chip, core = t // 2, lax.rem(t, 2)
    other = 2 * chip + 1 - core
    near = group // 2
    tree = t // group
    line = [lax.rem(chip + k, chips) for k in range(1, chips)]
    planes = [lax.rem(d + k, n_d) for k in range(1, n_d)]
    owners = [(j * group + t // trees) for j in range(trees)]
    givers = [lax.rem(t, group) * trees + i for i in range(trees)]
    barrier([(d, lax.rem(t + k, n_t)) for k in range(1, n_t)] + [(p, t) for p in planes])
    part = w_ref.shape[1] // n_d

    copies = []
    mine = w_ref.at[:, span(d, part), :]
    for j in range(trees):
        slot = u_ref.at[lax.rem(t, trees), :, span(d, part), :]

        @pl.when(owners[j] != t)
        def _():
            send(mine, slot, sw.at[j], rw.at[lax.rem(t, trees)], (d, owners[j]))

        @pl.when(owners[j] == t)
        def _():
            u_ref[lax.rem(t, trees), :, span(d, part), :] = w_ref[:, span(d, part), :]

    def block(c, k):
        return o_ref.at[span(2 * c + k, rows)]

    for k, c in enumerate(line):
        copies.append(send(x_ref.at[c // near], block(chip, core), ss.at[k], rs.at[k], (d, 2 * c + core)))
    o_ref[span(t, rows), :] = x_ref[tree]
    copies.append(send(x_ref.at[tree], block(chip, core), sb.at[chips - 1], rb.at[chips - 1], (d, other)))
    for i in range(trees):
        slot = u_ref.at[i, :, span(d, part), :]

        @pl.when(givers[i] != t)
        def _():
            pltpu.make_async_remote_copy(
                src_ref=mine, dst_ref=slot, send_sem=sw.at[0], recv_sem=rw.at[i],
                device_id=(d, givers[i]), device_id_type=MESH,
            ).wait_recv()

    mine_all = u_ref.at[:, :, span(d, part), :]
    for k, p in enumerate(planes):
        copies.append(send(mine_all, mine_all, sp.at[k], rp.at[k], (p, t)))
    for k in range(chips - 1):
        source = lax.rem(chip + chips - 1 - k, chips)
        copies[k].wait_recv()
        copies.append(send(block(source, core), block(source, core), sb.at[k], rb.at[k], (d, other)))
    for j in range(trees):

        @pl.when(owners[j] != t)
        def _():
            pltpu.make_async_remote_copy(
                src_ref=mine, dst_ref=mine, send_sem=sw.at[j], recv_sem=rw.at[0],
                device_id=(d, owners[j]), device_id_type=MESH,
            ).wait_send()

    for i, copy in enumerate(copies):
        if i < chips - 1:
            copy.wait_send()
        else:
            copy.wait()


def gather_tree(n_d, n_t, normed, weight):
    trees, rows, wide = normed.shape
    chips = n_t // 2
    dma = pltpu.SemaphoreType.DMA
    return pl.pallas_call(
        functools.partial(gather_kernel, n_d, n_t),
        in_specs=[VMEM] * 2,
        out_specs=[VMEM] * 2,
        out_shape=[
            jax.ShapeDtypeStruct((n_t * rows, wide), bf16),
            jax.ShapeDtypeStruct((trees,) + weight.shape, bf16),
        ],
        scratch_shapes=[
            dma((chips - 1,)), dma((chips - 1,)), dma((chips,)), dma((chips,)),
            dma((trees,)), dma((trees,)), dma((n_d - 1,)), dma((n_d - 1,)),
        ],
        compiler_params=pltpu.CompilerParams(collective_id=0, has_side_effects=True),
        name="gather_tree",
    )(normed, weight)


def heads_kernel(n_t, trees, back, x_ref, o_ref, ss, rs):
    d, t = lax.axis_index("dp"), lax.axis_index("tensor")
    group = n_t // trees
    others = [lax.rem(t + k, n_t) for k in range(1, n_t)]
    barrier([(d, o) for o in others])
    if back:
        rows, width = x_ref.shape[1], x_ref.shape[2] // group
        cut = lambda o: x_ref.at[o // group, :, span(lax.rem(o, group), width)]
        place = o_ref.at[span(t, rows), :]
    else:
        rows, width = o_ref.shape[1], x_ref.shape[1]
        cut = lambda o: x_ref.at[span(o, rows), :]
        place = o_ref.at[t // group, :, span(lax.rem(t, group), width)]
    copies = [
        send(cut(o), place, ss.at[k], rs.at[k], (d, o)) for k, o in enumerate(others)
    ]
    place[...] = cut(t)[...]
    for copy in copies:
        copy.wait()


def exchange_heads(n_t, trees, x, back):
    if back:
        _, rows, wide = x.shape
        shape = (n_t * rows, wide * trees // n_t)
    else:
        shape = (trees, x.shape[0] // n_t, x.shape[1] * (n_t // trees))
    dma = pltpu.SemaphoreType.DMA
    return pl.pallas_call(
        functools.partial(heads_kernel, n_t, trees, back),
        in_specs=[VMEM],
        out_specs=VMEM,
        out_shape=jax.ShapeDtypeStruct(shape, bf16),
        scratch_shapes=[dma((n_t - 1,)), dma((n_t - 1,))],
        compiler_params=pltpu.CompilerParams(collective_id=2 if back else 1, has_side_effects=True),
        name="heads_back" if back else "heads_out",
    )(x)


def qkv_kernel(x_ref, w_ref, cos_ref, sin_ref, mq_ref, mk_ref, q_ref, k_ref, v_ref, kt_ref, vt_ref):
    x = x_ref[...]
    heads = q_ref.shape[0]
    cosine, sine = cos_ref[...], sin_ref[...]
    mq, mk = mq_ref[...], mk_ref[...]
    lane = lane_of(cosine.shape)
    low = lax.rem(lane, HEAD_DIM) < HEAD_DIM // 2
    first = lane < HEAD_DIM
    mv = jnp.where((lane >= HEAD_DIM) & (lane < HEAD_DIM + 3), 1.0, 0.0)
    tail = jnp.where(row_of((VROWS - HEAD_DIM, x.shape[0])) == 0, 1.0, 0.0).astype(bf16)

    def both(slab):
        return slab, pltpu.roll(slab, HEAD_DIM, 1)

    def rotate(slab):
        partner = jnp.where(
            low, pltpu.roll(slab, LANES - HEAD_DIM // 2, 1), pltpu.roll(slab, HEAD_DIM // 2, 1)
        )
        return slab * cosine + partner * sine

    q_all, k_all, v_all = (dot(x, w_ref[i]) for i in range(3))
    for h in range(0, heads, 2):
        cols = slice(h * HEAD_DIM, (h + 2) * HEAD_DIM)
        for g, slab in enumerate(both(rotate(q_all[:, cols]) * HEAD_DIM**-0.5)):
            q_ref[h + g] = jnp.where(first, slab, mq).astype(bf16)
        keys = rotate(k_all[:, cols])
        for g, slab in enumerate(both(keys)):
            k_ref[h + g] = jnp.where(first, slab, mk).astype(bf16)
        flat = keys.T.astype(bf16)
        for g, slab in enumerate(both(v_all[:, cols])):
            v_ref[h + g] = jnp.where(first, slab, mv).astype(bf16)
        flat_v = v_all[:, cols].T.astype(bf16)
        for g in range(2):
            part = slice(g * HEAD_DIM, (g + 1) * HEAD_DIM)
            kt_ref[h + g] = flat[part]
            vt_ref[h + g, :HEAD_DIM] = flat_v[part]
            vt_ref[h + g, HEAD_DIM:] = tail


def project(x, w, cosine, sine, mq, mk):
    rows, wide = x.shape
    heads = w.shape[2] // HEAD_DIM
    table = pl.BlockSpec((BLOCK, LANES), lambda i: (i, 0))
    slab = pl.BlockSpec((heads, BLOCK, LANES), lambda i: (0, i, 0))
    shape = jax.ShapeDtypeStruct((heads, rows, LANES), bf16)
    return pl.pallas_call(
        qkv_kernel,
        grid=(rows // BLOCK,),
        in_specs=[
            pl.BlockSpec((BLOCK, wide), lambda i: (i, 0)),
            pl.BlockSpec(w.shape, lambda i: (0, 0, 0)),
            table, table, table, table,
        ],
        out_specs=[
            slab, slab, slab,
            pl.BlockSpec((heads, HEAD_DIM, BLOCK), lambda i: (0, 0, i)),
            pl.BlockSpec((heads, VROWS, BLOCK), lambda i: (0, 0, i)),
        ],
        out_shape=[
            shape, shape, shape,
            jax.ShapeDtypeStruct((heads, HEAD_DIM, rows), bf16),
            jax.ShapeDtypeStruct((heads, VROWS, rows), bf16),
        ],
        name="project",
    )(x, w, cosine, sine, mq, mk)


def fwd_kernel(q_ref, k_ref, vt_ref, o_ref, qb_ref):
    qi = pl.program_id(1)
    heads = q_ref.shape[0]
    row, col = row_of((BLOCK, BLOCK)), lane_of((BLOCK, BLOCK))
    qs = [q_ref[h] for h in range(heads)]

    def scores(h, j):
        return dot(k_ref[h, span(j, BLOCK), :], qs[h], NT)

    state = []
    for h in range(heads):
        s = jnp.where(row <= col, scores(h, qi), masked_score)
        m = jnp.max(s, axis=0, keepdims=True)
        p = jnp.exp(s - m)
        state.append((m, dot(vt_ref[h, :, span(qi, BLOCK)], p.astype(bf16))))

    def step(j, carry):
        out = []
        for h in range(heads):
            m, acc = carry[h]
            s = scores(h, j)
            top = jnp.maximum(m, jnp.max(s, axis=0, keepdims=True))
            p = jnp.exp(s - top)
            acc = acc * jnp.exp(m - top) + dot(vt_ref[h, :, span(j, BLOCK)], p.astype(bf16))
            out.append((top, acc))
        return tuple(out)

    state = lax.fori_loop(0, qi, step, tuple(state))
    r = row_of((LANES, BLOCK))
    for h in range(0, heads, 2):
        outs = []
        for g in (h, h + 1):
            m, acc = state[g]
            total = acc[HEAD_DIM : HEAD_DIM + 1]
            outs.append(acc[:HEAD_DIM] / total)
            a, b, c = split3(-(m + jnp.log(total)))
            extra = jnp.where(r == 80, a, jnp.where(r == 81, b, jnp.where(r == 82, c, 0.0))).T
            qb_ref[g] = qs[g] + extra.astype(bf16)
        o_ref[:, h * HEAD_DIM : (h + 2) * HEAD_DIM] = jnp.concatenate(outs, axis=0).T.astype(bf16)


def attend(q, k, vt):
    heads, rows, _ = q.shape
    together = min(4, heads)
    slab = pl.BlockSpec((together, rows, LANES), lambda h, i: (h, 0, 0))
    block = pl.BlockSpec((together, BLOCK, LANES), lambda h, i: (h, i, 0))
    return pl.pallas_call(
        fwd_kernel,
        grid=(heads // together, rows // BLOCK),
        in_specs=[block, slab, pl.BlockSpec((together, VROWS, rows), lambda h, i: (h, 0, 0))],
        out_specs=[pl.BlockSpec((BLOCK, together * HEAD_DIM), lambda h, i: (i, h)), block],
        out_shape=[
            jax.ShapeDtypeStruct((rows, heads * HEAD_DIM), bf16),
            jax.ShapeDtypeStruct(q.shape, bf16),
        ],
        name="attend",
    )(q, k, vt)


def bwd_kernel(q_ref, k_ref, v_ref, kt_ref, d_ref, o_ref, cos_ref, sin_ref, m_ref, sums, wide):
    j = pl.program_id(0)
    heads, rows, _ = q_ref.shape
    nq = rows // BLOCK
    row, col = row_of((BLOCK, BLOCK)), lane_of((BLOCK, BLOCK))
    lane = lane_of((BLOCK, LANES))
    first = lane < HEAD_DIM

    @pl.when(j == 0)
    def _():
        sums[...] = jnp.zeros_like(sums)

        def widen(i, _):
            at = span(i, BLOCK)
            for h in range(0, heads, 2):
                cols = slice(h * HEAD_DIM, (h + 2) * HEAD_DIM)
                slab = d_ref[at, cols].astype(f32)
                prod = slab * o_ref[at, cols].astype(f32)
                for g, (s, mine) in enumerate(((slab, first), (pltpu.roll(slab, HEAD_DIM, 1), ~first))):
                    inner = -jnp.sum(jnp.where(mine, prod, 0.0), axis=1, keepdims=True)
                    a, b, c = split3(inner)
                    n = HEAD_DIM
                    tail = jnp.where(lane == n, a, jnp.where(lane == n + 1, b, jnp.where(lane == n + 2, c, 0.0)))
                    wide[h + g, at, :] = jnp.where(first, s, tail).astype(bf16)
            return 0

        lax.fori_loop(0, nq, widen, 0)

    ks = [k_ref[h] for h in range(heads)]
    vs = [v_ref[h] for h in range(heads)]
    kts = [kt_ref[h] for h in range(heads)]

    def pair(h, i, mask):
        at = span(i, BLOCK)
        q = q_ref[h, at, :]
        d = wide[h, at, :]
        s = dot(ks[h], q, NT)
        if mask:
            s = jnp.where(row <= col, s, masked_score)
        p = jnp.exp(s)
        back = (p * dot(vs[h], d, NT)).astype(bf16)
        sums[h, :, at] += dot(kts[h], back)
        return dot(back, q), dot(p.astype(bf16), d)

    def step(i, carry):
        out = []
        for h in range(heads):
            dk, dv = pair(h, i, False)
            out.append((carry[h][0] + dk, carry[h][1] + dv))
        return tuple(out)

    state = tuple(pair(h, j, True) for h in range(heads))
    state = lax.fori_loop(j + 1, nq, step, state)

    def join(a, b):
        return jnp.where(first, a, pltpu.roll(b, HEAD_DIM, 1))

    cosine, sine = cos_ref[...], sin_ref[...]
    low = lax.rem(lane, HEAD_DIM) < HEAD_DIM // 2

    def unrotate(slab):
        partner = jnp.where(
            low, pltpu.roll(slab, LANES - HEAD_DIM // 2, 1), pltpu.roll(slab, HEAD_DIM // 2, 1)
        )
        return slab * cosine - partner * sine

    at = span(j, BLOCK)
    total = heads * HEAD_DIM
    for h in range(0, heads, 2):
        dq = jnp.concatenate([sums[h, :, at], sums[h + 1, :, at]], axis=0).T * HEAD_DIM**-0.5
        dk = join(state[h][0], state[h + 1][0])
        dv = join(state[h][1], state[h + 1][1])
        for n, part in enumerate((unrotate(dq), unrotate(dk), dv)):
            begin = n * total + h * HEAD_DIM
            m_ref[:, begin : begin + 2 * HEAD_DIM] = part.astype(bf16)


def attend_back(q, k, v, kt, d, o, cosine, sine):
    heads, rows, _ = q.shape
    whole = lambda a: pl.BlockSpec(a.shape, lambda j: (0,) * a.ndim)
    block = pl.BlockSpec((heads, BLOCK, LANES), lambda j: (0, j, 0))
    table = pl.BlockSpec((BLOCK, LANES), lambda j: (j, 0))
    return pl.pallas_call(
        bwd_kernel,
        grid=(rows // BLOCK,),
        in_specs=[
            whole(q), block, block,
            pl.BlockSpec((heads, HEAD_DIM, BLOCK), lambda j: (0, 0, j)),
            whole(d), whole(o), table, table,
        ],
        out_specs=pl.BlockSpec((BLOCK, 3 * heads * HEAD_DIM), lambda j: (j, 0)),
        out_shape=jax.ShapeDtypeStruct((rows, 3 * heads * HEAD_DIM), bf16),
        scratch_shapes=[
            pltpu.VMEM((heads, HEAD_DIM, rows), f32),
            pltpu.VMEM((heads, rows, LANES), bf16),
        ],
        name="attend_back",
    )(q, k, v, kt, d, o, cosine, sine)


def ln_parts(v):
    centered = v - jnp.mean(v, axis=-1, keepdims=True)
    r = lax.rsqrt(jnp.mean(centered * centered, axis=-1, keepdims=True) + norm_eps)
    return centered * r, r


def ln_back(e, n, r, gain):
    f = e * gain
    return r * (f - jnp.mean(f, axis=-1, keepdims=True) - n * jnp.mean(f * n, axis=-1, keepdims=True))


def feed_kernel(
    att_ref, x_ref, cot_ref, ow_ref, par_ref, up_ref, down_ref,
    out_ref, hid_ref, ba_ref, upg_ref, downg_ref, outg_ref, vec_ref,
    hidden, branch, acc, feed_in, back_feed, active, slope,
):
    phase, n = pl.program_id(0), pl.program_id(1)
    last = pl.num_programs(1) - 1
    par = lambda i: par_ref[i : i + 1]
    total = lambda v: jnp.sum(v, axis=0, keepdims=True)

    @pl.when((phase == 0) & (n == 0))
    def _():
        b = dot(att_ref[...], ow_ref[...])
        branch[...] = b
        h = x_ref[...].astype(f32) + ln_parts(b)[0] * par(0) + par(1)
        hidden[...] = h
        feed_in[...] = (ln_parts(h)[0] * par(2) + par(3)).astype(bf16)
        acc[...] = jnp.zeros_like(acc)

    up = up_ref[...].reshape(feed_in.shape[1], -1)
    down = down_ref[...].reshape(-1, feed_in.shape[1])

    @pl.when(phase == 0)
    def _():
        u = dot(feed_in[...], up)
        t = jnp.tanh(0.7978845608028654 * (u + 0.044715 * u * u * u))
        half = 0.5 * (1.0 + t)
        a = (u * half).astype(bf16)
        active[n] = a
        slope[n] = half + 0.5 * u * (1.0 - t * t) * (
            0.7978845608028654 * (1.0 + 3 * 0.044715 * u * u)
        )
        acc[...] += dot(a, down)

    @pl.when((phase == 1) & (n == 0))
    def _():
        e = cot_ref[...].astype(f32)
        norm, r = ln_parts(acc[...])
        out_ref[...] = (hidden[...] + norm * par(4) + par(5)).astype(bf16)
        vec_ref[4:5] = total(e * norm)
        vec_ref[5:6] = total(e)
        back_feed[...] = ln_back(e, norm, r, par(4)).astype(bf16)
        acc[...] = jnp.zeros_like(acc)

    @pl.when(phase == 1)
    def _():
        b = back_feed[...]
        upper = (dot(b, down, NT) * slope[n]).astype(bf16)
        acc[...] += dot(upper, up, NT)
        downg_ref[0] = dot(active[n], b, TN).astype(bf16)
        upg_ref[0] = dot(feed_in[...], upper, TN).astype(bf16)

    @pl.when((phase == 1) & (n == last))
    def _():
        e = acc[...]
        norm, r = ln_parts(hidden[...])
        vec_ref[2:3] = total(e * norm)
        vec_ref[3:4] = total(e)
        h = cot_ref[...].astype(f32) + ln_back(e, norm, r, par(2))
        hid_ref[...] = h
        norm, r = ln_parts(branch[...])
        vec_ref[0:1] = total(h * norm)
        vec_ref[1:2] = total(h)
        b = ln_back(h, norm, r, par(0)).astype(bf16)
        ba_ref[...] = dot(b, ow_ref[...], NT).astype(bf16)
        outg_ref[...] = dot(att_ref[...], b, TN).astype(bf16)


def feed(att, x, cot, ow, par, up, down):
    rows, wide = att.shape
    n_d, n_t, _, width = up.shape
    one = lambda a: pl.BlockSpec(a.shape, lambda p, n: (0,) * len(a.shape), pipeline_mode=pl.Buffered(1))
    sds = jax.ShapeDtypeStruct
    outs = [
        sds((rows, wide), bf16), sds((rows, wide), f32), sds((rows, wide), bf16),
        sds((n_t, wide, width), bf16), sds((n_t, width, wide), bf16), sds((wide, wide), bf16),
        sds((8, wide), f32),
    ]
    chunk = lambda a: pl.BlockSpec((1,) + a.shape[1:], lambda p, n: (p * n, 0, 0))
    weight = lambda a: pl.BlockSpec((a.shape[0], 1) + a.shape[2:], lambda p, n: (0, n, 0, 0))
    return pl.pallas_call(
        feed_kernel,
        grid=(2, n_t),
        in_specs=[one(a) for a in (att, x, cot, ow, par)] + [weight(up), weight(down)],
        out_specs=[one(o) for o in outs[:3]] + [chunk(outs[3]), chunk(outs[4])] + [one(o) for o in outs[5:]],
        out_shape=outs,
        scratch_shapes=[
            pltpu.VMEM((rows, wide), f32), pltpu.VMEM((rows, wide), f32), pltpu.VMEM((rows, wide), f32),
            pltpu.VMEM((rows, wide), bf16), pltpu.VMEM((rows, wide), bf16),
            pltpu.VMEM((n_t, rows, width), bf16), pltpu.VMEM((n_t, rows, width), f32),
        ],
        compiler_params=pltpu.CompilerParams(vmem_limit_bytes=64 << 20),
        name="feed",
    )(att, x, cot, ow, par, up, down)
def add_rows(target, source, step=64):
    rows = target.shape[0]
    step = min(step, rows)
    while rows % step:
        step //= 2

    def body(i, _):
        at = span(i, step)
        target[at, :] = target[at, :] + source[at, :]
        return 0

    lax.fori_loop(0, rows // step, body, 0)


def orders(n_d):
    bits = n_d.bit_length() - 1
    return [list(range(bits)), list(range(bits - 1, -1, -1))]


def combos(bits):
    masks = [0]
    for b in bits:
        masks = masks + [m ^ (1 << b) for m in masks]
    return masks


def finish_kernel(
    n_d, n_t, sum_ref, x_ref, hid_ref, par_ref, vec_in, up_ref, down_ref, og_ref, ig_ref,
    bt_ref, vec_ref, up_out, down_out, og_out, ig_out,
    mine_up, mine_down, mine_og, mine_ig, side_up, side_down, side_og,
    hop_up, hop_down, hop_og, hop_ig, far_up, far_down, far_og, far_ig,
    full_up, full_down, full_og, full_ig,
    r_side, r_out, r_land, vec_now, vec_got, vec_far,
    s_load, s_side, r_sides, s_hop, r_hop, s_far, r_far, s_all, r_all, s_own, r_own,
    s_red, r_red, s_redside, r_redside, s_vec, r_vec,
):
    d, t = lax.axis_index("dp"), lax.axis_index("tensor")
    trees, rows, wide = x_ref.shape
    chips = n_t // 2
    near = chips // trees
    group = n_t // trees
    chip, core = t // 2, lax.rem(t, 2)
    other = 2 * chip + 1 - core
    line = [lax.rem(chip + k, chips) for k in range(1, chips)]
    dest = line + [chip]
    peers = [lax.rem(d + k, n_d) for k in range(1, n_d)]
    bits = n_d.bit_length() - 1
    barrier([(d, lax.rem(t + k, n_t)) for k in range(1, n_t)] + [(p, t) for p in peers])

    red_pairs = []
    for k, c in enumerate(dest):
        theirs = sum_ref.at[span(2 * c + 1 - core, rows), :]
        red_pairs.append(send(theirs, r_side.at[k], s_redside.at[k], r_redside.at[k], (d, other)))

    items = [
        (up_ref, mine_up, side_up, hop_up, far_up, full_up, up_out),
        (down_ref, mine_down, side_down, hop_down, far_down, full_down, down_out),
        (og_ref, mine_og, side_og, hop_og, far_og, full_og, og_out),
        (ig_ref, mine_ig, None, hop_ig, far_ig, full_ig, ig_out),
    ]
    units = [(n, k) for k in range(chips) for n in range(3)]
    units = units[:3] + [(3, i) for i in range(trees)] + units[3:]
    number = {u: i for i, u in enumerate(units)}
    loads, sides = {}, {}
    for u in units:
        n, k = u
        source, mine, side = items[n][:3]
        i = number[u]
        if n < 3:
            sides[u] = send(source.at[2 * dest[k] + 1 - core], side.at[k], s_side.at[i], r_sides.at[i], (d, other))
            loads[u] = pltpu.make_async_copy(source.at[2 * dest[k] + core], mine.at[k], s_load.at[i])
        else:
            loads[u] = pltpu.make_async_copy(source.at[k], mine.at[k], s_load.at[i])
        loads[u].start()

    red_copies = []
    for k, c in enumerate(line):
        red_pairs[k].wait_recv()
        r_out[k] = sum_ref[span(2 * c + core, rows), :] + r_side[k]
        red_copies.append(send(r_out.at[k], r_land.at[k], s_red.at[k], r_red.at[k], (d, 2 * c + core)))

    hops = {}

    def cut(n, k, part, stream):
        mine = items[n][1]
        height, width = mine.shape[1] // n_d, mine.shape[2] // (2 if n < 3 else 1)
        return mine.at[k, span(part, height), pl.ds(stream * width, width)]

    def streams(n, k):
        return orders(n_d) if n < 3 else [orders(n_d)[k % 2]]

    def begin(u):
        n, k = u
        loads[u].wait()
        if n < 3:
            sides[u].wait_recv()
            add_rows(items[n][1].at[k], items[n][2].at[k])
        hop(u, 0)

    def hop(u, step):
        n, k = u
        slot = 0 if step == 0 else n_d - (n_d >> step)
        for stream, order in enumerate(streams(n, k)):
            partner = lax.bitwise_xor(d, 1 << order[step])
            for j, m in enumerate(combos(order[step + 1 :])):
                i = (slot + j) * 2 + stream
                hops[u, step, stream, j] = send(
                    cut(n, k, lax.bitwise_xor(partner, m), stream),
                    items[n][3].at[k, i],
                    s_hop.at[number[u], i],
                    r_hop.at[number[u], i],
                    (partner, t),
                )

    def land(u, step):
        n, k = u
        slot = 0 if step == 0 else n_d - (n_d >> step)
        for stream, order in enumerate(streams(n, k)):
            for j, m in enumerate(combos(order[step + 1 :])):
                i = (slot + j) * 2 + stream
                hops[u, step, stream, j].wait_recv()
                add_rows(cut(n, k, lax.bitwise_xor(d, m), stream), items[n][3].at[k, i])
        if step + 1 < bits:
            hop(u, step + 1)
        else:
            away(u)

    fars = {}

    def piece(n, k):
        mine = items[n][1]
        return mine.at[k, span(d, mine.shape[1] // n_d), :]

    def owner(i):
        return lax.rem(t, group) * trees + i

    def away(u):
        n, k = u
        far = items[n][4]
        if n < 3:
            if k < chips - 1:
                fars[u] = send(piece(n, k), far.at[k], s_far.at[n, k], r_far.at[n, k], (d, 2 * dest[k] + core))
        else:
            here = t // group

            @pl.when(owner(k) != t)
            def _():
                send(piece(n, k), far.at[here], s_own.at[k], r_own.at[here], (d, owner(k)))

            @pl.when(owner(k) == t)
            def _():
                far[here] = piece(n, k)[...]

    def reduced():
        red_pairs[chips - 1].wait_recv()
        back = [None] * trees
        own = sum_ref[span(t, rows), :].astype(f32) + r_side[chips - 1].astype(f32)
        hit = chip // near
        x = x_ref[...].astype(f32)
        for k in range(chips - 1):
            red_copies[k].wait_recv()
        for tree in range(trees):
            e = jnp.where(hit == tree, own, 0.0)
            for k in range(chips - 1):
                source = lax.rem(chip + chips - 1 - k, chips)
                e = e + jnp.where(source // near == tree, r_land[k].astype(f32), 0.0)
            norm, r = ln_parts(x[tree])
            g, b = jnp.sum(e * norm, axis=0, keepdims=True), jnp.sum(e, axis=0, keepdims=True)
            bt_ref[tree] = (hid_ref[tree] + ln_back(e, norm, r, par_ref[6:7])).astype(bf16)
            back[tree] = (g, b)
        vec_now[0:6] = vec_in[0:6]
        vec_now[6:7] = sum(g for g, _ in back)
        vec_now[7:8] = sum(b for _, b in back)

    vec_partners = [(d, other)] + [(lax.bitwise_xor(d, 1 << b), t) for b in range(bits)]
    vec_copies = []

    def vec_step(i):
        if i > 0:
            vec_copies[i - 1].wait()
            vec_now[...] = vec_now[...] + vec_got[i - 1]
        if i < len(vec_partners):
            vec_got[len(vec_partners) + i] = vec_now[...]
            vec_copies.append(
                send(vec_got.at[len(vec_partners) + i], vec_got.at[i], s_vec.at[i], r_vec.at[i], vec_partners[i])
            )
        else:
            vec_far[chip] = vec_now[...]
            for k, c in enumerate(line):
                n = len(vec_partners) + k
                vec_copies.append(
                    send(vec_far.at[chip], vec_far.at[chip], s_vec.at[n], r_vec.at[n], (d, 2 * c + core))
                )

    count = len(units)
    vec_at = count - 1 - len(vec_partners)
    for i in range(count + bits):
        if i < count:
            begin(units[i])
        for step in range(bits):
            if 0 <= i - 1 - step < count:
                land(units[i - 1 - step], step)
        if i == vec_at - 1:
            reduced()
        if vec_at <= i <= vec_at + len(vec_partners):
            vec_step(i - vec_at)

    spreads = []
    for n in range(4):
        source, mine, side, hops_ref, far, full, out = items[n]
        height = full.shape[0] // n_d
        if n < 3:
            for k in range(chips - 1):
                fars[n, k].wait_recv()
            total = mine[chips - 1, span(d, height), :].astype(f32)
            for k in range(chips - 1):
                total = total + far[k].astype(f32)
        else:
            for j in range(trees):
                giver = j * group + t // trees

                @pl.when(giver != t)
                def _():
                    pltpu.make_async_remote_copy(
                        src_ref=far.at[j], dst_ref=far.at[j], send_sem=s_own.at[0], recv_sem=r_own.at[j],
                        device_id=(d, giver), device_id_type=MESH,
                    ).wait_recv()

            total = far[0].astype(f32)
            for j in range(1, trees):
                total = total + far[j].astype(f32)
        at = span(d, height)
        full[at, :] = total.astype(bf16)
        for j, p in enumerate(peers):
            spreads.append(send(full.at[at, :], full.at[at, :], s_all.at[n, j], r_all.at[n, j], (p, t)))
    for k in range(chips - 1):
        vec_copies[len(vec_partners) + k].wait()
    total = vec_far[0]
    for c in range(1, chips):
        total = total + vec_far[c]
    vec_ref[...] = total
    for n in range(4):
        full, out = items[n][5:7]
        for j in range(n_d - 1):
            spreads[n * (n_d - 1) + j].wait_recv()

        height = 64
        while full.shape[0] % height:
            height //= 2

        def widen(i, _):
            out[span(i, height), :] = full[span(i, height), :].astype(f32)
            return 0

        lax.fori_loop(0, full.shape[0] // height, widen, 0)

    for k in range(trees):

        @pl.when(owner(k) != t)
        def _():
            pltpu.make_async_remote_copy(
                src_ref=piece(3, k), dst_ref=piece(3, k), send_sem=s_own.at[k], recv_sem=r_own.at[0],
                device_id=(d, owner(k)), device_id_type=MESH,
            ).wait_send()

    for copy in red_pairs + red_copies + list(sides.values()) + list(hops.values()) + list(fars.values()) + spreads:
        copy.wait_send()


def finish(n_d, n_t, partial, x, hidden, par, vec, up_g, down_g, out_g, in_g):
    trees, rows, wide = x.shape
    chips = n_t // 2
    bits = n_d.bit_length() - 1
    dma = pltpu.SemaphoreType.DMA
    sds = jax.ShapeDtypeStruct
    any_ = pl.BlockSpec(memory_space=pl.ANY)
    shapes = [a.shape[1:] for a in (up_g, down_g, out_g, in_g)]
    counts = [chips] * 3 + [trees]
    vm = lambda lead, shape, kind=bf16: pltpu.VMEM(tuple(lead) + tuple(shape), kind)
    mine = [vm((c,), s) for c, s in zip(counts, shapes)]
    side = [vm((c,), s) for c, s in zip(counts[:3], shapes[:3])]
    slots = 2 * (n_d - 1)
    hop = [vm((c, slots), (s[0] // n_d, s[1] // 2)) for c, s in zip(counts[:3], shapes[:3])]
    hop.append(vm((trees, slots), (shapes[3][0] // n_d, shapes[3][1])))
    far = [vm((c,), (s[0] // n_d, s[1])) for c, s in zip([chips - 1] * 3 + [trees], shapes)]
    full = [vm((), s) for s in shapes]
    n_units = 3 * chips + trees
    partners = 1 + bits
    return pl.pallas_call(
        functools.partial(finish_kernel, n_d, n_t),
        in_specs=[VMEM] * 5 + [any_] * 4,
        out_specs=[VMEM] * 6,
        out_shape=[sds(x.shape, bf16), sds((8, wide), f32)] + [sds(s, f32) for s in shapes],
        scratch_shapes=mine + side + hop + far + full + [
            vm((chips, rows), (wide,)), vm((chips - 1, rows), (wide,)), vm((chips - 1, rows), (wide,)),
            vm((8,), (wide,), f32), vm((2 * partners, 8), (wide,), f32), vm((chips, 8), (wide,), f32),
            dma((n_units,)), dma((n_units,)), dma((n_units,)),
            dma((n_units, slots)), dma((n_units, slots)),
            dma((3, chips - 1)), dma((3, chips - 1)),
            dma((4, n_d - 1)), dma((4, n_d - 1)),
            dma((trees,)), dma((trees,)),
            dma((chips - 1,)), dma((chips - 1,)), dma((chips,)), dma((chips,)),
            dma((partners + chips - 1,)), dma((partners + chips - 1,)),
        ],
        compiler_params=pltpu.CompilerParams(
            collective_id=3, has_side_effects=True, vmem_limit_bytes=67043328
        ),
        name="finish",
    )(partial, x, hidden, par, vec, up_g, down_g, out_g, in_g)
def shards(
    n_d, n_t,
    tokens, cotangent, lengths, parents, first_gain, first_shift, in_weight, out_weight,
    second_gain, second_shift, third_gain, third_shift, up_weight, down_weight, fourth_gain, fourth_shift,
):
    trees, rows, wide = tokens.shape
    group = n_t // trees
    d, t = lax.axis_index("dp"), lax.axis_index("tensor")
    tree = t // group
    width = out_weight.shape[0]

    def part(w):
        return lax.dynamic_slice_in_dim(w, d * (w.shape[0] // n_d), w.shape[0] // n_d, 0)

    def everyone(w):
        full = lax.all_gather(part(w), ("dp", "tensor"), axis=0, tiled=False)
        return full.reshape((n_d, n_t) + full.shape[1:])

    out_all, up_all, down_all = everyone(out_weight), everyone(up_weight), everyone(down_weight)
    out_all = out_all.transpose(1, 0, 2, 3).reshape(-1, wide)

    mine = lambda a: lax.dynamic_index_in_dim(a, tree, 0, keepdims=False)
    cosine, sine, mq, mk = tables(mine(lengths), mine(parents), n_t * rows)

    x = tokens.astype(f32)
    normed = layer_norm(x, first_gain, first_shift)
    gathered, w = gather_tree(n_d, n_t, normed.astype(bf16), in_weight.transpose(1, 0, 2))
    w = w.transpose(1, 2, 0, 3).reshape(3, wide, -1)
    q, k, v, kt, vt = project(gathered, w, cosine, sine, mq, mk)
    attended, qb = attend(q, k, vt)
    att = exchange_heads(n_t, trees, attended, False)
    par = jnp.stack(
        [second_gain, second_shift, third_gain, third_shift, fourth_gain, fourth_shift, first_gain, first_shift]
    )
    flat = lambda a: a.reshape(trees * rows, a.shape[-1])
    output, back_hidden, back_att, up_g, down_g, out_g, vec = feed(
        flat(att), flat(tokens), flat(cotangent), out_all, par, up_all, down_all
    )
    d_heads = exchange_heads(n_t, trees, back_att.reshape(trees, rows, wide), True)
    back_mixed = attend_back(qb, k, v, kt, d_heads, attended, cosine, sine)
    w_flat = w.transpose(1, 0, 2).reshape(wide, -1)
    partial = lax.dot_general(back_mixed, w_flat, NT, preferred_element_type=f32).astype(bf16)
    in_part = lax.dot_general(gathered, back_mixed, TN, preferred_element_type=f32)
    in_part = in_part.astype(bf16).reshape(wide, 3, trees, width).transpose(2, 1, 0, 3)
    back_tokens, vec, up_sum, down_sum, out_sum, in_sum = finish(
        n_d, n_t, partial, tokens, back_hidden.reshape(x.shape), par, vec,
        up_g, down_g, out_g.reshape(n_t, width, wide), in_part.reshape(trees, 3 * wide, width),
    )
    return (
        output.reshape(tokens.shape),
        back_tokens,
        vec[6], vec[7],
        in_sum.reshape(3, wide, width).transpose(1, 0, 2),
        out_sum,
        vec[0], vec[1], vec[2], vec[3],
        up_sum,
        down_sum,
        vec[4], vec[5],
    )


def solution(mesh):
    in_specs = (
        P("dp", "tensor", None), P("dp", "tensor", None), P("dp", None), P("dp", None),
        P(), P(), P(None, None, "tensor"), P("tensor", None), P(), P(), P(), P(),
        P(None, "tensor"), P("tensor", None), P(), P(),
    )
    out_specs = (
        P("dp", "tensor", None), P("dp", "tensor", None), P(), P(), P(None, None, "tensor"),
        P("tensor", None), P(), P(), P(), P(), P(None, "tensor"), P("tensor", None), P(), P(),
    )
    run = functools.partial(shards, mesh.shape["dp"], mesh.shape["tensor"])
    return jax.shard_map(run, mesh=mesh, in_specs=in_specs, out_specs=out_specs, check_vma=False)
```

```python
import functools
import jax
import jax.numpy as jnp
from jax import lax
from jax.experimental import pallas as pl
from jax.experimental.pallas import tpu as pltpu
from jax.sharding import PartitionSpec as P

HEAD_DIM = 64
LANES = 128
VROWS = 80
BLOCK = 256
TRUNK = 512
SEGMENTS = 13

rope_base = 10000.0
norm_eps = 1e-05
masked_score = -1e30
f32, bf16 = jnp.float32, jnp.bfloat16
NN = (((1,), (0,)), ((), ()))
NT = (((1,), (1,)), ((), ()))
TN = (((0,), (0,)), ((), ()))
MESH = pl.DeviceIdType.MESH
VMEM = pl.BlockSpec(memory_space=pltpu.VMEM)
HBM = pl.BlockSpec(memory_space=pltpu.HBM)


def dot(a, b, dims=NN):
    return lax.dot_general(a, b, dims, preferred_element_type=f32)


def lane_of(shape):
    return lax.broadcasted_iota(jnp.int32, shape, len(shape) - 1)


def row_of(shape):
    return lax.broadcasted_iota(jnp.int32, shape, len(shape) - 2)


def span(i, n):
    return pl.ds(pl.multiple_of(i * n, n), n)


def split3(v):
    hi = v.astype(bf16).astype(f32)
    mid = (v - hi).astype(bf16).astype(f32)
    return hi, mid, v - hi - mid


def layer_norm(values, gain, shift):
    average = jnp.mean(values, axis=-1, keepdims=True)
    centered = values - average
    spread = jnp.mean(centered * centered, axis=-1, keepdims=True)
    return centered * lax.rsqrt(spread + norm_eps) * gain + shift


def tree_layout(tree_lengths, tree_parents, rows):
    seg_sizes = jnp.concatenate([jnp.full((1,), TRUNK, jnp.int32), tree_lengths])
    ends = jnp.cumsum(seg_sizes)
    starts = ends - seg_sizes
    places = jnp.arange(rows, dtype=jnp.int32)
    labels = jnp.arange(SEGMENTS, dtype=jnp.int32)
    segment = jnp.sum((places[:, None] >= ends[None, :]).astype(jnp.int32), axis=1)
    own_hot = (segment[:, None] == labels[None, :]).astype(jnp.int32)
    parent = jnp.sum(own_hot * tree_parents[None, :], axis=1)
    parent_hot = (parent[:, None] == labels[None, :]).astype(jnp.int32)
    grandparent = jnp.sum(parent_hot * tree_parents[None, :], axis=1)
    parent_size = jnp.sum(parent_hot * seg_sizes[None, :], axis=1)
    depth_start = jnp.where(segment > 0, TRUNK, 0).astype(jnp.int32) + jnp.where(
        parent > 0, parent_size, 0
    )
    position = places - jnp.sum(own_hot * starts[None, :], axis=1) + depth_start
    return (segment, parent, grandparent, position)


def tables(tree_lengths, tree_parents, rows):
    segment, parent, grand, position = tree_layout(tree_lengths, tree_parents, rows)
    lane = jnp.arange(LANES, dtype=jnp.int32)
    half = HEAD_DIM // 2
    inverse = rope_base ** (-(lane % half).astype(f32) * 2.0 / HEAD_DIM)
    angle = position.astype(f32)[:, None] * inverse[None, :]
    cosine = jnp.cos(angle)
    sine = jnp.where((lane % HEAD_DIM) < half, -1.0, 1.0)[None, :] * jnp.sin(angle)
    label = (lane - HEAD_DIM)[None, :]
    own = segment[:, None] == label
    path = own | (parent[:, None] == label) | (grand[:, None] == label)
    hidden = (label >= 0) & (label < SEGMENTS) & ~path
    queries = jnp.where(hidden, masked_score, 0.0).astype(f32)
    ones = (label >= 16) & (label < 19)
    keys = jnp.where(own | ones, 1.0, 0.0).astype(f32)
    return cosine, sine, queries, keys
def barrier(partners):
    semaphore = pltpu.get_barrier_semaphore()
    for partner in partners:
        pl.semaphore_signal(semaphore, inc=1, device_id=partner, device_id_type=MESH)
    pl.semaphore_wait(semaphore, len(partners))


def send(source, target, send_sem, recv_sem, device):
    copy = pltpu.make_async_remote_copy(
        src_ref=source,
        dst_ref=target,
        send_sem=send_sem,
        recv_sem=recv_sem,
        device_id=device,
        device_id_type=MESH,
    )
    copy.start()
    return copy


def orders(n_d):
    bits = n_d.bit_length() - 1
    return [list(range(bits)), list(range(bits - 1, -1, -1))]


def combos(bits):
    masks = [0]
    for b in bits:
        masks = masks + [m ^ (1 << b) for m in masks]
    return masks


class Spread:
    def __init__(self, n_d, n_t, shards, alls, sems):
        self.n_d, self.n_t, self.shards, self.alls = n_d, n_t, shards, alls
        self.zs, self.zr, self.ps, self.pr, self.ys, self.yr, self.own = sems
        self.d, self.t = lax.axis_index("dp"), lax.axis_index("tensor")
        self.chips = n_t // 2
        self.chip, self.core = self.t // 2, lax.rem(self.t, 2)
        self.other = 2 * self.chip + 1 - self.core
        self.bits = n_d.bit_length() - 1
        self.arrays = range(len(shards))

    @staticmethod
    def sems(count, n_d, n_t):
        dma = pltpu.SemaphoreType.DMA
        hops, slots = n_t // 2 - 1, 2 * (n_d - 1)
        z, p, y = (count, 2 * hops), (count, 2 * hops, slots), (count, 2 * hops + 1)
        return [dma(z), dma(z), dma(p), dma(p), dma(y), dma(y), dma((count,))]

    def exists(self, c):
        return (c >= 0) & (c < self.chips)

    def rows(self, a):
        return self.shards[a].shape[0] // self.n_d

    def slot(self, way, h):
        return h - 1 + (self.chips - 1 if way < 0 else 0)

    def remote(self, src, dst, ssem, rsem, device):
        return pltpu.make_async_remote_copy(
            src_ref=src, dst_ref=dst, send_sem=ssem, recv_sem=rsem, device_id=device, device_id_type=MESH
        )

    def along(self, a, way, h, arriving):
        source = self.chip - way * (h if arriving else h - 1)
        at = span(self.d, self.rows(a))
        dst = self.alls[a].at[2 * source + self.core, at]
        src = self.shards[a].at[at] if h == 1 and not arriving else dst
        peer = self.chip - way if arriving else self.chip + way
        i = self.slot(way, h)
        return self.remote(src, dst, self.zs.at[a, i], self.zr.at[a, i], (self.d, 2 * peer + self.core))

    def across(self, a, way, h, step, arriving):
        source = self.chip - way * h
        q, half = self.rows(a), self.shards[a].shape[1] // 2
        out = []
        for stream, order in enumerate(orders(self.n_d)):
            partner = lax.bitwise_xor(self.d, 1 << order[step])
            for j, m in enumerate(combos(order[:step])):
                block = lax.bitwise_xor(partner if arriving else self.d, m)
                ref = self.alls[a].at[2 * source + self.core, span(block, q), pl.ds(stream * half, half)]
                i = stream * (self.n_d - 1) + (1 << step) - 1 + j
                k = self.slot(way, h)
                out.append(self.remote(ref, ref, self.ps.at[a, k, i], self.pr.at[a, k, i], (partner, self.t)))
        return out

    def beside(self, a, way, h, arriving=False):
        source = self.chip - way * h
        ref = self.alls[a].at[2 * source + (1 - self.core if arriving else self.core)]
        k = self.slot(way, h)
        return self.remote(ref, ref, self.ys.at[a, k], self.yr.at[a, k], (self.d, self.other))

    def mine(self, a, arriving=False):
        k = 2 * (self.chips - 1)
        dst = self.alls[a].at[self.other if arriving else self.t]
        return self.remote(self.shards[a], dst, self.ys.at[a, k], self.yr.at[a, k], (self.d, self.other))

    def keep(self, a):
        return pltpu.make_async_copy(self.shards[a], self.alls[a].at[self.t], self.own.at[a])

    def begin(self):
        for way in (1, -1):

            @pl.when(self.exists(self.chip + way))
            def _():
                for a in self.arrays:
                    self.along(a, way, 1, False).start()

        for a in self.arrays:
            self.keep(a).start()
            self.mine(a).start()

    def phase(self, p, h):
        for way in (1, -1):

            @pl.when(self.exists(self.chip - way * h))
            def _():
                for a in self.arrays:
                    if p == 0:
                        self.along(a, way, h, True).wait_recv()
                        if h < self.chips - 1:

                            @pl.when(self.exists(self.chip + way))
                            def _():
                                self.along(a, way, h + 1, False).start()
                    else:
                        for copy in self.across(a, way, h, p - 1, True):
                            copy.wait_recv()
                    if p < self.bits:
                        for copy in self.across(a, way, h, p, False):
                            copy.start()
                    else:
                        self.beside(a, way, h).start()

    def groups(self):
        return self.chips - 1 + self.bits

    def group(self, g):
        for h in range(1, self.chips):
            if 0 <= g - (h - 1) <= self.bits:
                self.phase(g - (h - 1), h)

    def end(self):
        for h in range(1, self.chips):
            for way in (1, -1):

                @pl.when(self.exists(self.chip + way) & self.exists(self.chip - way * (h - 1)))
                def _():
                    for a in self.arrays:
                        self.along(a, way, h, False).wait_send()

                @pl.when(self.exists(self.chip - way * h))
                def _():
                    for a in self.arrays:
                        for step in range(self.bits):
                            for copy in self.across(a, way, h, step, False):
                                copy.wait_send()
                        self.beside(a, way, h).wait_send()
                        self.beside(a, way, h, True).wait_recv()

        for a in self.arrays:
            self.keep(a).wait()
            self.mine(a).wait_send()
            self.mine(a, True).wait_recv()


def gather_kernel(n_d, n_t, x_ref, w_ref, f_ref, o_ref, u_ref, all_ref, rs, ss, rb, sb, rw, sw, rp, sp, *sems):
    d, t = lax.axis_index("dp"), lax.axis_index("tensor")
    trees, rows, _ = x_ref.shape
    chips = n_t // 2
    group = n_t // trees
    chip, core = t // 2, lax.rem(t, 2)
    other = 2 * chip + 1 - core
    near = group // 2
    tree = t // group
    line = [lax.rem(chip + k, chips) for k in range(1, chips)]
    planes = [lax.rem(d + k, n_d) for k in range(1, n_d)]
    owners = [(j * group + t // trees) for j in range(trees)]
    givers = [lax.rem(t, group) * trees + i for i in range(trees)]
    barrier([(d, lax.rem(t + k, n_t)) for k in range(1, n_t)] + [(p, t) for p in planes])
    part = w_ref.shape[1] // n_d

    copies = []
    mine = w_ref.at[:, span(d, part), :]
    for j in range(trees):
        slot = u_ref.at[lax.rem(t, trees), :, span(d, part), :]

        @pl.when(owners[j] != t)
        def _():
            send(mine, slot, sw.at[j], rw.at[lax.rem(t, trees)], (d, owners[j]))

        @pl.when(owners[j] == t)
        def _():
            u_ref[lax.rem(t, trees), :, span(d, part), :] = w_ref[:, span(d, part), :]

    def block(c, k):
        return o_ref.at[span(2 * c + k, rows)]

    for k, c in enumerate(line):
        copies.append(send(x_ref.at[c // near], block(chip, core), ss.at[k], rs.at[k], (d, 2 * c + core)))
    weights = Spread(n_d, n_t, [f_ref], [all_ref], sems)
    weights.begin()
    o_ref[span(t, rows), :] = x_ref[tree]
    copies.append(send(x_ref.at[tree], block(chip, core), sb.at[chips - 1], rb.at[chips - 1], (d, other)))
    for i in range(trees):
        slot = u_ref.at[i, :, span(d, part), :]

        @pl.when(givers[i] != t)
        def _():
            pltpu.make_async_remote_copy(
                src_ref=mine, dst_ref=slot, send_sem=sw.at[0], recv_sem=rw.at[i],
                device_id=(d, givers[i]), device_id_type=MESH,
            ).wait_recv()

    mine_all = u_ref.at[:, :, span(d, part), :]
    for k, p in enumerate(planes):
        copies.append(send(mine_all, mine_all, sp.at[k], rp.at[k], (p, t)))
    for k in range(chips - 1):
        source = lax.rem(chip + chips - 1 - k, chips)
        copies[k].wait_recv()
        copies.append(send(block(source, core), block(source, core), sb.at[k], rb.at[k], (d, other)))
    for g in range(weights.groups()):
        weights.group(g)
    weights.end()
    for j in range(trees):

        @pl.when(owners[j] != t)
        def _():
            pltpu.make_async_remote_copy(
                src_ref=mine, dst_ref=mine, send_sem=sw.at[j], recv_sem=rw.at[0],
                device_id=(d, owners[j]), device_id_type=MESH,
            ).wait_send()

    for i, copy in enumerate(copies):
        if i < chips - 1:
            copy.wait_send()
        else:
            copy.wait()


def gather_tree(n_d, n_t, normed, weight, down):
    trees, rows, wide = normed.shape
    chips = n_t // 2
    dma = pltpu.SemaphoreType.DMA
    return pl.pallas_call(
        functools.partial(gather_kernel, n_d, n_t),
        in_specs=[VMEM] * 3,
        out_specs=[VMEM] * 2 + [HBM],
        out_shape=[
            jax.ShapeDtypeStruct((n_t * rows, wide), bf16),
            jax.ShapeDtypeStruct((trees,) + weight.shape, bf16),
            jax.ShapeDtypeStruct((n_t,) + down.shape, bf16),
        ],
        scratch_shapes=[
            dma((chips - 1,)), dma((chips - 1,)), dma((chips,)), dma((chips,)),
            dma((trees,)), dma((trees,)), dma((n_d - 1,)), dma((n_d - 1,)),
        ] + Spread.sems(1, n_d, n_t),
        compiler_params=pltpu.CompilerParams(collective_id=0, has_side_effects=True),
        name="gather_tree",
    )(normed, weight, down)


def heads_kernel(n_t, trees, x_ref, o_ref, ss, rs):
    d, t = lax.axis_index("dp"), lax.axis_index("tensor")
    group = n_t // trees
    others = [lax.rem(t + k, n_t) for k in range(1, n_t)]
    barrier([(d, o) for o in others])
    rows, width = x_ref.shape[1], x_ref.shape[2] // group
    cut = lambda o: x_ref.at[o // group, :, span(lax.rem(o, group), width)]
    place = o_ref.at[span(t, rows), :]
    copies = [
        send(cut(o), place, ss.at[k], rs.at[k], (d, o)) for k, o in enumerate(others)
    ]
    place[...] = cut(t)[...]
    for copy in copies:
        copy.wait()


def exchange_heads(n_t, trees, x):
    _, rows, wide = x.shape
    dma = pltpu.SemaphoreType.DMA
    return pl.pallas_call(
        functools.partial(heads_kernel, n_t, trees),
        in_specs=[VMEM],
        out_specs=VMEM,
        out_shape=jax.ShapeDtypeStruct((n_t * rows, wide * trees // n_t), bf16),
        scratch_shapes=[dma((n_t - 1,)), dma((n_t - 1,))],
        compiler_params=pltpu.CompilerParams(collective_id=2, has_side_effects=True),
        name="heads_back",
    )(x)


def qkv_kernel(x_ref, w_ref, cos_ref, sin_ref, mq_ref, mk_ref, q_ref, k_ref, v_ref, kt_ref, vt_ref):
    x = x_ref[...]
    heads = q_ref.shape[0]
    cosine, sine = cos_ref[...], sin_ref[...]
    mq, mk = mq_ref[...], mk_ref[...]
    lane = lane_of(cosine.shape)
    low = lax.rem(lane, HEAD_DIM) < HEAD_DIM // 2
    first = lane < HEAD_DIM
    mv = jnp.where((lane >= HEAD_DIM) & (lane < HEAD_DIM + 3), 1.0, 0.0)
    tail = jnp.where(row_of((VROWS - HEAD_DIM, x.shape[0])) == 0, 1.0, 0.0).astype(bf16)

    def both(slab):
        return slab, pltpu.roll(slab, HEAD_DIM, 1)

    def rotate(slab):
        partner = jnp.where(
            low, pltpu.roll(slab, LANES - HEAD_DIM // 2, 1), pltpu.roll(slab, HEAD_DIM // 2, 1)
        )
        return slab * cosine + partner * sine

    q_all, k_all, v_all = (dot(x, w_ref[i]) for i in range(3))
    for h in range(0, heads, 2):
        cols = slice(h * HEAD_DIM, (h + 2) * HEAD_DIM)
        for g, slab in enumerate(both(rotate(q_all[:, cols]) * HEAD_DIM**-0.5)):
            q_ref[h + g] = jnp.where(first, slab, mq).astype(bf16)
        keys = rotate(k_all[:, cols])
        for g, slab in enumerate(both(keys)):
            k_ref[h + g] = jnp.where(first, slab, mk).astype(bf16)
        flat = keys.T.astype(bf16)
        for g, slab in enumerate(both(v_all[:, cols])):
            v_ref[h + g] = jnp.where(first, slab, mv).astype(bf16)
        flat_v = v_all[:, cols].T.astype(bf16)
        for g in range(2):
            part = slice(g * HEAD_DIM, (g + 1) * HEAD_DIM)
            kt_ref[h + g] = flat[part]
            vt_ref[h + g, :HEAD_DIM] = flat_v[part]
            vt_ref[h + g, HEAD_DIM:] = tail


def project(x, w, cosine, sine, mq, mk):
    rows, wide = x.shape
    heads = w.shape[2] // HEAD_DIM
    table = pl.BlockSpec((BLOCK, LANES), lambda i: (i, 0))
    slab = pl.BlockSpec((heads, BLOCK, LANES), lambda i: (0, i, 0))
    shape = jax.ShapeDtypeStruct((heads, rows, LANES), bf16)
    return pl.pallas_call(
        qkv_kernel,
        grid=(rows // BLOCK,),
        in_specs=[
            pl.BlockSpec((BLOCK, wide), lambda i: (i, 0)),
            pl.BlockSpec(w.shape, lambda i: (0, 0, 0)),
            table, table, table, table,
        ],
        out_specs=[
            slab, slab, slab,
            pl.BlockSpec((heads, HEAD_DIM, BLOCK), lambda i: (0, 0, i)),
            pl.BlockSpec((heads, VROWS, BLOCK), lambda i: (0, 0, i)),
        ],
        out_shape=[
            shape, shape, shape,
            jax.ShapeDtypeStruct((heads, HEAD_DIM, rows), bf16),
            jax.ShapeDtypeStruct((heads, VROWS, rows), bf16),
        ],
        name="project",
    )(x, w, cosine, sine, mq, mk)


def fwd_kernel(
    n_d, n_t, trees, q_ref, k_ref, vt_ref, ow_ref, up_ref, o_ref, qb_ref, att_ref, ow_all, up_all,
    kept, ss, rs, here, *sems,
):
    qi = pl.program_id(0)
    steps = pl.num_programs(0)
    heads = q_ref.shape[0]
    row, col = row_of((BLOCK, BLOCK)), lane_of((BLOCK, BLOCK))
    d, t = lax.axis_index("dp"), lax.axis_index("tensor")
    group = n_t // trees
    rows, width = att_ref.shape[1], o_ref.shape[1]
    per = BLOCK // rows
    weights = Spread(n_d, n_t, [up_ref, ow_ref], [up_all, ow_all], sems)
    first_group = max(0, k_ref.shape[1] // BLOCK - 4)
    place = att_ref.at[t // group, :, span(lax.rem(t, group), width)]

    def outgoing(i, r, k):
        return pltpu.make_async_remote_copy(
            src_ref=kept.at[i, pl.ds(r * rows, rows)], dst_ref=place, send_sem=ss.at[k], recv_sem=rs.at[k],
            device_id=(d, lax.rem(t + k, n_t)), device_id_type=MESH,
        )

    @pl.when(qi == 0)
    def _():
        barrier(
            [(d, lax.rem(t + k, n_t)) for k in range(1, n_t)] + [(lax.rem(d + k, n_d), t) for k in range(1, n_d)]
        )
        weights.begin()

    for g in range(weights.groups()):
        if first_group + g < k_ref.shape[1] // BLOCK:

            @pl.when(qi == first_group + g)
            def _():
                weights.group(g)

    qs = [q_ref[h] for h in range(heads)]

    def scores(h, j):
        return dot(k_ref[h, span(j, BLOCK), :], qs[h], NT)

    state = []
    for h in range(heads):
        s = jnp.where(row <= col, scores(h, qi), masked_score)
        m = jnp.max(s, axis=0, keepdims=True)
        p = jnp.exp(s - m)
        state.append((m, dot(vt_ref[h, :, span(qi, BLOCK)], p.astype(bf16))))

    def step(j, carry):
        out = []
        for h in range(heads):
            m, acc = carry[h]
            s = scores(h, j)
            top = jnp.maximum(m, jnp.max(s, axis=0, keepdims=True))
            p = jnp.exp(s - top)
            acc = acc * jnp.exp(m - top) + dot(vt_ref[h, :, span(j, BLOCK)], p.astype(bf16))
            out.append((top, acc))
        return tuple(out)

    state = lax.fori_loop(0, qi, step, tuple(state))
    r = row_of((LANES, BLOCK))
    for h in range(0, heads, 2):
        outs = []
        for g in (h, h + 1):
            m, acc = state[g]
            total = acc[HEAD_DIM : HEAD_DIM + 1]
            outs.append(acc[:HEAD_DIM] / total)
            a, b, c = split3(-(m + jnp.log(total)))
            extra = jnp.where(r == 80, a, jnp.where(r == 81, b, jnp.where(r == 82, c, 0.0))).T
            qb_ref[g] = qs[g] + extra.astype(bf16)
        slab = jnp.concatenate(outs, axis=0).T.astype(bf16)
        o_ref[:, h * HEAD_DIM : (h + 2) * HEAD_DIM] = slab
        kept[qi, :, h * HEAD_DIM : (h + 2) * HEAD_DIM] = slab

    def local(r):
        return pltpu.make_async_copy(kept.at[t // per, pl.ds(r * rows, rows)], place, here.at[0])

    for r in range(per):
        k = lax.rem(qi * per + r + n_t - t, n_t)

        @pl.when(k != 0)
        def _():
            outgoing(qi, r, k).start()

        @pl.when(k == 0)
        def _():
            local(r).start()

    @pl.when(qi == steps - 1)
    def _():
        for g in range(k_ref.shape[1] // BLOCK - first_group, weights.groups()):
            weights.group(g)
        for k in range(1, n_t):
            outgoing(0, 0, k).wait()
        local(0).wait()
        weights.end()


def attend(n_d, n_t, trees, q, k, vt, ow, up):
    heads, rows, _ = q.shape
    slab = pl.BlockSpec((heads, rows, LANES), lambda i: (0, 0, 0))
    block = pl.BlockSpec((heads, BLOCK, LANES), lambda i: (0, i, 0))
    wide = heads * HEAD_DIM
    dma = pltpu.SemaphoreType.DMA
    sds = jax.ShapeDtypeStruct
    return pl.pallas_call(
        functools.partial(fwd_kernel, n_d, n_t, trees),
        grid=(rows // BLOCK,),
        in_specs=[block, slab, pl.BlockSpec((heads, VROWS, rows), lambda i: (0, 0, 0)), VMEM, VMEM],
        out_specs=[pl.BlockSpec((BLOCK, wide), lambda i: (i, 0)), block, HBM, HBM, HBM],
        out_shape=[
            sds((rows, wide), bf16),
            sds(q.shape, bf16),
            sds((trees, rows // n_t, wide * n_t // trees), bf16),
            sds((n_t,) + ow.shape, bf16),
            sds((n_t,) + up.shape, bf16),
        ],
        scratch_shapes=[
            pltpu.VMEM((rows // BLOCK, BLOCK, wide), bf16), dma((n_t,)), dma((n_t,)), dma((1,)),
        ] + Spread.sems(2, n_d, n_t),
        compiler_params=pltpu.CompilerParams(collective_id=1, has_side_effects=True),
        name="attend",
    )(q, k, vt, ow, up)


def bwd_kernel(q_ref, k_ref, v_ref, kt_ref, d_ref, o_ref, cos_ref, sin_ref, m_ref, sums, wide):
    j = pl.program_id(0)
    heads, rows, _ = q_ref.shape
    nq = rows // BLOCK
    row, col = row_of((BLOCK, BLOCK)), lane_of((BLOCK, BLOCK))
    lane = lane_of((BLOCK, LANES))
    first = lane < HEAD_DIM

    @pl.when(j == 0)
    def _():
        sums[...] = jnp.zeros_like(sums)

        def widen(i, _):
            at = span(i, BLOCK)
            for h in range(0, heads, 2):
                cols = slice(h * HEAD_DIM, (h + 2) * HEAD_DIM)
                slab = d_ref[at, cols].astype(f32)
                prod = slab * o_ref[at, cols].astype(f32)
                for g, (s, mine) in enumerate(((slab, first), (pltpu.roll(slab, HEAD_DIM, 1), ~first))):
                    inner = -jnp.sum(jnp.where(mine, prod, 0.0), axis=1, keepdims=True)
                    a, b, c = split3(inner)
                    n = HEAD_DIM
                    tail = jnp.where(lane == n, a, jnp.where(lane == n + 1, b, jnp.where(lane == n + 2, c, 0.0)))
                    wide[h + g, at, :] = jnp.where(first, s, tail).astype(bf16)
            return 0

        lax.fori_loop(0, nq, widen, 0)

    ks = [k_ref[h] for h in range(heads)]
    vs = [v_ref[h] for h in range(heads)]
    kts = [kt_ref[h] for h in range(heads)]

    def pair(h, i, mask):
        at = span(i, BLOCK)
        q = q_ref[h, at, :]
        d = wide[h, at, :]
        s = dot(ks[h], q, NT)
        if mask:
            s = jnp.where(row <= col, s, masked_score)
        p = jnp.exp(s)
        back = (p * dot(vs[h], d, NT)).astype(bf16)
        sums[h, :, at] += dot(kts[h], back)
        return dot(back, q), dot(p.astype(bf16), d)

    def step(i, carry):
        out = []
        for h in range(heads):
            dk, dv = pair(h, i, False)
            out.append((carry[h][0] + dk, carry[h][1] + dv))
        return tuple(out)

    state = tuple(pair(h, j, True) for h in range(heads))
    state = lax.fori_loop(j + 1, nq, step, state)

    def join(a, b):
        return jnp.where(first, a, pltpu.roll(b, HEAD_DIM, 1))

    cosine, sine = cos_ref[...], sin_ref[...]
    low = lax.rem(lane, HEAD_DIM) < HEAD_DIM // 2

    def unrotate(slab):
        partner = jnp.where(
            low, pltpu.roll(slab, LANES - HEAD_DIM // 2, 1), pltpu.roll(slab, HEAD_DIM // 2, 1)
        )
        return slab * cosine - partner * sine

    at = span(j, BLOCK)
    total = heads * HEAD_DIM
    for h in range(0, heads, 2):
        dq = jnp.concatenate([sums[h, :, at], sums[h + 1, :, at]], axis=0).T * HEAD_DIM**-0.5
        dk = join(state[h][0], state[h + 1][0])
        dv = join(state[h][1], state[h + 1][1])
        for n, part in enumerate((unrotate(dq), unrotate(dk), dv)):
            begin = n * total + h * HEAD_DIM
            m_ref[:, begin : begin + 2 * HEAD_DIM] = part.astype(bf16)


def attend_back(q, k, v, kt, d, o, cosine, sine):
    heads, rows, _ = q.shape
    whole = lambda a: pl.BlockSpec(a.shape, lambda j: (0,) * a.ndim)
    block = pl.BlockSpec((heads, BLOCK, LANES), lambda j: (0, j, 0))
    table = pl.BlockSpec((BLOCK, LANES), lambda j: (j, 0))
    return pl.pallas_call(
        bwd_kernel,
        grid=(rows // BLOCK,),
        in_specs=[
            whole(q), block, block,
            pl.BlockSpec((heads, HEAD_DIM, BLOCK), lambda j: (0, 0, j)),
            whole(d), whole(o), table, table,
        ],
        out_specs=pl.BlockSpec((BLOCK, 3 * heads * HEAD_DIM), lambda j: (j, 0)),
        out_shape=jax.ShapeDtypeStruct((rows, 3 * heads * HEAD_DIM), bf16),
        scratch_shapes=[
            pltpu.VMEM((heads, HEAD_DIM, rows), f32),
            pltpu.VMEM((heads, rows, LANES), bf16),
        ],
        name="attend_back",
    )(q, k, v, kt, d, o, cosine, sine)


def ln_parts(v):
    centered = v - jnp.mean(v, axis=-1, keepdims=True)
    r = lax.rsqrt(jnp.mean(centered * centered, axis=-1, keepdims=True) + norm_eps)
    return centered * r, r


def ln_back(e, n, r, gain):
    f = e * gain
    return r * (f - jnp.mean(f, axis=-1, keepdims=True) - n * jnp.mean(f * n, axis=-1, keepdims=True))


def feed_kernel(
    att_ref, x_ref, cot_ref, ow_ref, par_ref, up_ref, down_ref,
    out_ref, hid_ref, ba_ref, upg_ref, downg_ref, outg_ref, vec_ref,
    hidden, branch, acc, feed_in, back_feed, active, slope,
):
    phase, n = pl.program_id(0), pl.program_id(1)
    last = pl.num_programs(1) - 1
    par = lambda i: par_ref[i : i + 1]
    total = lambda v: jnp.sum(v, axis=0, keepdims=True)

    @pl.when((phase == 0) & (n == 0))
    def _():
        b = dot(att_ref[...], ow_ref[...])
        branch[...] = b
        h = x_ref[...].astype(f32) + ln_parts(b)[0] * par(0) + par(1)
        hidden[...] = h
        feed_in[...] = (ln_parts(h)[0] * par(2) + par(3)).astype(bf16)
        acc[...] = jnp.zeros_like(acc)

    up, down = up_ref[0], down_ref[0]

    @pl.when(phase == 0)
    def _():
        u = dot(feed_in[...], up)
        t = jnp.tanh(0.7978845608028654 * (u + 0.044715 * u * u * u))
        half = 0.5 * (1.0 + t)
        a = (u * half).astype(bf16)
        active[n] = a
        slope[n] = half + 0.5 * u * (1.0 - t * t) * (
            0.7978845608028654 * (1.0 + 3 * 0.044715 * u * u)
        )
        acc[...] += dot(a, down)

    @pl.when((phase == 1) & (n == 0))
    def _():
        e = cot_ref[...].astype(f32)
        norm, r = ln_parts(acc[...])
        out_ref[...] = (hidden[...] + norm * par(4) + par(5)).astype(bf16)
        vec_ref[4:5] = total(e * norm)
        vec_ref[5:6] = total(e)
        back_feed[...] = ln_back(e, norm, r, par(4)).astype(bf16)
        acc[...] = jnp.zeros_like(acc)

    @pl.when(phase == 1)
    def _():
        b = back_feed[...]
        upper = (dot(b, down, NT) * slope[n]).astype(bf16)
        acc[...] += dot(upper, up, NT)
        downg_ref[0] = dot(active[n], b, TN).astype(bf16)
        upg_ref[0] = dot(feed_in[...], upper, TN).astype(bf16)

    @pl.when((phase == 1) & (n == last))
    def _():
        e = acc[...]
        norm, r = ln_parts(hidden[...])
        vec_ref[2:3] = total(e * norm)
        vec_ref[3:4] = total(e)
        h = cot_ref[...].astype(f32) + ln_back(e, norm, r, par(2))
        hid_ref[...] = h
        norm, r = ln_parts(branch[...])
        vec_ref[0:1] = total(h * norm)
        vec_ref[1:2] = total(h)
        b = ln_back(h, norm, r, par(0)).astype(bf16)
        ba_ref[...] = dot(b, ow_ref[...], NT).astype(bf16)
        outg_ref[...] = dot(att_ref[...], b, TN).astype(bf16)


def feed(att, x, cot, ow, par, up, down):
    rows, wide = att.shape
    n_t, _, width = up.shape
    one = lambda a: pl.BlockSpec(a.shape, lambda p, n: (0,) * len(a.shape), pipeline_mode=pl.Buffered(1))
    sds = jax.ShapeDtypeStruct
    outs = [
        sds((rows, wide), bf16), sds((rows, wide), f32), sds((rows, wide), bf16),
        sds((n_t, wide, width), bf16), sds((n_t, width, wide), bf16), sds((wide, wide), bf16),
        sds((8, wide), f32),
    ]
    chunk = lambda a: pl.BlockSpec((1,) + a.shape[1:], lambda p, n: (p * n, 0, 0))
    weight = lambda a: pl.BlockSpec((1,) + a.shape[1:], lambda p, n: (n, 0, 0))
    return pl.pallas_call(
        feed_kernel,
        grid=(2, n_t),
        in_specs=[one(a) for a in (att, x, cot, ow, par)] + [weight(up), weight(down)],
        out_specs=[one(o) for o in outs[:3]] + [chunk(outs[3]), chunk(outs[4])] + [one(o) for o in outs[5:]],
        out_shape=outs,
        scratch_shapes=[
            pltpu.VMEM((rows, wide), f32), pltpu.VMEM((rows, wide), f32), pltpu.VMEM((rows, wide), f32),
            pltpu.VMEM((rows, wide), bf16), pltpu.VMEM((rows, wide), bf16),
            pltpu.VMEM((n_t, rows, width), bf16), pltpu.VMEM((n_t, rows, width), f32),
        ],
        compiler_params=pltpu.CompilerParams(vmem_limit_bytes=64 << 20),
        name="feed",
    )(att, x, cot, ow, par, up, down)
def add_rows(target, source, step=64):
    rows = target.shape[0]
    step = min(step, rows)
    while rows % step:
        step //= 2

    def body(i, _):
        at = span(i, step)
        target[at, :] = target[at, :] + source[at, :]
        return 0

    lax.fori_loop(0, rows // step, body, 0)


def finish_kernel(
    n_d, n_t, sum_ref, x_ref, hid_ref, par_ref, vec_in, up_ref, down_ref, og_ref, ig_ref,
    bt_ref, vec_ref, up_out, down_out, og_out, ig_out,
    mine_up, mine_down, mine_og, mine_ig, side_up, side_down, side_og,
    hop_up, hop_down, hop_og, hop_ig, far_up, far_down, far_og, far_ig,
    full_up, full_down, full_og, full_ig,
    r_side, r_out, r_land, vec_now, vec_got, vec_far,
    s_load, s_side, r_sides, s_hop, r_hop, s_far, r_far, s_all, r_all, s_own, r_own,
    s_red, r_red, s_redside, r_redside, s_vec, r_vec,
):
    d, t = lax.axis_index("dp"), lax.axis_index("tensor")
    trees, rows, wide = x_ref.shape
    chips = n_t // 2
    near = chips // trees
    group = n_t // trees
    chip, core = t // 2, lax.rem(t, 2)
    other = 2 * chip + 1 - core
    line = [lax.rem(chip + k, chips) for k in range(1, chips)]
    dest = line + [chip]
    peers = [lax.rem(d + k, n_d) for k in range(1, n_d)]
    bits = n_d.bit_length() - 1
    barrier([(d, lax.rem(t + k, n_t)) for k in range(1, n_t)] + [(p, t) for p in peers])

    red_pairs = []
    for k, c in enumerate(dest):
        theirs = sum_ref.at[span(2 * c + 1 - core, rows), :]
        red_pairs.append(send(theirs, r_side.at[k], s_redside.at[k], r_redside.at[k], (d, other)))

    items = [
        (up_ref, mine_up, side_up, hop_up, far_up, full_up, up_out),
        (down_ref, mine_down, side_down, hop_down, far_down, full_down, down_out),
        (og_ref, mine_og, side_og, hop_og, far_og, full_og, og_out),
        (ig_ref, mine_ig, None, hop_ig, far_ig, full_ig, ig_out),
    ]
    units = [(n, k) for k in range(chips) for n in range(3)]
    units = units[:3] + [(3, i) for i in range(trees)] + units[3:]
    number = {u: i for i, u in enumerate(units)}
    loads, sides = {}, {}
    for u in units:
        n, k = u
        source, mine, side = items[n][:3]
        i = number[u]
        if n < 3:
            sides[u] = send(source.at[2 * dest[k] + 1 - core], side.at[k], s_side.at[i], r_sides.at[i], (d, other))
            loads[u] = pltpu.make_async_copy(source.at[2 * dest[k] + core], mine.at[k], s_load.at[i])
        else:
            loads[u] = pltpu.make_async_copy(source.at[k], mine.at[k], s_load.at[i])
        loads[u].start()

    red_copies = []
    for k, c in enumerate(line):
        red_pairs[k].wait_recv()
        r_out[k] = sum_ref[span(2 * c + core, rows), :] + r_side[k]
        red_copies.append(send(r_out.at[k], r_land.at[k], s_red.at[k], r_red.at[k], (d, 2 * c + core)))

    hops = {}

    def cut(n, k, part, stream):
        mine = items[n][1]
        height, width = mine.shape[1] // n_d, mine.shape[2] // (2 if n < 3 else 1)
        return mine.at[k, span(part, height), pl.ds(stream * width, width)]

    def streams(n, k):
        return orders(n_d) if n < 3 else [orders(n_d)[k % 2]]

    def begin(u):
        n, k = u
        loads[u].wait()
        if n < 3:
            sides[u].wait_recv()
            add_rows(items[n][1].at[k], items[n][2].at[k])
        hop(u, 0)

    def hop(u, step):
        n, k = u
        slot = 0 if step == 0 else n_d - (n_d >> step)
        for stream, order in enumerate(streams(n, k)):
            partner = lax.bitwise_xor(d, 1 << order[step])
            for j, m in enumerate(combos(order[step + 1 :])):
                i = (slot + j) * 2 + stream
                hops[u, step, stream, j] = send(
                    cut(n, k, lax.bitwise_xor(partner, m), stream),
                    items[n][3].at[k, i],
                    s_hop.at[number[u], i],
                    r_hop.at[number[u], i],
                    (partner, t),
                )

    def land(u, step):
        n, k = u
        slot = 0 if step == 0 else n_d - (n_d >> step)
        for stream, order in enumerate(streams(n, k)):
            for j, m in enumerate(combos(order[step + 1 :])):
                i = (slot + j) * 2 + stream
                hops[u, step, stream, j].wait_recv()
                add_rows(cut(n, k, lax.bitwise_xor(d, m), stream), items[n][3].at[k, i])
        if step + 1 < bits:
            hop(u, step + 1)
        else:
            away(u)

    fars = {}

    def piece(n, k):
        mine = items[n][1]
        return mine.at[k, span(d, mine.shape[1] // n_d), :]

    def owner(i):
        return lax.rem(t, group) * trees + i

    def away(u):
        n, k = u
        far = items[n][4]
        if n < 3:
            if k < chips - 1:
                fars[u] = send(piece(n, k), far.at[k], s_far.at[n, k], r_far.at[n, k], (d, 2 * dest[k] + core))
        else:
            here = t // group

            @pl.when(owner(k) != t)
            def _():
                send(piece(n, k), far.at[here], s_own.at[k], r_own.at[here], (d, owner(k)))

            @pl.when(owner(k) == t)
            def _():
                far[here] = piece(n, k)[...]

    def reduced():
        red_pairs[chips - 1].wait_recv()
        back = [None] * trees
        own = sum_ref[span(t, rows), :].astype(f32) + r_side[chips - 1].astype(f32)
        hit = chip // near
        x = x_ref[...].astype(f32)
        for k in range(chips - 1):
            red_copies[k].wait_recv()
        for tree in range(trees):
            e = jnp.where(hit == tree, own, 0.0)
            for k in range(chips - 1):
                source = lax.rem(chip + chips - 1 - k, chips)
                e = e + jnp.where(source // near == tree, r_land[k].astype(f32), 0.0)
            norm, r = ln_parts(x[tree])
            g, b = jnp.sum(e * norm, axis=0, keepdims=True), jnp.sum(e, axis=0, keepdims=True)
            bt_ref[tree] = (hid_ref[tree] + ln_back(e, norm, r, par_ref[6:7])).astype(bf16)
            back[tree] = (g, b)
        vec_now[0:6] = vec_in[0:6]
        vec_now[6:7] = sum(g for g, _ in back)
        vec_now[7:8] = sum(b for _, b in back)

    vec_partners = [(d, other)] + [(lax.bitwise_xor(d, 1 << b), t) for b in range(bits)]
    vec_copies = []

    def vec_step(i):
        if i > 0:
            vec_copies[i - 1].wait()
            vec_now[...] = vec_now[...] + vec_got[i - 1]
        if i < len(vec_partners):
            vec_got[len(vec_partners) + i] = vec_now[...]
            vec_copies.append(
                send(vec_got.at[len(vec_partners) + i], vec_got.at[i], s_vec.at[i], r_vec.at[i], vec_partners[i])
            )
        else:
            vec_far[chip] = vec_now[...]
            for k, c in enumerate(line):
                n = len(vec_partners) + k
                vec_copies.append(
                    send(vec_far.at[chip], vec_far.at[chip], s_vec.at[n], r_vec.at[n], (d, 2 * c + core))
                )

    count = len(units)
    vec_at = count - 1 - len(vec_partners)
    for i in range(count + bits):
        if i < count:
            begin(units[i])
        for step in range(bits):
            if 0 <= i - 1 - step < count:
                land(units[i - 1 - step], step)
        if i == vec_at - 1:
            reduced()
        if vec_at <= i <= vec_at + len(vec_partners):
            vec_step(i - vec_at)

    spreads = []
    for n in range(4):
        source, mine, side, hops_ref, far, full, out = items[n]
        height = full.shape[0] // n_d
        if n < 3:
            for k in range(chips - 1):
                fars[n, k].wait_recv()
            total = mine[chips - 1, span(d, height), :].astype(f32)
            for k in range(chips - 1):
                total = total + far[k].astype(f32)
        else:
            for j in range(trees):
                giver = j * group + t // trees

                @pl.when(giver != t)
                def _():
                    pltpu.make_async_remote_copy(
                        src_ref=far.at[j], dst_ref=far.at[j], send_sem=s_own.at[0], recv_sem=r_own.at[j],
                        device_id=(d, giver), device_id_type=MESH,
                    ).wait_recv()

            total = far[0].astype(f32)
            for j in range(1, trees):
                total = total + far[j].astype(f32)
        at = span(d, height)
        full[at, :] = total.astype(bf16)
        for j, p in enumerate(peers):
            spreads.append(send(full.at[at, :], full.at[at, :], s_all.at[n, j], r_all.at[n, j], (p, t)))
    for k in range(chips - 1):
        vec_copies[len(vec_partners) + k].wait()
    total = vec_far[0]
    for c in range(1, chips):
        total = total + vec_far[c]
    vec_ref[...] = total
    for n in range(4):
        full, out = items[n][5:7]
        for j in range(n_d - 1):
            spreads[n * (n_d - 1) + j].wait_recv()

        height = 64
        while full.shape[0] % height:
            height //= 2

        def widen(i, _):
            out[span(i, height), :] = full[span(i, height), :].astype(f32)
            return 0

        lax.fori_loop(0, full.shape[0] // height, widen, 0)

    for k in range(trees):

        @pl.when(owner(k) != t)
        def _():
            pltpu.make_async_remote_copy(
                src_ref=piece(3, k), dst_ref=piece(3, k), send_sem=s_own.at[k], recv_sem=r_own.at[0],
                device_id=(d, owner(k)), device_id_type=MESH,
            ).wait_send()

    for copy in red_pairs + red_copies + list(sides.values()) + list(hops.values()) + list(fars.values()) + spreads:
        copy.wait_send()


def finish(n_d, n_t, partial, x, hidden, par, vec, up_g, down_g, out_g, in_g):
    trees, rows, wide = x.shape
    chips = n_t // 2
    bits = n_d.bit_length() - 1
    dma = pltpu.SemaphoreType.DMA
    sds = jax.ShapeDtypeStruct
    any_ = pl.BlockSpec(memory_space=pl.ANY)
    shapes = [a.shape[1:] for a in (up_g, down_g, out_g, in_g)]
    counts = [chips] * 3 + [trees]
    vm = lambda lead, shape, kind=bf16: pltpu.VMEM(tuple(lead) + tuple(shape), kind)
    mine = [vm((c,), s) for c, s in zip(counts, shapes)]
    side = [vm((c,), s) for c, s in zip(counts[:3], shapes[:3])]
    slots = 2 * (n_d - 1)
    hop = [vm((c, slots), (s[0] // n_d, s[1] // 2)) for c, s in zip(counts[:3], shapes[:3])]
    hop.append(vm((trees, slots), (shapes[3][0] // n_d, shapes[3][1])))
    far = [vm((c,), (s[0] // n_d, s[1])) for c, s in zip([chips - 1] * 3 + [trees], shapes)]
    full = [vm((), s) for s in shapes]
    n_units = 3 * chips + trees
    partners = 1 + bits
    return pl.pallas_call(
        functools.partial(finish_kernel, n_d, n_t),
        in_specs=[VMEM] * 5 + [any_] * 4,
        out_specs=[VMEM] * 6,
        out_shape=[sds(x.shape, bf16), sds((8, wide), f32)] + [sds(s, f32) for s in shapes],
        scratch_shapes=mine + side + hop + far + full + [
            vm((chips, rows), (wide,)), vm((chips - 1, rows), (wide,)), vm((chips - 1, rows), (wide,)),
            vm((8,), (wide,), f32), vm((2 * partners, 8), (wide,), f32), vm((chips, 8), (wide,), f32),
            dma((n_units,)), dma((n_units,)), dma((n_units,)),
            dma((n_units, slots)), dma((n_units, slots)),
            dma((3, chips - 1)), dma((3, chips - 1)),
            dma((4, n_d - 1)), dma((4, n_d - 1)),
            dma((trees,)), dma((trees,)),
            dma((chips - 1,)), dma((chips - 1,)), dma((chips,)), dma((chips,)),
            dma((partners + chips - 1,)), dma((partners + chips - 1,)),
        ],
        compiler_params=pltpu.CompilerParams(
            collective_id=3, has_side_effects=True, vmem_limit_bytes=67043328
        ),
        name="finish",
    )(partial, x, hidden, par, vec, up_g, down_g, out_g, in_g)
def shards(
    n_d, n_t,
    tokens, cotangent, lengths, parents, first_gain, first_shift, in_weight, out_weight,
    second_gain, second_shift, third_gain, third_shift, up_weight, down_weight, fourth_gain, fourth_shift,
):
    trees, rows, wide = tokens.shape
    group = n_t // trees
    d, t = lax.axis_index("dp"), lax.axis_index("tensor")
    tree = t // group
    width = out_weight.shape[0]

    mine = lambda a: lax.dynamic_index_in_dim(a, tree, 0, keepdims=False)
    cosine, sine, mq, mk = tables(mine(lengths), mine(parents), n_t * rows)

    x = tokens.astype(f32)
    normed = layer_norm(x, first_gain, first_shift)
    gathered, w, down_all = gather_tree(
        n_d, n_t, normed.astype(bf16), in_weight.transpose(1, 0, 2), down_weight
    )
    w = w.transpose(1, 2, 0, 3).reshape(3, wide, -1)
    q, k, v, kt, vt = project(gathered, w, cosine, sine, mq, mk)
    attended, qb, att, out_all, up_all = attend(n_d, n_t, trees, q, k, vt, out_weight, up_weight)
    par = jnp.stack(
        [second_gain, second_shift, third_gain, third_shift, fourth_gain, fourth_shift, first_gain, first_shift]
    )
    flat = lambda a: a.reshape(trees * rows, a.shape[-1])
    output, back_hidden, back_att, up_g, down_g, out_g, vec = feed(
        flat(att), flat(tokens), flat(cotangent), out_all.reshape(-1, wide), par, up_all, down_all
    )
    d_heads = exchange_heads(n_t, trees, back_att.reshape(trees, rows, wide))
    back_mixed = attend_back(qb, k, v, kt, d_heads, attended, cosine, sine)
    w_flat = w.transpose(1, 0, 2).reshape(wide, -1)
    partial = lax.dot_general(back_mixed, w_flat, NT, preferred_element_type=f32).astype(bf16)
    in_part = lax.dot_general(gathered, back_mixed, TN, preferred_element_type=f32)
    in_part = in_part.astype(bf16).reshape(wide, 3, trees, width).transpose(2, 1, 0, 3)
    back_tokens, vec, up_sum, down_sum, out_sum, in_sum = finish(
        n_d, n_t, partial, tokens, back_hidden.reshape(x.shape), par, vec,
        up_g, down_g, out_g.reshape(n_t, width, wide), in_part.reshape(trees, 3 * wide, width),
    )
    return (
        output.reshape(tokens.shape),
        back_tokens,
        vec[6], vec[7],
        in_sum.reshape(3, wide, width).transpose(1, 0, 2),
        out_sum,
        vec[0], vec[1], vec[2], vec[3],
        up_sum,
        down_sum,
        vec[4], vec[5],
    )


def solution(mesh):
    in_specs = (
        P("dp", "tensor", None), P("dp", "tensor", None), P("dp", None), P("dp", None),
        P(), P(), P(None, None, "tensor"), P("tensor", None), P(), P(), P(), P(),
        P(None, "tensor"), P("tensor", None), P(), P(),
    )
    out_specs = (
        P("dp", "tensor", None), P("dp", "tensor", None), P(), P(), P(None, None, "tensor"),
        P("tensor", None), P(), P(), P(), P(), P(None, "tensor"), P("tensor", None), P(), P(),
    )
    run = functools.partial(shards, mesh.shape["dp"], mesh.shape["tensor"])
    return jax.shard_map(run, mesh=mesh, in_specs=in_specs, out_specs=out_specs, check_vma=False)
```

```python
import functools
import jax
import jax.numpy as jnp
from jax import lax
from jax.experimental import pallas as pl
from jax.experimental.pallas import tpu as pltpu
from jax.sharding import PartitionSpec as P

HEAD_DIM = 64
LANES = 128
VROWS = 80
BLOCK = 256
TRUNK = 512
SEGMENTS = 13

rope_base = 10000.0
norm_eps = 1e-05
masked_score = -1e30
f32, bf16 = jnp.float32, jnp.bfloat16
NN = (((1,), (0,)), ((), ()))
NT = (((1,), (1,)), ((), ()))
TN = (((0,), (0,)), ((), ()))
MESH = pl.DeviceIdType.MESH
VMEM = pl.BlockSpec(memory_space=pltpu.VMEM)
HBM = pl.BlockSpec(memory_space=pltpu.HBM)


def dot(a, b, dims=NN):
    return lax.dot_general(a, b, dims, preferred_element_type=f32)


def lane_of(shape):
    return lax.broadcasted_iota(jnp.int32, shape, len(shape) - 1)


def row_of(shape):
    return lax.broadcasted_iota(jnp.int32, shape, len(shape) - 2)


def span(i, n):
    return pl.ds(pl.multiple_of(i * n, n), n)


def split3(v):
    hi = v.astype(bf16).astype(f32)
    mid = (v - hi).astype(bf16).astype(f32)
    return hi, mid, v - hi - mid


def layer_norm(values, gain, shift):
    average = jnp.mean(values, axis=-1, keepdims=True)
    centered = values - average
    spread = jnp.mean(centered * centered, axis=-1, keepdims=True)
    return centered * lax.rsqrt(spread + norm_eps) * gain + shift


def tree_layout(tree_lengths, tree_parents, rows):
    seg_sizes = jnp.concatenate([jnp.full((1,), TRUNK, jnp.int32), tree_lengths])
    ends = jnp.cumsum(seg_sizes)
    starts = ends - seg_sizes
    places = jnp.arange(rows, dtype=jnp.int32)
    labels = jnp.arange(SEGMENTS, dtype=jnp.int32)
    segment = jnp.sum((places[:, None] >= ends[None, :]).astype(jnp.int32), axis=1)
    own_hot = (segment[:, None] == labels[None, :]).astype(jnp.int32)
    parent = jnp.sum(own_hot * tree_parents[None, :], axis=1)
    parent_hot = (parent[:, None] == labels[None, :]).astype(jnp.int32)
    grandparent = jnp.sum(parent_hot * tree_parents[None, :], axis=1)
    parent_size = jnp.sum(parent_hot * seg_sizes[None, :], axis=1)
    depth_start = jnp.where(segment > 0, TRUNK, 0).astype(jnp.int32) + jnp.where(
        parent > 0, parent_size, 0
    )
    position = places - jnp.sum(own_hot * starts[None, :], axis=1) + depth_start
    return (segment, parent, grandparent, position)


def tables(tree_lengths, tree_parents, rows):
    segment, parent, grand, position = tree_layout(tree_lengths, tree_parents, rows)
    lane = jnp.arange(LANES, dtype=jnp.int32)
    half = HEAD_DIM // 2
    inverse = rope_base ** (-(lane % half).astype(f32) * 2.0 / HEAD_DIM)
    angle = position.astype(f32)[:, None] * inverse[None, :]
    cosine = jnp.cos(angle)
    sine = jnp.where((lane % HEAD_DIM) < half, -1.0, 1.0)[None, :] * jnp.sin(angle)
    label = (lane - HEAD_DIM)[None, :]
    own = segment[:, None] == label
    path = own | (parent[:, None] == label) | (grand[:, None] == label)
    hidden = (label >= 0) & (label < SEGMENTS) & ~path
    queries = jnp.where(hidden, masked_score, 0.0).astype(f32)
    ones = (label >= 16) & (label < 19)
    keys = jnp.where(own | ones, 1.0, 0.0).astype(f32)
    return cosine, sine, queries, keys
def barrier(partners):
    semaphore = pltpu.get_barrier_semaphore()
    for partner in partners:
        pl.semaphore_signal(semaphore, inc=1, device_id=partner, device_id_type=MESH)
    pl.semaphore_wait(semaphore, len(partners))


def send(source, target, send_sem, recv_sem, device):
    copy = pltpu.make_async_remote_copy(
        src_ref=source,
        dst_ref=target,
        send_sem=send_sem,
        recv_sem=recv_sem,
        device_id=device,
        device_id_type=MESH,
    )
    copy.start()
    return copy


def add_rows(target, source, step=64):
    rows = target.shape[0]
    step = min(step, rows)
    while rows % step:
        step //= 2

    def body(i, _):
        at = span(i, step)
        target[at, :] = target[at, :] + source[at, :]
        return 0

    lax.fori_loop(0, rows // step, body, 0)


def orders(n_d):
    bits = n_d.bit_length() - 1
    return [list(range(bits)), list(range(bits - 1, -1, -1))]


def combos(bits):
    masks = [0]
    for b in bits:
        masks = masks + [m ^ (1 << b) for m in masks]
    return masks


class Spread:
    def __init__(self, n_d, n_t, shards, alls, sems):
        self.n_d, self.n_t, self.shards, self.alls = n_d, n_t, shards, alls
        self.zs, self.zr, self.ps, self.pr, self.ys, self.yr, self.own = sems
        self.d, self.t = lax.axis_index("dp"), lax.axis_index("tensor")
        self.chips = n_t // 2
        self.chip, self.core = self.t // 2, lax.rem(self.t, 2)
        self.other = 2 * self.chip + 1 - self.core
        self.bits = n_d.bit_length() - 1
        self.arrays = range(len(shards))

    @staticmethod
    def sems(count, n_d, n_t):
        dma = pltpu.SemaphoreType.DMA
        hops, slots = n_t // 2 - 1, 2 * (n_d - 1)
        z, p, y = (count, 2 * hops), (count, 2 * hops, slots), (count, 2 * hops + 1)
        return [dma(z), dma(z), dma(p), dma(p), dma(y), dma(y), dma((count,))]

    def exists(self, c):
        return (c >= 0) & (c < self.chips)

    def rows(self, a):
        return self.shards[a].shape[0] // self.n_d

    def slot(self, way, h):
        return h - 1 + (self.chips - 1 if way < 0 else 0)

    def remote(self, src, dst, ssem, rsem, device):
        return pltpu.make_async_remote_copy(
            src_ref=src, dst_ref=dst, send_sem=ssem, recv_sem=rsem, device_id=device, device_id_type=MESH
        )

    def along(self, a, way, h, arriving):
        source = self.chip - way * (h if arriving else h - 1)
        at = span(self.d, self.rows(a))
        dst = self.alls[a].at[2 * source + self.core, at]
        src = self.shards[a].at[at] if h == 1 and not arriving else dst
        peer = self.chip - way if arriving else self.chip + way
        i = self.slot(way, h)
        return self.remote(src, dst, self.zs.at[a, i], self.zr.at[a, i], (self.d, 2 * peer + self.core))

    def across(self, a, way, h, step, arriving):
        source = self.chip - way * h
        q, half = self.rows(a), self.shards[a].shape[1] // 2
        out = []
        for stream, order in enumerate(orders(self.n_d)):
            partner = lax.bitwise_xor(self.d, 1 << order[step])
            for j, m in enumerate(combos(order[:step])):
                block = lax.bitwise_xor(partner if arriving else self.d, m)
                ref = self.alls[a].at[2 * source + self.core, span(block, q), pl.ds(stream * half, half)]
                i = stream * (self.n_d - 1) + (1 << step) - 1 + j
                k = self.slot(way, h)
                out.append(self.remote(ref, ref, self.ps.at[a, k, i], self.pr.at[a, k, i], (partner, self.t)))
        return out

    def beside(self, a, way, h, arriving=False):
        source = self.chip - way * h
        ref = self.alls[a].at[2 * source + (1 - self.core if arriving else self.core)]
        k = self.slot(way, h)
        return self.remote(ref, ref, self.ys.at[a, k], self.yr.at[a, k], (self.d, self.other))

    def mine(self, a, arriving=False):
        k = 2 * (self.chips - 1)
        dst = self.alls[a].at[self.other if arriving else self.t]
        return self.remote(self.shards[a], dst, self.ys.at[a, k], self.yr.at[a, k], (self.d, self.other))

    def keep(self, a):
        return pltpu.make_async_copy(self.shards[a], self.alls[a].at[self.t], self.own.at[a])

    def begin(self):
        for way in (1, -1):

            @pl.when(self.exists(self.chip + way))
            def _():
                for a in self.arrays:
                    self.along(a, way, 1, False).start()

        for a in self.arrays:
            self.keep(a).start()
            self.mine(a).start()

    def phase(self, p, h):
        for way in (1, -1):

            @pl.when(self.exists(self.chip - way * h))
            def _():
                for a in self.arrays:
                    if p == 0:
                        self.along(a, way, h, True).wait_recv()
                        if h < self.chips - 1:

                            @pl.when(self.exists(self.chip + way))
                            def _():
                                self.along(a, way, h + 1, False).start()
                    else:
                        for copy in self.across(a, way, h, p - 1, True):
                            copy.wait_recv()
                    if p < self.bits:
                        for copy in self.across(a, way, h, p, False):
                            copy.start()
                    else:
                        self.beside(a, way, h).start()

    def groups(self):
        return self.chips - 1 + self.bits

    def group(self, g):
        for h in range(1, self.chips):
            if 0 <= g - (h - 1) <= self.bits:
                self.phase(g - (h - 1), h)

    def end(self):
        for h in range(1, self.chips):
            for way in (1, -1):

                @pl.when(self.exists(self.chip + way) & self.exists(self.chip - way * (h - 1)))
                def _():
                    for a in self.arrays:
                        self.along(a, way, h, False).wait_send()

                @pl.when(self.exists(self.chip - way * h))
                def _():
                    for a in self.arrays:
                        for step in range(self.bits):
                            for copy in self.across(a, way, h, step, False):
                                copy.wait_send()
                        self.beside(a, way, h).wait_send()
                        self.beside(a, way, h, True).wait_recv()

        for a in self.arrays:
            self.keep(a).wait()
            self.mine(a).wait_send()
            self.mine(a, True).wait_recv()


def gather_kernel(n_d, n_t, x_ref, w_ref, f_ref, o_ref, u_ref, all_ref, rs, ss, rb, sb, rw, sw, rp, sp, *sems):
    d, t = lax.axis_index("dp"), lax.axis_index("tensor")
    trees, rows, _ = x_ref.shape
    chips = n_t // 2
    group = n_t // trees
    chip, core = t // 2, lax.rem(t, 2)
    other = 2 * chip + 1 - core
    near = group // 2
    tree = t // group
    line = [lax.rem(chip + k, chips) for k in range(1, chips)]
    planes = [lax.rem(d + k, n_d) for k in range(1, n_d)]
    owners = [(j * group + t // trees) for j in range(trees)]
    givers = [lax.rem(t, group) * trees + i for i in range(trees)]
    barrier([(d, lax.rem(t + k, n_t)) for k in range(1, n_t)] + [(p, t) for p in planes])
    part = w_ref.shape[1] // n_d

    copies = []
    mine = w_ref.at[:, span(d, part), :]
    for j in range(trees):
        slot = u_ref.at[lax.rem(t, trees), :, span(d, part), :]

        @pl.when(owners[j] != t)
        def _():
            send(mine, slot, sw.at[j], rw.at[lax.rem(t, trees)], (d, owners[j]))

        @pl.when(owners[j] == t)
        def _():
            u_ref[lax.rem(t, trees), :, span(d, part), :] = w_ref[:, span(d, part), :]

    def block(c, k):
        return o_ref.at[span(2 * c + k, rows)]

    for k, c in enumerate(line):
        copies.append(send(x_ref.at[c // near], block(chip, core), ss.at[k], rs.at[k], (d, 2 * c + core)))
    weights = Spread(n_d, n_t, [f_ref], [all_ref], sems)
    weights.begin()
    o_ref[span(t, rows), :] = x_ref[tree]
    copies.append(send(x_ref.at[tree], block(chip, core), sb.at[chips - 1], rb.at[chips - 1], (d, other)))
    for i in range(trees):
        slot = u_ref.at[i, :, span(d, part), :]

        @pl.when(givers[i] != t)
        def _():
            pltpu.make_async_remote_copy(
                src_ref=mine, dst_ref=slot, send_sem=sw.at[0], recv_sem=rw.at[i],
                device_id=(d, givers[i]), device_id_type=MESH,
            ).wait_recv()

    mine_all = u_ref.at[:, :, span(d, part), :]
    for k, p in enumerate(planes):
        copies.append(send(mine_all, mine_all, sp.at[k], rp.at[k], (p, t)))
    for k in range(chips - 1):
        source = lax.rem(chip + chips - 1 - k, chips)
        copies[k].wait_recv()
        copies.append(send(block(source, core), block(source, core), sb.at[k], rb.at[k], (d, other)))
    for g in range(weights.groups()):
        weights.group(g)
    weights.end()
    for j in range(trees):

        @pl.when(owners[j] != t)
        def _():
            pltpu.make_async_remote_copy(
                src_ref=mine, dst_ref=mine, send_sem=sw.at[j], recv_sem=rw.at[0],
                device_id=(d, owners[j]), device_id_type=MESH,
            ).wait_send()

    for i, copy in enumerate(copies):
        if i < chips - 1:
            copy.wait_send()
        else:
            copy.wait()


def gather_tree(n_d, n_t, normed, weight, down):
    trees, rows, wide = normed.shape
    chips = n_t // 2
    dma = pltpu.SemaphoreType.DMA
    return pl.pallas_call(
        functools.partial(gather_kernel, n_d, n_t),
        in_specs=[VMEM] * 3,
        out_specs=[VMEM] * 2 + [HBM],
        out_shape=[
            jax.ShapeDtypeStruct((n_t * rows, wide), bf16),
            jax.ShapeDtypeStruct((trees,) + weight.shape, bf16),
            jax.ShapeDtypeStruct((n_t,) + down.shape, bf16),
        ],
        scratch_shapes=[
            dma((chips - 1,)), dma((chips - 1,)), dma((chips,)), dma((chips,)),
            dma((trees,)), dma((trees,)), dma((n_d - 1,)), dma((n_d - 1,)),
        ] + Spread.sems(1, n_d, n_t),
        compiler_params=pltpu.CompilerParams(collective_id=0, has_side_effects=True),
        name="gather_tree",
    )(normed, weight, down)


def qkv_kernel(x_ref, w_ref, cos_ref, sin_ref, mq_ref, mk_ref, q_ref, k_ref, v_ref, kt_ref, vt_ref):
    x = x_ref[...]
    heads = q_ref.shape[0]
    cosine, sine = cos_ref[...], sin_ref[...]
    mq, mk = mq_ref[...], mk_ref[...]
    lane = lane_of(cosine.shape)
    low = lax.rem(lane, HEAD_DIM) < HEAD_DIM // 2
    first = lane < HEAD_DIM
    mv = jnp.where((lane >= HEAD_DIM) & (lane < HEAD_DIM + 3), 1.0, 0.0)
    tail = jnp.where(row_of((VROWS - HEAD_DIM, x.shape[0])) == 0, 1.0, 0.0).astype(bf16)

    def both(slab):
        return slab, pltpu.roll(slab, HEAD_DIM, 1)

    def rotate(slab):
        partner = jnp.where(
            low, pltpu.roll(slab, LANES - HEAD_DIM // 2, 1), pltpu.roll(slab, HEAD_DIM // 2, 1)
        )
        return slab * cosine + partner * sine

    q_all, k_all, v_all = (dot(x, w_ref[i]) for i in range(3))
    for h in range(0, heads, 2):
        cols = slice(h * HEAD_DIM, (h + 2) * HEAD_DIM)
        for g, slab in enumerate(both(rotate(q_all[:, cols]) * HEAD_DIM**-0.5)):
            q_ref[h + g] = jnp.where(first, slab, mq).astype(bf16)
        keys = rotate(k_all[:, cols])
        for g, slab in enumerate(both(keys)):
            k_ref[h + g] = jnp.where(first, slab, mk).astype(bf16)
        flat = keys.T.astype(bf16)
        for g, slab in enumerate(both(v_all[:, cols])):
            v_ref[h + g] = jnp.where(first, slab, mv).astype(bf16)
        flat_v = v_all[:, cols].T.astype(bf16)
        for g in range(2):
            part = slice(g * HEAD_DIM, (g + 1) * HEAD_DIM)
            kt_ref[h + g] = flat[part]
            vt_ref[h + g, :HEAD_DIM] = flat_v[part]
            vt_ref[h + g, HEAD_DIM:] = tail


def project(x, w, cosine, sine, mq, mk):
    rows, wide = x.shape
    heads = w.shape[2] // HEAD_DIM
    table = pl.BlockSpec((BLOCK, LANES), lambda i: (i, 0))
    slab = pl.BlockSpec((heads, BLOCK, LANES), lambda i: (0, i, 0))
    shape = jax.ShapeDtypeStruct((heads, rows, LANES), bf16)
    return pl.pallas_call(
        qkv_kernel,
        grid=(rows // BLOCK,),
        in_specs=[
            pl.BlockSpec((BLOCK, wide), lambda i: (i, 0)),
            pl.BlockSpec(w.shape, lambda i: (0, 0, 0)),
            table, table, table, table,
        ],
        out_specs=[
            slab, slab, slab,
            pl.BlockSpec((heads, HEAD_DIM, BLOCK), lambda i: (0, 0, i)),
            pl.BlockSpec((heads, VROWS, BLOCK), lambda i: (0, 0, i)),
        ],
        out_shape=[
            shape, shape, shape,
            jax.ShapeDtypeStruct((heads, HEAD_DIM, rows), bf16),
            jax.ShapeDtypeStruct((heads, VROWS, rows), bf16),
        ],
        name="project",
    )(x, w, cosine, sine, mq, mk)


def fwd_kernel(
    n_d, n_t, trees, q_ref, k_ref, vt_ref, ow_ref, up_ref, o_ref, qb_ref, att_ref, ow_all, up_all,
    kept, ss, rs, here, *sems,
):
    qi = pl.program_id(0)
    steps = pl.num_programs(0)
    heads = q_ref.shape[0]
    row, col = row_of((BLOCK, BLOCK)), lane_of((BLOCK, BLOCK))
    d, t = lax.axis_index("dp"), lax.axis_index("tensor")
    group = n_t // trees
    rows, width = att_ref.shape[1], o_ref.shape[1]
    per = BLOCK // rows
    weights = Spread(n_d, n_t, [up_ref, ow_ref], [up_all, ow_all], sems)
    first_group = max(0, k_ref.shape[1] // BLOCK - 4)
    place = att_ref.at[t // group, :, span(lax.rem(t, group), width)]

    def outgoing(i, r, k):
        return pltpu.make_async_remote_copy(
            src_ref=kept.at[i, pl.ds(r * rows, rows)], dst_ref=place, send_sem=ss.at[k], recv_sem=rs.at[k],
            device_id=(d, lax.rem(t + k, n_t)), device_id_type=MESH,
        )

    @pl.when(qi == 0)
    def _():
        barrier(
            [(d, lax.rem(t + k, n_t)) for k in range(1, n_t)] + [(lax.rem(d + k, n_d), t) for k in range(1, n_d)]
        )
        weights.begin()

    for g in range(weights.groups()):
        if first_group + g < k_ref.shape[1] // BLOCK:

            @pl.when(qi == first_group + g)
            def _():
                weights.group(g)

    qs = [q_ref[h] for h in range(heads)]

    def scores(h, j):
        return dot(k_ref[h, span(j, BLOCK), :], qs[h], NT)

    state = []
    for h in range(heads):
        s = jnp.where(row <= col, scores(h, qi), masked_score)
        m = jnp.max(s, axis=0, keepdims=True)
        p = jnp.exp(s - m)
        state.append((m, dot(vt_ref[h, :, span(qi, BLOCK)], p.astype(bf16))))

    def step(j, carry):
        out = []
        for h in range(heads):
            m, acc = carry[h]
            s = scores(h, j)
            top = jnp.maximum(m, jnp.max(s, axis=0, keepdims=True))
            p = jnp.exp(s - top)
            acc = acc * jnp.exp(m - top) + dot(vt_ref[h, :, span(j, BLOCK)], p.astype(bf16))
            out.append((top, acc))
        return tuple(out)

    state = lax.fori_loop(0, qi, step, tuple(state))
    r = row_of((LANES, BLOCK))
    for h in range(0, heads, 2):
        outs = []
        for g in (h, h + 1):
            m, acc = state[g]
            total = acc[HEAD_DIM : HEAD_DIM + 1]
            outs.append(acc[:HEAD_DIM] / total)
            a, b, c = split3(-(m + jnp.log(total)))
            extra = jnp.where(r == 80, a, jnp.where(r == 81, b, jnp.where(r == 82, c, 0.0))).T
            qb_ref[g] = qs[g] + extra.astype(bf16)
        slab = jnp.concatenate(outs, axis=0).T.astype(bf16)
        o_ref[:, h * HEAD_DIM : (h + 2) * HEAD_DIM] = slab
        kept[qi, :, h * HEAD_DIM : (h + 2) * HEAD_DIM] = slab

    def local(r):
        return pltpu.make_async_copy(kept.at[t // per, pl.ds(r * rows, rows)], place, here.at[0])

    for r in range(per):
        k = lax.rem(qi * per + r + n_t - t, n_t)

        @pl.when(k != 0)
        def _():
            outgoing(qi, r, k).start()

        @pl.when(k == 0)
        def _():
            local(r).start()

    @pl.when(qi == steps - 1)
    def _():
        for g in range(k_ref.shape[1] // BLOCK - first_group, weights.groups()):
            weights.group(g)
        for k in range(1, n_t):
            outgoing(0, 0, k).wait()
        local(0).wait()
        weights.end()


def attend(n_d, n_t, trees, q, k, vt, ow, up):
    heads, rows, _ = q.shape
    slab = pl.BlockSpec((heads, rows, LANES), lambda i: (0, 0, 0))
    block = pl.BlockSpec((heads, BLOCK, LANES), lambda i: (0, i, 0))
    wide = heads * HEAD_DIM
    dma = pltpu.SemaphoreType.DMA
    sds = jax.ShapeDtypeStruct
    return pl.pallas_call(
        functools.partial(fwd_kernel, n_d, n_t, trees),
        grid=(rows // BLOCK,),
        in_specs=[block, slab, pl.BlockSpec((heads, VROWS, rows), lambda i: (0, 0, 0)), VMEM, VMEM],
        out_specs=[pl.BlockSpec((BLOCK, wide), lambda i: (i, 0)), block, HBM, HBM, HBM],
        out_shape=[
            sds((rows, wide), bf16),
            sds(q.shape, bf16),
            sds((trees, rows // n_t, wide * n_t // trees), bf16),
            sds((n_t,) + ow.shape, bf16),
            sds((n_t,) + up.shape, bf16),
        ],
        scratch_shapes=[
            pltpu.VMEM((rows // BLOCK, BLOCK, wide), bf16), dma((n_t,)), dma((n_t,)), dma((1,)),
        ] + Spread.sems(2, n_d, n_t),
        compiler_params=pltpu.CompilerParams(collective_id=1, has_side_effects=True),
        name="attend",
    )(q, k, vt, ow, up)


class Reduce:
    def __init__(self, n_d, n_t, sources, totals, scratch):
        self.n_d, self.n_t, self.sources, self.totals = n_d, n_t, sources, totals
        count = len(sources)
        self.mine, self.side, self.land_at, self.far = (
            scratch[i * count : (i + 1) * count] for i in range(4)
        )
        self.s_load, self.s_side, self.r_side, self.s_hop, self.r_hop, self.s_far, self.r_far = scratch[4 * count :]
        self.d, self.t = lax.axis_index("dp"), lax.axis_index("tensor")
        self.chips = n_t // 2
        self.chip, self.core = self.t // 2, lax.rem(self.t, 2)
        self.other = 2 * self.chip + 1 - self.core
        self.dest = [lax.rem(self.chip + k, self.chips) for k in range(1, self.chips)] + [self.chip]
        self.bits = n_d.bit_length() - 1
        self.units = [(n, k) for k in range(self.chips) for n in range(count)]

    @staticmethod
    def scratch(n_d, n_t, shapes):
        dma = pltpu.SemaphoreType.DMA
        chips, slots, count = n_t // 2, 2 * (n_d - 1), len(shapes)
        vm = lambda lead, r, c: pltpu.VMEM(lead + (r, c), bf16)
        units = count * chips
        return (
            [vm((chips,), r, c) for r, c in shapes] * 2
            + [vm((chips, slots), r // n_d, c // 2) for r, c in shapes]
            + [vm((chips - 1,), r // n_d, c) for r, c in shapes]
            + [dma((units,)), dma((units,)), dma((units,)), dma((units, slots)), dma((units, slots))]
            + [dma((units,)), dma((units,))]
        )

    def remote(self, src, dst, ssem, rsem, device):
        return pltpu.make_async_remote_copy(
            src_ref=src, dst_ref=dst, send_sem=ssem, recv_sem=rsem, device_id=device, device_id_type=MESH
        )

    def load(self, u):
        n, k = self.units[u]
        source = self.sources[n].at[2 * self.dest[k] + self.core]
        return pltpu.make_async_copy(source, self.mine[n].at[k], self.s_load.at[u])

    def beside(self, u):
        n, k = self.units[u]
        source = self.sources[n].at[2 * self.dest[k] + 1 - self.core]
        return self.remote(source, self.side[n].at[k], self.s_side.at[u], self.r_side.at[u], (self.d, self.other))

    def cut(self, u, part, stream):
        n, k = self.units[u]
        _, height, width = self.mine[n].shape
        height, width = height // self.n_d, width // 2
        return self.mine[n].at[k, span(part, height), pl.ds(stream * width, width)]

    def hops(self, u, step):
        n, k = self.units[u]
        slot = 0 if step == 0 else self.n_d - (self.n_d >> step)
        out = []
        for stream, order in enumerate(orders(self.n_d)):
            partner = lax.bitwise_xor(self.d, 1 << order[step])
            for j, m in enumerate(combos(order[step + 1 :])):
                i = (slot + j) * 2 + stream
                landing = self.land_at[n].at[k, i]
                copy = self.remote(
                    self.cut(u, lax.bitwise_xor(partner, m), stream), landing,
                    self.s_hop.at[u, i], self.r_hop.at[u, i], (partner, self.t),
                )
                out.append((copy, self.cut(u, lax.bitwise_xor(self.d, m), stream), landing))
        return out

    def piece(self, u):
        n, k = self.units[u]
        return self.mine[n].at[k, span(self.d, self.mine[n].shape[1] // self.n_d), :]

    def away(self, u):
        n, k = self.units[u]
        return self.remote(
            self.piece(u), self.far[n].at[k], self.s_far.at[u], self.r_far.at[u],
            (self.d, 2 * self.dest[k] + self.core),
        )

    def begin(self):
        for u in range(len(self.units)):
            self.load(u).start()
            self.beside(u).start()

    def events(self):
        return len(self.units) + self.bits

    def event(self, e):
        if e < len(self.units):
            n, k = self.units[e]
            self.load(e).wait()
            self.beside(e).wait_recv()
            add_rows(self.mine[n].at[k], self.side[n].at[k])
            for copy, _, _ in self.hops(e, 0):
                copy.start()
        for step in range(self.bits):
            u = e - 1 - step
            if 0 <= u < len(self.units):
                for copy, target, landing in self.hops(u, step):
                    copy.wait_recv()
                    add_rows(target, landing)
                if step + 1 < self.bits:
                    for copy, _, _ in self.hops(u, step + 1):
                        copy.start()
                elif self.units[u][1] < self.chips - 1:
                    self.away(u).start()

    def end(self):
        for u, (n, k) in enumerate(self.units):
            if k < self.chips - 1:
                self.away(u).wait_recv()
            else:
                total = self.piece(u)[...].astype(f32)
                for i in range(self.chips - 1):
                    total = total + self.far[n][i].astype(f32)
                self.totals[n][...] = total.astype(bf16)
        for u, (n, k) in enumerate(self.units):
            self.beside(u).wait_send()
            for step in range(self.bits):
                for copy, _, _ in self.hops(u, step):
                    copy.wait_send()
            if k < self.chips - 1:
                self.away(u).wait_send()


def bwd_kernel(
    n_d, n_t, q_ref, k_ref, v_ref, kt_ref, x_ref, o_ref, cos_ref, sin_ref, up_ref, down_ref, og_ref,
    m_ref, up_tot, down_tot, og_tot, sums, wide, d_ref, hs, hr, *scratch,
):
    j = pl.program_id(0)
    heads, rows, _ = q_ref.shape
    nq = rows // BLOCK
    row, col = row_of((BLOCK, BLOCK)), lane_of((BLOCK, BLOCK))
    lane = lane_of((BLOCK, LANES))
    first = lane < HEAD_DIM
    d, t = lax.axis_index("dp"), lax.axis_index("tensor")
    trees, part, _ = x_ref.shape
    group, width = n_t // trees, heads * HEAD_DIM
    gradients = Reduce(n_d, n_t, [up_ref, down_ref, og_ref], [up_tot, down_tot, og_tot], scratch)
    ahead = 3
    points = 10

    def point(p):
        left = gradients.events() - ahead
        for e in range(ahead + p * left // points, ahead + (p + 1) * left // points):
            gradients.event(e)

    def cut(o):
        return x_ref.at[o // group, :, span(lax.rem(o, group), width)]

    def outgoing(k):
        o = lax.rem(t + k, n_t)
        return gradients.remote(cut(o), d_ref.at[span(t, part), :], hs.at[k], hr.at[k], (d, o))

    @pl.when(j == 0)
    def _():
        barrier(
            [(d, lax.rem(t + k, n_t)) for k in range(1, n_t)] + [(lax.rem(d + k, n_d), t) for k in range(1, n_d)]
        )
        for k in range(1, n_t):
            outgoing(k).start()
        gradients.begin()
        d_ref[span(t, part), :] = cut(t)[...]
        sums[...] = jnp.zeros_like(sums)
        for e in range(ahead):
            gradients.event(e)
        for k in range(1, n_t):
            outgoing(k).wait()

        def widen(i, _):
            at = span(i, BLOCK)
            for h in range(0, heads, 2):
                cols = slice(h * HEAD_DIM, (h + 2) * HEAD_DIM)
                slab = d_ref[at, cols].astype(f32)
                prod = slab * o_ref[at, cols].astype(f32)
                for g, (s, mine) in enumerate(((slab, first), (pltpu.roll(slab, HEAD_DIM, 1), ~first))):
                    inner = -jnp.sum(jnp.where(mine, prod, 0.0), axis=1, keepdims=True)
                    a, b, c = split3(inner)
                    n = HEAD_DIM
                    tail = jnp.where(lane == n, a, jnp.where(lane == n + 1, b, jnp.where(lane == n + 2, c, 0.0)))
                    wide[h + g, at, :] = jnp.where(first, s, tail).astype(bf16)
            return 0

        lax.fori_loop(0, nq, widen, 0)

    for p in range(0, points, 2):
        if p // 2 < nq:

            @pl.when(j == p // 2)
            def _():
                point(p)

    ks = [k_ref[h] for h in range(heads)]
    vs = [v_ref[h] for h in range(heads)]
    kts = [kt_ref[h] for h in range(heads)]

    def pair(h, i, mask):
        at = span(i, BLOCK)
        q = q_ref[h, at, :]
        d = wide[h, at, :]
        s = dot(ks[h], q, NT)
        if mask:
            s = jnp.where(row <= col, s, masked_score)
        p = jnp.exp(s)
        back = (p * dot(vs[h], d, NT)).astype(bf16)
        sums[h, :, at] += dot(kts[h], back)
        return dot(back, q), dot(p.astype(bf16), d)

    def step(i, carry):
        out = []
        for h in range(heads):
            dk, dv = pair(h, i, False)
            out.append((carry[h][0] + dk, carry[h][1] + dv))
        return tuple(out)

    state = tuple(pair(h, j, True) for h in range(heads))
    middle = (j + 1 + nq) // 2
    state = lax.fori_loop(j + 1, middle, step, state)
    for p in range(1, points, 2):
        if p // 2 < nq:

            @pl.when(j == p // 2)
            def _():
                point(p)

    state = lax.fori_loop(middle, nq, step, state)

    def join(a, b):
        return jnp.where(first, a, pltpu.roll(b, HEAD_DIM, 1))

    cosine, sine = cos_ref[...], sin_ref[...]
    low = lax.rem(lane, HEAD_DIM) < HEAD_DIM // 2

    def unrotate(slab):
        partner = jnp.where(
            low, pltpu.roll(slab, LANES - HEAD_DIM // 2, 1), pltpu.roll(slab, HEAD_DIM // 2, 1)
        )
        return slab * cosine - partner * sine

    at = span(j, BLOCK)
    total = heads * HEAD_DIM
    for h in range(0, heads, 2):
        dq = jnp.concatenate([sums[h, :, at], sums[h + 1, :, at]], axis=0).T * HEAD_DIM**-0.5
        dk = join(state[h][0], state[h + 1][0])
        dv = join(state[h][1], state[h + 1][1])
        for n, part in enumerate((unrotate(dq), unrotate(dk), dv)):
            begin = n * total + h * HEAD_DIM
            m_ref[:, begin : begin + 2 * HEAD_DIM] = part.astype(bf16)

    @pl.when(j == nq - 1)
    def _():
        for p in range(2 * nq, points):
            point(p)
        gradients.end()


def attend_back(n_d, n_t, q, k, v, kt, x, o, cosine, sine, up_g, down_g, out_g):
    heads, rows, _ = q.shape
    whole = lambda a: pl.BlockSpec(a.shape, lambda j: (0,) * a.ndim, pipeline_mode=pl.Buffered(1))
    block = pl.BlockSpec((heads, BLOCK, LANES), lambda j: (0, j, 0))
    table = pl.BlockSpec((BLOCK, LANES), lambda j: (j, 0))
    wide = heads * HEAD_DIM
    dma = pltpu.SemaphoreType.DMA
    sds = jax.ShapeDtypeStruct
    shapes = [a.shape[1:] for a in (up_g, down_g, out_g)]
    return pl.pallas_call(
        functools.partial(bwd_kernel, n_d, n_t),
        grid=(rows // BLOCK,),
        in_specs=[
            whole(q), block, block,
            pl.BlockSpec((heads, HEAD_DIM, BLOCK), lambda j: (0, 0, j)),
            VMEM, whole(o), table, table, HBM, HBM, HBM,
        ],
        out_specs=[pl.BlockSpec((BLOCK, 3 * wide), lambda j: (j, 0)), VMEM, VMEM, VMEM],
        out_shape=[sds((rows, 3 * wide), bf16)] + [sds((r // n_d, c), bf16) for r, c in shapes],
        scratch_shapes=[
            pltpu.VMEM((heads, HEAD_DIM, rows), f32),
            pltpu.VMEM((heads, rows, LANES), bf16),
            pltpu.VMEM((rows, wide), bf16),
            dma((n_t,)), dma((n_t,)),
        ] + Reduce.scratch(n_d, n_t, shapes),
        compiler_params=pltpu.CompilerParams(
            collective_id=2, has_side_effects=True, vmem_limit_bytes=67043328
        ),
        name="attend_back",
    )(q, k, v, kt, x, o, cosine, sine, up_g, down_g, out_g)


def ln_parts(v):
    centered = v - jnp.mean(v, axis=-1, keepdims=True)
    r = lax.rsqrt(jnp.mean(centered * centered, axis=-1, keepdims=True) + norm_eps)
    return centered * r, r


def ln_back(e, n, r, gain):
    f = e * gain
    return r * (f - jnp.mean(f, axis=-1, keepdims=True) - n * jnp.mean(f * n, axis=-1, keepdims=True))


def feed_kernel(
    att_ref, x_ref, cot_ref, ow_ref, par_ref, up_ref, down_ref,
    out_ref, hid_ref, ba_ref, upg_ref, downg_ref, outg_ref, vec_ref,
    hidden, branch, acc, feed_in, back_feed, active, slope,
):
    phase, n = pl.program_id(0), pl.program_id(1)
    last = pl.num_programs(1) - 1
    par = lambda i: par_ref[i : i + 1]
    total = lambda v: jnp.sum(v, axis=0, keepdims=True)

    @pl.when((phase == 0) & (n == 0))
    def _():
        b = dot(att_ref[...], ow_ref[...])
        branch[...] = b
        h = x_ref[...].astype(f32) + ln_parts(b)[0] * par(0) + par(1)
        hidden[...] = h
        feed_in[...] = (ln_parts(h)[0] * par(2) + par(3)).astype(bf16)
        acc[...] = jnp.zeros_like(acc)

    up, down = up_ref[0], down_ref[0]

    @pl.when(phase == 0)
    def _():
        u = dot(feed_in[...], up)
        t = jnp.tanh(0.7978845608028654 * (u + 0.044715 * u * u * u))
        half = 0.5 * (1.0 + t)
        a = (u * half).astype(bf16)
        active[n] = a
        slope[n] = half + 0.5 * u * (1.0 - t * t) * (
            0.7978845608028654 * (1.0 + 3 * 0.044715 * u * u)
        )
        acc[...] += dot(a, down)

    @pl.when((phase == 1) & (n == 0))
    def _():
        e = cot_ref[...].astype(f32)
        norm, r = ln_parts(acc[...])
        out_ref[...] = (hidden[...] + norm * par(4) + par(5)).astype(bf16)
        vec_ref[4:5] = total(e * norm)
        vec_ref[5:6] = total(e)
        back_feed[...] = ln_back(e, norm, r, par(4)).astype(bf16)
        acc[...] = jnp.zeros_like(acc)

    @pl.when(phase == 1)
    def _():
        b = back_feed[...]
        upper = (dot(b, down, NT) * slope[n]).astype(bf16)
        acc[...] += dot(upper, up, NT)
        downg_ref[0] = dot(active[n], b, TN).astype(bf16)
        upg_ref[0] = dot(feed_in[...], upper, TN).astype(bf16)

    @pl.when((phase == 1) & (n == last))
    def _():
        e = acc[...]
        norm, r = ln_parts(hidden[...])
        vec_ref[2:3] = total(e * norm)
        vec_ref[3:4] = total(e)
        h = cot_ref[...].astype(f32) + ln_back(e, norm, r, par(2))
        hid_ref[...] = h
        norm, r = ln_parts(branch[...])
        vec_ref[0:1] = total(h * norm)
        vec_ref[1:2] = total(h)
        b = ln_back(h, norm, r, par(0)).astype(bf16)
        ba_ref[...] = dot(b, ow_ref[...], NT).astype(bf16)
        outg_ref[...] = dot(att_ref[...], b, TN).astype(bf16)


def feed(att, x, cot, ow, par, up, down):
    rows, wide = att.shape
    n_t, _, width = up.shape
    one = lambda a: pl.BlockSpec(a.shape, lambda p, n: (0,) * len(a.shape), pipeline_mode=pl.Buffered(1))
    sds = jax.ShapeDtypeStruct
    outs = [
        sds((rows, wide), bf16), sds((rows, wide), f32), sds((rows, wide), bf16),
        sds((n_t, wide, width), bf16), sds((n_t, width, wide), bf16), sds((wide, wide), bf16),
        sds((8, wide), f32),
    ]
    chunk = lambda a: pl.BlockSpec((1,) + a.shape[1:], lambda p, n: (p * n, 0, 0))
    weight = lambda a: pl.BlockSpec((1,) + a.shape[1:], lambda p, n: (n, 0, 0))
    return pl.pallas_call(
        feed_kernel,
        grid=(2, n_t),
        in_specs=[one(a) for a in (att, x, cot, ow, par)] + [weight(up), weight(down)],
        out_specs=[one(o) for o in outs[:3]] + [chunk(outs[3]), chunk(outs[4])] + [one(o) for o in outs[5:]],
        out_shape=outs,
        scratch_shapes=[
            pltpu.VMEM((rows, wide), f32), pltpu.VMEM((rows, wide), f32), pltpu.VMEM((rows, wide), f32),
            pltpu.VMEM((rows, wide), bf16), pltpu.VMEM((rows, wide), bf16),
            pltpu.VMEM((n_t, rows, width), bf16), pltpu.VMEM((n_t, rows, width), f32),
        ],
        compiler_params=pltpu.CompilerParams(vmem_limit_bytes=64 << 20),
        name="feed",
    )(att, x, cot, ow, par, up, down)
def finish_kernel(
    n_d, n_t, sum_ref, x_ref, hid_ref, par_ref, vec_in, up_tot, down_tot, og_tot, ig_ref,
    bt_ref, vec_ref, up_out, down_out, og_out, ig_out,
    mine, landed, far, full_up, full_down, full_og, full_ig,
    r_side, r_out, r_land, vec_now, vec_got, vec_far,
    s_load, s_hop, r_hop, s_all, r_all, s_own, r_own,
    s_red, r_red, s_redside, r_redside, s_vec, r_vec,
):
    d, t = lax.axis_index("dp"), lax.axis_index("tensor")
    trees, rows, wide = x_ref.shape
    chips = n_t // 2
    near = chips // trees
    group = n_t // trees
    chip, core = t // 2, lax.rem(t, 2)
    other = 2 * chip + 1 - core
    line = [lax.rem(chip + k, chips) for k in range(1, chips)]
    dest = line + [chip]
    peers = [lax.rem(d + k, n_d) for k in range(1, n_d)]
    bits = n_d.bit_length() - 1
    barrier([(d, lax.rem(t + k, n_t)) for k in range(1, n_t)] + [(p, t) for p in peers])
    totals = [up_tot, down_tot, og_tot]
    fulls = [full_up, full_down, full_og, full_ig]
    outs = [up_out, down_out, og_out, ig_out]

    red_pairs = []
    for k, c in enumerate(dest):
        theirs = sum_ref.at[span(2 * c + 1 - core, rows), :]
        red_pairs.append(send(theirs, r_side.at[k], s_redside.at[k], r_redside.at[k], (d, other)))
    loads = []
    for k in range(trees):
        loads.append(pltpu.make_async_copy(ig_ref.at[k], mine.at[k], s_load.at[k]))
        loads[k].start()
    hops, spreads = {}, []

    def cut(k, part):
        return mine.at[k, span(part, mine.shape[1] // n_d), :]

    def hop(k, step):
        slot = 0 if step == 0 else n_d - (n_d >> step)
        order = orders(n_d)[k % 2]
        partner = lax.bitwise_xor(d, 1 << order[step])
        for j, m in enumerate(combos(order[step + 1 :])):
            hops[k, step, j] = send(
                cut(k, lax.bitwise_xor(partner, m)), landed.at[k, slot + j],
                s_hop.at[k, slot + j], r_hop.at[k, slot + j], (partner, t),
            )

    def land(k, step):
        slot = 0 if step == 0 else n_d - (n_d >> step)
        for j, m in enumerate(combos(orders(n_d)[k % 2][step + 1 :])):
            hops[k, step, j].wait_recv()
            add_rows(cut(k, lax.bitwise_xor(d, m)), landed.at[k, slot + j])
        if step + 1 < bits:
            hop(k, step + 1)
        else:
            away(k)

    def spread(n, source):
        at = span(d, fulls[n].shape[0] // n_d)
        for j, p in enumerate(peers):
            spreads.append(send(source, fulls[n].at[at, :], s_all.at[n, j], r_all.at[n, j], (p, t)))

    def owner(i):
        return lax.rem(t, group) * trees + i

    def away(k):
        here = t // group

        @pl.when(owner(k) != t)
        def _():
            send(cut(k, d), far.at[here], s_own.at[k], r_own.at[here], (d, owner(k)))

        @pl.when(owner(k) == t)
        def _():
            far[here] = cut(k, d)[...]

    for k in range(trees):
        loads[k].wait()
        hop(k, 0)
    spread(0, totals[0])
    red_copies = []
    for k, c in enumerate(line):
        red_pairs[k].wait_recv()
        r_out[k] = sum_ref[span(2 * c + core, rows), :] + r_side[k]
        red_copies.append(send(r_out.at[k], r_land.at[k], s_red.at[k], r_red.at[k], (d, 2 * c + core)))
    for n in range(3):
        fulls[n][span(d, fulls[n].shape[0] // n_d), :] = totals[n][...]
    for step in range(bits):
        for k in range(trees):
            land(k, step)
        if step == 0:
            spread(1, totals[1])
            spread(2, totals[2])

    def reduced():
        red_pairs[chips - 1].wait_recv()
        back = [None] * trees
        own = sum_ref[span(t, rows), :].astype(f32) + r_side[chips - 1].astype(f32)
        hit = chip // near
        x = x_ref[...].astype(f32)
        for k in range(chips - 1):
            red_copies[k].wait_recv()
        for tree in range(trees):
            e = jnp.where(hit == tree, own, 0.0)
            for k in range(chips - 1):
                source = lax.rem(chip + chips - 1 - k, chips)
                e = e + jnp.where(source // near == tree, r_land[k].astype(f32), 0.0)
            norm, r = ln_parts(x[tree])
            g, b = jnp.sum(e * norm, axis=0, keepdims=True), jnp.sum(e, axis=0, keepdims=True)
            bt_ref[tree] = (hid_ref[tree] + ln_back(e, norm, r, par_ref[6:7])).astype(bf16)
            back[tree] = (g, b)
        vec_now[0:6] = vec_in[0:6]
        vec_now[6:7] = sum(g for g, _ in back)
        vec_now[7:8] = sum(b for _, b in back)

    vec_partners = [(d, other)] + [(lax.bitwise_xor(d, 1 << b), t) for b in range(bits)]
    vec_copies = []

    def vec_step(i):
        if i > 0:
            vec_copies[i - 1].wait()
            vec_now[...] = vec_now[...] + vec_got[i - 1]
        if i < len(vec_partners):
            vec_got[len(vec_partners) + i] = vec_now[...]
            vec_copies.append(
                send(vec_got.at[len(vec_partners) + i], vec_got.at[i], s_vec.at[i], r_vec.at[i], vec_partners[i])
            )
        else:
            vec_far[chip] = vec_now[...]
            for k, c in enumerate(line):
                n = len(vec_partners) + k
                vec_copies.append(
                    send(vec_far.at[chip], vec_far.at[chip], s_vec.at[n], r_vec.at[n], (d, 2 * c + core))
                )

    def widen_all(n):
        full, out = fulls[n], outs[n]
        for j in range(n_d - 1):
            spread_of[n][j].wait_recv()
        height = 64
        while full.shape[0] % height:
            height //= 2

        def widen(i, _):
            out[span(i, height), :] = full[span(i, height), :].astype(f32)
            return 0

        lax.fori_loop(0, full.shape[0] // height, widen, 0)

    for j in range(trees):
        giver = j * group + t // trees

        @pl.when(giver != t)
        def _():
            pltpu.make_async_remote_copy(
                src_ref=far.at[j], dst_ref=far.at[j], send_sem=s_own.at[0], recv_sem=r_own.at[j],
                device_id=(d, giver), device_id_type=MESH,
            ).wait_recv()

    total = far[0].astype(f32)
    for j in range(1, trees):
        total = total + far[j].astype(f32)
    at = span(d, full_ig.shape[0] // n_d)
    full_ig[at, :] = total.astype(bf16)
    spread(3, full_ig.at[at, :])
    spread_of = [spreads[n * (n_d - 1) : (n + 1) * (n_d - 1)] for n in range(4)]

    reduced()
    for i in range(len(vec_partners) + 1):
        vec_step(i)
        if i < 3:
            widen_all(i)
    for n in range(len(vec_partners) + 1, 3):
        widen_all(n)
    widen_all(3)
    for k in range(chips - 1):
        vec_copies[len(vec_partners) + k].wait()
    total = vec_far[0]
    for c in range(1, chips):
        total = total + vec_far[c]
    vec_ref[...] = total

    for k in range(trees):

        @pl.when(owner(k) != t)
        def _():
            pltpu.make_async_remote_copy(
                src_ref=cut(k, d), dst_ref=cut(k, d), send_sem=s_own.at[k], recv_sem=r_own.at[0],
                device_id=(d, owner(k)), device_id_type=MESH,
            ).wait_send()

    for copy in red_pairs + red_copies + list(hops.values()) + spreads:
        copy.wait_send()


def finish(n_d, n_t, partial, x, hidden, par, vec, up_t, down_t, out_t, in_g):
    trees, rows, wide = x.shape
    chips = n_t // 2
    bits = n_d.bit_length() - 1
    dma = pltpu.SemaphoreType.DMA
    sds = jax.ShapeDtypeStruct
    shapes = [(a.shape[0] * n_d, a.shape[1]) for a in (up_t, down_t, out_t)] + [in_g.shape[1:]]
    vm = lambda lead, shape, kind=bf16: pltpu.VMEM(tuple(lead) + tuple(shape), kind)
    part = (shapes[3][0] // n_d, shapes[3][1])
    partners = 1 + bits
    return pl.pallas_call(
        functools.partial(finish_kernel, n_d, n_t),
        in_specs=[VMEM] * 8 + [HBM],
        out_specs=[VMEM] * 6,
        out_shape=[sds(x.shape, bf16), sds((8, wide), f32)] + [sds(s, f32) for s in shapes],
        scratch_shapes=[vm((trees,), shapes[3]), vm((trees, n_d - 1), part), vm((trees,), part)]
        + [vm((), s) for s in shapes] + [
            vm((chips, rows), (wide,)), vm((chips - 1, rows), (wide,)), vm((chips - 1, rows), (wide,)),
            vm((8,), (wide,), f32), vm((2 * partners, 8), (wide,), f32), vm((chips, 8), (wide,), f32),
            dma((trees,)), dma((trees, n_d - 1)), dma((trees, n_d - 1)),
            dma((4, n_d - 1)), dma((4, n_d - 1)),
            dma((trees,)), dma((trees,)),
            dma((chips - 1,)), dma((chips - 1,)), dma((chips,)), dma((chips,)),
            dma((partners + chips - 1,)), dma((partners + chips - 1,)),
        ],
        compiler_params=pltpu.CompilerParams(
            collective_id=3, has_side_effects=True, vmem_limit_bytes=67043328
        ),
        name="finish",
    )(partial, x, hidden, par, vec, up_t, down_t, out_t, in_g)


def shards(
    n_d, n_t,
    tokens, cotangent, lengths, parents, first_gain, first_shift, in_weight, out_weight,
    second_gain, second_shift, third_gain, third_shift, up_weight, down_weight, fourth_gain, fourth_shift,
):
    trees, rows, wide = tokens.shape
    group = n_t // trees
    d, t = lax.axis_index("dp"), lax.axis_index("tensor")
    tree = t // group
    width = out_weight.shape[0]

    mine = lambda a: lax.dynamic_index_in_dim(a, tree, 0, keepdims=False)
    cosine, sine, mq, mk = tables(mine(lengths), mine(parents), n_t * rows)

    x = tokens.astype(f32)
    normed = layer_norm(x, first_gain, first_shift)
    gathered, w, down_all = gather_tree(
        n_d, n_t, normed.astype(bf16), in_weight.transpose(1, 0, 2), down_weight
    )
    w = w.transpose(1, 2, 0, 3).reshape(3, wide, -1)
    q, k, v, kt, vt = project(gathered, w, cosine, sine, mq, mk)
    attended, qb, att, out_all, up_all = attend(n_d, n_t, trees, q, k, vt, out_weight, up_weight)
    par = jnp.stack(
        [second_gain, second_shift, third_gain, third_shift, fourth_gain, fourth_shift, first_gain, first_shift]
    )
    flat = lambda a: a.reshape(trees * rows, a.shape[-1])
    output, back_hidden, back_att, up_g, down_g, out_g, vec = feed(
        flat(att), flat(tokens), flat(cotangent), out_all.reshape(-1, wide), par, up_all, down_all
    )
    back_mixed, up_t, down_t, out_t = attend_back(
        n_d, n_t, qb, k, v, kt, back_att.reshape(trees, rows, wide), attended, cosine, sine,
        up_g, down_g, out_g.reshape(n_t, width, wide),
    )
    w_flat = w.transpose(1, 0, 2).reshape(wide, -1)
    partial = lax.dot_general(back_mixed, w_flat, NT, preferred_element_type=f32).astype(bf16)
    in_part = lax.dot_general(gathered, back_mixed, TN, preferred_element_type=f32)
    in_part = in_part.astype(bf16).reshape(wide, 3, trees, width).transpose(2, 1, 0, 3)
    back_tokens, vec, up_sum, down_sum, out_sum, in_sum = finish(
        n_d, n_t, partial, tokens, back_hidden.reshape(x.shape), par, vec,
        up_t, down_t, out_t, in_part.reshape(trees, 3 * wide, width),
    )
    return (
        output.reshape(tokens.shape),
        back_tokens,
        vec[6], vec[7],
        in_sum.reshape(3, wide, width).transpose(1, 0, 2),
        out_sum,
        vec[0], vec[1], vec[2], vec[3],
        up_sum,
        down_sum,
        vec[4], vec[5],
    )


def solution(mesh):
    in_specs = (
        P("dp", "tensor", None), P("dp", "tensor", None), P("dp", None), P("dp", None),
        P(), P(), P(None, None, "tensor"), P("tensor", None), P(), P(), P(), P(),
        P(None, "tensor"), P("tensor", None), P(), P(),
    )
    out_specs = (
        P("dp", "tensor", None), P("dp", "tensor", None), P(), P(), P(None, None, "tensor"),
        P("tensor", None), P(), P(), P(), P(), P(None, "tensor"), P("tensor", None), P(), P(),
    )
    run = functools.partial(shards, mesh.shape["dp"], mesh.shape["tensor"])
    return jax.shard_map(run, mesh=mesh, in_specs=in_specs, out_specs=out_specs, check_vma=False)
```

```python
import functools
import jax
import jax.numpy as jnp
from jax import lax
from jax.experimental import pallas as pl
from jax.experimental.pallas import tpu as pltpu
from jax.sharding import PartitionSpec as P

HEAD_DIM = 64
LANES = 128
VROWS = 80
BLOCK = 256
TRUNK = 512
SEGMENTS = 13

rope_base = 10000.0
norm_eps = 1e-05
masked_score = -1e30
f32, bf16 = jnp.float32, jnp.bfloat16
NN = (((1,), (0,)), ((), ()))
NT = (((1,), (1,)), ((), ()))
TN = (((0,), (0,)), ((), ()))
MESH = pl.DeviceIdType.MESH
VMEM = pl.BlockSpec(memory_space=pltpu.VMEM)
HBM = pl.BlockSpec(memory_space=pltpu.HBM)


def dot(a, b, dims=NN):
    return lax.dot_general(a, b, dims, preferred_element_type=f32)


def lane_of(shape):
    return lax.broadcasted_iota(jnp.int32, shape, len(shape) - 1)


def row_of(shape):
    return lax.broadcasted_iota(jnp.int32, shape, len(shape) - 2)


def span(i, n):
    return pl.ds(pl.multiple_of(i * n, n), n)


def split3(v):
    hi = v.astype(bf16).astype(f32)
    mid = (v - hi).astype(bf16).astype(f32)
    return hi, mid, v - hi - mid


def layer_norm(values, gain, shift):
    average = jnp.mean(values, axis=-1, keepdims=True)
    centered = values - average
    spread = jnp.mean(centered * centered, axis=-1, keepdims=True)
    return centered * lax.rsqrt(spread + norm_eps) * gain + shift


def tree_layout(tree_lengths, tree_parents, rows):
    seg_sizes = jnp.concatenate([jnp.full((1,), TRUNK, jnp.int32), tree_lengths])
    ends = jnp.cumsum(seg_sizes)
    starts = ends - seg_sizes
    places = jnp.arange(rows, dtype=jnp.int32)
    labels = jnp.arange(SEGMENTS, dtype=jnp.int32)
    segment = jnp.sum((places[:, None] >= ends[None, :]).astype(jnp.int32), axis=1)
    own_hot = (segment[:, None] == labels[None, :]).astype(jnp.int32)
    parent = jnp.sum(own_hot * tree_parents[None, :], axis=1)
    parent_hot = (parent[:, None] == labels[None, :]).astype(jnp.int32)
    grandparent = jnp.sum(parent_hot * tree_parents[None, :], axis=1)
    parent_size = jnp.sum(parent_hot * seg_sizes[None, :], axis=1)
    depth_start = jnp.where(segment > 0, TRUNK, 0).astype(jnp.int32) + jnp.where(
        parent > 0, parent_size, 0
    )
    position = places - jnp.sum(own_hot * starts[None, :], axis=1) + depth_start
    return (segment, parent, grandparent, position)


def tables(tree_lengths, tree_parents, rows):
    segment, parent, grand, position = tree_layout(tree_lengths, tree_parents, rows)
    lane = jnp.arange(LANES, dtype=jnp.int32)
    half = HEAD_DIM // 2
    inverse = rope_base ** (-(lane % half).astype(f32) * 2.0 / HEAD_DIM)
    angle = position.astype(f32)[:, None] * inverse[None, :]
    cosine = jnp.cos(angle)
    sine = jnp.where((lane % HEAD_DIM) < half, -1.0, 1.0)[None, :] * jnp.sin(angle)
    label = (lane - HEAD_DIM)[None, :]
    own = segment[:, None] == label
    path = own | (parent[:, None] == label) | (grand[:, None] == label)
    hidden = (label >= 0) & (label < SEGMENTS) & ~path
    queries = jnp.where(hidden, masked_score, 0.0).astype(f32)
    ones = (label >= 16) & (label < 19)
    keys = jnp.where(own | ones, 1.0, 0.0).astype(f32)
    return cosine, sine, queries, keys
def barrier(partners):
    semaphore = pltpu.get_barrier_semaphore()
    for partner in partners:
        pl.semaphore_signal(semaphore, inc=1, device_id=partner, device_id_type=MESH)
    pl.semaphore_wait(semaphore, len(partners))


def send(source, target, send_sem, recv_sem, device):
    copy = pltpu.make_async_remote_copy(
        src_ref=source,
        dst_ref=target,
        send_sem=send_sem,
        recv_sem=recv_sem,
        device_id=device,
        device_id_type=MESH,
    )
    copy.start()
    return copy


def add_rows(target, source, step=64):
    rows = target.shape[0]
    step = min(step, rows)
    while rows % step:
        step //= 2

    def body(i, _):
        at = span(i, step)
        target[at, :] = target[at, :] + source[at, :]
        return 0

    lax.fori_loop(0, rows // step, body, 0)


def orders(n_d):
    bits = n_d.bit_length() - 1
    return [list(range(bits)), list(range(bits - 1, -1, -1))]


def combos(bits):
    masks = [0]
    for b in bits:
        masks = masks + [m ^ (1 << b) for m in masks]
    return masks


class Spread:
    def __init__(self, n_d, n_t, shards, alls, sems):
        self.n_d, self.n_t, self.shards, self.alls = n_d, n_t, shards, alls
        self.zs, self.zr, self.ps, self.pr, self.ys, self.yr, self.own = sems
        self.d, self.t = lax.axis_index("dp"), lax.axis_index("tensor")
        self.chips = n_t // 2
        self.chip, self.core = self.t // 2, lax.rem(self.t, 2)
        self.other = 2 * self.chip + 1 - self.core
        self.bits = n_d.bit_length() - 1
        self.arrays = range(len(shards))

    @staticmethod
    def sems(count, n_d, n_t):
        dma = pltpu.SemaphoreType.DMA
        hops, slots = n_t // 2 - 1, 2 * (n_d - 1)
        z, p, y = (count, 2 * hops), (count, 2 * hops, slots), (count, 2 * hops + 1)
        return [dma(z), dma(z), dma(p), dma(p), dma(y), dma(y), dma((count,))]

    def exists(self, c):
        return (c >= 0) & (c < self.chips)

    def rows(self, a):
        return self.shards[a].shape[0] // self.n_d

    def slot(self, way, h):
        return h - 1 + (self.chips - 1 if way < 0 else 0)

    def remote(self, src, dst, ssem, rsem, device):
        return pltpu.make_async_remote_copy(
            src_ref=src, dst_ref=dst, send_sem=ssem, recv_sem=rsem, device_id=device, device_id_type=MESH
        )

    def along(self, a, way, h, arriving):
        source = self.chip - way * (h if arriving else h - 1)
        at = span(self.d, self.rows(a))
        dst = self.alls[a].at[2 * source + self.core, at]
        src = self.shards[a].at[at] if h == 1 and not arriving else dst
        peer = self.chip - way if arriving else self.chip + way
        i = self.slot(way, h)
        return self.remote(src, dst, self.zs.at[a, i], self.zr.at[a, i], (self.d, 2 * peer + self.core))

    def across(self, a, way, h, step, arriving):
        source = self.chip - way * h
        q, half = self.rows(a), self.shards[a].shape[1] // 2
        out = []
        for stream, order in enumerate(orders(self.n_d)):
            partner = lax.bitwise_xor(self.d, 1 << order[step])
            for j, m in enumerate(combos(order[:step])):
                block = lax.bitwise_xor(partner if arriving else self.d, m)
                ref = self.alls[a].at[2 * source + self.core, span(block, q), pl.ds(stream * half, half)]
                i = stream * (self.n_d - 1) + (1 << step) - 1 + j
                k = self.slot(way, h)
                out.append(self.remote(ref, ref, self.ps.at[a, k, i], self.pr.at[a, k, i], (partner, self.t)))
        return out

    def beside(self, a, way, h, arriving=False):
        source = self.chip - way * h
        ref = self.alls[a].at[2 * source + (1 - self.core if arriving else self.core)]
        k = self.slot(way, h)
        return self.remote(ref, ref, self.ys.at[a, k], self.yr.at[a, k], (self.d, self.other))

    def mine(self, a, arriving=False):
        k = 2 * (self.chips - 1)
        dst = self.alls[a].at[self.other if arriving else self.t]
        return self.remote(self.shards[a], dst, self.ys.at[a, k], self.yr.at[a, k], (self.d, self.other))

    def keep(self, a):
        return pltpu.make_async_copy(self.shards[a], self.alls[a].at[self.t], self.own.at[a])

    def begin(self):
        for way in (1, -1):

            @pl.when(self.exists(self.chip + way))
            def _():
                for a in self.arrays:
                    self.along(a, way, 1, False).start()

        for a in self.arrays:
            self.keep(a).start()
            self.mine(a).start()

    def phase(self, p, h):
        for way in (1, -1):

            @pl.when(self.exists(self.chip - way * h))
            def _():
                for a in self.arrays:
                    if p == 0:
                        self.along(a, way, h, True).wait_recv()
                        if h < self.chips - 1:

                            @pl.when(self.exists(self.chip + way))
                            def _():
                                self.along(a, way, h + 1, False).start()
                    else:
                        for copy in self.across(a, way, h, p - 1, True):
                            copy.wait_recv()
                    if p < self.bits:
                        for copy in self.across(a, way, h, p, False):
                            copy.start()
                    else:
                        self.beside(a, way, h).start()

    def groups(self):
        return self.chips - 1 + self.bits

    def group(self, g):
        for h in range(1, self.chips):
            if 0 <= g - (h - 1) <= self.bits:
                self.phase(g - (h - 1), h)

    def end(self):
        for h in range(1, self.chips):
            for way in (1, -1):

                @pl.when(self.exists(self.chip + way) & self.exists(self.chip - way * (h - 1)))
                def _():
                    for a in self.arrays:
                        self.along(a, way, h, False).wait_send()

                @pl.when(self.exists(self.chip - way * h))
                def _():
                    for a in self.arrays:
                        for step in range(self.bits):
                            for copy in self.across(a, way, h, step, False):
                                copy.wait_send()
                        self.beside(a, way, h).wait_send()
                        self.beside(a, way, h, True).wait_recv()

        for a in self.arrays:
            self.keep(a).wait()
            self.mine(a).wait_send()
            self.mine(a, True).wait_recv()


def gather_kernel(
    n_d, n_t, x_ref, w_ref, f_ref, o_ref, u_ref, all_ref,
    passing, rs, ss, rb, sb, rw, sw, rp, sp, *sems,
):
    d, t = lax.axis_index("dp"), lax.axis_index("tensor")
    trees, rows, _ = x_ref.shape
    chips = n_t // 2
    group = n_t // trees
    chip, core = t // 2, lax.rem(t, 2)
    other = 2 * chip + 1 - core
    near = group // 2
    tree = t // group
    planes = [lax.rem(d + k, n_d) for k in range(1, n_d)]
    owners = [(j * group + t // trees) for j in range(trees)]
    givers = [lax.rem(t, group) * trees + i for i in range(trees)]
    barrier([(d, lax.rem(t + k, n_t)) for k in range(1, n_t)] + [(p, t) for p in planes])
    part = w_ref.shape[1] // n_d
    weights = Spread(n_d, n_t, [f_ref], [all_ref], sems)
    exists = weights.exists

    copies = []
    mine = w_ref.at[:, span(d, part), :]
    for j in range(trees):
        slot = u_ref.at[lax.rem(t, trees), :, span(d, part), :]

        @pl.when(owners[j] != t)
        def _():
            send(mine, slot, sw.at[j], rw.at[lax.rem(t, trees)], (d, owners[j]))

        @pl.when(owners[j] == t)
        def _():
            u_ref[lax.rem(t, trees), :, span(d, part), :] = w_ref[:, span(d, part), :]

    weights.begin()

    def block(c):
        return o_ref.at[span(2 * c + core, rows)]

    def beyond(c, way, j):
        return (j * near + near - 1 >= c) if way > 0 else (j * near <= c)

    def hop(way, h, j, here):
        source = chip - way * (h - 1)
        if h == 1:
            src = x_ref.at[j]
        else:
            src = block(source) if here else passing.at[j, source]
        return src, source

    def pass_on(way, h):
        for j in range(trees):

            @pl.when(exists(chip - way * (h - 1)) & exists(chip + way) & beyond(chip + way, way, j))
            def _():
                i = weights.slot(way, h)
                to = chip + way
                for here in (True, False) if h > 1 else (True,):
                    src, source = hop(way, h, j, here)
                    for there in (True, False):
                        at_home = (tree == j) if here else (tree != j)
                        lands = (to // near == j) if there else (to // near != j)

                        @pl.when((at_home & lands) if h > 1 else lands)
                        def _():
                            dst = block(source) if there else passing.at[j, source]
                            send(src, dst, ss.at[j, i], rs.at[j, i], (d, 2 * to + core))

    def row_copy(j, i):
        return weights.remote(x_ref.at[j], passing.at[j, 0], ss.at[j, i], rs.at[j, i], (d, other))

    def share(way, h):
        source = chip - way * h
        i = weights.slot(way, h)
        return weights.remote(block(source), block(source), sb.at[i], rb.at[i], (d, other))

    def arrive(way, h):
        for j in range(trees):

            @pl.when(exists(chip - way * h) & beyond(chip, way, j))
            def _():
                row_copy(j, weights.slot(way, h)).wait_recv()

        if h < chips - 1:
            pass_on(way, h + 1)

        @pl.when(exists(chip - way * h))
        def _():
            share(way, h).start()

    for way in (1, -1):
        pass_on(way, 1)
    o_ref[span(t, rows), :] = x_ref[tree]
    last = 2 * (chips - 1)
    copies.append(send(x_ref.at[tree], block(chip), sb.at[last], rb.at[last], (d, other)))
    weights.group(0)
    for i in range(trees):
        slot = u_ref.at[i, :, span(d, part), :]

        @pl.when(givers[i] != t)
        def _():
            pltpu.make_async_remote_copy(
                src_ref=mine, dst_ref=slot, send_sem=sw.at[0], recv_sem=rw.at[i],
                device_id=(d, givers[i]), device_id_type=MESH,
            ).wait_recv()

    mine_all = u_ref.at[:, :, span(d, part), :]
    for k, p in enumerate(planes):
        copies.append(send(mine_all, mine_all, sp.at[k], rp.at[k], (p, t)))
    for h in range(1, chips):
        for way in (1, -1):
            arrive(way, h)
        weights.group(h)
    for g in range(chips, weights.groups()):
        weights.group(g)
    weights.end()
    for j in range(trees):

        @pl.when(owners[j] != t)
        def _():
            pltpu.make_async_remote_copy(
                src_ref=mine, dst_ref=mine, send_sem=sw.at[j], recv_sem=rw.at[0],
                device_id=(d, owners[j]), device_id_type=MESH,
            ).wait_send()

    for way in (1, -1):
        for h in range(1, chips):
            for j in range(trees):

                @pl.when(exists(chip - way * (h - 1)) & exists(chip + way) & beyond(chip + way, way, j))
                def _():
                    row_copy(j, weights.slot(way, h)).wait_send()

            @pl.when(exists(chip - way * h))
            def _():
                share(way, h).wait()

    for copy in copies:
        copy.wait()


def gather_tree(n_d, n_t, normed, weight, down):
    trees, rows, wide = normed.shape
    chips = n_t // 2
    hops = 2 * (chips - 1)
    dma = pltpu.SemaphoreType.DMA
    return pl.pallas_call(
        functools.partial(gather_kernel, n_d, n_t),
        in_specs=[VMEM] * 3,
        out_specs=[VMEM] * 2 + [HBM],
        out_shape=[
            jax.ShapeDtypeStruct((n_t * rows, wide), bf16),
            jax.ShapeDtypeStruct((trees,) + weight.shape, bf16),
            jax.ShapeDtypeStruct((n_t,) + down.shape, bf16),
        ],
        scratch_shapes=[
            pltpu.VMEM((trees, chips, rows, wide), bf16),
            dma((trees, hops)), dma((trees, hops)), dma((hops + 1,)), dma((hops + 1,)),
            dma((trees,)), dma((trees,)), dma((n_d - 1,)), dma((n_d - 1,)),
        ] + Spread.sems(1, n_d, n_t),
        compiler_params=pltpu.CompilerParams(collective_id=0, has_side_effects=True),
        name="gather_tree",
    )(normed, weight, down)


def qkv_kernel(x_ref, w_ref, cos_ref, sin_ref, mq_ref, mk_ref, q_ref, k_ref, v_ref, kt_ref, vt_ref):
    x = x_ref[...]
    heads = q_ref.shape[0]
    cosine, sine = cos_ref[...], sin_ref[...]
    mq, mk = mq_ref[...], mk_ref[...]
    lane = lane_of(cosine.shape)
    low = lax.rem(lane, HEAD_DIM) < HEAD_DIM // 2
    first = lane < HEAD_DIM
    mv = jnp.where((lane >= HEAD_DIM) & (lane < HEAD_DIM + 3), 1.0, 0.0)
    tail = jnp.where(row_of((VROWS - HEAD_DIM, x.shape[0])) == 0, 1.0, 0.0).astype(bf16)

    def both(slab):
        return slab, pltpu.roll(slab, HEAD_DIM, 1)

    def rotate(slab):
        partner = jnp.where(
            low, pltpu.roll(slab, LANES - HEAD_DIM // 2, 1), pltpu.roll(slab, HEAD_DIM // 2, 1)
        )
        return slab * cosine + partner * sine

    q_all, k_all, v_all = (dot(x, w_ref[i]) for i in range(3))
    for h in range(0, heads, 2):
        cols = slice(h * HEAD_DIM, (h + 2) * HEAD_DIM)
        for g, slab in enumerate(both(rotate(q_all[:, cols]) * HEAD_DIM**-0.5)):
            q_ref[h + g] = jnp.where(first, slab, mq).astype(bf16)
        keys = rotate(k_all[:, cols])
        for g, slab in enumerate(both(keys)):
            k_ref[h + g] = jnp.where(first, slab, mk).astype(bf16)
        flat = keys.T.astype(bf16)
        for g, slab in enumerate(both(v_all[:, cols])):
            v_ref[h + g] = jnp.where(first, slab, mv).astype(bf16)
        flat_v = v_all[:, cols].T.astype(bf16)
        for g in range(2):
            part = slice(g * HEAD_DIM, (g + 1) * HEAD_DIM)
            kt_ref[h + g] = flat[part]
            vt_ref[h + g, :HEAD_DIM] = flat_v[part]
            vt_ref[h + g, HEAD_DIM:] = tail


def project(x, w, cosine, sine, mq, mk):
    rows, wide = x.shape
    heads = w.shape[2] // HEAD_DIM
    table = pl.BlockSpec((BLOCK, LANES), lambda i: (i, 0))
    slab = pl.BlockSpec((heads, BLOCK, LANES), lambda i: (0, i, 0))
    shape = jax.ShapeDtypeStruct((heads, rows, LANES), bf16)
    return pl.pallas_call(
        qkv_kernel,
        grid=(rows // BLOCK,),
        in_specs=[
            pl.BlockSpec((BLOCK, wide), lambda i: (i, 0)),
            pl.BlockSpec(w.shape, lambda i: (0, 0, 0)),
            table, table, table, table,
        ],
        out_specs=[
            slab, slab, slab,
            pl.BlockSpec((heads, HEAD_DIM, BLOCK), lambda i: (0, 0, i)),
            pl.BlockSpec((heads, VROWS, BLOCK), lambda i: (0, 0, i)),
        ],
        out_shape=[
            shape, shape, shape,
            jax.ShapeDtypeStruct((heads, HEAD_DIM, rows), bf16),
            jax.ShapeDtypeStruct((heads, VROWS, rows), bf16),
        ],
        name="project",
    )(x, w, cosine, sine, mq, mk)


def fwd_kernel(
    n_d, n_t, trees, q_ref, k_ref, vt_ref, ow_ref, up_ref, o_ref, qb_ref, att_ref, ow_all, up_all,
    ss, rs, here, *sems,
):
    turn = pl.program_id(0)
    steps = pl.num_programs(0)
    heads = q_ref.shape[0]
    row, col = row_of((BLOCK, BLOCK)), lane_of((BLOCK, BLOCK))
    d, t = lax.axis_index("dp"), lax.axis_index("tensor")
    group = n_t // trees
    rows, width = att_ref.shape[1], o_ref.shape[1]
    per = BLOCK // rows
    qi = jnp.where(turn == steps - 1, t // per, jnp.where(turn >= t // per, turn + 1, turn))
    at = span(qi, BLOCK)
    weights = Spread(n_d, n_t, [up_ref, ow_ref], [up_all, ow_all], sems)
    first_group = max(0, k_ref.shape[1] // BLOCK - 4)
    place = att_ref.at[t // group, :, span(lax.rem(t, group), width)]

    def outgoing(i, r, k):
        return pltpu.make_async_remote_copy(
            src_ref=o_ref.at[span(i * per + r, rows)], dst_ref=place, send_sem=ss.at[k], recv_sem=rs.at[k],
            device_id=(d, lax.rem(t + k, n_t)), device_id_type=MESH,
        )

    @pl.when(turn == 0)
    def _():
        barrier(
            [(d, lax.rem(t + k, n_t)) for k in range(1, n_t)] + [(lax.rem(d + k, n_d), t) for k in range(1, n_d)]
        )
        weights.begin()

    for g in range(weights.groups()):
        if first_group + g < k_ref.shape[1] // BLOCK:

            @pl.when(turn == first_group + g)
            def _():
                weights.group(g)

    qs = [q_ref[h, at, :] for h in range(heads)]

    def scores(h, j):
        return dot(k_ref[h, span(j, BLOCK), :], qs[h], NT)

    state = []
    for h in range(heads):
        s = jnp.where(row <= col, scores(h, qi), masked_score)
        m = jnp.max(s, axis=0, keepdims=True)
        p = jnp.exp(s - m)
        state.append((m, dot(vt_ref[h, :, span(qi, BLOCK)], p.astype(bf16))))

    def step(j, carry):
        out = []
        for h in range(heads):
            m, acc = carry[h]
            s = scores(h, j)
            top = jnp.maximum(m, jnp.max(s, axis=0, keepdims=True))
            p = jnp.exp(s - top)
            acc = acc * jnp.exp(m - top) + dot(vt_ref[h, :, span(j, BLOCK)], p.astype(bf16))
            out.append((top, acc))
        return tuple(out)

    state = lax.fori_loop(0, qi, step, tuple(state))
    r = row_of((LANES, BLOCK))
    for h in range(0, heads, 2):
        outs = []
        for g in (h, h + 1):
            m, acc = state[g]
            total = acc[HEAD_DIM : HEAD_DIM + 1]
            outs.append(acc[:HEAD_DIM] / total)
            a, b, c = split3(-(m + jnp.log(total)))
            extra = jnp.where(r == 80, a, jnp.where(r == 81, b, jnp.where(r == 82, c, 0.0))).T
            qb_ref[g, at, :] = qs[g] + extra.astype(bf16)
        o_ref[at, h * HEAD_DIM : (h + 2) * HEAD_DIM] = jnp.concatenate(outs, axis=0).T.astype(bf16)

    def local(r):
        return pltpu.make_async_copy(o_ref.at[span(t // per * per + r, rows)], place, here.at[0])

    for r in range(per):
        k = lax.rem(qi * per + r + n_t - t, n_t)

        @pl.when(k != 0)
        def _():
            outgoing(qi, r, k).start()

        @pl.when(k == 0)
        def _():
            local(r).start()

    @pl.when(turn == steps - 1)
    def _():
        for g in range(k_ref.shape[1] // BLOCK - first_group, weights.groups()):
            weights.group(g)
        for k in range(1, n_t):
            outgoing(0, 0, k).wait()
        local(0).wait()
        weights.end()


def attend(n_d, n_t, trees, q, k, vt, ow, up):
    heads, rows, _ = q.shape
    wide = heads * HEAD_DIM
    dma = pltpu.SemaphoreType.DMA
    sds = jax.ShapeDtypeStruct
    return pl.pallas_call(
        functools.partial(fwd_kernel, n_d, n_t, trees),
        grid=(rows // BLOCK,),
        in_specs=[VMEM] * 5,
        out_specs=[VMEM, VMEM, HBM, HBM, HBM],
        out_shape=[
            sds((rows, wide), bf16),
            sds(q.shape, bf16),
            sds((trees, rows // n_t, wide * n_t // trees), bf16),
            sds((n_t,) + ow.shape, bf16),
            sds((n_t,) + up.shape, bf16),
        ],
        scratch_shapes=[
            dma((n_t,)), dma((n_t,)), dma((1,)),
        ] + Spread.sems(2, n_d, n_t),
        compiler_params=pltpu.CompilerParams(collective_id=1, has_side_effects=True),
        name="attend",
    )(q, k, vt, ow, up)


class Reduce:
    def __init__(self, n_d, n_t, sources, totals, scratch):
        self.n_d, self.n_t, self.sources, self.totals = n_d, n_t, sources, totals
        count = len(sources)
        self.mine, self.side, self.land_at, self.far = (
            scratch[i * count : (i + 1) * count] for i in range(4)
        )
        self.s_load, self.s_side, self.r_side, self.s_hop, self.r_hop, self.s_far, self.r_far = scratch[4 * count :]
        self.d, self.t = lax.axis_index("dp"), lax.axis_index("tensor")
        self.chips = n_t // 2
        self.chip, self.core = self.t // 2, lax.rem(self.t, 2)
        self.other = 2 * self.chip + 1 - self.core
        self.dest = [lax.rem(self.chip + k, self.chips) for k in range(1, self.chips)] + [self.chip]
        self.bits = n_d.bit_length() - 1
        self.units = [(n, k) for k in range(self.chips) for n in range(count)]

    @staticmethod
    def scratch(n_d, n_t, shapes):
        dma = pltpu.SemaphoreType.DMA
        chips, slots, count = n_t // 2, 2 * (n_d - 1), len(shapes)
        vm = lambda lead, r, c: pltpu.VMEM(lead + (r, c), bf16)
        units = count * chips
        return (
            [vm((chips,), r, c) for r, c in shapes] * 2
            + [vm((chips, slots), r // n_d, c // 2) for r, c in shapes]
            + [vm((chips - 1,), r // n_d, c) for r, c in shapes]
            + [dma((units,)), dma((units,)), dma((units,)), dma((units, slots)), dma((units, slots))]
            + [dma((units,)), dma((units,))]
        )

    def remote(self, src, dst, ssem, rsem, device):
        return pltpu.make_async_remote_copy(
            src_ref=src, dst_ref=dst, send_sem=ssem, recv_sem=rsem, device_id=device, device_id_type=MESH
        )

    def load(self, u):
        n, k = self.units[u]
        source = self.sources[n].at[2 * self.dest[k] + self.core]
        return pltpu.make_async_copy(source, self.mine[n].at[k], self.s_load.at[u])

    def beside(self, u):
        n, k = self.units[u]
        source = self.sources[n].at[2 * self.dest[k] + 1 - self.core]
        return self.remote(source, self.side[n].at[k], self.s_side.at[u], self.r_side.at[u], (self.d, self.other))

    def cut(self, u, part, stream):
        n, k = self.units[u]
        _, height, width = self.mine[n].shape
        height, width = height // self.n_d, width // 2
        return self.mine[n].at[k, span(part, height), pl.ds(stream * width, width)]

    def hops(self, u, step):
        n, k = self.units[u]
        slot = 0 if step == 0 else self.n_d - (self.n_d >> step)
        out = []
        for stream, order in enumerate(orders(self.n_d)):
            partner = lax.bitwise_xor(self.d, 1 << order[step])
            for j, m in enumerate(combos(order[step + 1 :])):
                i = (slot + j) * 2 + stream
                landing = self.land_at[n].at[k, i]
                copy = self.remote(
                    self.cut(u, lax.bitwise_xor(partner, m), stream), landing,
                    self.s_hop.at[u, i], self.r_hop.at[u, i], (partner, self.t),
                )
                out.append((copy, self.cut(u, lax.bitwise_xor(self.d, m), stream), landing))
        return out

    def piece(self, u):
        n, k = self.units[u]
        return self.mine[n].at[k, span(self.d, self.mine[n].shape[1] // self.n_d), :]

    def away(self, u):
        n, k = self.units[u]
        return self.remote(
            self.piece(u), self.far[n].at[k], self.s_far.at[u], self.r_far.at[u],
            (self.d, 2 * self.dest[k] + self.core),
        )

    def begin(self):
        for u in range(len(self.units)):
            self.load(u).start()
            self.beside(u).start()

    def events(self):
        return len(self.units) + self.bits

    def event(self, e):
        if e < len(self.units):
            n, k = self.units[e]
            self.load(e).wait()
            self.beside(e).wait_recv()
            add_rows(self.mine[n].at[k], self.side[n].at[k])
            for copy, _, _ in self.hops(e, 0):
                copy.start()
        for step in range(self.bits):
            u = e - 1 - step
            if 0 <= u < len(self.units):
                for copy, target, landing in self.hops(u, step):
                    copy.wait_recv()
                    add_rows(target, landing)
                if step + 1 < self.bits:
                    for copy, _, _ in self.hops(u, step + 1):
                        copy.start()
                elif self.units[u][1] < self.chips - 1:
                    self.away(u).start()

    def end(self):
        for u, (n, k) in enumerate(self.units):
            if k < self.chips - 1:
                self.away(u).wait_recv()
            else:
                total = self.piece(u)[...].astype(f32)
                for i in range(self.chips - 1):
                    total = total + self.far[n][i].astype(f32)
                self.totals[n][...] = total.astype(bf16)
        for u, (n, k) in enumerate(self.units):
            self.beside(u).wait_send()
            for step in range(self.bits):
                for copy, _, _ in self.hops(u, step):
                    copy.wait_send()
            if k < self.chips - 1:
                self.away(u).wait_send()


def bwd_kernel(
    n_d, n_t, q_ref, k_ref, v_ref, kt_ref, x_ref, o_ref, cos_ref, sin_ref, up_ref, down_ref, og_ref,
    m_ref, up_tot, down_tot, og_tot, sums, wide, d_ref, hs, hr, *scratch,
):
    j = pl.program_id(0)
    heads, rows, _ = q_ref.shape
    nq = rows // BLOCK
    row, col = row_of((BLOCK, BLOCK)), lane_of((BLOCK, BLOCK))
    lane = lane_of((BLOCK, LANES))
    first = lane < HEAD_DIM
    d, t = lax.axis_index("dp"), lax.axis_index("tensor")
    trees, part, _ = x_ref.shape
    group, width = n_t // trees, heads * HEAD_DIM
    gradients = Reduce(n_d, n_t, [up_ref, down_ref, og_ref], [up_tot, down_tot, og_tot], scratch)
    ahead = 3
    points = 10

    def point(p):
        left = gradients.events() - ahead
        for e in range(ahead + p * left // points, ahead + (p + 1) * left // points):
            gradients.event(e)

    def cut(o):
        return x_ref.at[o // group, :, span(lax.rem(o, group), width)]

    def outgoing(k):
        o = lax.rem(t + k, n_t)
        return gradients.remote(cut(o), d_ref.at[span(t, part), :], hs.at[k], hr.at[k], (d, o))

    @pl.when(j == 0)
    def _():
        barrier(
            [(d, lax.rem(t + k, n_t)) for k in range(1, n_t)] + [(lax.rem(d + k, n_d), t) for k in range(1, n_d)]
        )
        for k in range(1, n_t):
            outgoing(k).start()
        gradients.begin()
        d_ref[span(t, part), :] = cut(t)[...]
        sums[...] = jnp.zeros_like(sums)
        for e in range(ahead):
            gradients.event(e)
        for k in range(1, n_t):
            outgoing(k).wait()

        def widen(i, _):
            at = span(i, BLOCK)
            for h in range(0, heads, 2):
                cols = slice(h * HEAD_DIM, (h + 2) * HEAD_DIM)
                slab = d_ref[at, cols].astype(f32)
                prod = slab * o_ref[at, cols].astype(f32)
                for g, (s, mine) in enumerate(((slab, first), (pltpu.roll(slab, HEAD_DIM, 1), ~first))):
                    inner = -jnp.sum(jnp.where(mine, prod, 0.0), axis=1, keepdims=True)
                    a, b, c = split3(inner)
                    n = HEAD_DIM
                    tail = jnp.where(lane == n, a, jnp.where(lane == n + 1, b, jnp.where(lane == n + 2, c, 0.0)))
                    wide[h + g, at, :] = jnp.where(first, s, tail).astype(bf16)
            return 0

        lax.fori_loop(0, nq, widen, 0)

    for p in range(0, points, 2):
        if p // 2 < nq:

            @pl.when(j == p // 2)
            def _():
                point(p)

    ks = [k_ref[h] for h in range(heads)]
    vs = [v_ref[h] for h in range(heads)]
    kts = [kt_ref[h] for h in range(heads)]

    def pair(h, i, mask):
        at = span(i, BLOCK)
        q = q_ref[h, at, :]
        d = wide[h, at, :]
        s = dot(ks[h], q, NT)
        if mask:
            s = jnp.where(row <= col, s, masked_score)
        p = jnp.exp(s)
        back = (p * dot(vs[h], d, NT)).astype(bf16)
        sums[h, :, at] += dot(kts[h], back)
        return dot(back, q), dot(p.astype(bf16), d)

    def step(i, carry):
        out = []
        for h in range(heads):
            dk, dv = pair(h, i, False)
            out.append((carry[h][0] + dk, carry[h][1] + dv))
        return tuple(out)

    state = tuple(pair(h, j, True) for h in range(heads))
    middle = (j + 1 + nq) // 2
    state = lax.fori_loop(j + 1, middle, step, state)
    for p in range(1, points, 2):
        if p // 2 < nq:

            @pl.when(j == p // 2)
            def _():
                point(p)

    state = lax.fori_loop(middle, nq, step, state)

    def join(a, b):
        return jnp.where(first, a, pltpu.roll(b, HEAD_DIM, 1))

    cosine, sine = cos_ref[...], sin_ref[...]
    low = lax.rem(lane, HEAD_DIM) < HEAD_DIM // 2

    def unrotate(slab):
        partner = jnp.where(
            low, pltpu.roll(slab, LANES - HEAD_DIM // 2, 1), pltpu.roll(slab, HEAD_DIM // 2, 1)
        )
        return slab * cosine - partner * sine

    at = span(j, BLOCK)
    total = heads * HEAD_DIM
    for h in range(0, heads, 2):
        dq = jnp.concatenate([sums[h, :, at], sums[h + 1, :, at]], axis=0).T * HEAD_DIM**-0.5
        dk = join(state[h][0], state[h + 1][0])
        dv = join(state[h][1], state[h + 1][1])
        for n, part in enumerate((unrotate(dq), unrotate(dk), dv)):
            begin = n * total + h * HEAD_DIM
            m_ref[:, begin : begin + 2 * HEAD_DIM] = part.astype(bf16)

    @pl.when(j == nq - 1)
    def _():
        for p in range(2 * nq, points):
            point(p)
        gradients.end()


def attend_back(n_d, n_t, q, k, v, kt, x, o, cosine, sine, up_g, down_g, out_g):
    heads, rows, _ = q.shape
    whole = lambda a: pl.BlockSpec(a.shape, lambda j: (0,) * a.ndim, pipeline_mode=pl.Buffered(1))
    block = pl.BlockSpec((heads, BLOCK, LANES), lambda j: (0, j, 0))
    table = pl.BlockSpec((BLOCK, LANES), lambda j: (j, 0))
    wide = heads * HEAD_DIM
    dma = pltpu.SemaphoreType.DMA
    sds = jax.ShapeDtypeStruct
    shapes = [a.shape[1:] for a in (up_g, down_g, out_g)]
    return pl.pallas_call(
        functools.partial(bwd_kernel, n_d, n_t),
        grid=(rows // BLOCK,),
        in_specs=[
            whole(q), block, block,
            pl.BlockSpec((heads, HEAD_DIM, BLOCK), lambda j: (0, 0, j)),
            VMEM, whole(o), table, table, HBM, HBM, HBM,
        ],
        out_specs=[pl.BlockSpec((BLOCK, 3 * wide), lambda j: (j, 0)), VMEM, VMEM, VMEM],
        out_shape=[sds((rows, 3 * wide), bf16)] + [sds((r // n_d, c), bf16) for r, c in shapes],
        scratch_shapes=[
            pltpu.VMEM((heads, HEAD_DIM, rows), f32),
            pltpu.VMEM((heads, rows, LANES), bf16),
            pltpu.VMEM((rows, wide), bf16),
            dma((n_t,)), dma((n_t,)),
        ] + Reduce.scratch(n_d, n_t, shapes),
        compiler_params=pltpu.CompilerParams(
            collective_id=2, has_side_effects=True, vmem_limit_bytes=67043328
        ),
        name="attend_back",
    )(q, k, v, kt, x, o, cosine, sine, up_g, down_g, out_g)


def ln_parts(v):
    centered = v - jnp.mean(v, axis=-1, keepdims=True)
    r = lax.rsqrt(jnp.mean(centered * centered, axis=-1, keepdims=True) + norm_eps)
    return centered * r, r


def ln_back(e, n, r, gain):
    f = e * gain
    return r * (f - jnp.mean(f, axis=-1, keepdims=True) - n * jnp.mean(f * n, axis=-1, keepdims=True))


def feed_kernel(
    att_ref, x_ref, cot_ref, ow_ref, par_ref, up_ref, down_ref,
    out_ref, hid_ref, ba_ref, upg_ref, downg_ref, outg_ref, vec_ref,
    hidden, branch, acc, feed_in, back_feed, active, slope,
):
    phase, n = pl.program_id(0), pl.program_id(1)
    last = pl.num_programs(1) - 1
    par = lambda i: par_ref[i : i + 1]
    total = lambda v: jnp.sum(v, axis=0, keepdims=True)

    @pl.when((phase == 0) & (n == 0))
    def _():
        b = dot(att_ref[...], ow_ref[...])
        branch[...] = b
        h = x_ref[...].astype(f32) + ln_parts(b)[0] * par(0) + par(1)
        hidden[...] = h
        feed_in[...] = (ln_parts(h)[0] * par(2) + par(3)).astype(bf16)
        acc[...] = jnp.zeros_like(acc)

    up, down = up_ref[0], down_ref[0]

    @pl.when(phase == 0)
    def _():
        u = dot(feed_in[...], up)
        t = jnp.tanh(0.7978845608028654 * (u + 0.044715 * u * u * u))
        half = 0.5 * (1.0 + t)
        a = (u * half).astype(bf16)
        active[n] = a
        slope[n] = half + 0.5 * u * (1.0 - t * t) * (
            0.7978845608028654 * (1.0 + 3 * 0.044715 * u * u)
        )
        acc[...] += dot(a, down)

    @pl.when((phase == 1) & (n == 0))
    def _():
        e = cot_ref[...].astype(f32)
        norm, r = ln_parts(acc[...])
        out_ref[...] = (hidden[...] + norm * par(4) + par(5)).astype(bf16)
        vec_ref[4:5] = total(e * norm)
        vec_ref[5:6] = total(e)
        back_feed[...] = ln_back(e, norm, r, par(4)).astype(bf16)
        acc[...] = jnp.zeros_like(acc)

    @pl.when(phase == 1)
    def _():
        b = back_feed[...]
        upper = (dot(b, down, NT) * slope[n]).astype(bf16)
        acc[...] += dot(upper, up, NT)
        downg_ref[0] = dot(active[n], b, TN).astype(bf16)
        upg_ref[0] = dot(feed_in[...], upper, TN).astype(bf16)

    @pl.when((phase == 1) & (n == last))
    def _():
        e = acc[...]
        norm, r = ln_parts(hidden[...])
        vec_ref[2:3] = total(e * norm)
        vec_ref[3:4] = total(e)
        h = cot_ref[...].astype(f32) + ln_back(e, norm, r, par(2))
        hid_ref[...] = h
        norm, r = ln_parts(branch[...])
        vec_ref[0:1] = total(h * norm)
        vec_ref[1:2] = total(h)
        b = ln_back(h, norm, r, par(0)).astype(bf16)
        ba_ref[...] = dot(b, ow_ref[...], NT).astype(bf16)
        outg_ref[...] = dot(att_ref[...], b, TN).astype(bf16)


def feed(att, x, cot, ow, par, up, down):
    rows, wide = att.shape
    n_t, _, width = up.shape
    one = lambda a: pl.BlockSpec(a.shape, lambda p, n: (0,) * len(a.shape), pipeline_mode=pl.Buffered(1))
    sds = jax.ShapeDtypeStruct
    outs = [
        sds((rows, wide), bf16), sds((rows, wide), f32), sds((rows, wide), bf16),
        sds((n_t, wide, width), bf16), sds((n_t, width, wide), bf16), sds((wide, wide), bf16),
        sds((8, wide), f32),
    ]
    chunk = lambda a: pl.BlockSpec((1,) + a.shape[1:], lambda p, n: (p * n, 0, 0))
    weight = lambda a: pl.BlockSpec((1,) + a.shape[1:], lambda p, n: (n, 0, 0))
    return pl.pallas_call(
        feed_kernel,
        grid=(2, n_t),
        in_specs=[one(a) for a in (att, x, cot, ow, par)] + [weight(up), weight(down)],
        out_specs=[one(o) for o in outs[:3]] + [chunk(outs[3]), chunk(outs[4])] + [one(o) for o in outs[5:]],
        out_shape=outs,
        scratch_shapes=[
            pltpu.VMEM((rows, wide), f32), pltpu.VMEM((rows, wide), f32), pltpu.VMEM((rows, wide), f32),
            pltpu.VMEM((rows, wide), bf16), pltpu.VMEM((rows, wide), bf16),
            pltpu.VMEM((n_t, rows, width), bf16), pltpu.VMEM((n_t, rows, width), f32),
        ],
        compiler_params=pltpu.CompilerParams(vmem_limit_bytes=64 << 20),
        name="feed",
    )(att, x, cot, ow, par, up, down)
def finish_kernel(
    n_d, n_t, sum_ref, x_ref, hid_ref, par_ref, vec_in, up_tot, down_tot, og_tot, ig_ref,
    bt_ref, vec_ref, up_out, down_out, og_out, ig_out,
    mine, landed, far, full_up, full_down, full_og, full_ig,
    r_side, r_out, r_land, vec_now, vec_got, vec_far,
    s_load, s_hop, r_hop, s_all, r_all, s_own, r_own,
    s_red, r_red, s_redside, r_redside, s_vec, r_vec,
):
    d, t = lax.axis_index("dp"), lax.axis_index("tensor")
    trees, rows, wide = x_ref.shape
    chips = n_t // 2
    near = chips // trees
    group = n_t // trees
    chip, core = t // 2, lax.rem(t, 2)
    other = 2 * chip + 1 - core
    line = [lax.rem(chip + k, chips) for k in range(1, chips)]
    dest = line + [chip]
    peers = [lax.rem(d + k, n_d) for k in range(1, n_d)]
    bits = n_d.bit_length() - 1
    barrier([(d, lax.rem(t + k, n_t)) for k in range(1, n_t)] + [(p, t) for p in peers])
    totals = [up_tot, down_tot, og_tot]
    fulls = [full_up, full_down, full_og, full_ig]
    outs = [up_out, down_out, og_out, ig_out]

    red_pairs = []
    for k, c in enumerate(dest):
        theirs = sum_ref.at[span(2 * c + 1 - core, rows), :]
        red_pairs.append(send(theirs, r_side.at[k], s_redside.at[k], r_redside.at[k], (d, other)))
    loads = []
    for k in range(trees):
        loads.append(pltpu.make_async_copy(ig_ref.at[k], mine.at[k], s_load.at[k]))
        loads[k].start()
    hops, spreads = {}, []

    def cut(k, part):
        return mine.at[k, span(part, mine.shape[1] // n_d), :]

    def hop(k, step):
        slot = 0 if step == 0 else n_d - (n_d >> step)
        order = orders(n_d)[k % 2]
        partner = lax.bitwise_xor(d, 1 << order[step])
        for j, m in enumerate(combos(order[step + 1 :])):
            hops[k, step, j] = send(
                cut(k, lax.bitwise_xor(partner, m)), landed.at[k, slot + j],
                s_hop.at[k, slot + j], r_hop.at[k, slot + j], (partner, t),
            )

    def land(k, step):
        slot = 0 if step == 0 else n_d - (n_d >> step)
        for j, m in enumerate(combos(orders(n_d)[k % 2][step + 1 :])):
            hops[k, step, j].wait_recv()
            add_rows(cut(k, lax.bitwise_xor(d, m)), landed.at[k, slot + j])
        if step + 1 < bits:
            hop(k, step + 1)
        else:
            away(k)

    def spread(n, source):
        at = span(d, fulls[n].shape[0] // n_d)
        for j, p in enumerate(peers):
            spreads.append(send(source, fulls[n].at[at, :], s_all.at[n, j], r_all.at[n, j], (p, t)))

    def owner(i):
        return lax.rem(t, group) * trees + i

    def away(k):
        here = t // group

        @pl.when(owner(k) != t)
        def _():
            send(cut(k, d), far.at[here], s_own.at[k], r_own.at[here], (d, owner(k)))

        @pl.when(owner(k) == t)
        def _():
            far[here] = cut(k, d)[...]

    for k in range(trees):
        loads[k].wait()
        hop(k, 0)
    spread(0, totals[0])
    red_copies = []
    for k, c in enumerate(line):
        red_pairs[k].wait_recv()
        r_out[k] = sum_ref[span(2 * c + core, rows), :] + r_side[k]
        red_copies.append(send(r_out.at[k], r_land.at[k], s_red.at[k], r_red.at[k], (d, 2 * c + core)))
    for n in range(3):
        fulls[n][span(d, fulls[n].shape[0] // n_d), :] = totals[n][...]
    for step in range(bits):
        for k in range(trees):
            land(k, step)
        if step == 0:
            spread(1, totals[1])
            spread(2, totals[2])

    def reduced():
        red_pairs[chips - 1].wait_recv()
        back = [None] * trees
        own = sum_ref[span(t, rows), :].astype(f32) + r_side[chips - 1].astype(f32)
        hit = chip // near
        x = x_ref[...].astype(f32)
        for k in range(chips - 1):
            red_copies[k].wait_recv()
        for tree in range(trees):
            e = jnp.where(hit == tree, own, 0.0)
            for k in range(chips - 1):
                source = lax.rem(chip + chips - 1 - k, chips)
                e = e + jnp.where(source // near == tree, r_land[k].astype(f32), 0.0)
            norm, r = ln_parts(x[tree])
            g, b = jnp.sum(e * norm, axis=0, keepdims=True), jnp.sum(e, axis=0, keepdims=True)
            bt_ref[tree] = (hid_ref[tree] + ln_back(e, norm, r, par_ref[6:7])).astype(bf16)
            back[tree] = (g, b)
        vec_now[0:6] = vec_in[0:6]
        vec_now[6:7] = sum(g for g, _ in back)
        vec_now[7:8] = sum(b for _, b in back)

    vec_partners = [(d, other)] + [(lax.bitwise_xor(d, 1 << b), t) for b in range(bits)]
    vec_copies = []

    def vec_step(i):
        if i > 0:
            vec_copies[i - 1].wait()
            vec_now[...] = vec_now[...] + vec_got[i - 1]
        if i < len(vec_partners):
            vec_got[len(vec_partners) + i] = vec_now[...]
            vec_copies.append(
                send(vec_got.at[len(vec_partners) + i], vec_got.at[i], s_vec.at[i], r_vec.at[i], vec_partners[i])
            )
        else:
            vec_far[chip] = vec_now[...]
            for k, c in enumerate(line):
                n = len(vec_partners) + k
                vec_copies.append(
                    send(vec_far.at[chip], vec_far.at[chip], s_vec.at[n], r_vec.at[n], (d, 2 * c + core))
                )

    def widen_all(n):
        full, out = fulls[n], outs[n]
        for j in range(n_d - 1):
            spread_of[n][j].wait_recv()
        height = 64
        while full.shape[0] % height:
            height //= 2

        def widen(i, _):
            out[span(i, height), :] = full[span(i, height), :].astype(f32)
            return 0

        lax.fori_loop(0, full.shape[0] // height, widen, 0)

    for j in range(trees):
        giver = j * group + t // trees

        @pl.when(giver != t)
        def _():
            pltpu.make_async_remote_copy(
                src_ref=far.at[j], dst_ref=far.at[j], send_sem=s_own.at[0], recv_sem=r_own.at[j],
                device_id=(d, giver), device_id_type=MESH,
            ).wait_recv()

    total = far[0].astype(f32)
    for j in range(1, trees):
        total = total + far[j].astype(f32)
    at = span(d, full_ig.shape[0] // n_d)
    full_ig[at, :] = total.astype(bf16)
    spread(3, full_ig.at[at, :])
    spread_of = [spreads[n * (n_d - 1) : (n + 1) * (n_d - 1)] for n in range(4)]

    reduced()
    for i in range(len(vec_partners) + 1):
        vec_step(i)
        if i < 3:
            widen_all(i)
    for n in range(len(vec_partners) + 1, 3):
        widen_all(n)
    widen_all(3)
    for k in range(chips - 1):
        vec_copies[len(vec_partners) + k].wait()
    total = vec_far[0]
    for c in range(1, chips):
        total = total + vec_far[c]
    vec_ref[...] = total

    for k in range(trees):

        @pl.when(owner(k) != t)
        def _():
            pltpu.make_async_remote_copy(
                src_ref=cut(k, d), dst_ref=cut(k, d), send_sem=s_own.at[k], recv_sem=r_own.at[0],
                device_id=(d, owner(k)), device_id_type=MESH,
            ).wait_send()

    for copy in red_pairs + red_copies + list(hops.values()) + spreads:
        copy.wait_send()


def finish(n_d, n_t, partial, x, hidden, par, vec, up_t, down_t, out_t, in_g):
    trees, rows, wide = x.shape
    chips = n_t // 2
    bits = n_d.bit_length() - 1
    dma = pltpu.SemaphoreType.DMA
    sds = jax.ShapeDtypeStruct
    shapes = [(a.shape[0] * n_d, a.shape[1]) for a in (up_t, down_t, out_t)] + [in_g.shape[1:]]
    vm = lambda lead, shape, kind=bf16: pltpu.VMEM(tuple(lead) + tuple(shape), kind)
    part = (shapes[3][0] // n_d, shapes[3][1])
    partners = 1 + bits
    return pl.pallas_call(
        functools.partial(finish_kernel, n_d, n_t),
        in_specs=[VMEM] * 8 + [HBM],
        out_specs=[VMEM] * 6,
        out_shape=[sds(x.shape, bf16), sds((8, wide), f32)] + [sds(s, f32) for s in shapes],
        scratch_shapes=[vm((trees,), shapes[3]), vm((trees, n_d - 1), part), vm((trees,), part)]
        + [vm((), s) for s in shapes] + [
            vm((chips, rows), (wide,)), vm((chips - 1, rows), (wide,)), vm((chips - 1, rows), (wide,)),
            vm((8,), (wide,), f32), vm((2 * partners, 8), (wide,), f32), vm((chips, 8), (wide,), f32),
            dma((trees,)), dma((trees, n_d - 1)), dma((trees, n_d - 1)),
            dma((4, n_d - 1)), dma((4, n_d - 1)),
            dma((trees,)), dma((trees,)),
            dma((chips - 1,)), dma((chips - 1,)), dma((chips,)), dma((chips,)),
            dma((partners + chips - 1,)), dma((partners + chips - 1,)),
        ],
        compiler_params=pltpu.CompilerParams(
            collective_id=3, has_side_effects=True, vmem_limit_bytes=67043328
        ),
        name="finish",
    )(partial, x, hidden, par, vec, up_t, down_t, out_t, in_g)


def shards(
    n_d, n_t,
    tokens, cotangent, lengths, parents, first_gain, first_shift, in_weight, out_weight,
    second_gain, second_shift, third_gain, third_shift, up_weight, down_weight, fourth_gain, fourth_shift,
):
    trees, rows, wide = tokens.shape
    group = n_t // trees
    d, t = lax.axis_index("dp"), lax.axis_index("tensor")
    tree = t // group
    width = out_weight.shape[0]

    mine = lambda a: lax.dynamic_index_in_dim(a, tree, 0, keepdims=False)
    cosine, sine, mq, mk = tables(mine(lengths), mine(parents), n_t * rows)

    x = tokens.astype(f32)
    normed = layer_norm(x, first_gain, first_shift)
    gathered, w, down_all = gather_tree(
        n_d, n_t, normed.astype(bf16), in_weight.transpose(1, 0, 2), down_weight
    )
    w = w.transpose(1, 2, 0, 3).reshape(3, wide, -1)
    q, k, v, kt, vt = project(gathered, w, cosine, sine, mq, mk)
    attended, qb, att, out_all, up_all = attend(n_d, n_t, trees, q, k, vt, out_weight, up_weight)
    par = jnp.stack(
        [second_gain, second_shift, third_gain, third_shift, fourth_gain, fourth_shift, first_gain, first_shift]
    )
    flat = lambda a: a.reshape(trees * rows, a.shape[-1])
    output, back_hidden, back_att, up_g, down_g, out_g, vec = feed(
        flat(att), flat(tokens), flat(cotangent), out_all.reshape(-1, wide), par, up_all, down_all
    )
    back_mixed, up_t, down_t, out_t = attend_back(
        n_d, n_t, qb, k, v, kt, back_att.reshape(trees, rows, wide), attended, cosine, sine,
        up_g, down_g, out_g.reshape(n_t, width, wide),
    )
    w_flat = w.transpose(1, 0, 2).reshape(wide, -1)
    partial = lax.dot_general(back_mixed, w_flat, NT, preferred_element_type=f32).astype(bf16)
    in_part = lax.dot_general(gathered, back_mixed, TN, preferred_element_type=f32)
    in_part = in_part.astype(bf16).reshape(wide, 3, trees, width).transpose(2, 1, 0, 3)
    back_tokens, vec, up_sum, down_sum, out_sum, in_sum = finish(
        n_d, n_t, partial, tokens, back_hidden.reshape(x.shape), par, vec,
        up_t, down_t, out_t, in_part.reshape(trees, 3 * wide, width),
    )
    return (
        output.reshape(tokens.shape),
        back_tokens,
        vec[6], vec[7],
        in_sum.reshape(3, wide, width).transpose(1, 0, 2),
        out_sum,
        vec[0], vec[1], vec[2], vec[3],
        up_sum,
        down_sum,
        vec[4], vec[5],
    )


def solution(mesh):
    in_specs = (
        P("dp", "tensor", None), P("dp", "tensor", None), P("dp", None), P("dp", None),
        P(), P(), P(None, None, "tensor"), P("tensor", None), P(), P(), P(), P(),
        P(None, "tensor"), P("tensor", None), P(), P(),
    )
    out_specs = (
        P("dp", "tensor", None), P("dp", "tensor", None), P(), P(), P(None, None, "tensor"),
        P("tensor", None), P(), P(), P(), P(), P(None, "tensor"), P("tensor", None), P(), P(),
    )
    run = functools.partial(shards, mesh.shape["dp"], mesh.shape["tensor"])
    return jax.shard_map(run, mesh=mesh, in_specs=in_specs, out_specs=out_specs, check_vma=False)
```

```python
import functools
import jax
import jax.numpy as jnp
from jax import lax
from jax.experimental import pallas as pl
from jax.experimental.pallas import tpu as pltpu
from jax.sharding import PartitionSpec as P

HEAD_DIM = 64
LANES = 128
VROWS = 80
BLOCK = 256
TRUNK = 512
SEGMENTS = 13

rope_base = 10000.0
norm_eps = 1e-05
masked_score = -1e30
f32, bf16 = jnp.float32, jnp.bfloat16
NN = (((1,), (0,)), ((), ()))
NT = (((1,), (1,)), ((), ()))
TN = (((0,), (0,)), ((), ()))
MESH = pl.DeviceIdType.MESH
VMEM = pl.BlockSpec(memory_space=pltpu.VMEM)
HBM = pl.BlockSpec(memory_space=pltpu.HBM)


def dot(a, b, dims=NN):
    return lax.dot_general(a, b, dims, preferred_element_type=f32)


def lane_of(shape):
    return lax.broadcasted_iota(jnp.int32, shape, len(shape) - 1)


def row_of(shape):
    return lax.broadcasted_iota(jnp.int32, shape, len(shape) - 2)


def span(i, n):
    return pl.ds(pl.multiple_of(i * n, n), n)


def split3(v):
    hi = v.astype(bf16).astype(f32)
    mid = (v - hi).astype(bf16).astype(f32)
    return hi, mid, v - hi - mid


def layer_norm(values, gain, shift):
    average = jnp.mean(values, axis=-1, keepdims=True)
    centered = values - average
    spread = jnp.mean(centered * centered, axis=-1, keepdims=True)
    return centered * lax.rsqrt(spread + norm_eps) * gain + shift


def tree_layout(tree_lengths, tree_parents, rows):
    seg_sizes = jnp.concatenate([jnp.full((1,), TRUNK, jnp.int32), tree_lengths])
    ends = jnp.cumsum(seg_sizes)
    starts = ends - seg_sizes
    places = jnp.arange(rows, dtype=jnp.int32)
    labels = jnp.arange(SEGMENTS, dtype=jnp.int32)
    segment = jnp.sum((places[:, None] >= ends[None, :]).astype(jnp.int32), axis=1)
    own_hot = (segment[:, None] == labels[None, :]).astype(jnp.int32)
    parent = jnp.sum(own_hot * tree_parents[None, :], axis=1)
    parent_hot = (parent[:, None] == labels[None, :]).astype(jnp.int32)
    grandparent = jnp.sum(parent_hot * tree_parents[None, :], axis=1)
    parent_size = jnp.sum(parent_hot * seg_sizes[None, :], axis=1)
    depth_start = jnp.where(segment > 0, TRUNK, 0).astype(jnp.int32) + jnp.where(
        parent > 0, parent_size, 0
    )
    position = places - jnp.sum(own_hot * starts[None, :], axis=1) + depth_start
    return (segment, parent, grandparent, position)


def tables(tree_lengths, tree_parents, rows):
    segment, parent, grand, position = tree_layout(tree_lengths, tree_parents, rows)
    lane = jnp.arange(LANES, dtype=jnp.int32)
    half = HEAD_DIM // 2
    inverse = rope_base ** (-(lane % half).astype(f32) * 2.0 / HEAD_DIM)
    angle = position.astype(f32)[:, None] * inverse[None, :]
    cosine = jnp.cos(angle)
    sine = jnp.where((lane % HEAD_DIM) < half, -1.0, 1.0)[None, :] * jnp.sin(angle)
    label = (lane - HEAD_DIM)[None, :]
    own = segment[:, None] == label
    path = own | (parent[:, None] == label) | (grand[:, None] == label)
    hidden = (label >= 0) & (label < SEGMENTS) & ~path
    queries = jnp.where(hidden, masked_score, 0.0).astype(f32)
    ones = (label >= 16) & (label < 19)
    keys = jnp.where(own | ones, 1.0, 0.0).astype(f32)
    return cosine, sine, queries, keys
def barrier(partners):
    semaphore = pltpu.get_barrier_semaphore()
    for partner in partners:
        pl.semaphore_signal(semaphore, inc=1, device_id=partner, device_id_type=MESH)
    pl.semaphore_wait(semaphore, len(partners))


def send(source, target, send_sem, recv_sem, device):
    copy = pltpu.make_async_remote_copy(
        src_ref=source,
        dst_ref=target,
        send_sem=send_sem,
        recv_sem=recv_sem,
        device_id=device,
        device_id_type=MESH,
    )
    copy.start()
    return copy


def add_rows(target, source, step=64):
    rows = target.shape[0]
    step = min(step, rows)
    while rows % step:
        step //= 2

    def body(i, _):
        at = span(i, step)
        target[at, :] = target[at, :] + source[at, :]
        return 0

    lax.fori_loop(0, rows // step, body, 0)


def orders(n_d):
    bits = n_d.bit_length() - 1
    return [list(range(bits)), list(range(bits - 1, -1, -1))]


def combos(bits):
    masks = [0]
    for b in bits:
        masks = masks + [m ^ (1 << b) for m in masks]
    return masks


def halves(rows, width, tile=16):
    return (rows // 2, width) if rows % (2 * tile) == 0 else (rows, width // 2)


def half(part, stream, rows, width):
    height, wide = halves(rows, width)
    if height < rows:
        return span(2 * part + stream, height), slice(None)
    return span(part, rows), pl.ds(stream * wide, wide)


class Spread:
    def __init__(self, n_d, n_t, shards, alls, sems):
        self.n_d, self.n_t, self.shards, self.alls = n_d, n_t, shards, alls
        self.zs, self.zr, self.ps, self.pr, self.ys, self.yr, self.own = sems
        self.d, self.t = lax.axis_index("dp"), lax.axis_index("tensor")
        self.chips = n_t // 2
        self.chip, self.core = self.t // 2, lax.rem(self.t, 2)
        self.other = 2 * self.chip + 1 - self.core
        self.bits = n_d.bit_length() - 1
        self.arrays = range(len(shards))

    @staticmethod
    def sems(count, n_d, n_t):
        dma = pltpu.SemaphoreType.DMA
        hops, slots = n_t // 2 - 1, 2 * (n_d - 1)
        z, p, y = (count, 2 * hops), (count, 2 * hops, slots), (count, 2 * hops + 1)
        return [dma(z), dma(z), dma(p), dma(p), dma(y), dma(y), dma((count,))]

    def exists(self, c):
        return (c >= 0) & (c < self.chips)

    def rows(self, a):
        return self.shards[a].shape[0] // self.n_d

    def slot(self, way, h):
        return h - 1 + (self.chips - 1 if way < 0 else 0)

    def remote(self, src, dst, ssem, rsem, device):
        return pltpu.make_async_remote_copy(
            src_ref=src, dst_ref=dst, send_sem=ssem, recv_sem=rsem, device_id=device, device_id_type=MESH
        )

    def along(self, a, way, h, arriving):
        source = self.chip - way * (h if arriving else h - 1)
        at = span(self.d, self.rows(a))
        dst = self.alls[a].at[2 * source + self.core, at]
        src = self.shards[a].at[at] if h == 1 and not arriving else dst
        peer = self.chip - way if arriving else self.chip + way
        i = self.slot(way, h)
        return self.remote(src, dst, self.zs.at[a, i], self.zr.at[a, i], (self.d, 2 * peer + self.core))

    def across(self, a, way, h, step, arriving):
        source = self.chip - way * h
        out = []
        for stream, order in enumerate(orders(self.n_d)):
            partner = lax.bitwise_xor(self.d, 1 << order[step])
            for j, m in enumerate(combos(order[:step])):
                block = lax.bitwise_xor(partner if arriving else self.d, m)
                rows, cols = half(block, stream, self.rows(a), self.shards[a].shape[1])
                ref = self.alls[a].at[2 * source + self.core, rows, cols]
                i = stream * (self.n_d - 1) + (1 << step) - 1 + j
                k = self.slot(way, h)
                out.append(self.remote(ref, ref, self.ps.at[a, k, i], self.pr.at[a, k, i], (partner, self.t)))
        return out

    def beside(self, a, way, h, arriving=False):
        source = self.chip - way * h
        ref = self.alls[a].at[2 * source + (1 - self.core if arriving else self.core)]
        k = self.slot(way, h)
        return self.remote(ref, ref, self.ys.at[a, k], self.yr.at[a, k], (self.d, self.other))

    def mine(self, a, arriving=False):
        k = 2 * (self.chips - 1)
        dst = self.alls[a].at[self.other if arriving else self.t]
        return self.remote(self.shards[a], dst, self.ys.at[a, k], self.yr.at[a, k], (self.d, self.other))

    def keep(self, a):
        return pltpu.make_async_copy(self.shards[a], self.alls[a].at[self.t], self.own.at[a])

    def begin(self):
        for way in (1, -1):

            @pl.when(self.exists(self.chip + way))
            def _():
                for a in self.arrays:
                    self.along(a, way, 1, False).start()

        for a in self.arrays:
            self.keep(a).start()
            self.mine(a).start()

    def phase(self, p, h):
        for way in (1, -1):

            @pl.when(self.exists(self.chip - way * h))
            def _():
                for a in self.arrays:
                    if p == 0:
                        self.along(a, way, h, True).wait_recv()
                        if h < self.chips - 1:

                            @pl.when(self.exists(self.chip + way))
                            def _():
                                self.along(a, way, h + 1, False).start()
                    else:
                        for copy in self.across(a, way, h, p - 1, True):
                            copy.wait_recv()
                    if p < self.bits:
                        for copy in self.across(a, way, h, p, False):
                            copy.start()
                    else:
                        self.beside(a, way, h).start()

    def groups(self):
        return self.chips - 1 + self.bits

    def group(self, g):
        for h in range(1, self.chips):
            if 0 <= g - (h - 1) <= self.bits:
                self.phase(g - (h - 1), h)

    def end(self):
        for h in range(1, self.chips):
            for way in (1, -1):

                @pl.when(self.exists(self.chip + way) & self.exists(self.chip - way * (h - 1)))
                def _():
                    for a in self.arrays:
                        self.along(a, way, h, False).wait_send()

                @pl.when(self.exists(self.chip - way * h))
                def _():
                    for a in self.arrays:
                        for step in range(self.bits):
                            for copy in self.across(a, way, h, step, False):
                                copy.wait_send()
                        self.beside(a, way, h).wait_send()
                        self.beside(a, way, h, True).wait_recv()

        for a in self.arrays:
            self.keep(a).wait()
            self.mine(a).wait_send()
            self.mine(a, True).wait_recv()


def gather_kernel(
    n_d, n_t, x_ref, w_ref, f_ref, o_ref, u_ref, all_ref,
    passing, rs, ss, rb, sb, rw, sw, rp, sp, *sems,
):
    d, t = lax.axis_index("dp"), lax.axis_index("tensor")
    trees, rows, _ = x_ref.shape
    chips = n_t // 2
    group = n_t // trees
    chip, core = t // 2, lax.rem(t, 2)
    other = 2 * chip + 1 - core
    near = group // 2
    tree = t // group
    planes = [lax.rem(d + k, n_d) for k in range(1, n_d)]
    owners = [(j * group + t // trees) for j in range(trees)]
    givers = [lax.rem(t, group) * trees + i for i in range(trees)]
    barrier([(d, lax.rem(t + k, n_t)) for k in range(1, n_t)] + [(p, t) for p in planes])
    part = w_ref.shape[1] // n_d
    weights = Spread(n_d, n_t, [f_ref], [all_ref], sems)
    exists = weights.exists

    copies = []
    mine = w_ref.at[:, span(d, part), :]
    for j in range(trees):
        slot = u_ref.at[lax.rem(t, trees), :, span(d, part), :]

        @pl.when(owners[j] != t)
        def _():
            send(mine, slot, sw.at[j], rw.at[lax.rem(t, trees)], (d, owners[j]))

        @pl.when(owners[j] == t)
        def _():
            u_ref[lax.rem(t, trees), :, span(d, part), :] = w_ref[:, span(d, part), :]

    weights.begin()

    def block(c):
        return o_ref.at[span(2 * c + core, rows)]

    def beyond(c, way, j):
        return (j * near + near - 1 >= c) if way > 0 else (j * near <= c)

    def hop(way, h, j, here):
        source = chip - way * (h - 1)
        if h == 1:
            src = x_ref.at[j]
        else:
            src = block(source) if here else passing.at[j, source]
        return src, source

    def pass_on(way, h):
        for j in range(trees):

            @pl.when(exists(chip - way * (h - 1)) & exists(chip + way) & beyond(chip + way, way, j))
            def _():
                i = weights.slot(way, h)
                to = chip + way
                for here in (True, False) if h > 1 else (True,):
                    src, source = hop(way, h, j, here)
                    for there in (True, False):
                        at_home = (tree == j) if here else (tree != j)
                        lands = (to // near == j) if there else (to // near != j)

                        @pl.when((at_home & lands) if h > 1 else lands)
                        def _():
                            dst = block(source) if there else passing.at[j, source]
                            send(src, dst, ss.at[j, i], rs.at[j, i], (d, 2 * to + core))

    def row_copy(j, i):
        return weights.remote(x_ref.at[j], passing.at[j, 0], ss.at[j, i], rs.at[j, i], (d, other))

    def share(way, h):
        source = chip - way * h
        i = weights.slot(way, h)
        return weights.remote(block(source), block(source), sb.at[i], rb.at[i], (d, other))

    def arrive(way, h):
        for j in range(trees):

            @pl.when(exists(chip - way * h) & beyond(chip, way, j))
            def _():
                row_copy(j, weights.slot(way, h)).wait_recv()

        if h < chips - 1:
            pass_on(way, h + 1)

        @pl.when(exists(chip - way * h))
        def _():
            share(way, h).start()

    for way in (1, -1):
        pass_on(way, 1)
    o_ref[span(t, rows), :] = x_ref[tree]
    last = 2 * (chips - 1)
    copies.append(send(x_ref.at[tree], block(chip), sb.at[last], rb.at[last], (d, other)))
    weights.group(0)
    for i in range(trees):
        slot = u_ref.at[i, :, span(d, part), :]

        @pl.when(givers[i] != t)
        def _():
            pltpu.make_async_remote_copy(
                src_ref=mine, dst_ref=slot, send_sem=sw.at[0], recv_sem=rw.at[i],
                device_id=(d, givers[i]), device_id_type=MESH,
            ).wait_recv()

    mine_all = u_ref.at[:, :, span(d, part), :]
    for k, p in enumerate(planes):
        copies.append(send(mine_all, mine_all, sp.at[k], rp.at[k], (p, t)))
    for h in range(1, chips):
        for way in (1, -1):
            arrive(way, h)
        weights.group(h)
    for g in range(chips, weights.groups()):
        weights.group(g)
    weights.end()
    for j in range(trees):

        @pl.when(owners[j] != t)
        def _():
            pltpu.make_async_remote_copy(
                src_ref=mine, dst_ref=mine, send_sem=sw.at[j], recv_sem=rw.at[0],
                device_id=(d, owners[j]), device_id_type=MESH,
            ).wait_send()

    for way in (1, -1):
        for h in range(1, chips):
            for j in range(trees):

                @pl.when(exists(chip - way * (h - 1)) & exists(chip + way) & beyond(chip + way, way, j))
                def _():
                    row_copy(j, weights.slot(way, h)).wait_send()

            @pl.when(exists(chip - way * h))
            def _():
                share(way, h).wait()

    for copy in copies:
        copy.wait()


def gather_tree(n_d, n_t, normed, weight, down):
    trees, rows, wide = normed.shape
    chips = n_t // 2
    hops = 2 * (chips - 1)
    dma = pltpu.SemaphoreType.DMA
    return pl.pallas_call(
        functools.partial(gather_kernel, n_d, n_t),
        in_specs=[VMEM] * 3,
        out_specs=[VMEM] * 2 + [HBM],
        out_shape=[
            jax.ShapeDtypeStruct((n_t * rows, wide), bf16),
            jax.ShapeDtypeStruct((trees,) + weight.shape, bf16),
            jax.ShapeDtypeStruct((n_t,) + down.shape, bf16),
        ],
        scratch_shapes=[
            pltpu.VMEM((trees, chips, rows, wide), bf16),
            dma((trees, hops)), dma((trees, hops)), dma((hops + 1,)), dma((hops + 1,)),
            dma((trees,)), dma((trees,)), dma((n_d - 1,)), dma((n_d - 1,)),
        ] + Spread.sems(1, n_d, n_t),
        compiler_params=pltpu.CompilerParams(collective_id=0, has_side_effects=True),
        name="gather_tree",
    )(normed, weight, down)


def qkv_kernel(x_ref, w_ref, cos_ref, sin_ref, mq_ref, mk_ref, q_ref, k_ref, v_ref, kt_ref, vt_ref):
    x = x_ref[...]
    heads = q_ref.shape[0]
    cosine, sine = cos_ref[...], sin_ref[...]
    mq, mk = mq_ref[...], mk_ref[...]
    lane = lane_of(cosine.shape)
    low = lax.rem(lane, HEAD_DIM) < HEAD_DIM // 2
    first = lane < HEAD_DIM
    mv = jnp.where((lane >= HEAD_DIM) & (lane < HEAD_DIM + 3), 1.0, 0.0)
    tail = jnp.where(row_of((VROWS - HEAD_DIM, x.shape[0])) == 0, 1.0, 0.0).astype(bf16)

    def both(slab):
        return slab, pltpu.roll(slab, HEAD_DIM, 1)

    def rotate(slab):
        partner = jnp.where(
            low, pltpu.roll(slab, LANES - HEAD_DIM // 2, 1), pltpu.roll(slab, HEAD_DIM // 2, 1)
        )
        return slab * cosine + partner * sine

    q_all, k_all, v_all = (dot(x, w_ref[i]) for i in range(3))
    for h in range(0, heads, 2):
        cols = slice(h * HEAD_DIM, (h + 2) * HEAD_DIM)
        for g, slab in enumerate(both(rotate(q_all[:, cols]) * HEAD_DIM**-0.5)):
            q_ref[h + g] = jnp.where(first, slab, mq).astype(bf16)
        keys = rotate(k_all[:, cols])
        for g, slab in enumerate(both(keys)):
            k_ref[h + g] = jnp.where(first, slab, mk).astype(bf16)
        flat = keys.T.astype(bf16)
        for g, slab in enumerate(both(v_all[:, cols])):
            v_ref[h + g] = jnp.where(first, slab, mv).astype(bf16)
        flat_v = v_all[:, cols].T.astype(bf16)
        for g in range(2):
            part = slice(g * HEAD_DIM, (g + 1) * HEAD_DIM)
            kt_ref[h + g] = flat[part]
            vt_ref[h + g, :HEAD_DIM] = flat_v[part]
            vt_ref[h + g, HEAD_DIM:] = tail


def project(x, w, cosine, sine, mq, mk):
    rows, wide = x.shape
    heads = w.shape[2] // HEAD_DIM
    table = pl.BlockSpec((BLOCK, LANES), lambda i: (i, 0))
    slab = pl.BlockSpec((heads, BLOCK, LANES), lambda i: (0, i, 0))
    shape = jax.ShapeDtypeStruct((heads, rows, LANES), bf16)
    return pl.pallas_call(
        qkv_kernel,
        grid=(rows // BLOCK,),
        in_specs=[
            pl.BlockSpec((BLOCK, wide), lambda i: (i, 0)),
            pl.BlockSpec(w.shape, lambda i: (0, 0, 0)),
            table, table, table, table,
        ],
        out_specs=[
            slab, slab, slab,
            pl.BlockSpec((heads, HEAD_DIM, BLOCK), lambda i: (0, 0, i)),
            pl.BlockSpec((heads, VROWS, BLOCK), lambda i: (0, 0, i)),
        ],
        out_shape=[
            shape, shape, shape,
            jax.ShapeDtypeStruct((heads, HEAD_DIM, rows), bf16),
            jax.ShapeDtypeStruct((heads, VROWS, rows), bf16),
        ],
        name="project",
    )(x, w, cosine, sine, mq, mk)


def fwd_kernel(
    n_d, n_t, trees, q_ref, k_ref, vt_ref, ow_ref, up_ref, o_ref, qb_ref, att_ref, ow_all, up_all,
    ss, rs, here, *sems,
):
    turn = pl.program_id(0)
    steps = pl.num_programs(0)
    heads = q_ref.shape[0]
    row, col = row_of((BLOCK, BLOCK)), lane_of((BLOCK, BLOCK))
    d, t = lax.axis_index("dp"), lax.axis_index("tensor")
    group = n_t // trees
    rows, width = att_ref.shape[1], o_ref.shape[1]
    per = BLOCK // rows
    qi = jnp.where(turn == steps - 1, t // per, jnp.where(turn >= t // per, turn + 1, turn))
    at = span(qi, BLOCK)
    weights = Spread(n_d, n_t, [up_ref, ow_ref], [up_all, ow_all], sems)
    first_group = max(0, k_ref.shape[1] // BLOCK - 4)
    place = att_ref.at[t // group, :, span(lax.rem(t, group), width)]

    def outgoing(i, r, k):
        return pltpu.make_async_remote_copy(
            src_ref=o_ref.at[span(i * per + r, rows)], dst_ref=place, send_sem=ss.at[k], recv_sem=rs.at[k],
            device_id=(d, lax.rem(t + k, n_t)), device_id_type=MESH,
        )

    @pl.when(turn == 0)
    def _():
        barrier(
            [(d, lax.rem(t + k, n_t)) for k in range(1, n_t)] + [(lax.rem(d + k, n_d), t) for k in range(1, n_d)]
        )
        weights.begin()

    for g in range(weights.groups()):
        if first_group + g < k_ref.shape[1] // BLOCK:

            @pl.when(turn == first_group + g)
            def _():
                weights.group(g)

    qs = [q_ref[h, at, :] for h in range(heads)]

    def scores(h, j):
        return dot(k_ref[h, span(j, BLOCK), :], qs[h], NT)

    state = []
    for h in range(heads):
        s = jnp.where(row <= col, scores(h, qi), masked_score)
        m = jnp.max(s, axis=0, keepdims=True)
        p = jnp.exp(s - m)
        state.append((m, dot(vt_ref[h, :, span(qi, BLOCK)], p.astype(bf16))))

    def step(j, carry):
        out = []
        for h in range(heads):
            m, acc = carry[h]
            s = scores(h, j)
            top = jnp.maximum(m, jnp.max(s, axis=0, keepdims=True))
            p = jnp.exp(s - top)
            acc = acc * jnp.exp(m - top) + dot(vt_ref[h, :, span(j, BLOCK)], p.astype(bf16))
            out.append((top, acc))
        return tuple(out)

    state = lax.fori_loop(0, qi, step, tuple(state))
    r = row_of((LANES, BLOCK))
    for h in range(0, heads, 2):
        outs = []
        for g in (h, h + 1):
            m, acc = state[g]
            total = acc[HEAD_DIM : HEAD_DIM + 1]
            outs.append(acc[:HEAD_DIM] / total)
            a, b, c = split3(-(m + jnp.log(total)))
            extra = jnp.where(r == 80, a, jnp.where(r == 81, b, jnp.where(r == 82, c, 0.0))).T
            qb_ref[g, at, :] = qs[g] + extra.astype(bf16)
        o_ref[at, h * HEAD_DIM : (h + 2) * HEAD_DIM] = jnp.concatenate(outs, axis=0).T.astype(bf16)

    def local(r):
        return pltpu.make_async_copy(o_ref.at[span(t // per * per + r, rows)], place, here.at[0])

    for r in range(per):
        k = lax.rem(qi * per + r + n_t - t, n_t)

        @pl.when(k != 0)
        def _():
            outgoing(qi, r, k).start()

        @pl.when(k == 0)
        def _():
            local(r).start()

    @pl.when(turn == steps - 1)
    def _():
        for g in range(k_ref.shape[1] // BLOCK - first_group, weights.groups()):
            weights.group(g)
        for k in range(1, n_t):
            outgoing(0, 0, k).wait()
        local(0).wait()
        weights.end()


def attend(n_d, n_t, trees, q, k, vt, ow, up):
    heads, rows, _ = q.shape
    wide = heads * HEAD_DIM
    dma = pltpu.SemaphoreType.DMA
    sds = jax.ShapeDtypeStruct
    return pl.pallas_call(
        functools.partial(fwd_kernel, n_d, n_t, trees),
        grid=(rows // BLOCK,),
        in_specs=[VMEM] * 5,
        out_specs=[VMEM, VMEM, HBM, HBM, HBM],
        out_shape=[
            sds((rows, wide), bf16),
            sds(q.shape, bf16),
            sds((trees, rows // n_t, wide * n_t // trees), bf16),
            sds((n_t,) + ow.shape, bf16),
            sds((n_t,) + up.shape, bf16),
        ],
        scratch_shapes=[
            dma((n_t,)), dma((n_t,)), dma((1,)),
        ] + Spread.sems(2, n_d, n_t),
        compiler_params=pltpu.CompilerParams(collective_id=1, has_side_effects=True),
        name="attend",
    )(q, k, vt, ow, up)


class Reduce:
    def __init__(self, n_d, n_t, sources, totals, scratch):
        self.n_d, self.n_t, self.sources, self.totals = n_d, n_t, sources, totals
        count = len(sources)
        self.mine, self.side, self.land_at, self.far = (
            scratch[i * count : (i + 1) * count] for i in range(4)
        )
        self.s_load, self.s_side, self.r_side, self.s_hop, self.r_hop, self.s_far, self.r_far = scratch[4 * count :]
        self.d, self.t = lax.axis_index("dp"), lax.axis_index("tensor")
        self.chips = n_t // 2
        self.chip, self.core = self.t // 2, lax.rem(self.t, 2)
        self.other = 2 * self.chip + 1 - self.core
        self.dest = [lax.rem(self.chip + k, self.chips) for k in range(1, self.chips)] + [self.chip]
        self.bits = n_d.bit_length() - 1
        self.units = [(n, k) for k in range(self.chips) for n in range(count)]

    @staticmethod
    def scratch(n_d, n_t, shapes):
        dma = pltpu.SemaphoreType.DMA
        chips, slots, count = n_t // 2, 2 * (n_d - 1), len(shapes)
        vm = lambda lead, r, c: pltpu.VMEM(lead + (r, c), bf16)
        units = count * chips
        return (
            [vm((chips,), r, c) for r, c in shapes] * 2
            + [vm((chips, slots), *halves(r // n_d, c)) for r, c in shapes]
            + [vm((chips - 1,), r // n_d, c) for r, c in shapes]
            + [dma((units,)), dma((units,)), dma((units,)), dma((units, slots)), dma((units, slots))]
            + [dma((units,)), dma((units,))]
        )

    def remote(self, src, dst, ssem, rsem, device):
        return pltpu.make_async_remote_copy(
            src_ref=src, dst_ref=dst, send_sem=ssem, recv_sem=rsem, device_id=device, device_id_type=MESH
        )

    def load(self, u):
        n, k = self.units[u]
        source = self.sources[n].at[2 * self.dest[k] + self.core]
        return pltpu.make_async_copy(source, self.mine[n].at[k], self.s_load.at[u])

    def beside(self, u):
        n, k = self.units[u]
        source = self.sources[n].at[2 * self.dest[k] + 1 - self.core]
        return self.remote(source, self.side[n].at[k], self.s_side.at[u], self.r_side.at[u], (self.d, self.other))

    def cut(self, u, part, stream):
        n, k = self.units[u]
        _, height, width = self.mine[n].shape
        rows, cols = half(part, stream, height // self.n_d, width)
        return self.mine[n].at[k, rows, cols]

    def hops(self, u, step):
        n, k = self.units[u]
        slot = 0 if step == 0 else self.n_d - (self.n_d >> step)
        out = []
        for stream, order in enumerate(orders(self.n_d)):
            partner = lax.bitwise_xor(self.d, 1 << order[step])
            for j, m in enumerate(combos(order[step + 1 :])):
                i = (slot + j) * 2 + stream
                landing = self.land_at[n].at[k, i]
                copy = self.remote(
                    self.cut(u, lax.bitwise_xor(partner, m), stream), landing,
                    self.s_hop.at[u, i], self.r_hop.at[u, i], (partner, self.t),
                )
                out.append((copy, self.cut(u, lax.bitwise_xor(self.d, m), stream), landing))
        return out

    def piece(self, u):
        n, k = self.units[u]
        return self.mine[n].at[k, span(self.d, self.mine[n].shape[1] // self.n_d), :]

    def away(self, u):
        n, k = self.units[u]
        return self.remote(
            self.piece(u), self.far[n].at[k], self.s_far.at[u], self.r_far.at[u],
            (self.d, 2 * self.dest[k] + self.core),
        )

    def begin(self):
        for u in range(len(self.units)):
            self.load(u).start()
            self.beside(u).start()

    def events(self):
        return len(self.units) + self.bits

    def event(self, e):
        if e < len(self.units):
            n, k = self.units[e]
            self.load(e).wait()
            self.beside(e).wait_recv()
            add_rows(self.mine[n].at[k], self.side[n].at[k])
            for copy, _, _ in self.hops(e, 0):
                copy.start()
        for step in range(self.bits):
            u = e - 1 - step
            if 0 <= u < len(self.units):
                for copy, target, landing in self.hops(u, step):
                    copy.wait_recv()
                    add_rows(target, landing)
                if step + 1 < self.bits:
                    for copy, _, _ in self.hops(u, step + 1):
                        copy.start()
                elif self.units[u][1] < self.chips - 1:
                    self.away(u).start()

    def end(self):
        for u, (n, k) in enumerate(self.units):
            if k < self.chips - 1:
                self.away(u).wait_recv()
            else:
                total = self.piece(u)[...].astype(f32)
                for i in range(self.chips - 1):
                    total = total + self.far[n][i].astype(f32)
                self.totals[n][...] = total.astype(bf16)
        for u, (n, k) in enumerate(self.units):
            self.beside(u).wait_send()
            for step in range(self.bits):
                for copy, _, _ in self.hops(u, step):
                    copy.wait_send()
            if k < self.chips - 1:
                self.away(u).wait_send()


def bwd_kernel(
    n_d, n_t, q_ref, k_ref, v_ref, kt_ref, x_ref, o_ref, cos_ref, sin_ref, up_ref, down_ref, og_ref,
    m_ref, up_tot, down_tot, og_tot, sums, wide, d_ref, hs, hr, *scratch,
):
    j = pl.program_id(0)
    heads, rows, _ = q_ref.shape
    nq = rows // BLOCK
    row, col = row_of((BLOCK, BLOCK)), lane_of((BLOCK, BLOCK))
    lane = lane_of((BLOCK, LANES))
    first = lane < HEAD_DIM
    d, t = lax.axis_index("dp"), lax.axis_index("tensor")
    trees, part, _ = x_ref.shape
    group, width = n_t // trees, heads * HEAD_DIM
    gradients = Reduce(n_d, n_t, [up_ref, down_ref, og_ref], [up_tot, down_tot, og_tot], scratch)
    ahead = 3
    points = 10

    def point(p):
        left = gradients.events() - ahead
        for e in range(ahead + p * left // points, ahead + (p + 1) * left // points):
            gradients.event(e)

    def cut(o):
        return x_ref.at[o // group, :, span(lax.rem(o, group), width)]

    def outgoing(k):
        o = lax.rem(t + k, n_t)
        return gradients.remote(cut(o), d_ref.at[span(t, part), :], hs.at[k], hr.at[k], (d, o))

    @pl.when(j == 0)
    def _():
        barrier(
            [(d, lax.rem(t + k, n_t)) for k in range(1, n_t)] + [(lax.rem(d + k, n_d), t) for k in range(1, n_d)]
        )
        for k in range(1, n_t):
            outgoing(k).start()
        gradients.begin()
        d_ref[span(t, part), :] = cut(t)[...]
        sums[...] = jnp.zeros_like(sums)
        for e in range(ahead):
            gradients.event(e)
        for k in range(1, n_t):
            outgoing(k).wait()

        def widen(i, _):
            at = span(i, BLOCK)
            for h in range(0, heads, 2):
                cols = slice(h * HEAD_DIM, (h + 2) * HEAD_DIM)
                slab = d_ref[at, cols].astype(f32)
                prod = slab * o_ref[at, cols].astype(f32)
                for g, (s, mine) in enumerate(((slab, first), (pltpu.roll(slab, HEAD_DIM, 1), ~first))):
                    inner = -jnp.sum(jnp.where(mine, prod, 0.0), axis=1, keepdims=True)
                    a, b, c = split3(inner)
                    n = HEAD_DIM
                    tail = jnp.where(lane == n, a, jnp.where(lane == n + 1, b, jnp.where(lane == n + 2, c, 0.0)))
                    wide[h + g, at, :] = jnp.where(first, s, tail).astype(bf16)
            return 0

        lax.fori_loop(0, nq, widen, 0)

    for p in range(0, points, 2):
        if p // 2 < nq:

            @pl.when(j == p // 2)
            def _():
                point(p)

    ks = [k_ref[h] for h in range(heads)]
    vs = [v_ref[h] for h in range(heads)]
    kts = [kt_ref[h] for h in range(heads)]

    def pair(h, i, mask):
        at = span(i, BLOCK)
        q = q_ref[h, at, :]
        d = wide[h, at, :]
        s = dot(ks[h], q, NT)
        if mask:
            s = jnp.where(row <= col, s, masked_score)
        p = jnp.exp(s)
        back = (p * dot(vs[h], d, NT)).astype(bf16)
        sums[h, :, at] += dot(kts[h], back)
        return dot(back, q), dot(p.astype(bf16), d)

    def step(i, carry):
        out = []
        for h in range(heads):
            dk, dv = pair(h, i, False)
            out.append((carry[h][0] + dk, carry[h][1] + dv))
        return tuple(out)

    state = tuple(pair(h, j, True) for h in range(heads))
    middle = (j + 1 + nq) // 2
    state = lax.fori_loop(j + 1, middle, step, state)
    for p in range(1, points, 2):
        if p // 2 < nq:

            @pl.when(j == p // 2)
            def _():
                point(p)

    state = lax.fori_loop(middle, nq, step, state)

    def join(a, b):
        return jnp.where(first, a, pltpu.roll(b, HEAD_DIM, 1))

    cosine, sine = cos_ref[...], sin_ref[...]
    low = lax.rem(lane, HEAD_DIM) < HEAD_DIM // 2

    def unrotate(slab):
        partner = jnp.where(
            low, pltpu.roll(slab, LANES - HEAD_DIM // 2, 1), pltpu.roll(slab, HEAD_DIM // 2, 1)
        )
        return slab * cosine - partner * sine

    at = span(j, BLOCK)
    total = heads * HEAD_DIM
    for h in range(0, heads, 2):
        dq = jnp.concatenate([sums[h, :, at], sums[h + 1, :, at]], axis=0).T * HEAD_DIM**-0.5
        dk = join(state[h][0], state[h + 1][0])
        dv = join(state[h][1], state[h + 1][1])
        for n, part in enumerate((unrotate(dq), unrotate(dk), dv)):
            begin = n * total + h * HEAD_DIM
            m_ref[:, begin : begin + 2 * HEAD_DIM] = part.astype(bf16)

    @pl.when(j == nq - 1)
    def _():
        for p in range(2 * nq, points):
            point(p)
        gradients.end()


def attend_back(n_d, n_t, q, k, v, kt, x, o, cosine, sine, up_g, down_g, out_g):
    heads, rows, _ = q.shape
    whole = lambda a: pl.BlockSpec(a.shape, lambda j: (0,) * a.ndim, pipeline_mode=pl.Buffered(1))
    block = pl.BlockSpec((heads, BLOCK, LANES), lambda j: (0, j, 0))
    table = pl.BlockSpec((BLOCK, LANES), lambda j: (j, 0))
    wide = heads * HEAD_DIM
    dma = pltpu.SemaphoreType.DMA
    sds = jax.ShapeDtypeStruct
    shapes = [a.shape[1:] for a in (up_g, down_g, out_g)]
    return pl.pallas_call(
        functools.partial(bwd_kernel, n_d, n_t),
        grid=(rows // BLOCK,),
        in_specs=[
            whole(q), block, block,
            pl.BlockSpec((heads, HEAD_DIM, BLOCK), lambda j: (0, 0, j)),
            VMEM, whole(o), table, table, HBM, HBM, HBM,
        ],
        out_specs=[pl.BlockSpec((BLOCK, 3 * wide), lambda j: (j, 0)), VMEM, VMEM, VMEM],
        out_shape=[sds((rows, 3 * wide), bf16)] + [sds((r // n_d, c), bf16) for r, c in shapes],
        scratch_shapes=[
            pltpu.VMEM((heads, HEAD_DIM, rows), f32),
            pltpu.VMEM((heads, rows, LANES), bf16),
            pltpu.VMEM((rows, wide), bf16),
            dma((n_t,)), dma((n_t,)),
        ] + Reduce.scratch(n_d, n_t, shapes),
        compiler_params=pltpu.CompilerParams(
            collective_id=2, has_side_effects=True, vmem_limit_bytes=67043328
        ),
        name="attend_back",
    )(q, k, v, kt, x, o, cosine, sine, up_g, down_g, out_g)


def ln_parts(v):
    centered = v - jnp.mean(v, axis=-1, keepdims=True)
    r = lax.rsqrt(jnp.mean(centered * centered, axis=-1, keepdims=True) + norm_eps)
    return centered * r, r


def ln_back(e, n, r, gain):
    f = e * gain
    return r * (f - jnp.mean(f, axis=-1, keepdims=True) - n * jnp.mean(f * n, axis=-1, keepdims=True))


def feed_kernel(
    att_ref, x_ref, cot_ref, ow_ref, par_ref, up_ref, down_ref,
    out_ref, hid_ref, ba_ref, upg_ref, downg_ref, outg_ref, vec_ref,
    hidden, branch, acc, feed_in, back_feed, active, slope,
):
    phase, n = pl.program_id(0), pl.program_id(1)
    last = pl.num_programs(1) - 1
    par = lambda i: par_ref[i : i + 1]
    total = lambda v: jnp.sum(v, axis=0, keepdims=True)

    @pl.when((phase == 0) & (n == 0))
    def _():
        b = dot(att_ref[...], ow_ref[...])
        branch[...] = b
        h = x_ref[...].astype(f32) + ln_parts(b)[0] * par(0) + par(1)
        hidden[...] = h
        feed_in[...] = (ln_parts(h)[0] * par(2) + par(3)).astype(bf16)
        acc[...] = jnp.zeros_like(acc)

    up, down = up_ref[0], down_ref[0]

    @pl.when(phase == 0)
    def _():
        u = dot(feed_in[...], up)
        t = jnp.tanh(0.7978845608028654 * (u + 0.044715 * u * u * u))
        half = 0.5 * (1.0 + t)
        a = (u * half).astype(bf16)
        active[n] = a
        slope[n] = half + 0.5 * u * (1.0 - t * t) * (
            0.7978845608028654 * (1.0 + 3 * 0.044715 * u * u)
        )
        acc[...] += dot(a, down)

    @pl.when((phase == 1) & (n == 0))
    def _():
        e = cot_ref[...].astype(f32)
        norm, r = ln_parts(acc[...])
        out_ref[...] = (hidden[...] + norm * par(4) + par(5)).astype(bf16)
        vec_ref[4:5] = total(e * norm)
        vec_ref[5:6] = total(e)
        back_feed[...] = ln_back(e, norm, r, par(4)).astype(bf16)
        acc[...] = jnp.zeros_like(acc)

    @pl.when(phase == 1)
    def _():
        b = back_feed[...]
        upper = (dot(b, down, NT) * slope[n]).astype(bf16)
        acc[...] += dot(upper, up, NT)
        downg_ref[0] = dot(active[n], b, TN).astype(bf16)
        upg_ref[0] = dot(feed_in[...], upper, TN).astype(bf16)

    @pl.when((phase == 1) & (n == last))
    def _():
        e = acc[...]
        norm, r = ln_parts(hidden[...])
        vec_ref[2:3] = total(e * norm)
        vec_ref[3:4] = total(e)
        h = cot_ref[...].astype(f32) + ln_back(e, norm, r, par(2))
        hid_ref[...] = h
        norm, r = ln_parts(branch[...])
        vec_ref[0:1] = total(h * norm)
        vec_ref[1:2] = total(h)
        b = ln_back(h, norm, r, par(0)).astype(bf16)
        ba_ref[...] = dot(b, ow_ref[...], NT).astype(bf16)
        outg_ref[...] = dot(att_ref[...], b, TN).astype(bf16)


def feed(att, x, cot, ow, par, up, down):
    rows, wide = att.shape
    n_t, _, width = up.shape
    one = lambda a: pl.BlockSpec(a.shape, lambda p, n: (0,) * len(a.shape), pipeline_mode=pl.Buffered(1))
    sds = jax.ShapeDtypeStruct
    outs = [
        sds((rows, wide), bf16), sds((rows, wide), f32), sds((rows, wide), bf16),
        sds((n_t, wide, width), bf16), sds((n_t, width, wide), bf16), sds((wide, wide), bf16),
        sds((8, wide), f32),
    ]
    chunk = lambda a: pl.BlockSpec((1,) + a.shape[1:], lambda p, n: (p * n, 0, 0))
    weight = lambda a: pl.BlockSpec((1,) + a.shape[1:], lambda p, n: (n, 0, 0))
    return pl.pallas_call(
        feed_kernel,
        grid=(2, n_t),
        in_specs=[one(a) for a in (att, x, cot, ow, par)] + [weight(up), weight(down)],
        out_specs=[one(o) for o in outs[:3]] + [chunk(outs[3]), chunk(outs[4])] + [one(o) for o in outs[5:]],
        out_shape=outs,
        scratch_shapes=[
            pltpu.VMEM((rows, wide), f32), pltpu.VMEM((rows, wide), f32), pltpu.VMEM((rows, wide), f32),
            pltpu.VMEM((rows, wide), bf16), pltpu.VMEM((rows, wide), bf16),
            pltpu.VMEM((n_t, rows, width), bf16), pltpu.VMEM((n_t, rows, width), f32),
        ],
        compiler_params=pltpu.CompilerParams(vmem_limit_bytes=64 << 20),
        name="feed",
    )(att, x, cot, ow, par, up, down)
def finish_kernel(
    n_d, n_t, bm_ref, w_ref, x_ref, hid_ref, par_ref, vec_in, up_tot, down_tot, og_tot, g_hbm,
    bt_ref, vec_ref, up_out, down_out, og_out, ig_out,
    g_ref, mine, landed, far, full_up, full_down, full_og, full_ig,
    r_give, r_keep, r_side, r_out, r_land, vec_now, vec_got, vec_far,
    s_load, s_hop, r_hop, s_all, r_all, s_own, r_own,
    s_red, r_red, s_redside, r_redside, s_vec, r_vec,
):
    d, t = lax.axis_index("dp"), lax.axis_index("tensor")
    trees, rows, wide = x_ref.shape
    chips = n_t // 2
    near = chips // trees
    group = n_t // trees
    chip, core = t // 2, lax.rem(t, 2)
    other = 2 * chip + 1 - core
    line = [lax.rem(chip + k, chips) for k in range(1, chips)]
    peers = [lax.rem(d + k, n_d) for k in range(1, n_d)]
    bits = n_d.bit_length() - 1
    barrier([(d, lax.rem(t + k, n_t)) for k in range(1, n_t)] + [(p, t) for p in peers])
    totals = [up_tot, down_tot, og_tot]
    fulls = [full_up, full_down, full_og, full_ig]
    outs = [up_out, down_out, og_out, ig_out]

    load = pltpu.make_async_copy(g_hbm, g_ref, s_load.at[0])
    load.start()
    hops, spreads = {}, []

    def cut(k, part):
        return mine.at[k, span(part, mine.shape[1] // n_d), :]

    def hop(k, step):
        slot = 0 if step == 0 else n_d - (n_d >> step)
        order = orders(n_d)[k % 2]
        partner = lax.bitwise_xor(d, 1 << order[step])
        for j, m in enumerate(combos(order[step + 1 :])):
            hops[k, step, j] = send(
                cut(k, lax.bitwise_xor(partner, m)), landed.at[k, slot + j],
                s_hop.at[k, slot + j], r_hop.at[k, slot + j], (partner, t),
            )

    def land(k, step):
        slot = 0 if step == 0 else n_d - (n_d >> step)
        for j, m in enumerate(combos(orders(n_d)[k % 2][step + 1 :])):
            hops[k, step, j].wait_recv()
            add_rows(cut(k, lax.bitwise_xor(d, m)), landed.at[k, slot + j])
        if step + 1 < bits:
            hop(k, step + 1)
        else:
            away(k)

    def spread(n, source):
        at = span(d, fulls[n].shape[0] // n_d)
        for j, p in enumerate(peers):
            spreads.append(send(source, fulls[n].at[at, :], s_all.at[n, j], r_all.at[n, j], (p, t)))

    def owner(i):
        return lax.rem(t, group) * trees + i

    def away(k):
        here = t // group

        @pl.when(owner(k) != t)
        def _():
            send(cut(k, d), far.at[here], s_own.at[k], r_own.at[here], (d, owner(k)))

        @pl.when(owner(k) == t)
        def _():
            far[here] = cut(k, d)[...]

    spread(0, totals[0])
    spread(2, totals[2])

    def chip_at(k):
        return lax.rem(chip + 1 + k, chips)

    def pair(k):
        return pltpu.make_async_remote_copy(
            src_ref=r_give.at[k], dst_ref=r_side.at[k], send_sem=s_redside.at[k], recv_sem=r_redside.at[k],
            device_id=(d, other), device_id_type=MESH,
        )

    def red(k):
        return pltpu.make_async_remote_copy(
            src_ref=r_out.at[k], dst_ref=r_land.at[k], send_sem=s_red.at[k], recv_sem=r_red.at[k],
            device_id=(d, 2 * chip_at(k) + core), device_id_type=MESH,
        )

    def rows_of(device):
        return dot(bm_ref[span(device, rows), :], w_ref[...], NT).astype(bf16)

    def step_rows(k, _):
        r_give[k] = rows_of(2 * chip_at(k) + 1 - core)
        r_keep[k] = rows_of(2 * chip_at(k) + core)
        pair(k).start()

        @pl.when(k > 0)
        def _():
            pair(k - 1).wait_recv()
            r_out[k - 1] = r_keep[k - 1] + r_side[k - 1]
            red(k - 1).start()

        return 0

    lax.fori_loop(0, chips, step_rows, 0)

    columns, width = bm_ref.shape[1] // 3, mine.shape[2]
    load.wait()

    def step_weight(i, _):
        p, c = i // (wide // BLOCK), lax.rem(i, wide // BLOCK)
        product = dot(g_ref[:, span(c, BLOCK)], bm_ref[:, span(p, columns)], TN).astype(bf16)
        for j in range(trees):
            mine[j, span(i, BLOCK), :] = product[:, j * width : (j + 1) * width]
        return 0

    lax.fori_loop(0, 3 * (wide // BLOCK), step_weight, 0)
    for k in range(trees):
        hop(k, 0)
    for n in range(3):
        fulls[n][span(d, fulls[n].shape[0] // n_d), :] = totals[n][...]
    for step in range(bits):
        for k in range(trees):
            land(k, step)
        if step == 0:
            spread(1, totals[1])

    def reduced():
        pair(chips - 1).wait_recv()
        for k in range(chips - 1):
            red(k).wait_recv()
        hit = chip // near
        vec_now[0:6] = vec_in[0:6]
        vec_now[6:8] = jnp.zeros((2, wide), f32)
        height = min(64, rows)
        for tree in range(trees):

            def body(i, _):
                at = span(i, height)
                own = r_keep[chips - 1, at, :].astype(f32) + r_side[chips - 1, at, :].astype(f32)
                e = jnp.where(hit == tree, own, 0.0)
                for k in range(chips - 1):
                    source = lax.rem(chip + chips - 1 - k, chips)
                    e = e + jnp.where(source // near == tree, r_land[k, at, :].astype(f32), 0.0)
                norm, r = ln_parts(x_ref[tree, at, :].astype(f32))
                vec_now[6:7] = vec_now[6:7] + jnp.sum(e * norm, axis=0, keepdims=True)
                vec_now[7:8] = vec_now[7:8] + jnp.sum(e, axis=0, keepdims=True)
                bt_ref[tree, at, :] = (hid_ref[tree, at, :] + ln_back(e, norm, r, par_ref[6:7])).astype(bf16)
                return 0

            lax.fori_loop(0, rows // height, body, 0)

    vec_partners = [(d, other)] + [(lax.bitwise_xor(d, 1 << b), t) for b in range(bits)]
    vec_copies = []

    def vec_step(i):
        if i > 0:
            vec_copies[i - 1].wait()
            vec_now[...] = vec_now[...] + vec_got[i - 1]
        if i < len(vec_partners):
            vec_got[len(vec_partners) + i] = vec_now[...]
            vec_copies.append(
                send(vec_got.at[len(vec_partners) + i], vec_got.at[i], s_vec.at[i], r_vec.at[i], vec_partners[i])
            )
        else:
            vec_far[chip] = vec_now[...]
            for k, c in enumerate(line):
                n = len(vec_partners) + k
                vec_copies.append(
                    send(vec_far.at[chip], vec_far.at[chip], s_vec.at[n], r_vec.at[n], (d, 2 * c + core))
                )

    def widen_all(n):
        full, out = fulls[n], outs[n]
        for j in range(n_d - 1):
            spread_of[n][j].wait_recv()
        height = 64
        while full.shape[0] % height:
            height //= 2

        def widen(i, _):
            out[span(i, height), :] = full[span(i, height), :].astype(f32)
            return 0

        lax.fori_loop(0, full.shape[0] // height, widen, 0)

    for j in range(trees):
        giver = j * group + t // trees

        @pl.when(giver != t)
        def _():
            pltpu.make_async_remote_copy(
                src_ref=far.at[j], dst_ref=far.at[j], send_sem=s_own.at[0], recv_sem=r_own.at[j],
                device_id=(d, giver), device_id_type=MESH,
            ).wait_recv()

    total = far[0].astype(f32)
    for j in range(1, trees):
        total = total + far[j].astype(f32)
    at = span(d, full_ig.shape[0] // n_d)
    full_ig[at, :] = total.astype(bf16)
    spread(3, full_ig.at[at, :])
    spread_of = [spreads[i * (n_d - 1) : (i + 1) * (n_d - 1)] for i in (0, 2, 1, 3)]

    reduced()
    for i in range(len(vec_partners) + 1):
        vec_step(i)
        if i < 3:
            widen_all(i)
    for n in range(len(vec_partners) + 1, 3):
        widen_all(n)
    widen_all(3)
    for k in range(chips - 1):
        vec_copies[len(vec_partners) + k].wait()
    total = vec_far[0]
    for c in range(1, chips):
        total = total + vec_far[c]
    vec_ref[...] = total

    for k in range(trees):

        @pl.when(owner(k) != t)
        def _():
            pltpu.make_async_remote_copy(
                src_ref=cut(k, d), dst_ref=cut(k, d), send_sem=s_own.at[k], recv_sem=r_own.at[0],
                device_id=(d, owner(k)), device_id_type=MESH,
            ).wait_send()

    for k in range(chips):
        pair(k).wait_send()
    for k in range(chips - 1):
        red(k).wait_send()
    for copy in list(hops.values()) + spreads:
        copy.wait_send()


def finish(n_d, n_t, mixed, w, x, hidden, par, vec, up_t, down_t, out_t, gathered, width):
    trees, rows, wide = x.shape
    chips = n_t // 2
    bits = n_d.bit_length() - 1
    dma = pltpu.SemaphoreType.DMA
    sds = jax.ShapeDtypeStruct
    shapes = [(a.shape[0] * n_d, a.shape[1]) for a in (up_t, down_t, out_t)] + [(3 * wide, width)]
    vm = lambda lead, shape, kind=bf16: pltpu.VMEM(tuple(lead) + tuple(shape), kind)
    part = (shapes[3][0] // n_d, shapes[3][1])
    partners = 1 + bits
    return pl.pallas_call(
        functools.partial(finish_kernel, n_d, n_t),
        in_specs=[VMEM] * 9 + [HBM],
        out_specs=[VMEM] * 6,
        out_shape=[sds(x.shape, bf16), sds((8, wide), f32)] + [sds(s, f32) for s in shapes],
        scratch_shapes=[vm((), gathered.shape), vm((trees,), shapes[3]), vm((trees, n_d - 1), part), vm((trees,), part)]
        + [vm((), s) for s in shapes] + [
            vm((chips, rows), (wide,)), vm((chips, rows), (wide,)), vm((chips, rows), (wide,)),
            vm((chips - 1, rows), (wide,)), vm((chips - 1, rows), (wide,)),
            vm((8,), (wide,), f32), vm((2 * partners, 8), (wide,), f32), vm((chips, 8), (wide,), f32),
            dma((1,)), dma((trees, n_d - 1)), dma((trees, n_d - 1)),
            dma((4, n_d - 1)), dma((4, n_d - 1)),
            dma((trees,)), dma((trees,)),
            dma((chips - 1,)), dma((chips - 1,)), dma((chips,)), dma((chips,)),
            dma((partners + chips - 1,)), dma((partners + chips - 1,)),
        ],
        compiler_params=pltpu.CompilerParams(
            collective_id=3, has_side_effects=True, vmem_limit_bytes=67043328
        ),
        name="finish",
    )(mixed, w, x, hidden, par, vec, up_t, down_t, out_t, gathered)


def shards(
    n_d, n_t,
    tokens, cotangent, lengths, parents, first_gain, first_shift, in_weight, out_weight,
    second_gain, second_shift, third_gain, third_shift, up_weight, down_weight, fourth_gain, fourth_shift,
):
    trees, rows, wide = tokens.shape
    group = n_t // trees
    d, t = lax.axis_index("dp"), lax.axis_index("tensor")
    tree = t // group
    width = out_weight.shape[0]

    mine = lambda a: lax.dynamic_index_in_dim(a, tree, 0, keepdims=False)
    cosine, sine, mq, mk = tables(mine(lengths), mine(parents), n_t * rows)

    x = tokens.astype(f32)
    normed = layer_norm(x, first_gain, first_shift)
    gathered, w, down_all = gather_tree(
        n_d, n_t, normed.astype(bf16), in_weight.transpose(1, 0, 2), down_weight
    )
    w = w.transpose(1, 2, 0, 3).reshape(3, wide, -1)
    q, k, v, kt, vt = project(gathered, w, cosine, sine, mq, mk)
    attended, qb, att, out_all, up_all = attend(n_d, n_t, trees, q, k, vt, out_weight, up_weight)
    par = jnp.stack(
        [second_gain, second_shift, third_gain, third_shift, fourth_gain, fourth_shift, first_gain, first_shift]
    )
    flat = lambda a: a.reshape(trees * rows, a.shape[-1])
    output, back_hidden, back_att, up_g, down_g, out_g, vec = feed(
        flat(att), flat(tokens), flat(cotangent), out_all.reshape(-1, wide), par, up_all, down_all
    )
    back_mixed, up_t, down_t, out_t = attend_back(
        n_d, n_t, qb, k, v, kt, back_att.reshape(trees, rows, wide), attended, cosine, sine,
        up_g, down_g, out_g.reshape(n_t, width, wide),
    )
    w_flat = w.transpose(1, 0, 2).reshape(wide, -1)
    back_tokens, vec, up_sum, down_sum, out_sum, in_sum = finish(
        n_d, n_t, back_mixed, w_flat, tokens, back_hidden.reshape(x.shape), par, vec,
        up_t, down_t, out_t, gathered, width,
    )
    return (
        output.reshape(tokens.shape),
        back_tokens,
        vec[6], vec[7],
        in_sum.reshape(3, wide, width).transpose(1, 0, 2),
        out_sum,
        vec[0], vec[1], vec[2], vec[3],
        up_sum,
        down_sum,
        vec[4], vec[5],
    )


def solution(mesh):
    in_specs = (
        P("dp", "tensor", None), P("dp", "tensor", None), P("dp", None), P("dp", None),
        P(), P(), P(None, None, "tensor"), P("tensor", None), P(), P(), P(), P(),
        P(None, "tensor"), P("tensor", None), P(), P(),
    )
    out_specs = (
        P("dp", "tensor", None), P("dp", "tensor", None), P(), P(), P(None, None, "tensor"),
        P("tensor", None), P(), P(), P(), P(), P(None, "tensor"), P("tensor", None), P(), P(),
    )
    run = functools.partial(shards, mesh.shape["dp"], mesh.shape["tensor"])
    return jax.shard_map(run, mesh=mesh, in_specs=in_specs, out_specs=out_specs, check_vma=False)
```

```python
import functools
import jax
import jax.numpy as jnp
from jax import lax
from jax.experimental import pallas as pl
from jax.experimental.pallas import tpu as pltpu
from jax.sharding import PartitionSpec as P

HEAD_DIM = 64
LANES = 128
VROWS = 80
BLOCK = 256
TRUNK = 512
SEGMENTS = 13

rope_base = 10000.0
norm_eps = 1e-05
masked_score = -1e30
f32, bf16 = jnp.float32, jnp.bfloat16
NN = (((1,), (0,)), ((), ()))
NT = (((1,), (1,)), ((), ()))
TN = (((0,), (0,)), ((), ()))
MESH = pl.DeviceIdType.MESH
VMEM = pl.BlockSpec(memory_space=pltpu.VMEM)
HBM = pl.BlockSpec(memory_space=pltpu.HBM)


def dot(a, b, dims=NN):
    return lax.dot_general(a, b, dims, preferred_element_type=f32)


def lane_of(shape):
    return lax.broadcasted_iota(jnp.int32, shape, len(shape) - 1)


def row_of(shape):
    return lax.broadcasted_iota(jnp.int32, shape, len(shape) - 2)


def span(i, n):
    return pl.ds(pl.multiple_of(i * n, n), n)


def split3(v):
    hi = v.astype(bf16).astype(f32)
    mid = (v - hi).astype(bf16).astype(f32)
    return hi, mid, v - hi - mid


def layer_norm(values, gain, shift):
    average = jnp.mean(values, axis=-1, keepdims=True)
    centered = values - average
    spread = jnp.mean(centered * centered, axis=-1, keepdims=True)
    return centered * lax.rsqrt(spread + norm_eps) * gain + shift


def tree_layout(tree_lengths, tree_parents, rows):
    seg_sizes = jnp.concatenate([jnp.full((1,), TRUNK, jnp.int32), tree_lengths])
    ends = jnp.cumsum(seg_sizes)
    starts = ends - seg_sizes
    places = jnp.arange(rows, dtype=jnp.int32)
    labels = jnp.arange(SEGMENTS, dtype=jnp.int32)
    segment = jnp.sum((places[:, None] >= ends[None, :]).astype(jnp.int32), axis=1)
    own_hot = (segment[:, None] == labels[None, :]).astype(jnp.int32)
    parent = jnp.sum(own_hot * tree_parents[None, :], axis=1)
    parent_hot = (parent[:, None] == labels[None, :]).astype(jnp.int32)
    grandparent = jnp.sum(parent_hot * tree_parents[None, :], axis=1)
    parent_size = jnp.sum(parent_hot * seg_sizes[None, :], axis=1)
    depth_start = jnp.where(segment > 0, TRUNK, 0).astype(jnp.int32) + jnp.where(
        parent > 0, parent_size, 0
    )
    position = places - jnp.sum(own_hot * starts[None, :], axis=1) + depth_start
    return (segment, parent, grandparent, position)


def tables(tree_lengths, tree_parents, rows):
    segment, parent, grand, position = tree_layout(tree_lengths, tree_parents, rows)
    lane = jnp.arange(LANES, dtype=jnp.int32)
    half = HEAD_DIM // 2
    inverse = rope_base ** (-(lane % half).astype(f32) * 2.0 / HEAD_DIM)
    angle = position.astype(f32)[:, None] * inverse[None, :]
    cosine = jnp.cos(angle)
    sine = jnp.where((lane % HEAD_DIM) < half, -1.0, 1.0)[None, :] * jnp.sin(angle)
    label = (lane - HEAD_DIM)[None, :]
    own = segment[:, None] == label
    path = own | (parent[:, None] == label) | (grand[:, None] == label)
    hidden = (label >= 0) & (label < SEGMENTS) & ~path
    queries = jnp.where(hidden, masked_score, 0.0).astype(f32)
    ones = (label >= 16) & (label < 19)
    keys = jnp.where(own | ones, 1.0, 0.0).astype(f32)
    return cosine, sine, queries, keys
def barrier(partners):
    semaphore = pltpu.get_barrier_semaphore()
    for partner in partners:
        pl.semaphore_signal(semaphore, inc=1, device_id=partner, device_id_type=MESH)
    pl.semaphore_wait(semaphore, len(partners))


def send(source, target, send_sem, recv_sem, device):
    copy = pltpu.make_async_remote_copy(
        src_ref=source,
        dst_ref=target,
        send_sem=send_sem,
        recv_sem=recv_sem,
        device_id=device,
        device_id_type=MESH,
    )
    copy.start()
    return copy


def add_rows(target, source, step=64):
    rows = target.shape[0]
    step = min(step, rows)
    while rows % step:
        step //= 2

    def body(i, _):
        at = span(i, step)
        target[at, :] = target[at, :] + source[at, :]
        return 0

    lax.fori_loop(0, rows // step, body, 0)


def orders(n_d):
    bits = n_d.bit_length() - 1
    return [list(range(bits)), list(range(bits - 1, -1, -1))]


def combos(bits):
    masks = [0]
    for b in bits:
        masks = masks + [m ^ (1 << b) for m in masks]
    return masks


def halves(rows, width, tile=16):
    return (rows // 2, width) if rows % (2 * tile) == 0 else (rows, width // 2)


def half(part, stream, rows, width):
    height, wide = halves(rows, width)
    if height < rows:
        return span(2 * part + stream, height), slice(None)
    return span(part, rows), pl.ds(stream * wide, wide)


class Spread:
    def __init__(self, n_d, n_t, shards, alls, sems):
        self.n_d, self.n_t, self.shards, self.alls = n_d, n_t, shards, alls
        self.zs, self.zr, self.ps, self.pr, self.ys, self.yr, self.own = sems
        self.d, self.t = lax.axis_index("dp"), lax.axis_index("tensor")
        self.chips = n_t // 2
        self.chip, self.core = self.t // 2, lax.rem(self.t, 2)
        self.other = 2 * self.chip + 1 - self.core
        self.bits = n_d.bit_length() - 1
        self.arrays = range(len(shards))

    @staticmethod
    def sems(count, n_d, n_t):
        dma = pltpu.SemaphoreType.DMA
        hops, slots = n_t // 2 - 1, 2 * (n_d - 1)
        z, p, y = (count, 2 * hops), (count, 2 * hops, slots), (count, 2 * hops + 1)
        return [dma(z), dma(z), dma(p), dma(p), dma(y), dma(y), dma((count,))]

    def exists(self, c):
        return (c >= 0) & (c < self.chips)

    def rows(self, a):
        return self.shards[a].shape[0] // self.n_d

    def slot(self, way, h):
        return h - 1 + (self.chips - 1 if way < 0 else 0)

    def remote(self, src, dst, ssem, rsem, device):
        return pltpu.make_async_remote_copy(
            src_ref=src, dst_ref=dst, send_sem=ssem, recv_sem=rsem, device_id=device, device_id_type=MESH
        )

    def along(self, a, way, h, arriving):
        source = self.chip - way * (h if arriving else h - 1)
        at = span(self.d, self.rows(a))
        dst = self.alls[a].at[2 * source + self.core, at]
        src = self.shards[a].at[at] if h == 1 and not arriving else dst
        peer = self.chip - way if arriving else self.chip + way
        i = self.slot(way, h)
        return self.remote(src, dst, self.zs.at[a, i], self.zr.at[a, i], (self.d, 2 * peer + self.core))

    def across(self, a, way, h, step, arriving):
        source = self.chip - way * h
        out = []
        for stream, order in enumerate(orders(self.n_d)):
            partner = lax.bitwise_xor(self.d, 1 << order[step])
            for j, m in enumerate(combos(order[:step])):
                block = lax.bitwise_xor(partner if arriving else self.d, m)
                rows, cols = half(block, stream, self.rows(a), self.shards[a].shape[1])
                ref = self.alls[a].at[2 * source + self.core, rows, cols]
                i = stream * (self.n_d - 1) + (1 << step) - 1 + j
                k = self.slot(way, h)
                out.append(self.remote(ref, ref, self.ps.at[a, k, i], self.pr.at[a, k, i], (partner, self.t)))
        return out

    def beside(self, a, way, h, arriving=False):
        source = self.chip - way * h
        ref = self.alls[a].at[2 * source + (1 - self.core if arriving else self.core)]
        k = self.slot(way, h)
        return self.remote(ref, ref, self.ys.at[a, k], self.yr.at[a, k], (self.d, self.other))

    def mine(self, a, arriving=False):
        k = 2 * (self.chips - 1)
        dst = self.alls[a].at[self.other if arriving else self.t]
        return self.remote(self.shards[a], dst, self.ys.at[a, k], self.yr.at[a, k], (self.d, self.other))

    def keep(self, a):
        return pltpu.make_async_copy(self.shards[a], self.alls[a].at[self.t], self.own.at[a])

    def begin(self):
        for way in (1, -1):

            @pl.when(self.exists(self.chip + way))
            def _():
                for a in self.arrays:
                    self.along(a, way, 1, False).start()

        for a in self.arrays:
            self.keep(a).start()
            self.mine(a).start()

    def phase(self, p, h):
        for way in (1, -1):

            @pl.when(self.exists(self.chip - way * h))
            def _():
                for a in self.arrays:
                    if p == 0:
                        self.along(a, way, h, True).wait_recv()
                        if h < self.chips - 1:

                            @pl.when(self.exists(self.chip + way))
                            def _():
                                self.along(a, way, h + 1, False).start()
                    else:
                        for copy in self.across(a, way, h, p - 1, True):
                            copy.wait_recv()
                    if p < self.bits:
                        for copy in self.across(a, way, h, p, False):
                            copy.start()
                    else:
                        self.beside(a, way, h).start()

    def groups(self):
        return self.chips - 1 + self.bits

    def group(self, g):
        for h in range(1, self.chips):
            if 0 <= g - (h - 1) <= self.bits:
                self.phase(g - (h - 1), h)

    def end(self):
        for h in range(1, self.chips):
            for way in (1, -1):

                @pl.when(self.exists(self.chip + way) & self.exists(self.chip - way * (h - 1)))
                def _():
                    for a in self.arrays:
                        self.along(a, way, h, False).wait_send()

                @pl.when(self.exists(self.chip - way * h))
                def _():
                    for a in self.arrays:
                        for step in range(self.bits):
                            for copy in self.across(a, way, h, step, False):
                                copy.wait_send()
                        self.beside(a, way, h).wait_send()
                        self.beside(a, way, h, True).wait_recv()

        for a in self.arrays:
            self.keep(a).wait()
            self.mine(a).wait_send()
            self.mine(a, True).wait_recv()


def gather_kernel(
    n_d, n_t, v_ref, gain_ref, w_ref, f_ref, o_ref, u_ref, all_ref,
    x_ref, passing, rs, ss, rb, sb, rw, sw, rp, sp, *sems,
):
    d, t = lax.axis_index("dp"), lax.axis_index("tensor")
    trees, rows, _ = x_ref.shape
    chips = n_t // 2
    group = n_t // trees
    chip, core = t // 2, lax.rem(t, 2)
    other = 2 * chip + 1 - core
    near = group // 2
    tree = t // group
    planes = [lax.rem(d + k, n_d) for k in range(1, n_d)]
    owners = [(j * group + t // trees) for j in range(trees)]
    givers = [lax.rem(t, group) * trees + i for i in range(trees)]
    barrier([(d, lax.rem(t + k, n_t)) for k in range(1, n_t)] + [(p, t) for p in planes])
    part = w_ref.shape[1] // n_d
    weights = Spread(n_d, n_t, [f_ref], [all_ref], sems)
    exists = weights.exists

    copies = []
    mine = w_ref.at[:, span(d, part), :]
    for j in range(trees):
        slot = u_ref.at[lax.rem(t, trees), :, span(d, part), :]

        @pl.when(owners[j] != t)
        def _():
            send(mine, slot, sw.at[j], rw.at[lax.rem(t, trees)], (d, owners[j]))

        @pl.when(owners[j] == t)
        def _():
            u_ref[lax.rem(t, trees), :, span(d, part), :] = w_ref[:, span(d, part), :]

    weights.begin()

    def block(c):
        return o_ref.at[span(2 * c + core, rows)]

    def beyond(c, way, j):
        return (j * near + near - 1 >= c) if way > 0 else (j * near <= c)

    def hop(way, h, j, here):
        source = chip - way * (h - 1)
        if h == 1:
            src = x_ref.at[j]
        else:
            src = block(source) if here else passing.at[j, source]
        return src, source

    def pass_on(way, h):
        for j in range(trees):

            @pl.when(exists(chip - way * (h - 1)) & exists(chip + way) & beyond(chip + way, way, j))
            def _():
                i = weights.slot(way, h)
                to = chip + way
                for here in (True, False) if h > 1 else (True,):
                    src, source = hop(way, h, j, here)
                    for there in (True, False):
                        at_home = (tree == j) if here else (tree != j)
                        lands = (to // near == j) if there else (to // near != j)

                        @pl.when((at_home & lands) if h > 1 else lands)
                        def _():
                            dst = block(source) if there else passing.at[j, source]
                            send(src, dst, ss.at[j, i], rs.at[j, i], (d, 2 * to + core))

    def row_copy(j, i):
        return weights.remote(x_ref.at[j], passing.at[j, 0], ss.at[j, i], rs.at[j, i], (d, other))

    def share(way, h):
        source = chip - way * h
        i = weights.slot(way, h)
        return weights.remote(block(source), block(source), sb.at[i], rb.at[i], (d, other))

    def arrive(way, h):
        for j in range(trees):

            @pl.when(exists(chip - way * h) & beyond(chip, way, j))
            def _():
                row_copy(j, weights.slot(way, h)).wait_recv()

        if h < chips - 1:
            pass_on(way, h + 1)

        @pl.when(exists(chip - way * h))
        def _():
            share(way, h).start()

    height = min(64, rows)

    def norm_rows(i, _):
        at = span(i, height)
        for j in range(trees):
            v = v_ref[j, at, :].astype(f32)
            x_ref[j, at, :] = layer_norm(v, gain_ref[6:7], gain_ref[7:8]).astype(bf16)
        return 0

    lax.fori_loop(0, rows // height, norm_rows, 0)
    o_ref[span(t, rows), :] = x_ref[tree]
    for way in (1, -1):
        pass_on(way, 1)
    last = 2 * (chips - 1)
    copies.append(send(x_ref.at[tree], block(chip), sb.at[last], rb.at[last], (d, other)))
    weights.group(0)
    for i in range(trees):
        slot = u_ref.at[i, :, span(d, part), :]

        @pl.when(givers[i] != t)
        def _():
            pltpu.make_async_remote_copy(
                src_ref=mine, dst_ref=slot, send_sem=sw.at[0], recv_sem=rw.at[i],
                device_id=(d, givers[i]), device_id_type=MESH,
            ).wait_recv()

    mine_all = u_ref.at[:, :, span(d, part), :]
    for k, p in enumerate(planes):
        copies.append(send(mine_all, mine_all, sp.at[k], rp.at[k], (p, t)))
    for h in range(1, chips):
        for way in (1, -1):
            arrive(way, h)
        weights.group(h)
    for g in range(chips, weights.groups()):
        weights.group(g)
    weights.end()
    for j in range(trees):

        @pl.when(owners[j] != t)
        def _():
            pltpu.make_async_remote_copy(
                src_ref=mine, dst_ref=mine, send_sem=sw.at[j], recv_sem=rw.at[0],
                device_id=(d, owners[j]), device_id_type=MESH,
            ).wait_send()

    for way in (1, -1):
        for h in range(1, chips):
            for j in range(trees):

                @pl.when(exists(chip - way * (h - 1)) & exists(chip + way) & beyond(chip + way, way, j))
                def _():
                    row_copy(j, weights.slot(way, h)).wait_send()

            @pl.when(exists(chip - way * h))
            def _():
                share(way, h).wait()

    for copy in copies:
        copy.wait()


def gather_tree(n_d, n_t, tokens, par, weight, down):
    trees, rows, wide = tokens.shape
    chips = n_t // 2
    hops = 2 * (chips - 1)
    dma = pltpu.SemaphoreType.DMA
    return pl.pallas_call(
        functools.partial(gather_kernel, n_d, n_t),
        in_specs=[VMEM] * 4,
        out_specs=[VMEM] * 2 + [HBM],
        out_shape=[
            jax.ShapeDtypeStruct((n_t * rows, wide), bf16),
            jax.ShapeDtypeStruct((trees,) + weight.shape, bf16),
            jax.ShapeDtypeStruct((n_t,) + down.shape, bf16),
        ],
        scratch_shapes=[
            pltpu.VMEM((trees, rows, wide), bf16), pltpu.VMEM((trees, chips, rows, wide), bf16),
            dma((trees, hops)), dma((trees, hops)), dma((hops + 1,)), dma((hops + 1,)),
            dma((trees,)), dma((trees,)), dma((n_d - 1,)), dma((n_d - 1,)),
        ] + Spread.sems(1, n_d, n_t),
        compiler_params=pltpu.CompilerParams(collective_id=0, has_side_effects=True),
        name="gather_tree",
    )(tokens, par, weight, down)


def qkv_kernel(x_ref, w_ref, cos_ref, sin_ref, mq_ref, mk_ref, q_ref, k_ref, v_ref, kt_ref, vt_ref):
    x = x_ref[...]
    heads = q_ref.shape[0]
    cosine, sine = cos_ref[...], sin_ref[...]
    mq, mk = mq_ref[...], mk_ref[...]
    lane = lane_of(cosine.shape)
    low = lax.rem(lane, HEAD_DIM) < HEAD_DIM // 2
    first = lane < HEAD_DIM
    mv = jnp.where((lane >= HEAD_DIM) & (lane < HEAD_DIM + 3), 1.0, 0.0)
    tail = jnp.where(row_of((VROWS - HEAD_DIM, x.shape[0])) == 0, 1.0, 0.0).astype(bf16)

    def both(slab):
        return slab, pltpu.roll(slab, HEAD_DIM, 1)

    def rotate(slab):
        partner = jnp.where(
            low, pltpu.roll(slab, LANES - HEAD_DIM // 2, 1), pltpu.roll(slab, HEAD_DIM // 2, 1)
        )
        return slab * cosine + partner * sine

    q_all, k_all, v_all = (dot(x, w_ref[i]) for i in range(3))
    for h in range(0, heads, 2):
        cols = slice(h * HEAD_DIM, (h + 2) * HEAD_DIM)
        for g, slab in enumerate(both(rotate(q_all[:, cols]) * HEAD_DIM**-0.5)):
            q_ref[h + g] = jnp.where(first, slab, mq).astype(bf16)
        keys = rotate(k_all[:, cols])
        for g, slab in enumerate(both(keys)):
            k_ref[h + g] = jnp.where(first, slab, mk).astype(bf16)
        flat = keys.T.astype(bf16)
        for g, slab in enumerate(both(v_all[:, cols])):
            v_ref[h + g] = jnp.where(first, slab, mv).astype(bf16)
        flat_v = v_all[:, cols].T.astype(bf16)
        for g in range(2):
            part = slice(g * HEAD_DIM, (g + 1) * HEAD_DIM)
            kt_ref[h + g] = flat[part]
            vt_ref[h + g, :HEAD_DIM] = flat_v[part]
            vt_ref[h + g, HEAD_DIM:] = tail


def project(x, w, cosine, sine, mq, mk):
    rows, wide = x.shape
    heads = w.shape[2] // HEAD_DIM
    table = pl.BlockSpec((BLOCK, LANES), lambda i: (i, 0))
    slab = pl.BlockSpec((heads, BLOCK, LANES), lambda i: (0, i, 0))
    shape = jax.ShapeDtypeStruct((heads, rows, LANES), bf16)
    return pl.pallas_call(
        qkv_kernel,
        grid=(rows // BLOCK,),
        in_specs=[
            pl.BlockSpec((BLOCK, wide), lambda i: (i, 0)),
            pl.BlockSpec(w.shape, lambda i: (0, 0, 0)),
            table, table, table, table,
        ],
        out_specs=[
            slab, slab, slab,
            pl.BlockSpec((heads, HEAD_DIM, BLOCK), lambda i: (0, 0, i)),
            pl.BlockSpec((heads, VROWS, BLOCK), lambda i: (0, 0, i)),
        ],
        out_shape=[
            shape, shape, shape,
            jax.ShapeDtypeStruct((heads, HEAD_DIM, rows), bf16),
            jax.ShapeDtypeStruct((heads, VROWS, rows), bf16),
        ],
        name="project",
    )(x, w, cosine, sine, mq, mk)


def fwd_kernel(
    n_d, n_t, trees, q_ref, k_ref, vt_ref, ow_ref, up_ref, o_ref, qb_ref, att_ref, ow_all, up_all,
    ss, rs, here, *sems,
):
    turn = pl.program_id(0)
    steps = pl.num_programs(0)
    heads = q_ref.shape[0]
    row, col = row_of((BLOCK, BLOCK)), lane_of((BLOCK, BLOCK))
    d, t = lax.axis_index("dp"), lax.axis_index("tensor")
    group = n_t // trees
    rows, width = att_ref.shape[1], o_ref.shape[1]
    per = BLOCK // rows
    qi = jnp.where(turn == steps - 1, t // per, jnp.where(turn >= t // per, turn + 1, turn))
    at = span(qi, BLOCK)
    weights = Spread(n_d, n_t, [up_ref, ow_ref], [up_all, ow_all], sems)
    first_group = max(0, k_ref.shape[1] // BLOCK - 4)
    place = att_ref.at[t // group, :, span(lax.rem(t, group), width)]

    def outgoing(i, r, k):
        return pltpu.make_async_remote_copy(
            src_ref=o_ref.at[span(i * per + r, rows)], dst_ref=place, send_sem=ss.at[k], recv_sem=rs.at[k],
            device_id=(d, lax.rem(t + k, n_t)), device_id_type=MESH,
        )

    @pl.when(turn == 0)
    def _():
        barrier(
            [(d, lax.rem(t + k, n_t)) for k in range(1, n_t)] + [(lax.rem(d + k, n_d), t) for k in range(1, n_d)]
        )
        weights.begin()

    for g in range(weights.groups()):
        if first_group + g < k_ref.shape[1] // BLOCK:

            @pl.when(turn == first_group + g)
            def _():
                weights.group(g)

    qs = [q_ref[h, at, :] for h in range(heads)]

    def scores(h, j):
        return dot(k_ref[h, span(j, BLOCK), :], qs[h], NT)

    state = []
    for h in range(heads):
        s = jnp.where(row <= col, scores(h, qi), masked_score)
        m = jnp.max(s, axis=0, keepdims=True)
        p = jnp.exp(s - m)
        state.append((m, dot(vt_ref[h, :, span(qi, BLOCK)], p.astype(bf16))))

    def step(j, carry):
        out = []
        for h in range(heads):
            m, acc = carry[h]
            s = scores(h, j)
            top = jnp.maximum(m, jnp.max(s, axis=0, keepdims=True))
            p = jnp.exp(s - top)
            acc = acc * jnp.exp(m - top) + dot(vt_ref[h, :, span(j, BLOCK)], p.astype(bf16))
            out.append((top, acc))
        return tuple(out)

    state = lax.fori_loop(0, qi, step, tuple(state))
    r = row_of((LANES, BLOCK))
    for h in range(0, heads, 2):
        outs = []
        for g in (h, h + 1):
            m, acc = state[g]
            total = acc[HEAD_DIM : HEAD_DIM + 1]
            outs.append(acc[:HEAD_DIM] / total)
            a, b, c = split3(-(m + jnp.log(total)))
            extra = jnp.where(r == 80, a, jnp.where(r == 81, b, jnp.where(r == 82, c, 0.0))).T
            qb_ref[g, at, :] = qs[g] + extra.astype(bf16)
        o_ref[at, h * HEAD_DIM : (h + 2) * HEAD_DIM] = jnp.concatenate(outs, axis=0).T.astype(bf16)

    def local(r):
        return pltpu.make_async_copy(o_ref.at[span(t // per * per + r, rows)], place, here.at[0])

    for r in range(per):
        k = lax.rem(qi * per + r + n_t - t, n_t)

        @pl.when(k != 0)
        def _():
            outgoing(qi, r, k).start()

        @pl.when(k == 0)
        def _():
            local(r).start()

    @pl.when(turn == steps - 1)
    def _():
        for g in range(k_ref.shape[1] // BLOCK - first_group, weights.groups()):
            weights.group(g)
        for k in range(1, n_t):
            outgoing(0, 0, k).wait()
        local(0).wait()
        weights.end()


def attend(n_d, n_t, trees, q, k, vt, ow, up):
    heads, rows, _ = q.shape
    wide = heads * HEAD_DIM
    dma = pltpu.SemaphoreType.DMA
    sds = jax.ShapeDtypeStruct
    return pl.pallas_call(
        functools.partial(fwd_kernel, n_d, n_t, trees),
        grid=(rows // BLOCK,),
        in_specs=[VMEM] * 5,
        out_specs=[VMEM, VMEM, HBM, HBM, HBM],
        out_shape=[
            sds((rows, wide), bf16),
            sds(q.shape, bf16),
            sds((trees, rows // n_t, wide * n_t // trees), bf16),
            sds((n_t,) + ow.shape, bf16),
            sds((n_t,) + up.shape, bf16),
        ],
        scratch_shapes=[
            dma((n_t,)), dma((n_t,)), dma((1,)),
        ] + Spread.sems(2, n_d, n_t),
        compiler_params=pltpu.CompilerParams(collective_id=1, has_side_effects=True),
        name="attend",
    )(q, k, vt, ow, up)


class Reduce:
    def __init__(self, n_d, n_t, sources, totals, scratch):
        self.n_d, self.n_t, self.sources, self.totals = n_d, n_t, sources, totals
        count = len(sources)
        self.mine, self.side, self.land_at, self.far = (
            scratch[i * count : (i + 1) * count] for i in range(4)
        )
        self.s_load, self.s_side, self.r_side, self.s_hop, self.r_hop, self.s_far, self.r_far = scratch[4 * count :]
        self.d, self.t = lax.axis_index("dp"), lax.axis_index("tensor")
        self.chips = n_t // 2
        self.chip, self.core = self.t // 2, lax.rem(self.t, 2)
        self.other = 2 * self.chip + 1 - self.core
        self.dest = [lax.rem(self.chip + k, self.chips) for k in range(1, self.chips)] + [self.chip]
        self.bits = n_d.bit_length() - 1
        self.units = [(n, k) for k in range(self.chips) for n in range(count)]

    @staticmethod
    def scratch(n_d, n_t, shapes):
        dma = pltpu.SemaphoreType.DMA
        chips, slots, count = n_t // 2, 2 * (n_d - 1), len(shapes)
        vm = lambda lead, r, c: pltpu.VMEM(lead + (r, c), bf16)
        units = count * chips
        return (
            [vm((chips,), r, c) for r, c in shapes] * 2
            + [vm((chips, slots), *halves(r // n_d, c)) for r, c in shapes]
            + [vm((chips - 1,), r // n_d, c) for r, c in shapes]
            + [dma((units,)), dma((units,)), dma((units,)), dma((units, slots)), dma((units, slots))]
            + [dma((units,)), dma((units,))]
        )

    def remote(self, src, dst, ssem, rsem, device):
        return pltpu.make_async_remote_copy(
            src_ref=src, dst_ref=dst, send_sem=ssem, recv_sem=rsem, device_id=device, device_id_type=MESH
        )

    def load(self, u):
        n, k = self.units[u]
        source = self.sources[n].at[2 * self.dest[k] + self.core]
        return pltpu.make_async_copy(source, self.mine[n].at[k], self.s_load.at[u])

    def beside(self, u):
        n, k = self.units[u]
        source = self.sources[n].at[2 * self.dest[k] + 1 - self.core]
        return self.remote(source, self.side[n].at[k], self.s_side.at[u], self.r_side.at[u], (self.d, self.other))

    def cut(self, u, part, stream):
        n, k = self.units[u]
        _, height, width = self.mine[n].shape
        rows, cols = half(part, stream, height // self.n_d, width)
        return self.mine[n].at[k, rows, cols]

    def hops(self, u, step):
        n, k = self.units[u]
        slot = 0 if step == 0 else self.n_d - (self.n_d >> step)
        out = []
        for stream, order in enumerate(orders(self.n_d)):
            partner = lax.bitwise_xor(self.d, 1 << order[step])
            for j, m in enumerate(combos(order[step + 1 :])):
                i = (slot + j) * 2 + stream
                landing = self.land_at[n].at[k, i]
                copy = self.remote(
                    self.cut(u, lax.bitwise_xor(partner, m), stream), landing,
                    self.s_hop.at[u, i], self.r_hop.at[u, i], (partner, self.t),
                )
                out.append((copy, self.cut(u, lax.bitwise_xor(self.d, m), stream), landing))
        return out

    def piece(self, u):
        n, k = self.units[u]
        return self.mine[n].at[k, span(self.d, self.mine[n].shape[1] // self.n_d), :]

    def away(self, u):
        n, k = self.units[u]
        return self.remote(
            self.piece(u), self.far[n].at[k], self.s_far.at[u], self.r_far.at[u],
            (self.d, 2 * self.dest[k] + self.core),
        )

    def begin(self):
        for u in range(len(self.units)):
            self.load(u).start()
            self.beside(u).start()

    def events(self):
        return len(self.units) + self.bits

    def event(self, e):
        if e < len(self.units):
            n, k = self.units[e]
            self.load(e).wait()
            self.beside(e).wait_recv()
            add_rows(self.mine[n].at[k], self.side[n].at[k])
            for copy, _, _ in self.hops(e, 0):
                copy.start()
        for step in range(self.bits):
            u = e - 1 - step
            if 0 <= u < len(self.units):
                for copy, target, landing in self.hops(u, step):
                    copy.wait_recv()
                    add_rows(target, landing)
                if step + 1 < self.bits:
                    for copy, _, _ in self.hops(u, step + 1):
                        copy.start()
                elif self.units[u][1] < self.chips - 1:
                    self.away(u).start()

    def end(self):
        for u, (n, k) in enumerate(self.units):
            if k < self.chips - 1:
                self.away(u).wait_recv()
            else:
                total = self.piece(u)[...].astype(f32)
                for i in range(self.chips - 1):
                    total = total + self.far[n][i].astype(f32)
                self.totals[n][...] = total.astype(bf16)
        for u, (n, k) in enumerate(self.units):
            self.beside(u).wait_send()
            for step in range(self.bits):
                for copy, _, _ in self.hops(u, step):
                    copy.wait_send()
            if k < self.chips - 1:
                self.away(u).wait_send()


def bwd_kernel(
    n_d, n_t, q_ref, k_ref, v_ref, kt_ref, x_ref, o_ref, cos_ref, sin_ref, up_ref, down_ref, og_ref,
    m_ref, up_tot, down_tot, og_tot, sums, wide, d_ref, hs, hr, *scratch,
):
    j = pl.program_id(0)
    heads, rows, _ = q_ref.shape
    nq = rows // BLOCK
    row, col = row_of((BLOCK, BLOCK)), lane_of((BLOCK, BLOCK))
    lane = lane_of((BLOCK, LANES))
    first = lane < HEAD_DIM
    d, t = lax.axis_index("dp"), lax.axis_index("tensor")
    trees, part, _ = x_ref.shape
    group, width = n_t // trees, heads * HEAD_DIM
    gradients = Reduce(n_d, n_t, [up_ref, down_ref, og_ref], [up_tot, down_tot, og_tot], scratch)
    ahead = 3
    points = 10

    def point(p):
        left = gradients.events() - ahead
        for e in range(ahead + p * left // points, ahead + (p + 1) * left // points):
            gradients.event(e)

    def cut(o):
        return x_ref.at[o // group, :, span(lax.rem(o, group), width)]

    def outgoing(k):
        o = lax.rem(t + k, n_t)
        return gradients.remote(cut(o), d_ref.at[span(t, part), :], hs.at[k], hr.at[k], (d, o))

    @pl.when(j == 0)
    def _():
        barrier(
            [(d, lax.rem(t + k, n_t)) for k in range(1, n_t)] + [(lax.rem(d + k, n_d), t) for k in range(1, n_d)]
        )
        for k in range(1, n_t):
            outgoing(k).start()
        gradients.begin()
        d_ref[span(t, part), :] = cut(t)[...]
        sums[...] = jnp.zeros_like(sums)
        for e in range(ahead):
            gradients.event(e)
        for k in range(1, n_t):
            outgoing(k).wait()

        def widen(i, _):
            at = span(i, BLOCK)
            for h in range(0, heads, 2):
                cols = slice(h * HEAD_DIM, (h + 2) * HEAD_DIM)
                slab = d_ref[at, cols].astype(f32)
                prod = slab * o_ref[at, cols].astype(f32)
                for g, (s, mine) in enumerate(((slab, first), (pltpu.roll(slab, HEAD_DIM, 1), ~first))):
                    inner = -jnp.sum(jnp.where(mine, prod, 0.0), axis=1, keepdims=True)
                    a, b, c = split3(inner)
                    n = HEAD_DIM
                    tail = jnp.where(lane == n, a, jnp.where(lane == n + 1, b, jnp.where(lane == n + 2, c, 0.0)))
                    wide[h + g, at, :] = jnp.where(first, s, tail).astype(bf16)
            return 0

        lax.fori_loop(0, nq, widen, 0)

    for p in range(0, points, 2):
        if p // 2 < nq:

            @pl.when(j == p // 2)
            def _():
                point(p)

    ks = [k_ref[h] for h in range(heads)]
    vs = [v_ref[h] for h in range(heads)]
    kts = [kt_ref[h] for h in range(heads)]

    def pair(h, i, mask):
        at = span(i, BLOCK)
        q = q_ref[h, at, :]
        d = wide[h, at, :]
        s = dot(ks[h], q, NT)
        if mask:
            s = jnp.where(row <= col, s, masked_score)
        p = jnp.exp(s)
        back = (p * dot(vs[h], d, NT)).astype(bf16)
        sums[h, :, at] += dot(kts[h], back)
        return dot(back, q), dot(p.astype(bf16), d)

    def step(i, carry):
        out = []
        for h in range(heads):
            dk, dv = pair(h, i, False)
            out.append((carry[h][0] + dk, carry[h][1] + dv))
        return tuple(out)

    state = tuple(pair(h, j, True) for h in range(heads))
    middle = (j + 1 + nq) // 2
    state = lax.fori_loop(j + 1, middle, step, state)
    for p in range(1, points, 2):
        if p // 2 < nq:

            @pl.when(j == p // 2)
            def _():
                point(p)

    state = lax.fori_loop(middle, nq, step, state)

    def join(a, b):
        return jnp.where(first, a, pltpu.roll(b, HEAD_DIM, 1))

    cosine, sine = cos_ref[...], sin_ref[...]
    low = lax.rem(lane, HEAD_DIM) < HEAD_DIM // 2

    def unrotate(slab):
        partner = jnp.where(
            low, pltpu.roll(slab, LANES - HEAD_DIM // 2, 1), pltpu.roll(slab, HEAD_DIM // 2, 1)
        )
        return slab * cosine - partner * sine

    at = span(j, BLOCK)
    total = heads * HEAD_DIM
    for h in range(0, heads, 2):
        dq = jnp.concatenate([sums[h, :, at], sums[h + 1, :, at]], axis=0).T * HEAD_DIM**-0.5
        dk = join(state[h][0], state[h + 1][0])
        dv = join(state[h][1], state[h + 1][1])
        for n, part in enumerate((unrotate(dq), unrotate(dk), dv)):
            begin = n * total + h * HEAD_DIM
            m_ref[:, begin : begin + 2 * HEAD_DIM] = part.astype(bf16)

    @pl.when(j == nq - 1)
    def _():
        for p in range(2 * nq, points):
            point(p)
        gradients.end()


def attend_back(n_d, n_t, q, k, v, kt, x, o, cosine, sine, up_g, down_g, out_g):
    heads, rows, _ = q.shape
    whole = lambda a: pl.BlockSpec(a.shape, lambda j: (0,) * a.ndim, pipeline_mode=pl.Buffered(1))
    block = pl.BlockSpec((heads, BLOCK, LANES), lambda j: (0, j, 0))
    table = pl.BlockSpec((BLOCK, LANES), lambda j: (j, 0))
    wide = heads * HEAD_DIM
    dma = pltpu.SemaphoreType.DMA
    sds = jax.ShapeDtypeStruct
    shapes = [a.shape[1:] for a in (up_g, down_g, out_g)]
    return pl.pallas_call(
        functools.partial(bwd_kernel, n_d, n_t),
        grid=(rows // BLOCK,),
        in_specs=[
            whole(q), block, block,
            pl.BlockSpec((heads, HEAD_DIM, BLOCK), lambda j: (0, 0, j)),
            VMEM, whole(o), table, table, HBM, HBM, HBM,
        ],
        out_specs=[pl.BlockSpec((BLOCK, 3 * wide), lambda j: (j, 0)), VMEM, VMEM, VMEM],
        out_shape=[sds((rows, 3 * wide), bf16)] + [sds((r // n_d, c), bf16) for r, c in shapes],
        scratch_shapes=[
            pltpu.VMEM((heads, HEAD_DIM, rows), f32),
            pltpu.VMEM((heads, rows, LANES), bf16),
            pltpu.VMEM((rows, wide), bf16),
            dma((n_t,)), dma((n_t,)),
        ] + Reduce.scratch(n_d, n_t, shapes),
        compiler_params=pltpu.CompilerParams(
            collective_id=2, has_side_effects=True, vmem_limit_bytes=67043328
        ),
        name="attend_back",
    )(q, k, v, kt, x, o, cosine, sine, up_g, down_g, out_g)


def ln_parts(v):
    centered = v - jnp.mean(v, axis=-1, keepdims=True)
    r = lax.rsqrt(jnp.mean(centered * centered, axis=-1, keepdims=True) + norm_eps)
    return centered * r, r


def ln_back(e, n, r, gain):
    f = e * gain
    return r * (f - jnp.mean(f, axis=-1, keepdims=True) - n * jnp.mean(f * n, axis=-1, keepdims=True))


def feed_kernel(
    att_ref, x_ref, cot_ref, ow_ref, par_ref, up_ref, down_ref,
    out_ref, hid_ref, ba_ref, upg_ref, downg_ref, outg_ref, vec_ref,
    hidden, branch, acc, feed_in, back_feed, active, slope,
):
    phase, n = pl.program_id(0), pl.program_id(1)
    last = pl.num_programs(1) - 1
    par = lambda i: par_ref[i : i + 1]
    total = lambda v: jnp.sum(v, axis=0, keepdims=True)

    @pl.when((phase == 0) & (n == 0))
    def _():
        b = dot(att_ref[...], ow_ref[...])
        branch[...] = b
        h = x_ref[...].astype(f32) + ln_parts(b)[0] * par(0) + par(1)
        hidden[...] = h
        feed_in[...] = (ln_parts(h)[0] * par(2) + par(3)).astype(bf16)
        acc[...] = jnp.zeros_like(acc)

    up, down = up_ref[0], down_ref[0]

    @pl.when(phase == 0)
    def _():
        u = dot(feed_in[...], up)
        t = jnp.tanh(0.7978845608028654 * (u + 0.044715 * u * u * u))
        half = 0.5 * (1.0 + t)
        a = (u * half).astype(bf16)
        active[n] = a
        slope[n] = half + 0.5 * u * (1.0 - t * t) * (
            0.7978845608028654 * (1.0 + 3 * 0.044715 * u * u)
        )
        acc[...] += dot(a, down)

    @pl.when((phase == 1) & (n == 0))
    def _():
        e = cot_ref[...].astype(f32)
        norm, r = ln_parts(acc[...])
        out_ref[...] = (hidden[...] + norm * par(4) + par(5)).astype(bf16)
        vec_ref[4:5] = total(e * norm)
        vec_ref[5:6] = total(e)
        back_feed[...] = ln_back(e, norm, r, par(4)).astype(bf16)
        acc[...] = jnp.zeros_like(acc)

    @pl.when(phase == 1)
    def _():
        b = back_feed[...]
        upper = (dot(b, down, NT) * slope[n]).astype(bf16)
        acc[...] += dot(upper, up, NT)
        downg_ref[0] = dot(active[n], b, TN).astype(bf16)
        upg_ref[0] = dot(feed_in[...], upper, TN).astype(bf16)

    @pl.when((phase == 1) & (n == last))
    def _():
        e = acc[...]
        norm, r = ln_parts(hidden[...])
        vec_ref[2:3] = total(e * norm)
        vec_ref[3:4] = total(e)
        h = cot_ref[...].astype(f32) + ln_back(e, norm, r, par(2))
        hid_ref[...] = h
        norm, r = ln_parts(branch[...])
        vec_ref[0:1] = total(h * norm)
        vec_ref[1:2] = total(h)
        b = ln_back(h, norm, r, par(0)).astype(bf16)
        ba_ref[...] = dot(b, ow_ref[...], NT).astype(bf16)
        outg_ref[...] = dot(att_ref[...], b, TN).astype(bf16)


def feed(att, x, cot, ow, par, up, down):
    rows, wide = att.shape
    n_t, _, width = up.shape
    one = lambda a: pl.BlockSpec(a.shape, lambda p, n: (0,) * len(a.shape), pipeline_mode=pl.Buffered(1))
    sds = jax.ShapeDtypeStruct
    outs = [
        sds((rows, wide), bf16), sds((rows, wide), f32), sds((rows, wide), bf16),
        sds((n_t, wide, width), bf16), sds((n_t, width, wide), bf16), sds((wide, wide), bf16),
        sds((8, wide), f32),
    ]
    chunk = lambda a: pl.BlockSpec((1,) + a.shape[1:], lambda p, n: (p * n, 0, 0))
    weight = lambda a: pl.BlockSpec((1,) + a.shape[1:], lambda p, n: (n, 0, 0))
    return pl.pallas_call(
        feed_kernel,
        grid=(2, n_t),
        in_specs=[one(a) for a in (att, x, cot, ow, par)] + [weight(up), weight(down)],
        out_specs=[one(o) for o in outs[:3]] + [chunk(outs[3]), chunk(outs[4])] + [one(o) for o in outs[5:]],
        out_shape=outs,
        scratch_shapes=[
            pltpu.VMEM((rows, wide), f32), pltpu.VMEM((rows, wide), f32), pltpu.VMEM((rows, wide), f32),
            pltpu.VMEM((rows, wide), bf16), pltpu.VMEM((rows, wide), bf16),
            pltpu.VMEM((n_t, rows, width), bf16), pltpu.VMEM((n_t, rows, width), f32),
        ],
        compiler_params=pltpu.CompilerParams(vmem_limit_bytes=64 << 20),
        name="feed",
    )(att, x, cot, ow, par, up, down)
def finish_kernel(
    n_d, n_t, bm_ref, w_ref, x_ref, hid_ref, par_ref, vec_in, up_tot, down_tot, og_tot, g_hbm,
    bt_ref, vec_ref, up_out, down_out, og_out, ig_out,
    g_ref, mine, landed, far, full_up, full_down, full_og, full_ig,
    r_give, r_keep, r_side, r_out, r_land, vec_now, vec_got, vec_far,
    s_load, s_hop, r_hop, s_all, r_all, s_own, r_own,
    s_red, r_red, s_redside, r_redside, s_vec, r_vec,
):
    d, t = lax.axis_index("dp"), lax.axis_index("tensor")
    trees, rows, wide = x_ref.shape
    chips = n_t // 2
    near = chips // trees
    group = n_t // trees
    chip, core = t // 2, lax.rem(t, 2)
    other = 2 * chip + 1 - core
    line = [lax.rem(chip + k, chips) for k in range(1, chips)]
    peers = [lax.rem(d + k, n_d) for k in range(1, n_d)]
    bits = n_d.bit_length() - 1
    barrier([(d, lax.rem(t + k, n_t)) for k in range(1, n_t)] + [(p, t) for p in peers])
    totals = [up_tot, down_tot, og_tot]
    fulls = [full_up, full_down, full_og, full_ig]
    outs = [up_out, down_out, og_out, ig_out]

    load = pltpu.make_async_copy(g_hbm, g_ref, s_load.at[0])
    load.start()
    hops, spreads = {}, []

    def cut(k, part):
        return mine.at[k, span(part, mine.shape[1] // n_d), :]

    def hop(k, step):
        slot = 0 if step == 0 else n_d - (n_d >> step)
        order = orders(n_d)[k % 2]
        partner = lax.bitwise_xor(d, 1 << order[step])
        for j, m in enumerate(combos(order[step + 1 :])):
            hops[k, step, j] = send(
                cut(k, lax.bitwise_xor(partner, m)), landed.at[k, slot + j],
                s_hop.at[k, slot + j], r_hop.at[k, slot + j], (partner, t),
            )

    def land(k, step):
        slot = 0 if step == 0 else n_d - (n_d >> step)
        for j, m in enumerate(combos(orders(n_d)[k % 2][step + 1 :])):
            hops[k, step, j].wait_recv()
            add_rows(cut(k, lax.bitwise_xor(d, m)), landed.at[k, slot + j])
        if step + 1 < bits:
            hop(k, step + 1)
        else:
            away(k)

    def spread(n, source):
        at = span(d, fulls[n].shape[0] // n_d)
        for j, p in enumerate(peers):
            spreads.append(send(source, fulls[n].at[at, :], s_all.at[n, j], r_all.at[n, j], (p, t)))

    def owner(i):
        return lax.rem(t, group) * trees + i

    def away(k):
        here = t // group

        @pl.when(owner(k) != t)
        def _():
            send(cut(k, d), far.at[here], s_own.at[k], r_own.at[here], (d, owner(k)))

        @pl.when(owner(k) == t)
        def _():
            far[here] = cut(k, d)[...]

    spread(0, totals[0])
    spread(2, totals[2])

    tree = chip // near

    def exists(c):
        return (c >= 0) & (c < chips)

    def at_step(i):
        return jnp.where(chip < chips // 2, chips - 1 - i, i)

    def past(way, x):
        return (x > chip) if way > 0 else (x < chip)

    def comes(way, j):
        return (j * near <= chip - 1) if way > 0 else (j * near + near - 1 >= chip + 1)

    def pair(x):
        return pltpu.make_async_remote_copy(
            src_ref=r_give.at[x], dst_ref=r_side.at[x], send_sem=s_redside.at[x], recv_sem=r_redside.at[x],
            device_id=(d, other), device_id_type=MESH,
        )

    def red(way, x, j, source, arriving=False):
        w = 0 if way > 0 else 1
        to = chip - way if arriving else chip + way
        return pltpu.make_async_remote_copy(
            src_ref=source, dst_ref=r_land.at[w, x, j], send_sem=s_red.at[w, x, j], recv_sem=r_red.at[w, x, j],
            device_id=(d, 2 * to + core), device_id_type=MESH,
        )

    def arrived(way, x, j):
        w = 0 if way > 0 else 1
        red(way, x, j, r_land.at[w, x, j], True).wait_recv()

    def rows_of(device):
        return dot(bm_ref[span(device, rows), :], w_ref[...], NT).astype(bf16)

    def first_rows(x):
        pair(x).wait_recv()

        @pl.when(x != chip)
        def _():
            r_out[x] = r_keep[x] + r_side[x]

        for way in (1, -1):

            @pl.when(past(way, x) & jnp.logical_not(comes(way, tree)))
            def _():
                red(way, x, tree, r_out.at[x]).start()

    def step_rows(i, _):
        x = at_step(i)
        r_give[x] = rows_of(2 * x + 1 - core)
        r_keep[x] = rows_of(2 * x + core)
        pair(x).start()

        @pl.when(i > 0)
        def _():
            first_rows(at_step(i - 1))

        return 0

    lax.fori_loop(0, chips, step_rows, 0)
    first_rows(at_step(chips - 1))

    def later_rows(i):
        x = at_step(i)
        for way in (1, -1):
            for j in range(trees):

                @pl.when(past(way, x) & comes(way, j))
                def _():
                    arrived(way, x, j)
                    passing = r_land.at[0 if way > 0 else 1, x, j]

                    @pl.when(tree == j)
                    def _():
                        add_rows(r_out.at[x], passing)
                        red(way, x, j, r_out.at[x]).start()

                    @pl.when(tree != j)
                    def _():
                        red(way, x, j, passing).start()

    columns, width = bm_ref.shape[1] // 3, mine.shape[2]
    load.wait()

    def step_weight(i, _):
        p, c = i // (wide // BLOCK), lax.rem(i, wide // BLOCK)
        product = dot(g_ref[:, span(c, BLOCK)], bm_ref[:, span(p, columns)], TN).astype(bf16)
        for j in range(trees):
            mine[j, span(i, BLOCK), :] = product[:, j * width : (j + 1) * width]
        return 0

    lax.fori_loop(0, 3 * (wide // BLOCK), step_weight, 0)
    for k in range(trees):
        hop(k, 0)
    for n in range(3):
        fulls[n][span(d, fulls[n].shape[0] // n_d), :] = totals[n][...]
    for i in range(max(chips, bits)):
        if i < chips:
            later_rows(i)
        if i < bits:
            for k in range(trees):
                land(k, i)
        if i == 0:
            spread(1, totals[1])

    def reduced():
        for w, way in enumerate((1, -1)):
            for j in range(trees):

                @pl.when(comes(way, j))
                def _():
                    arrived(way, chip, j)

                @pl.when(jnp.logical_not(comes(way, j)))
                def _():
                    r_land[w, chip, j] = jnp.zeros((rows, wide), bf16)

        vec_now[0:6] = vec_in[0:6]
        vec_now[6:8] = jnp.zeros((2, wide), f32)
        height = min(64, rows)
        for j in range(trees):

            def body(i, _):
                at = span(i, height)
                own = r_keep[chip, at, :].astype(f32) + r_side[chip, at, :].astype(f32)
                e = jnp.where(tree == j, own, 0.0)
                for w in range(2):
                    e = e + r_land[w, chip, j, at, :].astype(f32)
                norm, r = ln_parts(x_ref[j, at, :].astype(f32))
                vec_now[6:7] = vec_now[6:7] + jnp.sum(e * norm, axis=0, keepdims=True)
                vec_now[7:8] = vec_now[7:8] + jnp.sum(e, axis=0, keepdims=True)
                bt_ref[j, at, :] = (hid_ref[j, at, :] + ln_back(e, norm, r, par_ref[6:7])).astype(bf16)
                return 0

            lax.fori_loop(0, rows // height, body, 0)

    vec_partners = [(d, other)] + [(lax.bitwise_xor(d, 1 << b), t) for b in range(bits)]
    vec_copies = []

    def vec_step(i):
        if i > 0:
            vec_copies[i - 1].wait()
            vec_now[...] = vec_now[...] + vec_got[i - 1]
        if i < len(vec_partners):
            vec_got[len(vec_partners) + i] = vec_now[...]
            vec_copies.append(
                send(vec_got.at[len(vec_partners) + i], vec_got.at[i], s_vec.at[i], r_vec.at[i], vec_partners[i])
            )
        else:
            vec_far[chip] = vec_now[...]
            for k, c in enumerate(line):
                n = len(vec_partners) + k
                vec_copies.append(
                    send(vec_far.at[chip], vec_far.at[chip], s_vec.at[n], r_vec.at[n], (d, 2 * c + core))
                )

    def widen_all(n):
        full, out = fulls[n], outs[n]
        for j in range(n_d - 1):
            spread_of[n][j].wait_recv()
        height = 64
        while full.shape[0] % height:
            height //= 2

        def widen(i, _):
            out[span(i, height), :] = full[span(i, height), :].astype(f32)
            return 0

        lax.fori_loop(0, full.shape[0] // height, widen, 0)

    for j in range(trees):
        giver = j * group + t // trees

        @pl.when(giver != t)
        def _():
            pltpu.make_async_remote_copy(
                src_ref=far.at[j], dst_ref=far.at[j], send_sem=s_own.at[0], recv_sem=r_own.at[j],
                device_id=(d, giver), device_id_type=MESH,
            ).wait_recv()

    total = far[0].astype(f32)
    for j in range(1, trees):
        total = total + far[j].astype(f32)
    at = span(d, full_ig.shape[0] // n_d)
    full_ig[at, :] = total.astype(bf16)
    spread(3, full_ig.at[at, :])
    spread_of = [spreads[i * (n_d - 1) : (i + 1) * (n_d - 1)] for i in (0, 2, 1, 3)]

    reduced()
    for i in range(len(vec_partners) + 1):
        vec_step(i)
        if i < 3:
            widen_all(i)
    for n in range(len(vec_partners) + 1, 3):
        widen_all(n)
    widen_all(3)
    for k in range(chips - 1):
        vec_copies[len(vec_partners) + k].wait()
    total = vec_far[0]
    for c in range(1, chips):
        total = total + vec_far[c]
    vec_ref[...] = total

    for k in range(trees):

        @pl.when(owner(k) != t)
        def _():
            pltpu.make_async_remote_copy(
                src_ref=cut(k, d), dst_ref=cut(k, d), send_sem=s_own.at[k], recv_sem=r_own.at[0],
                device_id=(d, owner(k)), device_id_type=MESH,
            ).wait_send()

    for k in range(chips):
        pair(k).wait_send()
    for x in range(chips):
        for way in (1, -1):

            @pl.when(past(way, x))
            def _():
                red(way, x, tree, r_out.at[x]).wait_send()
                for j in range(trees):

                    @pl.when(comes(way, j) & (tree != j))
                    def _():
                        red(way, x, j, r_land.at[0 if way > 0 else 1, x, j]).wait_send()

    for copy in list(hops.values()) + spreads:
        copy.wait_send()


def finish(n_d, n_t, mixed, w, x, hidden, par, vec, up_t, down_t, out_t, gathered, width):
    trees, rows, wide = x.shape
    chips = n_t // 2
    bits = n_d.bit_length() - 1
    dma = pltpu.SemaphoreType.DMA
    sds = jax.ShapeDtypeStruct
    shapes = [(a.shape[0] * n_d, a.shape[1]) for a in (up_t, down_t, out_t)] + [(3 * wide, width)]
    vm = lambda lead, shape, kind=bf16: pltpu.VMEM(tuple(lead) + tuple(shape), kind)
    part = (shapes[3][0] // n_d, shapes[3][1])
    partners = 1 + bits
    return pl.pallas_call(
        functools.partial(finish_kernel, n_d, n_t),
        in_specs=[VMEM] * 9 + [HBM],
        out_specs=[VMEM] * 6,
        out_shape=[sds(x.shape, bf16), sds((8, wide), f32)] + [sds(s, f32) for s in shapes],
        scratch_shapes=[vm((), gathered.shape), vm((trees,), shapes[3]), vm((trees, n_d - 1), part), vm((trees,), part)]
        + [vm((), s) for s in shapes] + [
            vm((chips, rows), (wide,)), vm((chips, rows), (wide,)), vm((chips, rows), (wide,)),
            vm((chips, rows), (wide,)), vm((2, chips, trees, rows), (wide,)),
            vm((8,), (wide,), f32), vm((2 * partners, 8), (wide,), f32), vm((chips, 8), (wide,), f32),
            dma((1,)), dma((trees, n_d - 1)), dma((trees, n_d - 1)),
            dma((4, n_d - 1)), dma((4, n_d - 1)),
            dma((trees,)), dma((trees,)),
            dma((2, chips, trees)), dma((2, chips, trees)), dma((chips,)), dma((chips,)),
            dma((partners + chips - 1,)), dma((partners + chips - 1,)),
        ],
        compiler_params=pltpu.CompilerParams(
            collective_id=3, has_side_effects=True, vmem_limit_bytes=67043328
        ),
        name="finish",
    )(mixed, w, x, hidden, par, vec, up_t, down_t, out_t, gathered)


def shards(
    n_d, n_t,
    tokens, cotangent, lengths, parents, first_gain, first_shift, in_weight, out_weight,
    second_gain, second_shift, third_gain, third_shift, up_weight, down_weight, fourth_gain, fourth_shift,
):
    trees, rows, wide = tokens.shape
    group = n_t // trees
    d, t = lax.axis_index("dp"), lax.axis_index("tensor")
    tree = t // group
    width = out_weight.shape[0]

    mine = lambda a: lax.dynamic_index_in_dim(a, tree, 0, keepdims=False)
    cosine, sine, mq, mk = tables(mine(lengths), mine(parents), n_t * rows)

    par = jnp.stack(
        [second_gain, second_shift, third_gain, third_shift, fourth_gain, fourth_shift, first_gain, first_shift]
    )
    gathered, w, down_all = gather_tree(
        n_d, n_t, tokens, par, in_weight.transpose(1, 0, 2), down_weight
    )
    w = w.transpose(1, 2, 0, 3).reshape(3, wide, -1)
    q, k, v, kt, vt = project(gathered, w, cosine, sine, mq, mk)
    attended, qb, att, out_all, up_all = attend(n_d, n_t, trees, q, k, vt, out_weight, up_weight)
    flat = lambda a: a.reshape(trees * rows, a.shape[-1])
    output, back_hidden, back_att, up_g, down_g, out_g, vec = feed(
        flat(att), flat(tokens), flat(cotangent), out_all.reshape(-1, wide), par, up_all, down_all
    )
    back_mixed, up_t, down_t, out_t = attend_back(
        n_d, n_t, qb, k, v, kt, back_att.reshape(trees, rows, wide), attended, cosine, sine,
        up_g, down_g, out_g.reshape(n_t, width, wide),
    )
    w_flat = w.transpose(1, 0, 2).reshape(wide, -1)
    back_tokens, vec, up_sum, down_sum, out_sum, in_sum = finish(
        n_d, n_t, back_mixed, w_flat, tokens, back_hidden.reshape(tokens.shape), par, vec,
        up_t, down_t, out_t, gathered, width,
    )
    return (
        output.reshape(tokens.shape),
        back_tokens,
        vec[6], vec[7],
        in_sum.reshape(3, wide, width).transpose(1, 0, 2),
        out_sum,
        vec[0], vec[1], vec[2], vec[3],
        up_sum,
        down_sum,
        vec[4], vec[5],
    )


def solution(mesh):
    in_specs = (
        P("dp", "tensor", None), P("dp", "tensor", None), P("dp", None), P("dp", None),
        P(), P(), P(None, None, "tensor"), P("tensor", None), P(), P(), P(), P(),
        P(None, "tensor"), P("tensor", None), P(), P(),
    )
    out_specs = (
        P("dp", "tensor", None), P("dp", "tensor", None), P(), P(), P(None, None, "tensor"),
        P("tensor", None), P(), P(), P(), P(), P(None, "tensor"), P("tensor", None), P(), P(),
    )
    run = functools.partial(shards, mesh.shape["dp"], mesh.shape["tensor"])
    return jax.shard_map(run, mesh=mesh, in_specs=in_specs, out_specs=out_specs, check_vma=False)
```

```python
import functools
import jax
import jax.numpy as jnp
from jax import lax
from jax.experimental import pallas as pl
from jax.experimental.pallas import tpu as pltpu
from jax.sharding import PartitionSpec as P

HEAD_DIM = 64
LANES = 128
VROWS = 80
BLOCK = 256
TRUNK = 512
SEGMENTS = 13

rope_base = 10000.0
norm_eps = 1e-05
masked_score = -1e30
f32, bf16 = jnp.float32, jnp.bfloat16
NN = (((1,), (0,)), ((), ()))
NT = (((1,), (1,)), ((), ()))
TN = (((0,), (0,)), ((), ()))
MESH = pl.DeviceIdType.MESH
VMEM = pl.BlockSpec(memory_space=pltpu.VMEM)
HBM = pl.BlockSpec(memory_space=pltpu.HBM)


def dot(a, b, dims=NN):
    return lax.dot_general(a, b, dims, preferred_element_type=f32)


def lane_of(shape):
    return lax.broadcasted_iota(jnp.int32, shape, len(shape) - 1)


def row_of(shape):
    return lax.broadcasted_iota(jnp.int32, shape, len(shape) - 2)


def span(i, n):
    return pl.ds(pl.multiple_of(i * n, n), n)


def split3(v):
    hi = v.astype(bf16).astype(f32)
    mid = (v - hi).astype(bf16).astype(f32)
    return hi, mid, v - hi - mid


def layer_norm(values, gain, shift):
    average = jnp.mean(values, axis=-1, keepdims=True)
    centered = values - average
    spread = jnp.mean(centered * centered, axis=-1, keepdims=True)
    return centered * lax.rsqrt(spread + norm_eps) * gain + shift


def tree_layout(tree_lengths, tree_parents, rows):
    seg_sizes = jnp.concatenate([jnp.full((1,), TRUNK, jnp.int32), tree_lengths])
    ends = jnp.cumsum(seg_sizes)
    starts = ends - seg_sizes
    places = jnp.arange(rows, dtype=jnp.int32)
    labels = jnp.arange(SEGMENTS, dtype=jnp.int32)
    segment = jnp.sum((places[:, None] >= ends[None, :]).astype(jnp.int32), axis=1)
    own_hot = (segment[:, None] == labels[None, :]).astype(jnp.int32)
    parent = jnp.sum(own_hot * tree_parents[None, :], axis=1)
    parent_hot = (parent[:, None] == labels[None, :]).astype(jnp.int32)
    grandparent = jnp.sum(parent_hot * tree_parents[None, :], axis=1)
    parent_size = jnp.sum(parent_hot * seg_sizes[None, :], axis=1)
    depth_start = jnp.where(segment > 0, TRUNK, 0).astype(jnp.int32) + jnp.where(
        parent > 0, parent_size, 0
    )
    position = places - jnp.sum(own_hot * starts[None, :], axis=1) + depth_start
    return (segment, parent, grandparent, position)


def tables(tree_lengths, tree_parents, rows):
    segment, parent, grand, position = tree_layout(tree_lengths, tree_parents, rows)
    lane = jnp.arange(LANES, dtype=jnp.int32)
    half = HEAD_DIM // 2
    inverse = rope_base ** (-(lane % half).astype(f32) * 2.0 / HEAD_DIM)
    angle = position.astype(f32)[:, None] * inverse[None, :]
    cosine = jnp.cos(angle)
    sine = jnp.where((lane % HEAD_DIM) < half, -1.0, 1.0)[None, :] * jnp.sin(angle)
    label = (lane - HEAD_DIM)[None, :]
    own = segment[:, None] == label
    path = own | (parent[:, None] == label) | (grand[:, None] == label)
    hidden = (label >= 0) & (label < SEGMENTS) & ~path
    queries = jnp.where(hidden, masked_score, 0.0).astype(f32)
    ones = (label >= 16) & (label < 19)
    keys = jnp.where(own | ones, 1.0, 0.0).astype(f32)
    return cosine, sine, queries, keys
def barrier(partners):
    semaphore = pltpu.get_barrier_semaphore()
    for partner in partners:
        pl.semaphore_signal(semaphore, inc=1, device_id=partner, device_id_type=MESH)
    pl.semaphore_wait(semaphore, len(partners))


def send(source, target, send_sem, recv_sem, device):
    copy = pltpu.make_async_remote_copy(
        src_ref=source,
        dst_ref=target,
        send_sem=send_sem,
        recv_sem=recv_sem,
        device_id=device,
        device_id_type=MESH,
    )
    copy.start()
    return copy


def add_rows(target, source, step=64):
    rows = target.shape[0]
    step = min(step, rows)
    while rows % step:
        step //= 2

    def body(i, _):
        at = span(i, step)
        target[at, :] = target[at, :] + source[at, :]
        return 0

    lax.fori_loop(0, rows // step, body, 0)


def orders(n_d):
    bits = n_d.bit_length() - 1
    return [list(range(bits)), list(range(bits - 1, -1, -1))]


def combos(bits):
    masks = [0]
    for b in bits:
        masks = masks + [m ^ (1 << b) for m in masks]
    return masks


def halves(rows, width, tile=16):
    return (rows // 2, width) if rows % (2 * tile) == 0 else (rows, width // 2)


def half(part, stream, rows, width):
    height, wide = halves(rows, width)
    if height < rows:
        return span(2 * part + stream, height), slice(None)
    return span(part, rows), pl.ds(stream * wide, wide)


class Spread:
    def __init__(self, n_d, n_t, shards, alls, sems):
        self.n_d, self.n_t, self.shards, self.alls = n_d, n_t, shards, alls
        self.zs, self.zr, self.ps, self.pr, self.ys, self.yr, self.own = sems
        self.d, self.t = lax.axis_index("dp"), lax.axis_index("tensor")
        self.chips = n_t // 2
        self.chip, self.core = self.t // 2, lax.rem(self.t, 2)
        self.other = 2 * self.chip + 1 - self.core
        self.bits = n_d.bit_length() - 1
        self.arrays = range(len(shards))

    @staticmethod
    def sems(count, n_d, n_t):
        dma = pltpu.SemaphoreType.DMA
        hops, slots = n_t // 2 - 1, 2 * (n_d - 1)
        z, p, y = (count, 2 * hops), (count, 2 * hops, slots), (count, 2 * hops + 1)
        return [dma(z), dma(z), dma(p), dma(p), dma(y), dma(y), dma((count,))]

    def exists(self, c):
        return (c >= 0) & (c < self.chips)

    def rows(self, a):
        return self.shards[a].shape[0] // self.n_d

    def slot(self, way, h):
        return h - 1 + (self.chips - 1 if way < 0 else 0)

    def remote(self, src, dst, ssem, rsem, device):
        return pltpu.make_async_remote_copy(
            src_ref=src, dst_ref=dst, send_sem=ssem, recv_sem=rsem, device_id=device, device_id_type=MESH
        )

    def along(self, a, way, h, arriving):
        source = self.chip - way * (h if arriving else h - 1)
        at = span(self.d, self.rows(a))
        dst = self.alls[a].at[2 * source + self.core, at]
        src = self.shards[a].at[at] if h == 1 and not arriving else dst
        peer = self.chip - way if arriving else self.chip + way
        i = self.slot(way, h)
        return self.remote(src, dst, self.zs.at[a, i], self.zr.at[a, i], (self.d, 2 * peer + self.core))

    def across(self, a, way, h, step, arriving):
        source = self.chip - way * h
        out = []
        for stream, order in enumerate(orders(self.n_d)):
            partner = lax.bitwise_xor(self.d, 1 << order[step])
            for j, m in enumerate(combos(order[:step])):
                block = lax.bitwise_xor(partner if arriving else self.d, m)
                rows, cols = half(block, stream, self.rows(a), self.shards[a].shape[1])
                ref = self.alls[a].at[2 * source + self.core, rows, cols]
                i = stream * (self.n_d - 1) + (1 << step) - 1 + j
                k = self.slot(way, h)
                out.append(self.remote(ref, ref, self.ps.at[a, k, i], self.pr.at[a, k, i], (partner, self.t)))
        return out

    def beside(self, a, way, h, arriving=False):
        source = self.chip - way * h
        ref = self.alls[a].at[2 * source + (1 - self.core if arriving else self.core)]
        k = self.slot(way, h)
        return self.remote(ref, ref, self.ys.at[a, k], self.yr.at[a, k], (self.d, self.other))

    def mine(self, a, arriving=False):
        k = 2 * (self.chips - 1)
        dst = self.alls[a].at[self.other if arriving else self.t]
        return self.remote(self.shards[a], dst, self.ys.at[a, k], self.yr.at[a, k], (self.d, self.other))

    def keep(self, a):
        return pltpu.make_async_copy(self.shards[a], self.alls[a].at[self.t], self.own.at[a])

    def begin(self):
        for way in (1, -1):

            @pl.when(self.exists(self.chip + way))
            def _():
                for a in self.arrays:
                    self.along(a, way, 1, False).start()

        for a in self.arrays:
            self.keep(a).start()
            self.mine(a).start()

    def phase(self, p, h):
        for way in (1, -1):

            @pl.when(self.exists(self.chip - way * h))
            def _():
                for a in self.arrays:
                    if p == 0:
                        self.along(a, way, h, True).wait_recv()
                        if h < self.chips - 1:

                            @pl.when(self.exists(self.chip + way))
                            def _():
                                self.along(a, way, h + 1, False).start()
                    else:
                        for copy in self.across(a, way, h, p - 1, True):
                            copy.wait_recv()
                    if p < self.bits:
                        for copy in self.across(a, way, h, p, False):
                            copy.start()
                    else:
                        self.beside(a, way, h).start()

    def groups(self):
        return self.chips - 1 + self.bits

    def group(self, g):
        for h in range(1, self.chips):
            if 0 <= g - (h - 1) <= self.bits:
                self.phase(g - (h - 1), h)

    def end(self):
        for h in range(1, self.chips):
            for way in (1, -1):

                @pl.when(self.exists(self.chip + way) & self.exists(self.chip - way * (h - 1)))
                def _():
                    for a in self.arrays:
                        self.along(a, way, h, False).wait_send()

                @pl.when(self.exists(self.chip - way * h))
                def _():
                    for a in self.arrays:
                        for step in range(self.bits):
                            for copy in self.across(a, way, h, step, False):
                                copy.wait_send()
                        self.beside(a, way, h).wait_send()
                        self.beside(a, way, h, True).wait_recv()

        for a in self.arrays:
            self.keep(a).wait()
            self.mine(a).wait_send()
            self.mine(a, True).wait_recv()


def gather_kernel(
    n_d, n_t, v_ref, gain_ref, w_ref, f_ref, o_ref, u_ref, all_ref,
    x_ref, passing, rs, ss, rb, sb, rw, sw, rp, sp, *sems,
):
    d, t = lax.axis_index("dp"), lax.axis_index("tensor")
    trees, rows, _ = x_ref.shape
    chips = n_t // 2
    group = n_t // trees
    chip, core = t // 2, lax.rem(t, 2)
    other = 2 * chip + 1 - core
    near = group // 2
    tree = t // group
    planes = [lax.rem(d + k, n_d) for k in range(1, n_d)]
    owners = [(j * group + t // trees) for j in range(trees)]
    givers = [lax.rem(t, group) * trees + i for i in range(trees)]
    barrier([(d, lax.rem(t + k, n_t)) for k in range(1, n_t)] + [(p, t) for p in planes])
    part = w_ref.shape[1] // n_d
    weights = Spread(n_d, n_t, [f_ref], [all_ref], sems)
    exists = weights.exists

    copies = []
    mine = w_ref.at[:, span(d, part), :]
    for j in range(trees):
        slot = u_ref.at[lax.rem(t, trees), :, span(d, part), :]

        @pl.when(owners[j] != t)
        def _():
            send(mine, slot, sw.at[j], rw.at[lax.rem(t, trees)], (d, owners[j]))

        @pl.when(owners[j] == t)
        def _():
            u_ref[lax.rem(t, trees), :, span(d, part), :] = w_ref[:, span(d, part), :]

    weights.begin()

    def block(c):
        return o_ref.at[span(2 * c + core, rows)]

    def beyond(c, way, j):
        return (j * near + near - 1 >= c) if way > 0 else (j * near <= c)

    def hop(way, h, j, here):
        source = chip - way * (h - 1)
        if h == 1:
            src = x_ref.at[j]
        else:
            src = block(source) if here else passing.at[j, source]
        return src, source

    def pass_on(way, h):
        for j in range(trees):

            @pl.when(exists(chip - way * (h - 1)) & exists(chip + way) & beyond(chip + way, way, j))
            def _():
                i = weights.slot(way, h)
                to = chip + way
                for here in (True, False) if h > 1 else (True,):
                    src, source = hop(way, h, j, here)
                    for there in (True, False):
                        at_home = (tree == j) if here else (tree != j)
                        lands = (to // near == j) if there else (to // near != j)

                        @pl.when((at_home & lands) if h > 1 else lands)
                        def _():
                            dst = block(source) if there else passing.at[j, source]
                            send(src, dst, ss.at[j, i], rs.at[j, i], (d, 2 * to + core))

    def row_copy(j, i):
        return weights.remote(x_ref.at[j], passing.at[j, 0], ss.at[j, i], rs.at[j, i], (d, other))

    def share(way, h):
        source = chip - way * h
        i = weights.slot(way, h)
        return weights.remote(block(source), block(source), sb.at[i], rb.at[i], (d, other))

    def arrive(way, h):
        for j in range(trees):

            @pl.when(exists(chip - way * h) & beyond(chip, way, j))
            def _():
                row_copy(j, weights.slot(way, h)).wait_recv()

        if h < chips - 1:
            pass_on(way, h + 1)

        @pl.when(exists(chip - way * h))
        def _():
            share(way, h).start()

    height = min(64, rows)

    def norm_rows(i, _):
        at = span(i, height)
        for j in range(trees):
            v = v_ref[j, at, :].astype(f32)
            x_ref[j, at, :] = layer_norm(v, gain_ref[6:7], gain_ref[7:8]).astype(bf16)
        return 0

    lax.fori_loop(0, rows // height, norm_rows, 0)
    o_ref[span(t, rows), :] = x_ref[tree]
    for way in (1, -1):
        pass_on(way, 1)
    last = 2 * (chips - 1)
    copies.append(send(x_ref.at[tree], block(chip), sb.at[last], rb.at[last], (d, other)))
    weights.group(0)
    for i in range(trees):
        slot = u_ref.at[i, :, span(d, part), :]

        @pl.when(givers[i] != t)
        def _():
            pltpu.make_async_remote_copy(
                src_ref=mine, dst_ref=slot, send_sem=sw.at[0], recv_sem=rw.at[i],
                device_id=(d, givers[i]), device_id_type=MESH,
            ).wait_recv()

    mine_all = u_ref.at[:, :, span(d, part), :]
    for k, p in enumerate(planes):
        copies.append(send(mine_all, mine_all, sp.at[k], rp.at[k], (p, t)))
    for h in range(1, chips):
        for way in (1, -1):
            arrive(way, h)
        weights.group(h)
    for g in range(chips, weights.groups()):
        weights.group(g)
    weights.end()
    for j in range(trees):

        @pl.when(owners[j] != t)
        def _():
            pltpu.make_async_remote_copy(
                src_ref=mine, dst_ref=mine, send_sem=sw.at[j], recv_sem=rw.at[0],
                device_id=(d, owners[j]), device_id_type=MESH,
            ).wait_send()

    for way in (1, -1):
        for h in range(1, chips):
            for j in range(trees):

                @pl.when(exists(chip - way * (h - 1)) & exists(chip + way) & beyond(chip + way, way, j))
                def _():
                    row_copy(j, weights.slot(way, h)).wait_send()

            @pl.when(exists(chip - way * h))
            def _():
                share(way, h).wait()

    for copy in copies:
        copy.wait()


def gather_tree(n_d, n_t, tokens, par, weight, down):
    trees, rows, wide = tokens.shape
    chips = n_t // 2
    hops = 2 * (chips - 1)
    dma = pltpu.SemaphoreType.DMA
    return pl.pallas_call(
        functools.partial(gather_kernel, n_d, n_t),
        in_specs=[VMEM] * 4,
        out_specs=[VMEM] * 2 + [HBM],
        out_shape=[
            jax.ShapeDtypeStruct((n_t * rows, wide), bf16),
            jax.ShapeDtypeStruct((trees,) + weight.shape, bf16),
            jax.ShapeDtypeStruct((n_t,) + down.shape, bf16),
        ],
        scratch_shapes=[
            pltpu.VMEM((trees, rows, wide), bf16), pltpu.VMEM((trees, chips, rows, wide), bf16),
            dma((trees, hops)), dma((trees, hops)), dma((hops + 1,)), dma((hops + 1,)),
            dma((trees,)), dma((trees,)), dma((n_d - 1,)), dma((n_d - 1,)),
        ] + Spread.sems(1, n_d, n_t),
        compiler_params=pltpu.CompilerParams(collective_id=0, has_side_effects=True),
        name="gather_tree",
    )(tokens, par, weight, down)


def qkv_kernel(x_ref, w_ref, cos_ref, sin_ref, mq_ref, mk_ref, q_ref, k_ref, v_ref, kt_ref, vt_ref):
    x = x_ref[...]
    heads = q_ref.shape[0]
    cosine, sine = cos_ref[...], sin_ref[...]
    mq, mk = mq_ref[...], mk_ref[...]
    lane = lane_of(cosine.shape)
    low = lax.rem(lane, HEAD_DIM) < HEAD_DIM // 2
    first = lane < HEAD_DIM
    mv = jnp.where((lane >= HEAD_DIM) & (lane < HEAD_DIM + 3), 1.0, 0.0)
    tail = jnp.where(row_of((VROWS - HEAD_DIM, x.shape[0])) == 0, 1.0, 0.0).astype(bf16)

    def both(slab):
        return slab, pltpu.roll(slab, HEAD_DIM, 1)

    def rotate(slab):
        partner = jnp.where(
            low, pltpu.roll(slab, LANES - HEAD_DIM // 2, 1), pltpu.roll(slab, HEAD_DIM // 2, 1)
        )
        return slab * cosine + partner * sine

    q_all, k_all, v_all = (dot(x, w_ref[i]) for i in range(3))
    for h in range(0, heads, 2):
        cols = slice(h * HEAD_DIM, (h + 2) * HEAD_DIM)
        for g, slab in enumerate(both(rotate(q_all[:, cols]) * HEAD_DIM**-0.5)):
            q_ref[h + g] = jnp.where(first, slab, mq).astype(bf16)
        keys = rotate(k_all[:, cols])
        for g, slab in enumerate(both(keys)):
            k_ref[h + g] = jnp.where(first, slab, mk).astype(bf16)
        flat = keys.T.astype(bf16)
        for g, slab in enumerate(both(v_all[:, cols])):
            v_ref[h + g] = jnp.where(first, slab, mv).astype(bf16)
        flat_v = v_all[:, cols].T.astype(bf16)
        for g in range(2):
            part = slice(g * HEAD_DIM, (g + 1) * HEAD_DIM)
            kt_ref[h + g] = flat[part]
            vt_ref[h + g, :HEAD_DIM] = flat_v[part]
            vt_ref[h + g, HEAD_DIM:] = tail


def project(x, w, cosine, sine, mq, mk):
    rows, wide = x.shape
    heads = w.shape[2] // HEAD_DIM
    table = pl.BlockSpec((BLOCK, LANES), lambda i: (i, 0))
    slab = pl.BlockSpec((heads, BLOCK, LANES), lambda i: (0, i, 0))
    shape = jax.ShapeDtypeStruct((heads, rows, LANES), bf16)
    return pl.pallas_call(
        qkv_kernel,
        grid=(rows // BLOCK,),
        in_specs=[
            pl.BlockSpec((BLOCK, wide), lambda i: (i, 0)),
            pl.BlockSpec(w.shape, lambda i: (0, 0, 0)),
            table, table, table, table,
        ],
        out_specs=[
            slab, slab, slab,
            pl.BlockSpec((heads, HEAD_DIM, BLOCK), lambda i: (0, 0, i)),
            pl.BlockSpec((heads, VROWS, BLOCK), lambda i: (0, 0, i)),
        ],
        out_shape=[
            shape, shape, shape,
            jax.ShapeDtypeStruct((heads, HEAD_DIM, rows), bf16),
            jax.ShapeDtypeStruct((heads, VROWS, rows), bf16),
        ],
        name="project",
    )(x, w, cosine, sine, mq, mk)


def fwd_kernel(
    n_d, n_t, trees, q_ref, k_ref, vt_ref, ow_ref, up_ref, o_ref, qb_ref, att_ref, ow_all, up_all,
    ss, rs, here, *sems,
):
    turn = pl.program_id(0)
    steps = pl.num_programs(0)
    heads = q_ref.shape[0]
    row, col = row_of((BLOCK, BLOCK)), lane_of((BLOCK, BLOCK))
    d, t = lax.axis_index("dp"), lax.axis_index("tensor")
    group = n_t // trees
    rows, width = att_ref.shape[1], o_ref.shape[1]
    per = BLOCK // rows
    qi = jnp.where(turn == steps - 1, t // per, jnp.where(turn >= t // per, turn + 1, turn))
    at = span(qi, BLOCK)
    weights = Spread(n_d, n_t, [up_ref, ow_ref], [up_all, ow_all], sems)
    first_group = max(0, k_ref.shape[1] // BLOCK - 4)
    place = att_ref.at[t // group, :, span(lax.rem(t, group), width)]

    def outgoing(i, r, k):
        return pltpu.make_async_remote_copy(
            src_ref=o_ref.at[span(i * per + r, rows)], dst_ref=place, send_sem=ss.at[k], recv_sem=rs.at[k],
            device_id=(d, lax.rem(t + k, n_t)), device_id_type=MESH,
        )

    @pl.when(turn == 0)
    def _():
        barrier(
            [(d, lax.rem(t + k, n_t)) for k in range(1, n_t)] + [(lax.rem(d + k, n_d), t) for k in range(1, n_d)]
        )
        weights.begin()

    for g in range(weights.groups()):
        if first_group + g < k_ref.shape[1] // BLOCK:

            @pl.when(turn == first_group + g)
            def _():
                weights.group(g)

    qs = [q_ref[h, at, :] for h in range(heads)]

    def scores(h, j):
        return dot(k_ref[h, span(j, BLOCK), :], qs[h], NT)

    state = []
    for h in range(heads):
        s = jnp.where(row <= col, scores(h, qi), masked_score)
        m = jnp.max(s, axis=0, keepdims=True)
        p = jnp.exp(s - m)
        state.append((m, dot(vt_ref[h, :, span(qi, BLOCK)], p.astype(bf16))))

    def step(j, carry):
        out = []
        for h in range(heads):
            m, acc = carry[h]
            s = scores(h, j)
            top = jnp.maximum(m, jnp.max(s, axis=0, keepdims=True))
            p = jnp.exp(s - top)
            acc = acc * jnp.exp(m - top) + dot(vt_ref[h, :, span(j, BLOCK)], p.astype(bf16))
            out.append((top, acc))
        return tuple(out)

    state = lax.fori_loop(0, qi, step, tuple(state))
    r = row_of((LANES, BLOCK))
    for h in range(0, heads, 2):
        outs = []
        for g in (h, h + 1):
            m, acc = state[g]
            total = acc[HEAD_DIM : HEAD_DIM + 1]
            outs.append(acc[:HEAD_DIM] / total)
            a, b, c = split3(-(m + jnp.log(total)))
            extra = jnp.where(r == 80, a, jnp.where(r == 81, b, jnp.where(r == 82, c, 0.0))).T
            qb_ref[g, at, :] = qs[g] + extra.astype(bf16)
        o_ref[at, h * HEAD_DIM : (h + 2) * HEAD_DIM] = jnp.concatenate(outs, axis=0).T.astype(bf16)

    def local(r):
        return pltpu.make_async_copy(o_ref.at[span(t // per * per + r, rows)], place, here.at[0])

    for r in range(per):
        k = lax.rem(qi * per + r + n_t - t, n_t)

        @pl.when(k != 0)
        def _():
            outgoing(qi, r, k).start()

        @pl.when(k == 0)
        def _():
            local(r).start()

    @pl.when(turn == steps - 1)
    def _():
        for g in range(k_ref.shape[1] // BLOCK - first_group, weights.groups()):
            weights.group(g)
        for k in range(1, n_t):
            outgoing(0, 0, k).wait()
        local(0).wait()
        weights.end()


def attend(n_d, n_t, trees, q, k, vt, ow, up):
    heads, rows, _ = q.shape
    wide = heads * HEAD_DIM
    dma = pltpu.SemaphoreType.DMA
    sds = jax.ShapeDtypeStruct
    return pl.pallas_call(
        functools.partial(fwd_kernel, n_d, n_t, trees),
        grid=(rows // BLOCK,),
        in_specs=[VMEM] * 5,
        out_specs=[VMEM, VMEM, HBM, HBM, HBM],
        out_shape=[
            sds((rows, wide), bf16),
            sds(q.shape, bf16),
            sds((trees, rows // n_t, wide * n_t // trees), bf16),
            sds((n_t,) + ow.shape, bf16),
            sds((n_t,) + up.shape, bf16),
        ],
        scratch_shapes=[
            dma((n_t,)), dma((n_t,)), dma((1,)),
        ] + Spread.sems(2, n_d, n_t),
        compiler_params=pltpu.CompilerParams(collective_id=1, has_side_effects=True),
        name="attend",
    )(q, k, vt, ow, up)


class Reduce:
    def __init__(self, n_d, n_t, sources, totals, scratch):
        self.n_d, self.n_t, self.sources, self.totals = n_d, n_t, sources, totals
        count = len(sources)
        self.mine, self.side, self.land_at, self.far = (
            scratch[i * count : (i + 1) * count] for i in range(4)
        )
        self.s_load, self.s_side, self.r_side, self.s_hop, self.r_hop, self.s_far, self.r_far = scratch[4 * count :]
        self.d, self.t = lax.axis_index("dp"), lax.axis_index("tensor")
        self.chips = n_t // 2
        self.chip, self.core = self.t // 2, lax.rem(self.t, 2)
        self.other = 2 * self.chip + 1 - self.core
        self.dest = [lax.rem(self.chip + k, self.chips) for k in range(1, self.chips)] + [self.chip]
        self.bits = n_d.bit_length() - 1
        self.units = [(n, k) for k in range(self.chips) for n in range(count)]

    @staticmethod
    def scratch(n_d, n_t, shapes):
        dma = pltpu.SemaphoreType.DMA
        chips, slots, count = n_t // 2, 2 * (n_d - 1), len(shapes)
        vm = lambda lead, r, c: pltpu.VMEM(lead + (r, c), bf16)
        units = count * chips
        return (
            [vm((chips,), r, c) for r, c in shapes] * 2
            + [vm((chips, slots), *halves(r // n_d, c)) for r, c in shapes]
            + [vm((chips - 1,), r // n_d, c) for r, c in shapes]
            + [dma((units,)), dma((units,)), dma((units,)), dma((units, slots)), dma((units, slots))]
            + [dma((units,)), dma((units,))]
        )

    def remote(self, src, dst, ssem, rsem, device):
        return pltpu.make_async_remote_copy(
            src_ref=src, dst_ref=dst, send_sem=ssem, recv_sem=rsem, device_id=device, device_id_type=MESH
        )

    def load(self, u):
        n, k = self.units[u]
        source = self.sources[n].at[2 * self.dest[k] + self.core]
        return pltpu.make_async_copy(source, self.mine[n].at[k], self.s_load.at[u])

    def beside(self, u):
        n, k = self.units[u]
        source = self.sources[n].at[2 * self.dest[k] + 1 - self.core]
        return self.remote(source, self.side[n].at[k], self.s_side.at[u], self.r_side.at[u], (self.d, self.other))

    def cut(self, u, part, stream):
        n, k = self.units[u]
        _, height, width = self.mine[n].shape
        rows, cols = half(part, stream, height // self.n_d, width)
        return self.mine[n].at[k, rows, cols]

    def hops(self, u, step):
        n, k = self.units[u]
        slot = 0 if step == 0 else self.n_d - (self.n_d >> step)
        out = []
        for stream, order in enumerate(orders(self.n_d)):
            partner = lax.bitwise_xor(self.d, 1 << order[step])
            for j, m in enumerate(combos(order[step + 1 :])):
                i = (slot + j) * 2 + stream
                landing = self.land_at[n].at[k, i]
                copy = self.remote(
                    self.cut(u, lax.bitwise_xor(partner, m), stream), landing,
                    self.s_hop.at[u, i], self.r_hop.at[u, i], (partner, self.t),
                )
                out.append((copy, self.cut(u, lax.bitwise_xor(self.d, m), stream), landing))
        return out

    def piece(self, u):
        n, k = self.units[u]
        return self.mine[n].at[k, span(self.d, self.mine[n].shape[1] // self.n_d), :]

    def away(self, u):
        n, k = self.units[u]
        return self.remote(
            self.piece(u), self.far[n].at[k], self.s_far.at[u], self.r_far.at[u],
            (self.d, 2 * self.dest[k] + self.core),
        )

    def begin(self):
        for u in range(len(self.units)):
            self.load(u).start()
            self.beside(u).start()

    def events(self):
        return len(self.units) + self.bits

    def event(self, e):
        if e < len(self.units):
            n, k = self.units[e]
            self.load(e).wait()
            self.beside(e).wait_recv()
            add_rows(self.mine[n].at[k], self.side[n].at[k])
            for copy, _, _ in self.hops(e, 0):
                copy.start()
        for step in range(self.bits):
            u = e - 1 - step
            if 0 <= u < len(self.units):
                for copy, target, landing in self.hops(u, step):
                    copy.wait_recv()
                    add_rows(target, landing)
                if step + 1 < self.bits:
                    for copy, _, _ in self.hops(u, step + 1):
                        copy.start()
                elif self.units[u][1] < self.chips - 1:
                    self.away(u).start()

    def end(self):
        for u, (n, k) in enumerate(self.units):
            if k < self.chips - 1:
                self.away(u).wait_recv()
            else:
                total = self.piece(u)[...].astype(f32)
                for i in range(self.chips - 1):
                    total = total + self.far[n][i].astype(f32)
                self.totals[n][...] = total.astype(bf16)
        for u, (n, k) in enumerate(self.units):
            self.beside(u).wait_send()
            for step in range(self.bits):
                for copy, _, _ in self.hops(u, step):
                    copy.wait_send()
            if k < self.chips - 1:
                self.away(u).wait_send()


def bwd_kernel(
    n_d, n_t, q_ref, k_ref, v_ref, kt_ref, x_ref, o_ref, cos_ref, sin_ref, up_ref, down_ref, og_ref,
    m_ref, up_tot, down_tot, og_tot, sums, wide, d_ref, hs, hr, *scratch,
):
    j = pl.program_id(0)
    heads, rows, _ = q_ref.shape
    nq = rows // BLOCK
    row, col = row_of((BLOCK, BLOCK)), lane_of((BLOCK, BLOCK))
    lane = lane_of((BLOCK, LANES))
    first = lane < HEAD_DIM
    d, t = lax.axis_index("dp"), lax.axis_index("tensor")
    trees, part, _ = x_ref.shape
    group, width = n_t // trees, heads * HEAD_DIM
    gradients = Reduce(n_d, n_t, [up_ref, down_ref, og_ref], [up_tot, down_tot, og_tot], scratch)
    ahead = 5
    points = 10

    def point(p):
        left = gradients.events() - ahead
        for e in range(ahead + p * left // points, ahead + (p + 1) * left // points):
            gradients.event(e)

    def cut(o):
        return x_ref.at[o // group, :, span(lax.rem(o, group), width)]

    def outgoing(k):
        o = lax.rem(t + k, n_t)
        return gradients.remote(cut(o), d_ref.at[span(t, part), :], hs.at[k], hr.at[k], (d, o))

    @pl.when(j == 0)
    def _():
        barrier(
            [(d, lax.rem(t + k, n_t)) for k in range(1, n_t)] + [(lax.rem(d + k, n_d), t) for k in range(1, n_d)]
        )
        for k in range(1, n_t):
            outgoing(k).start()
        gradients.begin()
        d_ref[span(t, part), :] = cut(t)[...]
        sums[...] = jnp.zeros_like(sums)
        for e in range(ahead):
            gradients.event(e)
        for k in range(1, n_t):
            outgoing(k).wait()

        def widen(i, _):
            at = span(i, BLOCK)
            for h in range(0, heads, 2):
                cols = slice(h * HEAD_DIM, (h + 2) * HEAD_DIM)
                slab = d_ref[at, cols].astype(f32)
                prod = slab * o_ref[at, cols].astype(f32)
                for g, (s, mine) in enumerate(((slab, first), (pltpu.roll(slab, HEAD_DIM, 1), ~first))):
                    inner = -jnp.sum(jnp.where(mine, prod, 0.0), axis=1, keepdims=True)
                    a, b, c = split3(inner)
                    n = HEAD_DIM
                    tail = jnp.where(lane == n, a, jnp.where(lane == n + 1, b, jnp.where(lane == n + 2, c, 0.0)))
                    wide[h + g, at, :] = jnp.where(first, s, tail).astype(bf16)
            return 0

        lax.fori_loop(0, nq, widen, 0)

    for p in range(0, points, 2):
        if p // 2 < nq:

            @pl.when(j == p // 2)
            def _():
                point(p)

    ks = [k_ref[h] for h in range(heads)]
    vs = [v_ref[h] for h in range(heads)]
    kts = [kt_ref[h] for h in range(heads)]

    def pair(h, i, mask):
        at = span(i, BLOCK)
        q = q_ref[h, at, :]
        d = wide[h, at, :]
        s = dot(ks[h], q, NT)
        if mask:
            s = jnp.where(row <= col, s, masked_score)
        p = jnp.exp(s)
        back = (p * dot(vs[h], d, NT)).astype(bf16)
        sums[h, :, at] += dot(kts[h], back)
        return dot(back, q), dot(p.astype(bf16), d)

    def step(i, carry):
        out = []
        for h in range(heads):
            dk, dv = pair(h, i, False)
            out.append((carry[h][0] + dk, carry[h][1] + dv))
        return tuple(out)

    state = tuple(pair(h, j, True) for h in range(heads))
    middle = (j + 1 + nq) // 2
    state = lax.fori_loop(j + 1, middle, step, state)
    for p in range(1, points, 2):
        if p // 2 < nq:

            @pl.when(j == p // 2)
            def _():
                point(p)

    state = lax.fori_loop(middle, nq, step, state)

    def join(a, b):
        return jnp.where(first, a, pltpu.roll(b, HEAD_DIM, 1))

    cosine, sine = cos_ref[...], sin_ref[...]
    low = lax.rem(lane, HEAD_DIM) < HEAD_DIM // 2

    def unrotate(slab):
        partner = jnp.where(
            low, pltpu.roll(slab, LANES - HEAD_DIM // 2, 1), pltpu.roll(slab, HEAD_DIM // 2, 1)
        )
        return slab * cosine - partner * sine

    at = span(j, BLOCK)
    total = heads * HEAD_DIM
    for h in range(0, heads, 2):
        dq = jnp.concatenate([sums[h, :, at], sums[h + 1, :, at]], axis=0).T * HEAD_DIM**-0.5
        dk = join(state[h][0], state[h + 1][0])
        dv = join(state[h][1], state[h + 1][1])
        for n, part in enumerate((unrotate(dq), unrotate(dk), dv)):
            begin = n * total + h * HEAD_DIM
            m_ref[:, begin : begin + 2 * HEAD_DIM] = part.astype(bf16)

    @pl.when(j == nq - 1)
    def _():
        for p in range(2 * nq, points):
            point(p)
        gradients.end()


def attend_back(n_d, n_t, q, k, v, kt, x, o, cosine, sine, up_g, down_g, out_g):
    heads, rows, _ = q.shape
    whole = lambda a: pl.BlockSpec(a.shape, lambda j: (0,) * a.ndim, pipeline_mode=pl.Buffered(1))
    block = pl.BlockSpec((heads, BLOCK, LANES), lambda j: (0, j, 0))
    table = pl.BlockSpec((BLOCK, LANES), lambda j: (j, 0))
    wide = heads * HEAD_DIM
    dma = pltpu.SemaphoreType.DMA
    sds = jax.ShapeDtypeStruct
    shapes = [a.shape[1:] for a in (up_g, down_g, out_g)]
    return pl.pallas_call(
        functools.partial(bwd_kernel, n_d, n_t),
        grid=(rows // BLOCK,),
        in_specs=[
            whole(q), block, block,
            pl.BlockSpec((heads, HEAD_DIM, BLOCK), lambda j: (0, 0, j)),
            VMEM, whole(o), table, table, HBM, HBM, HBM,
        ],
        out_specs=[pl.BlockSpec((BLOCK, 3 * wide), lambda j: (j, 0)), VMEM, VMEM, VMEM],
        out_shape=[sds((rows, 3 * wide), bf16)] + [sds((r // n_d, c), bf16) for r, c in shapes],
        scratch_shapes=[
            pltpu.VMEM((heads, HEAD_DIM, rows), f32),
            pltpu.VMEM((heads, rows, LANES), bf16),
            pltpu.VMEM((rows, wide), bf16),
            dma((n_t,)), dma((n_t,)),
        ] + Reduce.scratch(n_d, n_t, shapes),
        compiler_params=pltpu.CompilerParams(
            collective_id=2, has_side_effects=True, vmem_limit_bytes=67043328
        ),
        name="attend_back",
    )(q, k, v, kt, x, o, cosine, sine, up_g, down_g, out_g)


def ln_parts(v):
    centered = v - jnp.mean(v, axis=-1, keepdims=True)
    r = lax.rsqrt(jnp.mean(centered * centered, axis=-1, keepdims=True) + norm_eps)
    return centered * r, r


def ln_back(e, n, r, gain):
    f = e * gain
    return r * (f - jnp.mean(f, axis=-1, keepdims=True) - n * jnp.mean(f * n, axis=-1, keepdims=True))


def feed_kernel(
    att_ref, x_ref, cot_ref, ow_ref, par_ref, up_ref, down_ref,
    out_ref, hid_ref, ba_ref, upg_ref, downg_ref, outg_ref, vec_ref,
    hidden, branch, acc, feed_in, back_feed, active, slope,
):
    phase, n = pl.program_id(0), pl.program_id(1)
    last = pl.num_programs(1) - 1
    par = lambda i: par_ref[i : i + 1]
    total = lambda v: jnp.sum(v, axis=0, keepdims=True)

    @pl.when((phase == 0) & (n == 0))
    def _():
        b = dot(att_ref[...], ow_ref[...])
        branch[...] = b
        h = x_ref[...].astype(f32) + ln_parts(b)[0] * par(0) + par(1)
        hidden[...] = h
        feed_in[...] = (ln_parts(h)[0] * par(2) + par(3)).astype(bf16)
        acc[...] = jnp.zeros_like(acc)

    up, down = up_ref[0], down_ref[0]

    @pl.when(phase == 0)
    def _():
        u = dot(feed_in[...], up)
        t = jnp.tanh(0.7978845608028654 * (u + 0.044715 * u * u * u))
        half = 0.5 * (1.0 + t)
        a = (u * half).astype(bf16)
        active[n] = a
        slope[n] = half + 0.5 * u * (1.0 - t * t) * (
            0.7978845608028654 * (1.0 + 3 * 0.044715 * u * u)
        )
        acc[...] += dot(a, down)

    @pl.when((phase == 1) & (n == 0))
    def _():
        e = cot_ref[...].astype(f32)
        norm, r = ln_parts(acc[...])
        out_ref[...] = (hidden[...] + norm * par(4) + par(5)).astype(bf16)
        vec_ref[4:5] = total(e * norm)
        vec_ref[5:6] = total(e)
        back_feed[...] = ln_back(e, norm, r, par(4)).astype(bf16)
        acc[...] = jnp.zeros_like(acc)

    @pl.when(phase == 1)
    def _():
        b = back_feed[...]
        upper = (dot(b, down, NT) * slope[n]).astype(bf16)
        acc[...] += dot(upper, up, NT)
        downg_ref[0] = dot(active[n], b, TN).astype(bf16)
        upg_ref[0] = dot(feed_in[...], upper, TN).astype(bf16)

    @pl.when((phase == 1) & (n == last))
    def _():
        e = acc[...]
        norm, r = ln_parts(hidden[...])
        vec_ref[2:3] = total(e * norm)
        vec_ref[3:4] = total(e)
        h = cot_ref[...].astype(f32) + ln_back(e, norm, r, par(2))
        hid_ref[...] = h
        norm, r = ln_parts(branch[...])
        vec_ref[0:1] = total(h * norm)
        vec_ref[1:2] = total(h)
        b = ln_back(h, norm, r, par(0)).astype(bf16)
        ba_ref[...] = dot(b, ow_ref[...], NT).astype(bf16)
        outg_ref[...] = dot(att_ref[...], b, TN).astype(bf16)


def feed(att, x, cot, ow, par, up, down):
    rows, wide = att.shape
    n_t, _, width = up.shape
    one = lambda a: pl.BlockSpec(a.shape, lambda p, n: (0,) * len(a.shape), pipeline_mode=pl.Buffered(1))
    sds = jax.ShapeDtypeStruct
    outs = [
        sds((rows, wide), bf16), sds((rows, wide), f32), sds((rows, wide), bf16),
        sds((n_t, wide, width), bf16), sds((n_t, width, wide), bf16), sds((wide, wide), bf16),
        sds((8, wide), f32),
    ]
    chunk = lambda a: pl.BlockSpec((1,) + a.shape[1:], lambda p, n: (p * n, 0, 0))
    weight = lambda a: pl.BlockSpec((1,) + a.shape[1:], lambda p, n: (n, 0, 0))
    return pl.pallas_call(
        feed_kernel,
        grid=(2, n_t),
        in_specs=[one(a) for a in (att, x, cot, ow, par)] + [weight(up), weight(down)],
        out_specs=[one(o) for o in outs[:3]] + [chunk(outs[3]), chunk(outs[4])] + [one(o) for o in outs[5:]],
        out_shape=outs,
        scratch_shapes=[
            pltpu.VMEM((rows, wide), f32), pltpu.VMEM((rows, wide), f32), pltpu.VMEM((rows, wide), f32),
            pltpu.VMEM((rows, wide), bf16), pltpu.VMEM((rows, wide), bf16),
            pltpu.VMEM((n_t, rows, width), bf16), pltpu.VMEM((n_t, rows, width), f32),
        ],
        compiler_params=pltpu.CompilerParams(vmem_limit_bytes=64 << 20),
        name="feed",
    )(att, x, cot, ow, par, up, down)
def finish_kernel(
    n_d, n_t, bm_ref, w_ref, x_ref, hid_ref, par_ref, vec_in, up_tot, down_tot, og_tot, g_hbm,
    bt_ref, vec_ref, full_up, full_down, full_og, full_ig,
    g_ref, mine, landed, far,
    r_give, r_keep, r_side, r_out, r_land, vec_now, vec_got, vec_far,
    s_load, s_hop, r_hop, s_all, r_all, s_own, r_own,
    s_red, r_red, s_redside, r_redside, s_vec, r_vec,
):
    d, t = lax.axis_index("dp"), lax.axis_index("tensor")
    trees, rows, wide = x_ref.shape
    chips = n_t // 2
    near = chips // trees
    group = n_t // trees
    chip, core = t // 2, lax.rem(t, 2)
    other = 2 * chip + 1 - core
    line = [lax.rem(chip + k, chips) for k in range(1, chips)]
    peers = [lax.rem(d + k, n_d) for k in range(1, n_d)]
    bits = n_d.bit_length() - 1
    barrier([(d, lax.rem(t + k, n_t)) for k in range(1, n_t)] + [(p, t) for p in peers])
    totals = [up_tot, down_tot, og_tot]
    fulls = [full_up, full_down, full_og, full_ig]

    load = pltpu.make_async_copy(g_hbm, g_ref, s_load.at[0])
    load.start()
    hops, spreads = {}, []

    def cut(k, part):
        return mine.at[k, span(part, mine.shape[1] // n_d), :]

    def hop(k, step):
        slot = 0 if step == 0 else n_d - (n_d >> step)
        order = orders(n_d)[k % 2]
        partner = lax.bitwise_xor(d, 1 << order[step])
        for j, m in enumerate(combos(order[step + 1 :])):
            hops[k, step, j] = send(
                cut(k, lax.bitwise_xor(partner, m)), landed.at[k, slot + j],
                s_hop.at[k, slot + j], r_hop.at[k, slot + j], (partner, t),
            )

    def land(k, step):
        slot = 0 if step == 0 else n_d - (n_d >> step)
        for j, m in enumerate(combos(orders(n_d)[k % 2][step + 1 :])):
            hops[k, step, j].wait_recv()
            add_rows(cut(k, lax.bitwise_xor(d, m)), landed.at[k, slot + j])
        if step + 1 < bits:
            hop(k, step + 1)
        else:
            away(k)

    def spread(n, source):
        at = span(d, fulls[n].shape[0] // n_d)
        for j, p in enumerate(peers):
            spreads.append(send(source, fulls[n].at[at, :], s_all.at[n, j], r_all.at[n, j], (p, t)))

    def owner(i):
        return lax.rem(t, group) * trees + i

    def away(k):
        here = t // group

        @pl.when(owner(k) != t)
        def _():
            send(cut(k, d), far.at[here], s_own.at[k], r_own.at[here], (d, owner(k)))

        @pl.when(owner(k) == t)
        def _():
            far[here] = cut(k, d)[...]

    spread(0, totals[0])
    spread(2, totals[2])

    tree = chip // near

    def exists(c):
        return (c >= 0) & (c < chips)

    def at_step(i):
        return jnp.where(chip < chips // 2, chips - 1 - i, i)

    def past(way, x):
        return (x > chip) if way > 0 else (x < chip)

    def comes(way, j):
        return (j * near <= chip - 1) if way > 0 else (j * near + near - 1 >= chip + 1)

    def pair(x):
        return pltpu.make_async_remote_copy(
            src_ref=r_give.at[x], dst_ref=r_side.at[x], send_sem=s_redside.at[x], recv_sem=r_redside.at[x],
            device_id=(d, other), device_id_type=MESH,
        )

    def red(way, x, j, source, arriving=False):
        w = 0 if way > 0 else 1
        to = chip - way if arriving else chip + way
        return pltpu.make_async_remote_copy(
            src_ref=source, dst_ref=r_land.at[w, x, j], send_sem=s_red.at[w, x, j], recv_sem=r_red.at[w, x, j],
            device_id=(d, 2 * to + core), device_id_type=MESH,
        )

    def arrived(way, x, j):
        w = 0 if way > 0 else 1
        red(way, x, j, r_land.at[w, x, j], True).wait_recv()

    def rows_of(device):
        return dot(bm_ref[span(device, rows), :], w_ref[...], NT).astype(bf16)

    def first_rows(x):
        pair(x).wait_recv()

        @pl.when(x != chip)
        def _():
            r_out[x] = r_keep[x] + r_side[x]

        for way in (1, -1):

            @pl.when(past(way, x) & jnp.logical_not(comes(way, tree)))
            def _():
                red(way, x, tree, r_out.at[x]).start()

    def step_rows(i, _):
        x = at_step(i)
        r_give[x] = rows_of(2 * x + 1 - core)
        r_keep[x] = rows_of(2 * x + core)
        pair(x).start()

        @pl.when(i > 0)
        def _():
            first_rows(at_step(i - 1))

        return 0

    lax.fori_loop(0, chips, step_rows, 0)
    first_rows(at_step(chips - 1))

    def later_rows(i):
        x = at_step(i)
        for way in (1, -1):
            for j in range(trees):

                @pl.when(past(way, x) & comes(way, j))
                def _():
                    arrived(way, x, j)
                    passing = r_land.at[0 if way > 0 else 1, x, j]

                    @pl.when(tree == j)
                    def _():
                        add_rows(r_out.at[x], passing)
                        red(way, x, j, r_out.at[x]).start()

                    @pl.when(tree != j)
                    def _():
                        red(way, x, j, passing).start()

    columns, width = bm_ref.shape[1] // 3, mine.shape[2]
    load.wait()

    def step_weight(i, _):
        p, c = i // (wide // BLOCK), lax.rem(i, wide // BLOCK)
        product = dot(g_ref[:, span(c, BLOCK)], bm_ref[:, span(p, columns)], TN).astype(bf16)
        for j in range(trees):
            mine[j, span(i, BLOCK), :] = product[:, j * width : (j + 1) * width]
        return 0

    lax.fori_loop(0, 3 * (wide // BLOCK), step_weight, 0)
    for k in range(trees):
        hop(k, 0)
    for n in range(3):
        fulls[n][span(d, fulls[n].shape[0] // n_d), :] = totals[n][...]
    for i in range(max(chips, bits)):
        if i < chips:
            later_rows(i)
        if i < bits:
            for k in range(trees):
                land(k, i)
        if i == 0:
            spread(1, totals[1])

    def reduced():
        for w, way in enumerate((1, -1)):
            for j in range(trees):

                @pl.when(comes(way, j))
                def _():
                    arrived(way, chip, j)

                @pl.when(jnp.logical_not(comes(way, j)))
                def _():
                    r_land[w, chip, j] = jnp.zeros((rows, wide), bf16)

        vec_now[0:6] = vec_in[0:6]
        vec_now[6:8] = jnp.zeros((2, wide), f32)
        height = min(64, rows)
        for j in range(trees):

            def body(i, _):
                at = span(i, height)
                own = r_keep[chip, at, :].astype(f32) + r_side[chip, at, :].astype(f32)
                e = jnp.where(tree == j, own, 0.0)
                for w in range(2):
                    e = e + r_land[w, chip, j, at, :].astype(f32)
                norm, r = ln_parts(x_ref[j, at, :].astype(f32))
                vec_now[6:7] = vec_now[6:7] + jnp.sum(e * norm, axis=0, keepdims=True)
                vec_now[7:8] = vec_now[7:8] + jnp.sum(e, axis=0, keepdims=True)
                bt_ref[j, at, :] = (hid_ref[j, at, :] + ln_back(e, norm, r, par_ref[6:7])).astype(bf16)
                return 0

            lax.fori_loop(0, rows // height, body, 0)

    for j in range(trees):
        giver = j * group + t // trees

        @pl.when(giver != t)
        def _():
            pltpu.make_async_remote_copy(
                src_ref=far.at[j], dst_ref=far.at[j], send_sem=s_own.at[0], recv_sem=r_own.at[j],
                device_id=(d, giver), device_id_type=MESH,
            ).wait_recv()

    total = far[0].astype(f32)
    for j in range(1, trees):
        total = total + far[j].astype(f32)
    at = span(d, full_ig.shape[0] // n_d)
    full_ig[at, :] = total.astype(bf16)
    spread(3, full_ig.at[at, :])

    reduced()

    copy = send(vec_now, vec_got.at[0], s_vec.at[0], r_vec.at[0], (d, other))
    copy.wait()
    vec_got[1 + d] = vec_now[...] + vec_got[0]
    row = vec_got.at[1 + d]
    vec_copies = [send(row, row, s_vec.at[1 + k], r_vec.at[1 + k], (p, t)) for k, p in enumerate(peers)]
    for copy in vec_copies:
        copy.wait()
    total = vec_got[1]
    for i in range(1, n_d):
        total = total + vec_got[1 + i]
    vec_far[chip] = total
    vec_copies = []
    for k in range(1, chips):
        c = lax.rem(chip + k, chips)
        n = n_d - 1 + k
        vec_copies.append(send(vec_far.at[chip], vec_far.at[chip], s_vec.at[n], r_vec.at[n], (d, 2 * c + core)))
    for copy in spreads:
        copy.wait_recv()
    for copy in vec_copies:
        copy.wait()
    total = vec_far[0]
    for c in range(1, chips):
        total = total + vec_far[c]
    vec_ref[...] = total

    for k in range(trees):

        @pl.when(owner(k) != t)
        def _():
            pltpu.make_async_remote_copy(
                src_ref=cut(k, d), dst_ref=cut(k, d), send_sem=s_own.at[k], recv_sem=r_own.at[0],
                device_id=(d, owner(k)), device_id_type=MESH,
            ).wait_send()

    for k in range(chips):
        pair(k).wait_send()
    for x in range(chips):
        for way in (1, -1):

            @pl.when(past(way, x))
            def _():
                red(way, x, tree, r_out.at[x]).wait_send()
                for j in range(trees):

                    @pl.when(comes(way, j) & (tree != j))
                    def _():
                        red(way, x, j, r_land.at[0 if way > 0 else 1, x, j]).wait_send()

    for copy in list(hops.values()) + spreads:
        copy.wait_send()


def finish(n_d, n_t, mixed, w, x, hidden, par, vec, up_t, down_t, out_t, gathered, width):
    trees, rows, wide = x.shape
    chips = n_t // 2
    bits = n_d.bit_length() - 1
    dma = pltpu.SemaphoreType.DMA
    sds = jax.ShapeDtypeStruct
    shapes = [(a.shape[0] * n_d, a.shape[1]) for a in (up_t, down_t, out_t)] + [(3 * wide, width)]
    vm = lambda lead, shape, kind=bf16: pltpu.VMEM(tuple(lead) + tuple(shape), kind)
    part = (shapes[3][0] // n_d, shapes[3][1])
    return pl.pallas_call(
        functools.partial(finish_kernel, n_d, n_t),
        in_specs=[VMEM] * 9 + [HBM],
        out_specs=[VMEM] * 6,
        out_shape=[sds(x.shape, bf16), sds((8, wide), f32)] + [sds(s, bf16) for s in shapes],
        scratch_shapes=[vm((), gathered.shape), vm((trees,), shapes[3]), vm((trees, n_d - 1), part), vm((trees,), part)]
        + [
            vm((chips, rows), (wide,)), vm((chips, rows), (wide,)), vm((chips, rows), (wide,)),
            vm((chips, rows), (wide,)), vm((2, chips, trees, rows), (wide,)),
            vm((8,), (wide,), f32), vm((1 + n_d, 8), (wide,), f32), vm((chips, 8), (wide,), f32),
            dma((1,)), dma((trees, n_d - 1)), dma((trees, n_d - 1)),
            dma((4, n_d - 1)), dma((4, n_d - 1)),
            dma((trees,)), dma((trees,)),
            dma((2, chips, trees)), dma((2, chips, trees)), dma((chips,)), dma((chips,)),
            dma((n_d + chips - 1,)), dma((n_d + chips - 1,)),
        ],
        compiler_params=pltpu.CompilerParams(
            collective_id=3, has_side_effects=True, vmem_limit_bytes=67043328
        ),
        name="finish",
    )(mixed, w, x, hidden, par, vec, up_t, down_t, out_t, gathered)


def shards(
    n_d, n_t,
    tokens, cotangent, lengths, parents, first_gain, first_shift, in_weight, out_weight,
    second_gain, second_shift, third_gain, third_shift, up_weight, down_weight, fourth_gain, fourth_shift,
):
    trees, rows, wide = tokens.shape
    group = n_t // trees
    d, t = lax.axis_index("dp"), lax.axis_index("tensor")
    tree = t // group
    width = out_weight.shape[0]

    mine = lambda a: lax.dynamic_index_in_dim(a, tree, 0, keepdims=False)
    cosine, sine, mq, mk = tables(mine(lengths), mine(parents), n_t * rows)

    par = jnp.stack(
        [second_gain, second_shift, third_gain, third_shift, fourth_gain, fourth_shift, first_gain, first_shift]
    )
    gathered, w, down_all = gather_tree(
        n_d, n_t, tokens, par, in_weight.transpose(1, 0, 2), down_weight
    )
    w = w.transpose(1, 2, 0, 3).reshape(3, wide, -1)
    q, k, v, kt, vt = project(gathered, w, cosine, sine, mq, mk)
    attended, qb, att, out_all, up_all = attend(n_d, n_t, trees, q, k, vt, out_weight, up_weight)
    flat = lambda a: a.reshape(trees * rows, a.shape[-1])
    output, back_hidden, back_att, up_g, down_g, out_g, vec = feed(
        flat(att), flat(tokens), flat(cotangent), out_all.reshape(-1, wide), par, up_all, down_all
    )
    back_mixed, up_t, down_t, out_t = attend_back(
        n_d, n_t, qb, k, v, kt, back_att.reshape(trees, rows, wide), attended, cosine, sine,
        up_g, down_g, out_g.reshape(n_t, width, wide),
    )
    w_flat = w.transpose(1, 0, 2).reshape(wide, -1)
    back_tokens, vec, up_sum, down_sum, out_sum, in_sum = finish(
        n_d, n_t, back_mixed, w_flat, tokens, back_hidden.reshape(tokens.shape), par, vec,
        up_t, down_t, out_t, gathered, width,
    )
    return (
        output.reshape(tokens.shape),
        back_tokens,
        vec[6], vec[7],
        in_sum.astype(f32).reshape(3, wide, width).transpose(1, 0, 2),
        out_sum.astype(f32),
        vec[0], vec[1], vec[2], vec[3],
        up_sum.astype(f32),
        down_sum.astype(f32),
        vec[4], vec[5],
    )


def solution(mesh):
    in_specs = (
        P("dp", "tensor", None), P("dp", "tensor", None), P("dp", None), P("dp", None),
        P(), P(), P(None, None, "tensor"), P("tensor", None), P(), P(), P(), P(),
        P(None, "tensor"), P("tensor", None), P(), P(),
    )
    out_specs = (
        P("dp", "tensor", None), P("dp", "tensor", None), P(), P(), P(None, None, "tensor"),
        P("tensor", None), P(), P(), P(), P(), P(None, "tensor"), P("tensor", None), P(), P(),
    )
    run = functools.partial(shards, mesh.shape["dp"], mesh.shape["tensor"])
    return jax.shard_map(run, mesh=mesh, in_specs=in_specs, out_specs=out_specs, check_vma=False)
```

```python
import functools
import jax
import jax.numpy as jnp
from jax import lax
from jax.experimental import pallas as pl
from jax.experimental.pallas import tpu as pltpu
from jax.sharding import PartitionSpec as P

HEAD_DIM = 64
LANES = 128
VROWS = 80
BLOCK = 256
TRUNK = 512
SEGMENTS = 13

rope_base = 10000.0
norm_eps = 1e-05
masked_score = -1e30
f32, bf16 = jnp.float32, jnp.bfloat16
NN = (((1,), (0,)), ((), ()))
NT = (((1,), (1,)), ((), ()))
TN = (((0,), (0,)), ((), ()))
MESH = pl.DeviceIdType.MESH
VMEM = pl.BlockSpec(memory_space=pltpu.VMEM)
HBM = pl.BlockSpec(memory_space=pltpu.HBM)


def dot(a, b, dims=NN):
    return lax.dot_general(a, b, dims, preferred_element_type=f32)


def lane_of(shape):
    return lax.broadcasted_iota(jnp.int32, shape, len(shape) - 1)


def row_of(shape):
    return lax.broadcasted_iota(jnp.int32, shape, len(shape) - 2)


def span(i, n):
    return pl.ds(pl.multiple_of(i * n, n), n)


def split3(v):
    hi = v.astype(bf16).astype(f32)
    mid = (v - hi).astype(bf16).astype(f32)
    return hi, mid, v - hi - mid


def layer_norm(values, gain, shift):
    average = jnp.mean(values, axis=-1, keepdims=True)
    centered = values - average
    spread = jnp.mean(centered * centered, axis=-1, keepdims=True)
    return centered * lax.rsqrt(spread + norm_eps) * gain + shift


def tree_layout(tree_lengths, tree_parents, rows):
    seg_sizes = jnp.concatenate([jnp.full((1,), TRUNK, jnp.int32), tree_lengths])
    ends = jnp.cumsum(seg_sizes)
    starts = ends - seg_sizes
    places = jnp.arange(rows, dtype=jnp.int32)
    labels = jnp.arange(SEGMENTS, dtype=jnp.int32)
    segment = jnp.sum((places[:, None] >= ends[None, :]).astype(jnp.int32), axis=1)
    own_hot = (segment[:, None] == labels[None, :]).astype(jnp.int32)
    parent = jnp.sum(own_hot * tree_parents[None, :], axis=1)
    parent_hot = (parent[:, None] == labels[None, :]).astype(jnp.int32)
    grandparent = jnp.sum(parent_hot * tree_parents[None, :], axis=1)
    parent_size = jnp.sum(parent_hot * seg_sizes[None, :], axis=1)
    depth_start = jnp.where(segment > 0, TRUNK, 0).astype(jnp.int32) + jnp.where(
        parent > 0, parent_size, 0
    )
    position = places - jnp.sum(own_hot * starts[None, :], axis=1) + depth_start
    return (segment, parent, grandparent, position)


def tables(tree_lengths, tree_parents, rows):
    segment, parent, grand, position = tree_layout(tree_lengths, tree_parents, rows)
    lane = jnp.arange(LANES, dtype=jnp.int32)
    half = HEAD_DIM // 2
    inverse = rope_base ** (-(lane % half).astype(f32) * 2.0 / HEAD_DIM)
    angle = position.astype(f32)[:, None] * inverse[None, :]
    cosine = jnp.cos(angle)
    sine = jnp.where((lane % HEAD_DIM) < half, -1.0, 1.0)[None, :] * jnp.sin(angle)
    label = (lane - HEAD_DIM)[None, :]
    own = segment[:, None] == label
    path = own | (parent[:, None] == label) | (grand[:, None] == label)
    hidden = (label >= 0) & (label < SEGMENTS) & ~path
    queries = jnp.where(hidden, masked_score, 0.0).astype(f32)
    ones = (label >= 16) & (label < 19)
    keys = jnp.where(own | ones, 1.0, 0.0).astype(f32)
    return cosine, sine, queries, keys
def barrier(partners):
    semaphore = pltpu.get_barrier_semaphore()
    for partner in partners:
        pl.semaphore_signal(semaphore, inc=1, device_id=partner, device_id_type=MESH)
    pl.semaphore_wait(semaphore, len(partners))


def send(source, target, send_sem, recv_sem, device):
    copy = pltpu.make_async_remote_copy(
        src_ref=source,
        dst_ref=target,
        send_sem=send_sem,
        recv_sem=recv_sem,
        device_id=device,
        device_id_type=MESH,
    )
    copy.start()
    return copy


def add_rows(target, source, step=64):
    rows = target.shape[0]
    step = min(step, rows)
    while rows % step:
        step //= 2

    def body(i, _):
        at = span(i, step)
        target[at, :] = target[at, :] + source[at, :]
        return 0

    lax.fori_loop(0, rows // step, body, 0)


def orders(n_d):
    bits = n_d.bit_length() - 1
    return [list(range(bits)), list(range(bits - 1, -1, -1))]


def combos(bits):
    masks = [0]
    for b in bits:
        masks = masks + [m ^ (1 << b) for m in masks]
    return masks


def halves(rows, width, tile=16):
    return (rows // 2, width) if rows % (2 * tile) == 0 else (rows, width // 2)


def half(part, stream, rows, width):
    height, wide = halves(rows, width)
    if height < rows:
        return span(2 * part + stream, height), slice(None)
    return span(part, rows), pl.ds(stream * wide, wide)


class Spread:
    def __init__(self, n_d, n_t, shards, alls, sems):
        self.n_d, self.n_t, self.shards, self.alls = n_d, n_t, shards, alls
        self.zs, self.zr, self.ps, self.pr, self.ys, self.yr, self.own = sems
        self.d, self.t = lax.axis_index("dp"), lax.axis_index("tensor")
        self.chips = n_t // 2
        self.chip, self.core = self.t // 2, lax.rem(self.t, 2)
        self.other = 2 * self.chip + 1 - self.core
        self.bits = n_d.bit_length() - 1
        self.arrays = range(len(shards))

    @staticmethod
    def sems(count, n_d, n_t):
        dma = pltpu.SemaphoreType.DMA
        hops, slots = n_t // 2 - 1, 2 * (n_d - 1)
        z, p, y = (count, 2 * hops), (count, 2 * hops, slots), (count, 2 * hops + 1)
        return [dma(z), dma(z), dma(p), dma(p), dma(y), dma(y), dma((count,))]

    def exists(self, c):
        return (c >= 0) & (c < self.chips)

    def rows(self, a):
        return self.shards[a].shape[0] // self.n_d

    def slot(self, way, h):
        return h - 1 + (self.chips - 1 if way < 0 else 0)

    def remote(self, src, dst, ssem, rsem, device):
        return pltpu.make_async_remote_copy(
            src_ref=src, dst_ref=dst, send_sem=ssem, recv_sem=rsem, device_id=device, device_id_type=MESH
        )

    def along(self, a, way, h, arriving):
        source = self.chip - way * (h if arriving else h - 1)
        at = span(self.d, self.rows(a))
        dst = self.alls[a].at[2 * source + self.core, at]
        src = self.shards[a].at[at] if h == 1 and not arriving else dst
        peer = self.chip - way if arriving else self.chip + way
        i = self.slot(way, h)
        return self.remote(src, dst, self.zs.at[a, i], self.zr.at[a, i], (self.d, 2 * peer + self.core))

    def across(self, a, way, h, step, arriving):
        source = self.chip - way * h
        out = []
        for stream, order in enumerate(orders(self.n_d)):
            partner = lax.bitwise_xor(self.d, 1 << order[step])
            for j, m in enumerate(combos(order[:step])):
                block = lax.bitwise_xor(partner if arriving else self.d, m)
                rows, cols = half(block, stream, self.rows(a), self.shards[a].shape[1])
                ref = self.alls[a].at[2 * source + self.core, rows, cols]
                i = stream * (self.n_d - 1) + (1 << step) - 1 + j
                k = self.slot(way, h)
                out.append(self.remote(ref, ref, self.ps.at[a, k, i], self.pr.at[a, k, i], (partner, self.t)))
        return out

    def beside(self, a, way, h, arriving=False):
        source = self.chip - way * h
        ref = self.alls[a].at[2 * source + (1 - self.core if arriving else self.core)]
        k = self.slot(way, h)
        return self.remote(ref, ref, self.ys.at[a, k], self.yr.at[a, k], (self.d, self.other))

    def mine(self, a, arriving=False):
        k = 2 * (self.chips - 1)
        dst = self.alls[a].at[self.other if arriving else self.t]
        return self.remote(self.shards[a], dst, self.ys.at[a, k], self.yr.at[a, k], (self.d, self.other))

    def keep(self, a):
        return pltpu.make_async_copy(self.shards[a], self.alls[a].at[self.t], self.own.at[a])

    def begin(self):
        for way in (1, -1):

            @pl.when(self.exists(self.chip + way))
            def _():
                for a in self.arrays:
                    self.along(a, way, 1, False).start()

        for a in self.arrays:
            self.keep(a).start()
            self.mine(a).start()

    def phase(self, p, h):
        for way in (1, -1):

            @pl.when(self.exists(self.chip - way * h))
            def _():
                for a in self.arrays:
                    if p == 0:
                        self.along(a, way, h, True).wait_recv()
                        if h < self.chips - 1:

                            @pl.when(self.exists(self.chip + way))
                            def _():
                                self.along(a, way, h + 1, False).start()
                    else:
                        for copy in self.across(a, way, h, p - 1, True):
                            copy.wait_recv()
                    if p < self.bits:
                        for copy in self.across(a, way, h, p, False):
                            copy.start()
                    else:
                        self.beside(a, way, h).start()

    def groups(self):
        return self.chips - 1 + self.bits

    def group(self, g):
        for h in range(1, self.chips):
            if 0 <= g - (h - 1) <= self.bits:
                self.phase(g - (h - 1), h)

    def end(self):
        for h in range(1, self.chips):
            for way in (1, -1):

                @pl.when(self.exists(self.chip + way) & self.exists(self.chip - way * (h - 1)))
                def _():
                    for a in self.arrays:
                        self.along(a, way, h, False).wait_send()

                @pl.when(self.exists(self.chip - way * h))
                def _():
                    for a in self.arrays:
                        for step in range(self.bits):
                            for copy in self.across(a, way, h, step, False):
                                copy.wait_send()
                        self.beside(a, way, h).wait_send()
                        self.beside(a, way, h, True).wait_recv()

        for a in self.arrays:
            self.keep(a).wait()
            self.mine(a).wait_send()
            self.mine(a, True).wait_recv()


def gather_kernel(
    n_d, n_t, v_ref, gain_ref, w_ref, f_ref, o_ref, u_ref, all_ref,
    x_ref, passing, rs, ss, rb, sb, rw, sw, rp, sp, *sems,
):
    d, t = lax.axis_index("dp"), lax.axis_index("tensor")
    trees, rows, _ = x_ref.shape
    chips = n_t // 2
    group = n_t // trees
    chip, core = t // 2, lax.rem(t, 2)
    other = 2 * chip + 1 - core
    near = group // 2
    tree = t // group
    planes = [lax.rem(d + k, n_d) for k in range(1, n_d)]
    owners = [(j * group + t // trees) for j in range(trees)]
    givers = [lax.rem(t, group) * trees + i for i in range(trees)]
    barrier([(d, lax.rem(t + k, n_t)) for k in range(1, n_t)] + [(p, t) for p in planes])
    part = w_ref.shape[1] // n_d
    weights = Spread(n_d, n_t, [f_ref], [all_ref], sems)
    exists = weights.exists

    copies = []
    mine = w_ref.at[:, span(d, part), :]
    for j in range(trees):
        slot = u_ref.at[lax.rem(t, trees), :, span(d, part), :]

        @pl.when(owners[j] != t)
        def _():
            send(mine, slot, sw.at[j], rw.at[lax.rem(t, trees)], (d, owners[j]))

        @pl.when(owners[j] == t)
        def _():
            u_ref[lax.rem(t, trees), :, span(d, part), :] = w_ref[:, span(d, part), :]

    weights.begin()

    def block(c):
        return o_ref.at[span(2 * c + core, rows)]

    def beyond(c, way, j):
        return (j * near + near - 1 >= c) if way > 0 else (j * near <= c)

    def hop(way, h, j, here):
        source = chip - way * (h - 1)
        if h == 1:
            src = x_ref.at[j]
        else:
            src = block(source) if here else passing.at[j, source]
        return src, source

    def pass_on(way, h):
        for j in range(trees):

            @pl.when(exists(chip - way * (h - 1)) & exists(chip + way) & beyond(chip + way, way, j))
            def _():
                i = weights.slot(way, h)
                to = chip + way
                for here in (True, False) if h > 1 else (True,):
                    src, source = hop(way, h, j, here)
                    for there in (True, False):
                        at_home = (tree == j) if here else (tree != j)
                        lands = (to // near == j) if there else (to // near != j)

                        @pl.when((at_home & lands) if h > 1 else lands)
                        def _():
                            dst = block(source) if there else passing.at[j, source]
                            send(src, dst, ss.at[j, i], rs.at[j, i], (d, 2 * to + core))

    def row_copy(j, i):
        return weights.remote(x_ref.at[j], passing.at[j, 0], ss.at[j, i], rs.at[j, i], (d, other))

    def share(way, h):
        source = chip - way * h
        i = weights.slot(way, h)
        return weights.remote(block(source), block(source), sb.at[i], rb.at[i], (d, other))

    def arrive(way, h):
        for j in range(trees):

            @pl.when(exists(chip - way * h) & beyond(chip, way, j))
            def _():
                row_copy(j, weights.slot(way, h)).wait_recv()

        if h < chips - 1:
            pass_on(way, h + 1)

        @pl.when(exists(chip - way * h))
        def _():
            share(way, h).start()

    height = min(64, rows)

    def norm_rows(i, _):
        at = span(i, height)
        for j in range(trees):
            v = v_ref[j, at, :].astype(f32)
            x_ref[j, at, :] = layer_norm(v, gain_ref[6:7], gain_ref[7:8]).astype(bf16)
        return 0

    lax.fori_loop(0, rows // height, norm_rows, 0)
    o_ref[span(t, rows), :] = x_ref[tree]
    for way in (1, -1):
        pass_on(way, 1)
    last = 2 * (chips - 1)
    copies.append(send(x_ref.at[tree], block(chip), sb.at[last], rb.at[last], (d, other)))
    weights.group(0)
    for i in range(trees):
        slot = u_ref.at[i, :, span(d, part), :]

        @pl.when(givers[i] != t)
        def _():
            pltpu.make_async_remote_copy(
                src_ref=mine, dst_ref=slot, send_sem=sw.at[0], recv_sem=rw.at[i],
                device_id=(d, givers[i]), device_id_type=MESH,
            ).wait_recv()

    mine_all = u_ref.at[:, :, span(d, part), :]
    for k, p in enumerate(planes):
        copies.append(send(mine_all, mine_all, sp.at[k], rp.at[k], (p, t)))
    for h in range(1, chips):
        for way in (1, -1):
            arrive(way, h)
        weights.group(h)
    for g in range(chips, weights.groups()):
        weights.group(g)
    weights.end()
    for j in range(trees):

        @pl.when(owners[j] != t)
        def _():
            pltpu.make_async_remote_copy(
                src_ref=mine, dst_ref=mine, send_sem=sw.at[j], recv_sem=rw.at[0],
                device_id=(d, owners[j]), device_id_type=MESH,
            ).wait_send()

    for way in (1, -1):
        for h in range(1, chips):
            for j in range(trees):

                @pl.when(exists(chip - way * (h - 1)) & exists(chip + way) & beyond(chip + way, way, j))
                def _():
                    row_copy(j, weights.slot(way, h)).wait_send()

            @pl.when(exists(chip - way * h))
            def _():
                share(way, h).wait()

    for copy in copies:
        copy.wait()


def gather_tree(n_d, n_t, tokens, par, weight, down):
    trees, rows, wide = tokens.shape
    chips = n_t // 2
    hops = 2 * (chips - 1)
    dma = pltpu.SemaphoreType.DMA
    return pl.pallas_call(
        functools.partial(gather_kernel, n_d, n_t),
        in_specs=[VMEM] * 4,
        out_specs=[VMEM] * 2 + [HBM],
        out_shape=[
            jax.ShapeDtypeStruct((n_t * rows, wide), bf16),
            jax.ShapeDtypeStruct((trees,) + weight.shape, bf16),
            jax.ShapeDtypeStruct((n_t,) + down.shape, bf16),
        ],
        scratch_shapes=[
            pltpu.VMEM((trees, rows, wide), bf16), pltpu.VMEM((trees, chips, rows, wide), bf16),
            dma((trees, hops)), dma((trees, hops)), dma((hops + 1,)), dma((hops + 1,)),
            dma((trees,)), dma((trees,)), dma((n_d - 1,)), dma((n_d - 1,)),
        ] + Spread.sems(1, n_d, n_t),
        compiler_params=pltpu.CompilerParams(collective_id=0, has_side_effects=True),
        name="gather_tree",
    )(tokens, par, weight, down)


def qkv_kernel(x_ref, w_ref, cos_ref, sin_ref, mq_ref, mk_ref, q_ref, k_ref, v_ref, kt_ref, vt_ref):
    x = x_ref[...]
    heads = q_ref.shape[0]
    cosine, sine = cos_ref[...], sin_ref[...]
    mq, mk = mq_ref[...], mk_ref[...]
    lane = lane_of(cosine.shape)
    low = lax.rem(lane, HEAD_DIM) < HEAD_DIM // 2
    first = lane < HEAD_DIM
    mv = jnp.where((lane >= HEAD_DIM) & (lane < HEAD_DIM + 3), 1.0, 0.0)
    tail = jnp.where(row_of((VROWS - HEAD_DIM, x.shape[0])) == 0, 1.0, 0.0).astype(bf16)

    def both(slab):
        return slab, pltpu.roll(slab, HEAD_DIM, 1)

    def rotate(slab):
        partner = jnp.where(
            low, pltpu.roll(slab, LANES - HEAD_DIM // 2, 1), pltpu.roll(slab, HEAD_DIM // 2, 1)
        )
        return slab * cosine + partner * sine

    q_all, k_all, v_all = (dot(x, w_ref[i]) for i in range(3))
    for h in range(0, heads, 2):
        cols = slice(h * HEAD_DIM, (h + 2) * HEAD_DIM)
        for g, slab in enumerate(both(rotate(q_all[:, cols]) * HEAD_DIM**-0.5)):
            q_ref[h + g] = jnp.where(first, slab, mq).astype(bf16)
        keys = rotate(k_all[:, cols])
        for g, slab in enumerate(both(keys)):
            k_ref[h + g] = jnp.where(first, slab, mk).astype(bf16)
        flat = keys.T.astype(bf16)
        for g, slab in enumerate(both(v_all[:, cols])):
            v_ref[h + g] = jnp.where(first, slab, mv).astype(bf16)
        flat_v = v_all[:, cols].T.astype(bf16)
        for g in range(2):
            part = slice(g * HEAD_DIM, (g + 1) * HEAD_DIM)
            kt_ref[h + g] = flat[part]
            vt_ref[h + g, :HEAD_DIM] = flat_v[part]
            vt_ref[h + g, HEAD_DIM:] = tail


def project(x, w, cosine, sine, mq, mk):
    rows, wide = x.shape
    heads = w.shape[2] // HEAD_DIM
    table = pl.BlockSpec((BLOCK, LANES), lambda i: (i, 0))
    slab = pl.BlockSpec((heads, BLOCK, LANES), lambda i: (0, i, 0))
    shape = jax.ShapeDtypeStruct((heads, rows, LANES), bf16)
    return pl.pallas_call(
        qkv_kernel,
        grid=(rows // BLOCK,),
        in_specs=[
            pl.BlockSpec((BLOCK, wide), lambda i: (i, 0)),
            pl.BlockSpec(w.shape, lambda i: (0, 0, 0)),
            table, table, table, table,
        ],
        out_specs=[
            slab, slab, slab,
            pl.BlockSpec((heads, HEAD_DIM, BLOCK), lambda i: (0, 0, i)),
            pl.BlockSpec((heads, VROWS, BLOCK), lambda i: (0, 0, i)),
        ],
        out_shape=[
            shape, shape, shape,
            jax.ShapeDtypeStruct((heads, HEAD_DIM, rows), bf16),
            jax.ShapeDtypeStruct((heads, VROWS, rows), bf16),
        ],
        name="project",
    )(x, w, cosine, sine, mq, mk)


def fwd_kernel(
    n_d, n_t, trees, q_ref, k_ref, vt_ref, ow_ref, up_ref, o_ref, qb_ref, att_ref, ow_all, up_all,
    ss, rs, here, *sems,
):
    turn = pl.program_id(0)
    steps = pl.num_programs(0)
    heads = q_ref.shape[0]
    row, col = row_of((BLOCK, BLOCK)), lane_of((BLOCK, BLOCK))
    d, t = lax.axis_index("dp"), lax.axis_index("tensor")
    group = n_t // trees
    rows, width = att_ref.shape[1], o_ref.shape[1]
    per = BLOCK // rows
    qi = jnp.where(turn == steps - 1, t // per, jnp.where(turn >= t // per, turn + 1, turn))
    at = span(qi, BLOCK)
    weights = Spread(n_d, n_t, [up_ref, ow_ref], [up_all, ow_all], sems)
    first_group = max(0, k_ref.shape[1] // BLOCK - 4)
    place = att_ref.at[t // group, :, span(lax.rem(t, group), width)]

    def outgoing(i, r, k):
        return pltpu.make_async_remote_copy(
            src_ref=o_ref.at[span(i * per + r, rows)], dst_ref=place, send_sem=ss.at[k], recv_sem=rs.at[k],
            device_id=(d, lax.rem(t + k, n_t)), device_id_type=MESH,
        )

    @pl.when(turn == 0)
    def _():
        barrier(
            [(d, lax.rem(t + k, n_t)) for k in range(1, n_t)] + [(lax.rem(d + k, n_d), t) for k in range(1, n_d)]
        )
        weights.begin()

    for g in range(weights.groups()):
        if first_group + g < k_ref.shape[1] // BLOCK:

            @pl.when(turn == first_group + g)
            def _():
                weights.group(g)

    qs = [q_ref[h, at, :] for h in range(heads)]

    def scores(h, j):
        return dot(k_ref[h, span(j, BLOCK), :], qs[h], NT)

    state = []
    for h in range(heads):
        s = jnp.where(row <= col, scores(h, qi), masked_score)
        m = jnp.max(s, axis=0, keepdims=True)
        p = jnp.exp(s - m)
        state.append((m, dot(vt_ref[h, :, span(qi, BLOCK)], p.astype(bf16))))

    def step(j, carry):
        out = []
        for h in range(heads):
            m, acc = carry[h]
            s = scores(h, j)
            top = jnp.maximum(m, jnp.max(s, axis=0, keepdims=True))
            p = jnp.exp(s - top)
            acc = acc * jnp.exp(m - top) + dot(vt_ref[h, :, span(j, BLOCK)], p.astype(bf16))
            out.append((top, acc))
        return tuple(out)

    state = lax.fori_loop(0, qi, step, tuple(state))
    r = row_of((LANES, BLOCK))
    for h in range(0, heads, 2):
        outs = []
        for g in (h, h + 1):
            m, acc = state[g]
            total = acc[HEAD_DIM : HEAD_DIM + 1]
            outs.append(acc[:HEAD_DIM] / total)
            a, b, c = split3(-(m + jnp.log(total)))
            extra = jnp.where(r == 80, a, jnp.where(r == 81, b, jnp.where(r == 82, c, 0.0))).T
            qb_ref[g, at, :] = qs[g] + extra.astype(bf16)
        o_ref[at, h * HEAD_DIM : (h + 2) * HEAD_DIM] = jnp.concatenate(outs, axis=0).T.astype(bf16)

    def local(r):
        return pltpu.make_async_copy(o_ref.at[span(t // per * per + r, rows)], place, here.at[0])

    for r in range(per):
        k = lax.rem(qi * per + r + n_t - t, n_t)

        @pl.when(k != 0)
        def _():
            outgoing(qi, r, k).start()

        @pl.when(k == 0)
        def _():
            local(r).start()

    @pl.when(turn == steps - 1)
    def _():
        for g in range(k_ref.shape[1] // BLOCK - first_group, weights.groups()):
            weights.group(g)
        for k in range(1, n_t):
            outgoing(0, 0, k).wait()
        local(0).wait()
        weights.end()


def attend(n_d, n_t, trees, q, k, vt, ow, up):
    heads, rows, _ = q.shape
    wide = heads * HEAD_DIM
    dma = pltpu.SemaphoreType.DMA
    sds = jax.ShapeDtypeStruct
    return pl.pallas_call(
        functools.partial(fwd_kernel, n_d, n_t, trees),
        grid=(rows // BLOCK,),
        in_specs=[VMEM] * 5,
        out_specs=[VMEM, VMEM, HBM, HBM, HBM],
        out_shape=[
            sds((rows, wide), bf16),
            sds(q.shape, bf16),
            sds((trees, rows // n_t, wide * n_t // trees), bf16),
            sds((n_t,) + ow.shape, bf16),
            sds((n_t,) + up.shape, bf16),
        ],
        scratch_shapes=[
            dma((n_t,)), dma((n_t,)), dma((1,)),
        ] + Spread.sems(2, n_d, n_t),
        compiler_params=pltpu.CompilerParams(collective_id=1, has_side_effects=True),
        name="attend",
    )(q, k, vt, ow, up)


class Reduce:
    def __init__(self, n_d, n_t, sources, totals, scratch):
        self.n_d, self.n_t, self.sources, self.totals = n_d, n_t, sources, totals
        count = len(sources)
        self.mine, self.side, self.land_at, self.far = (
            scratch[i * count : (i + 1) * count] for i in range(4)
        )
        self.s_load, self.s_side, self.r_side, self.s_hop, self.r_hop, self.s_far, self.r_far = scratch[4 * count :]
        self.d, self.t = lax.axis_index("dp"), lax.axis_index("tensor")
        self.chips = n_t // 2
        self.chip, self.core = self.t // 2, lax.rem(self.t, 2)
        self.other = 2 * self.chip + 1 - self.core
        self.dest = [lax.rem(self.chip + k, self.chips) for k in range(1, self.chips)] + [self.chip]
        self.bits = n_d.bit_length() - 1
        self.units = [(n, k) for k in range(self.chips) for n in range(count)]

    @staticmethod
    def scratch(n_d, n_t, shapes):
        dma = pltpu.SemaphoreType.DMA
        chips, slots, count = n_t // 2, 2 * (n_d - 1), len(shapes)
        vm = lambda lead, r, c: pltpu.VMEM(lead + (r, c), bf16)
        units = count * chips
        return (
            [vm((chips,), r, c) for r, c in shapes] * 2
            + [vm((chips, slots), *halves(r // n_d, c)) for r, c in shapes]
            + [vm((chips - 1,), r // n_d, c) for r, c in shapes]
            + [dma((units,)), dma((units,)), dma((units,)), dma((units, slots)), dma((units, slots))]
            + [dma((units,)), dma((units,))]
        )

    def remote(self, src, dst, ssem, rsem, device):
        return pltpu.make_async_remote_copy(
            src_ref=src, dst_ref=dst, send_sem=ssem, recv_sem=rsem, device_id=device, device_id_type=MESH
        )

    def load(self, u):
        n, k = self.units[u]
        source = self.sources[n].at[2 * self.dest[k] + self.core]
        return pltpu.make_async_copy(source, self.mine[n].at[k], self.s_load.at[u])

    def beside(self, u):
        n, k = self.units[u]
        source = self.sources[n].at[2 * self.dest[k] + 1 - self.core]
        return self.remote(source, self.side[n].at[k], self.s_side.at[u], self.r_side.at[u], (self.d, self.other))

    def cut(self, u, part, stream):
        n, k = self.units[u]
        _, height, width = self.mine[n].shape
        rows, cols = half(part, stream, height // self.n_d, width)
        return self.mine[n].at[k, rows, cols]

    def hops(self, u, step):
        n, k = self.units[u]
        slot = 0 if step == 0 else self.n_d - (self.n_d >> step)
        out = []
        for stream, order in enumerate(orders(self.n_d)):
            partner = lax.bitwise_xor(self.d, 1 << order[step])
            for j, m in enumerate(combos(order[step + 1 :])):
                i = (slot + j) * 2 + stream
                landing = self.land_at[n].at[k, i]
                copy = self.remote(
                    self.cut(u, lax.bitwise_xor(partner, m), stream), landing,
                    self.s_hop.at[u, i], self.r_hop.at[u, i], (partner, self.t),
                )
                out.append((copy, self.cut(u, lax.bitwise_xor(self.d, m), stream), landing))
        return out

    def piece(self, u):
        n, k = self.units[u]
        return self.mine[n].at[k, span(self.d, self.mine[n].shape[1] // self.n_d), :]

    def away(self, u):
        n, k = self.units[u]
        return self.remote(
            self.piece(u), self.far[n].at[k], self.s_far.at[u], self.r_far.at[u],
            (self.d, 2 * self.dest[k] + self.core),
        )

    def begin(self):
        for u in range(len(self.units)):
            self.load(u).start()
            self.beside(u).start()

    def events(self):
        return len(self.units) + self.bits

    def event(self, e):
        if e < len(self.units):
            n, k = self.units[e]
            self.load(e).wait()
            self.beside(e).wait_recv()
            add_rows(self.mine[n].at[k], self.side[n].at[k])
            for copy, _, _ in self.hops(e, 0):
                copy.start()
        for step in range(self.bits):
            u = e - 1 - step
            if 0 <= u < len(self.units):
                for copy, target, landing in self.hops(u, step):
                    copy.wait_recv()
                    add_rows(target, landing)
                if step + 1 < self.bits:
                    for copy, _, _ in self.hops(u, step + 1):
                        copy.start()
                elif self.units[u][1] < self.chips - 1:
                    self.away(u).start()

    def end(self):
        for u, (n, k) in enumerate(self.units):
            if k < self.chips - 1:
                self.away(u).wait_recv()
            else:
                total = self.piece(u)[...].astype(f32)
                for i in range(self.chips - 1):
                    total = total + self.far[n][i].astype(f32)
                self.totals[n][...] = total.astype(bf16)
        for u, (n, k) in enumerate(self.units):
            self.beside(u).wait_send()
            for step in range(self.bits):
                for copy, _, _ in self.hops(u, step):
                    copy.wait_send()
            if k < self.chips - 1:
                self.away(u).wait_send()


def bwd_kernel(
    n_d, n_t, q_ref, k_ref, v_ref, kt_ref, x_ref, o_ref, cos_ref, sin_ref, up_ref, down_ref, og_ref,
    m_ref, up_tot, down_tot, og_tot, sums, wide, d_ref, hs, hr, *scratch,
):
    j = pl.program_id(0)
    heads, rows, _ = q_ref.shape
    nq = rows // BLOCK
    row, col = row_of((BLOCK, BLOCK)), lane_of((BLOCK, BLOCK))
    lane = lane_of((BLOCK, LANES))
    first = lane < HEAD_DIM
    d, t = lax.axis_index("dp"), lax.axis_index("tensor")
    trees, part, _ = x_ref.shape
    group, width = n_t // trees, heads * HEAD_DIM
    gradients = Reduce(n_d, n_t, [up_ref, down_ref, og_ref], [up_tot, down_tot, og_tot], scratch)
    ahead = 6
    points = 10

    def point(p):
        left = gradients.events() - ahead
        for e in range(ahead + p * left // points, ahead + (p + 1) * left // points):
            gradients.event(e)

    def cut(o):
        return x_ref.at[o // group, :, span(lax.rem(o, group), width)]

    def outgoing(k):
        o = lax.rem(t + k, n_t)
        return gradients.remote(cut(o), d_ref.at[span(t, part), :], hs.at[k], hr.at[k], (d, o))

    @pl.when(j == 0)
    def _():
        barrier(
            [(d, lax.rem(t + k, n_t)) for k in range(1, n_t)] + [(lax.rem(d + k, n_d), t) for k in range(1, n_d)]
        )
        for k in range(1, n_t):
            outgoing(k).start()
        gradients.begin()
        d_ref[span(t, part), :] = cut(t)[...]
        sums[...] = jnp.zeros_like(sums)
        for e in range(ahead):
            gradients.event(e)
        for k in range(1, n_t):
            outgoing(k).wait()

        def widen(i, _):
            at = span(i, BLOCK)
            for h in range(0, heads, 2):
                cols = slice(h * HEAD_DIM, (h + 2) * HEAD_DIM)
                slab = d_ref[at, cols].astype(f32)
                prod = slab * o_ref[at, cols].astype(f32)
                for g, (s, mine) in enumerate(((slab, first), (pltpu.roll(slab, HEAD_DIM, 1), ~first))):
                    inner = -jnp.sum(jnp.where(mine, prod, 0.0), axis=1, keepdims=True)
                    a, b, c = split3(inner)
                    n = HEAD_DIM
                    tail = jnp.where(lane == n, a, jnp.where(lane == n + 1, b, jnp.where(lane == n + 2, c, 0.0)))
                    wide[h + g, at, :] = jnp.where(first, s, tail).astype(bf16)
            return 0

        lax.fori_loop(0, nq, widen, 0)

    for p in range(0, points, 2):
        if p // 2 < nq:

            @pl.when(j == p // 2)
            def _():
                point(p)

    ks = [k_ref[h] for h in range(heads)]
    vs = [v_ref[h] for h in range(heads)]
    kts = [kt_ref[h] for h in range(heads)]

    def pair(h, i, mask):
        at = span(i, BLOCK)
        q = q_ref[h, at, :]
        d = wide[h, at, :]
        s = dot(ks[h], q, NT)
        if mask:
            s = jnp.where(row <= col, s, masked_score)
        p = jnp.exp(s)
        back = (p * dot(vs[h], d, NT)).astype(bf16)
        sums[h, :, at] += dot(kts[h], back)
        return dot(back, q), dot(p.astype(bf16), d)

    def step(i, carry):
        out = []
        for h in range(heads):
            dk, dv = pair(h, i, False)
            out.append((carry[h][0] + dk, carry[h][1] + dv))
        return tuple(out)

    state = tuple(pair(h, j, True) for h in range(heads))
    middle = (j + 1 + nq) // 2
    state = lax.fori_loop(j + 1, middle, step, state)
    for p in range(1, points, 2):
        if p // 2 < nq:

            @pl.when(j == p // 2)
            def _():
                point(p)

    state = lax.fori_loop(middle, nq, step, state)

    def join(a, b):
        return jnp.where(first, a, pltpu.roll(b, HEAD_DIM, 1))

    cosine, sine = cos_ref[...], sin_ref[...]
    low = lax.rem(lane, HEAD_DIM) < HEAD_DIM // 2

    def unrotate(slab):
        partner = jnp.where(
            low, pltpu.roll(slab, LANES - HEAD_DIM // 2, 1), pltpu.roll(slab, HEAD_DIM // 2, 1)
        )
        return slab * cosine - partner * sine

    at = span(j, BLOCK)
    total = heads * HEAD_DIM
    for h in range(0, heads, 2):
        dq = jnp.concatenate([sums[h, :, at], sums[h + 1, :, at]], axis=0).T * HEAD_DIM**-0.5
        dk = join(state[h][0], state[h + 1][0])
        dv = join(state[h][1], state[h + 1][1])
        for n, part in enumerate((unrotate(dq), unrotate(dk), dv)):
            begin = n * total + h * HEAD_DIM
            m_ref[:, begin : begin + 2 * HEAD_DIM] = part.astype(bf16)

    @pl.when(j == nq - 1)
    def _():
        for p in range(2 * nq, points):
            point(p)
        gradients.end()


def attend_back(n_d, n_t, q, k, v, kt, x, o, cosine, sine, up_g, down_g, out_g):
    heads, rows, _ = q.shape
    whole = lambda a: pl.BlockSpec(a.shape, lambda j: (0,) * a.ndim, pipeline_mode=pl.Buffered(1))
    block = pl.BlockSpec((heads, BLOCK, LANES), lambda j: (0, j, 0))
    table = pl.BlockSpec((BLOCK, LANES), lambda j: (j, 0))
    wide = heads * HEAD_DIM
    dma = pltpu.SemaphoreType.DMA
    sds = jax.ShapeDtypeStruct
    shapes = [a.shape[1:] for a in (up_g, down_g, out_g)]
    return pl.pallas_call(
        functools.partial(bwd_kernel, n_d, n_t),
        grid=(rows // BLOCK,),
        in_specs=[
            whole(q), block, block,
            pl.BlockSpec((heads, HEAD_DIM, BLOCK), lambda j: (0, 0, j)),
            VMEM, whole(o), table, table, HBM, HBM, HBM,
        ],
        out_specs=[pl.BlockSpec((BLOCK, 3 * wide), lambda j: (j, 0)), VMEM, VMEM, VMEM],
        out_shape=[sds((rows, 3 * wide), bf16)] + [sds((r // n_d, c), bf16) for r, c in shapes],
        scratch_shapes=[
            pltpu.VMEM((heads, HEAD_DIM, rows), f32),
            pltpu.VMEM((heads, rows, LANES), bf16),
            pltpu.VMEM((rows, wide), bf16),
            dma((n_t,)), dma((n_t,)),
        ] + Reduce.scratch(n_d, n_t, shapes),
        compiler_params=pltpu.CompilerParams(
            collective_id=2, has_side_effects=True, vmem_limit_bytes=67043328
        ),
        name="attend_back",
    )(q, k, v, kt, x, o, cosine, sine, up_g, down_g, out_g)


def ln_parts(v):
    centered = v - jnp.mean(v, axis=-1, keepdims=True)
    r = lax.rsqrt(jnp.mean(centered * centered, axis=-1, keepdims=True) + norm_eps)
    return centered * r, r


def ln_back(e, n, r, gain):
    f = e * gain
    return r * (f - jnp.mean(f, axis=-1, keepdims=True) - n * jnp.mean(f * n, axis=-1, keepdims=True))


def feed_kernel(
    att_ref, x_ref, cot_ref, ow_ref, par_ref, up_ref, down_ref,
    out_ref, hid_ref, ba_ref, upg_ref, downg_ref, outg_ref, vec_ref,
    hidden, branch, acc, feed_in, back_feed, active, slope,
):
    phase, n = pl.program_id(0), pl.program_id(1)
    last = pl.num_programs(1) - 1
    par = lambda i: par_ref[i : i + 1]
    total = lambda v: jnp.sum(v, axis=0, keepdims=True)

    @pl.when((phase == 0) & (n == 0))
    def _():
        b = dot(att_ref[...], ow_ref[...])
        branch[...] = b
        h = x_ref[...].astype(f32) + ln_parts(b)[0] * par(0) + par(1)
        hidden[...] = h
        feed_in[...] = (ln_parts(h)[0] * par(2) + par(3)).astype(bf16)
        acc[...] = jnp.zeros_like(acc)

    up, down = up_ref[0], down_ref[0]

    @pl.when(phase == 0)
    def _():
        u = dot(feed_in[...], up)
        t = jnp.tanh(0.7978845608028654 * (u + 0.044715 * u * u * u))
        half = 0.5 * (1.0 + t)
        a = (u * half).astype(bf16)
        active[n] = a
        slope[n] = half + 0.5 * u * (1.0 - t * t) * (
            0.7978845608028654 * (1.0 + 3 * 0.044715 * u * u)
        )
        acc[...] += dot(a, down)

    @pl.when((phase == 1) & (n == 0))
    def _():
        e = cot_ref[...].astype(f32)
        norm, r = ln_parts(acc[...])
        out_ref[...] = (hidden[...] + norm * par(4) + par(5)).astype(bf16)
        vec_ref[4:5] = total(e * norm)
        vec_ref[5:6] = total(e)
        back_feed[...] = ln_back(e, norm, r, par(4)).astype(bf16)
        acc[...] = jnp.zeros_like(acc)

    @pl.when(phase == 1)
    def _():
        b = back_feed[...]
        upper = (dot(b, down, NT) * slope[n]).astype(bf16)
        acc[...] += dot(upper, up, NT)
        downg_ref[0] = dot(active[n], b, TN).astype(bf16)
        upg_ref[0] = dot(feed_in[...], upper, TN).astype(bf16)

    @pl.when((phase == 1) & (n == last))
    def _():
        e = acc[...]
        norm, r = ln_parts(hidden[...])
        vec_ref[2:3] = total(e * norm)
        vec_ref[3:4] = total(e)
        h = cot_ref[...].astype(f32) + ln_back(e, norm, r, par(2))
        hid_ref[...] = h
        norm, r = ln_parts(branch[...])
        vec_ref[0:1] = total(h * norm)
        vec_ref[1:2] = total(h)
        b = ln_back(h, norm, r, par(0)).astype(bf16)
        ba_ref[...] = dot(b, ow_ref[...], NT).astype(bf16)
        outg_ref[...] = dot(att_ref[...], b, TN).astype(bf16)


def feed(att, x, cot, ow, par, up, down):
    rows, wide = att.shape
    n_t, _, width = up.shape
    one = lambda a: pl.BlockSpec(a.shape, lambda p, n: (0,) * len(a.shape), pipeline_mode=pl.Buffered(1))
    sds = jax.ShapeDtypeStruct
    outs = [
        sds((rows, wide), bf16), sds((rows, wide), f32), sds((rows, wide), bf16),
        sds((n_t, wide, width), bf16), sds((n_t, width, wide), bf16), sds((wide, wide), bf16),
        sds((8, wide), f32),
    ]
    chunk = lambda a: pl.BlockSpec((1,) + a.shape[1:], lambda p, n: (p * n, 0, 0))
    weight = lambda a: pl.BlockSpec((1,) + a.shape[1:], lambda p, n: (n, 0, 0))
    return pl.pallas_call(
        feed_kernel,
        grid=(2, n_t),
        in_specs=[one(a) for a in (att, x, cot, ow, par)] + [weight(up), weight(down)],
        out_specs=[one(o) for o in outs[:3]] + [chunk(outs[3]), chunk(outs[4])] + [one(o) for o in outs[5:]],
        out_shape=outs,
        scratch_shapes=[
            pltpu.VMEM((rows, wide), f32), pltpu.VMEM((rows, wide), f32), pltpu.VMEM((rows, wide), f32),
            pltpu.VMEM((rows, wide), bf16), pltpu.VMEM((rows, wide), bf16),
            pltpu.VMEM((n_t, rows, width), bf16), pltpu.VMEM((n_t, rows, width), f32),
        ],
        compiler_params=pltpu.CompilerParams(vmem_limit_bytes=64 << 20),
        name="feed",
    )(att, x, cot, ow, par, up, down)
def finish_kernel(
    n_d, n_t, bm_ref, w_ref, x_ref, hid_ref, par_ref, vec_in, up_tot, down_tot, og_tot, g_hbm,
    bt_ref, vec_ref, full_up, full_down, full_og, full_ig,
    g_ref, mine, landed, far,
    r_give, r_keep, r_side, r_out, r_land, vec_now, vec_got, vec_far,
    s_load, s_hop, r_hop, s_all, r_all, s_own, r_own,
    s_red, r_red, s_redside, r_redside, s_vec, r_vec,
):
    d, t = lax.axis_index("dp"), lax.axis_index("tensor")
    trees, rows, wide = x_ref.shape
    chips = n_t // 2
    near = chips // trees
    group = n_t // trees
    chip, core = t // 2, lax.rem(t, 2)
    other = 2 * chip + 1 - core
    line = [lax.rem(chip + k, chips) for k in range(1, chips)]
    peers = [lax.rem(d + k, n_d) for k in range(1, n_d)]
    bits = n_d.bit_length() - 1
    barrier([(d, lax.rem(t + k, n_t)) for k in range(1, n_t)] + [(p, t) for p in peers])
    totals = [up_tot, down_tot, og_tot]
    fulls = [full_up, full_down, full_og, full_ig]

    load = pltpu.make_async_copy(g_hbm, g_ref, s_load.at[0])
    load.start()
    hops, spreads = {}, []

    def cut(k, part):
        return mine.at[k, span(part, mine.shape[1] // n_d), :]

    def hop(k, step):
        slot = 0 if step == 0 else n_d - (n_d >> step)
        order = orders(n_d)[k % 2]
        partner = lax.bitwise_xor(d, 1 << order[step])
        for j, m in enumerate(combos(order[step + 1 :])):
            hops[k, step, j] = send(
                cut(k, lax.bitwise_xor(partner, m)), landed.at[k, slot + j],
                s_hop.at[k, slot + j], r_hop.at[k, slot + j], (partner, t),
            )

    def land(k, step):
        slot = 0 if step == 0 else n_d - (n_d >> step)
        for j, m in enumerate(combos(orders(n_d)[k % 2][step + 1 :])):
            hops[k, step, j].wait_recv()
            add_rows(cut(k, lax.bitwise_xor(d, m)), landed.at[k, slot + j])
        if step + 1 < bits:
            hop(k, step + 1)
        else:
            away(k)

    def spread(n, source):
        at = span(d, fulls[n].shape[0] // n_d)
        for j, p in enumerate(peers):
            spreads.append(send(source, fulls[n].at[at, :], s_all.at[n, j], r_all.at[n, j], (p, t)))

    def owner(i):
        return lax.rem(t, group) * trees + i

    def away(k):
        here = t // group

        @pl.when(owner(k) != t)
        def _():
            send(cut(k, d), far.at[here], s_own.at[k], r_own.at[here], (d, owner(k)))

        @pl.when(owner(k) == t)
        def _():
            far[here] = cut(k, d)[...]

    spread(0, totals[0])
    spread(2, totals[2])

    tree = chip // near

    def exists(c):
        return (c >= 0) & (c < chips)

    def at_step(i):
        return jnp.where(chip < chips // 2, chips - 1 - i, i)

    def past(way, x):
        return (x > chip) if way > 0 else (x < chip)

    def comes(way, j):
        return (j * near <= chip - 1) if way > 0 else (j * near + near - 1 >= chip + 1)

    def pair(x):
        return pltpu.make_async_remote_copy(
            src_ref=r_give.at[x], dst_ref=r_side.at[x], send_sem=s_redside.at[x], recv_sem=r_redside.at[x],
            device_id=(d, other), device_id_type=MESH,
        )

    def red(way, x, j, source, arriving=False):
        w = 0 if way > 0 else 1
        to = chip - way if arriving else chip + way
        return pltpu.make_async_remote_copy(
            src_ref=source, dst_ref=r_land.at[w, x, j], send_sem=s_red.at[w, x, j], recv_sem=r_red.at[w, x, j],
            device_id=(d, 2 * to + core), device_id_type=MESH,
        )

    def arrived(way, x, j):
        w = 0 if way > 0 else 1
        red(way, x, j, r_land.at[w, x, j], True).wait_recv()

    def rows_of(device):
        return dot(bm_ref[span(device, rows), :], w_ref[...], NT).astype(bf16)

    def first_rows(x):
        pair(x).wait_recv()

        @pl.when(x != chip)
        def _():
            r_out[x] = r_keep[x] + r_side[x]

        for way in (1, -1):

            @pl.when(past(way, x) & jnp.logical_not(comes(way, tree)))
            def _():
                red(way, x, tree, r_out.at[x]).start()

    def step_rows(i, _):
        x = at_step(i)
        r_give[x] = rows_of(2 * x + 1 - core)
        r_keep[x] = rows_of(2 * x + core)
        pair(x).start()

        @pl.when(i > 0)
        def _():
            first_rows(at_step(i - 1))

        return 0

    lax.fori_loop(0, chips, step_rows, 0)
    first_rows(at_step(chips - 1))

    def later_rows(i):
        x = at_step(i)
        for way in (1, -1):
            for j in range(trees):

                @pl.when(past(way, x) & comes(way, j))
                def _():
                    arrived(way, x, j)
                    passing = r_land.at[0 if way > 0 else 1, x, j]

                    @pl.when(tree == j)
                    def _():
                        add_rows(r_out.at[x], passing)
                        red(way, x, j, r_out.at[x]).start()

                    @pl.when(tree != j)
                    def _():
                        red(way, x, j, passing).start()

    columns, width = bm_ref.shape[1] // 3, mine.shape[2]
    load.wait()

    def step_weight(i, _):
        p, c = i // (wide // BLOCK), lax.rem(i, wide // BLOCK)
        product = dot(g_ref[:, span(c, BLOCK)], bm_ref[:, span(p, columns)], TN).astype(bf16)
        for j in range(trees):
            mine[j, span(i, BLOCK), :] = product[:, j * width : (j + 1) * width]
        return 0

    lax.fori_loop(0, 3 * (wide // BLOCK), step_weight, 0)
    for k in range(trees):
        hop(k, 0)
    for n in range(3):
        fulls[n][span(d, fulls[n].shape[0] // n_d), :] = totals[n][...]
    for i in range(max(chips, bits)):
        if i < chips:
            later_rows(i)
        if i < bits:
            for k in range(trees):
                land(k, i)
        if i == 0:
            spread(1, totals[1])

    def reduced():
        for w, way in enumerate((1, -1)):
            for j in range(trees):

                @pl.when(comes(way, j))
                def _():
                    arrived(way, chip, j)

                @pl.when(jnp.logical_not(comes(way, j)))
                def _():
                    r_land[w, chip, j] = jnp.zeros((rows, wide), bf16)

        vec_now[0:6] = vec_in[0:6]
        vec_now[6:8] = jnp.zeros((2, wide), f32)
        height = min(64, rows)
        for j in range(trees):

            def body(i, _):
                at = span(i, height)
                own = r_keep[chip, at, :].astype(f32) + r_side[chip, at, :].astype(f32)
                e = jnp.where(tree == j, own, 0.0)
                for w in range(2):
                    e = e + r_land[w, chip, j, at, :].astype(f32)
                norm, r = ln_parts(x_ref[j, at, :].astype(f32))
                vec_now[6:7] = vec_now[6:7] + jnp.sum(e * norm, axis=0, keepdims=True)
                vec_now[7:8] = vec_now[7:8] + jnp.sum(e, axis=0, keepdims=True)
                bt_ref[j, at, :] = (hid_ref[j, at, :] + ln_back(e, norm, r, par_ref[6:7])).astype(bf16)
                return 0

            lax.fori_loop(0, rows // height, body, 0)

    for j in range(trees):
        giver = j * group + t // trees

        @pl.when(giver != t)
        def _():
            pltpu.make_async_remote_copy(
                src_ref=far.at[j], dst_ref=far.at[j], send_sem=s_own.at[0], recv_sem=r_own.at[j],
                device_id=(d, giver), device_id_type=MESH,
            ).wait_recv()

    total = far[0].astype(f32)
    for j in range(1, trees):
        total = total + far[j].astype(f32)
    at = span(d, full_ig.shape[0] // n_d)
    full_ig[at, :] = total.astype(bf16)
    spread(3, full_ig.at[at, :])

    reduced()

    copy = send(vec_now, vec_got.at[0], s_vec.at[0], r_vec.at[0], (d, other))
    copy.wait()
    vec_got[1 + d] = vec_now[...] + vec_got[0]
    row = vec_got.at[1 + d]
    vec_copies = [send(row, row, s_vec.at[1 + k], r_vec.at[1 + k], (p, t)) for k, p in enumerate(peers)]
    for copy in vec_copies:
        copy.wait()
    total = vec_got[1]
    for i in range(1, n_d):
        total = total + vec_got[1 + i]
    vec_far[chip] = total
    vec_copies = []
    for k in range(1, chips):
        c = lax.rem(chip + k, chips)
        n = n_d - 1 + k
        vec_copies.append(send(vec_far.at[chip], vec_far.at[chip], s_vec.at[n], r_vec.at[n], (d, 2 * c + core)))
    for copy in spreads:
        copy.wait_recv()
    for copy in vec_copies:
        copy.wait()
    total = vec_far[0]
    for c in range(1, chips):
        total = total + vec_far[c]
    vec_ref[...] = total

    for k in range(trees):

        @pl.when(owner(k) != t)
        def _():
            pltpu.make_async_remote_copy(
                src_ref=cut(k, d), dst_ref=cut(k, d), send_sem=s_own.at[k], recv_sem=r_own.at[0],
                device_id=(d, owner(k)), device_id_type=MESH,
            ).wait_send()

    for k in range(chips):
        pair(k).wait_send()
    for x in range(chips):
        for way in (1, -1):

            @pl.when(past(way, x))
            def _():
                red(way, x, tree, r_out.at[x]).wait_send()
                for j in range(trees):

                    @pl.when(comes(way, j) & (tree != j))
                    def _():
                        red(way, x, j, r_land.at[0 if way > 0 else 1, x, j]).wait_send()

    for copy in list(hops.values()) + spreads:
        copy.wait_send()


def finish(n_d, n_t, mixed, w, x, hidden, par, vec, up_t, down_t, out_t, gathered, width):
    trees, rows, wide = x.shape
    chips = n_t // 2
    bits = n_d.bit_length() - 1
    dma = pltpu.SemaphoreType.DMA
    sds = jax.ShapeDtypeStruct
    shapes = [(a.shape[0] * n_d, a.shape[1]) for a in (up_t, down_t, out_t)] + [(3 * wide, width)]
    vm = lambda lead, shape, kind=bf16: pltpu.VMEM(tuple(lead) + tuple(shape), kind)
    part = (shapes[3][0] // n_d, shapes[3][1])
    return pl.pallas_call(
        functools.partial(finish_kernel, n_d, n_t),
        in_specs=[VMEM] * 9 + [HBM],
        out_specs=[VMEM] * 6,
        out_shape=[sds(x.shape, bf16), sds((8, wide), f32)] + [sds(s, bf16) for s in shapes],
        scratch_shapes=[vm((), gathered.shape), vm((trees,), shapes[3]), vm((trees, n_d - 1), part), vm((trees,), part)]
        + [
            vm((chips, rows), (wide,)), vm((chips, rows), (wide,)), vm((chips, rows), (wide,)),
            vm((chips, rows), (wide,)), vm((2, chips, trees, rows), (wide,)),
            vm((8,), (wide,), f32), vm((1 + n_d, 8), (wide,), f32), vm((chips, 8), (wide,), f32),
            dma((1,)), dma((trees, n_d - 1)), dma((trees, n_d - 1)),
            dma((4, n_d - 1)), dma((4, n_d - 1)),
            dma((trees,)), dma((trees,)),
            dma((2, chips, trees)), dma((2, chips, trees)), dma((chips,)), dma((chips,)),
            dma((n_d + chips - 1,)), dma((n_d + chips - 1,)),
        ],
        compiler_params=pltpu.CompilerParams(
            collective_id=3, has_side_effects=True, vmem_limit_bytes=67043328
        ),
        name="finish",
    )(mixed, w, x, hidden, par, vec, up_t, down_t, out_t, gathered)


def shards(
    n_d, n_t,
    tokens, cotangent, lengths, parents, first_gain, first_shift, in_weight, out_weight,
    second_gain, second_shift, third_gain, third_shift, up_weight, down_weight, fourth_gain, fourth_shift,
):
    trees, rows, wide = tokens.shape
    group = n_t // trees
    d, t = lax.axis_index("dp"), lax.axis_index("tensor")
    tree = t // group
    width = out_weight.shape[0]

    mine = lambda a: lax.dynamic_index_in_dim(a, tree, 0, keepdims=False)
    cosine, sine, mq, mk = tables(mine(lengths), mine(parents), n_t * rows)

    par = jnp.stack(
        [second_gain, second_shift, third_gain, third_shift, fourth_gain, fourth_shift, first_gain, first_shift]
    )
    gathered, w, down_all = gather_tree(
        n_d, n_t, tokens, par, in_weight.transpose(1, 0, 2), down_weight
    )
    w = w.transpose(1, 2, 0, 3).reshape(3, wide, -1)
    q, k, v, kt, vt = project(gathered, w, cosine, sine, mq, mk)
    attended, qb, att, out_all, up_all = attend(n_d, n_t, trees, q, k, vt, out_weight, up_weight)
    flat = lambda a: a.reshape(trees * rows, a.shape[-1])
    output, back_hidden, back_att, up_g, down_g, out_g, vec = feed(
        flat(att), flat(tokens), flat(cotangent), out_all.reshape(-1, wide), par, up_all, down_all
    )
    back_mixed, up_t, down_t, out_t = attend_back(
        n_d, n_t, qb, k, v, kt, back_att.reshape(trees, rows, wide), attended, cosine, sine,
        up_g, down_g, out_g.reshape(n_t, width, wide),
    )
    w_flat = w.transpose(1, 0, 2).reshape(wide, -1)
    back_tokens, vec, up_sum, down_sum, out_sum, in_sum = finish(
        n_d, n_t, back_mixed, w_flat, tokens, back_hidden.reshape(tokens.shape), par, vec,
        up_t, down_t, out_t, gathered, width,
    )
    return (
        output.reshape(tokens.shape),
        back_tokens,
        vec[6], vec[7],
        in_sum.astype(f32).reshape(3, wide, width).transpose(1, 0, 2),
        out_sum.astype(f32),
        vec[0], vec[1], vec[2], vec[3],
        up_sum.astype(f32),
        down_sum.astype(f32),
        vec[4], vec[5],
    )


def solution(mesh):
    in_specs = (
        P("dp", "tensor", None), P("dp", "tensor", None), P("dp", None), P("dp", None),
        P(), P(), P(None, None, "tensor"), P("tensor", None), P(), P(), P(), P(),
        P(None, "tensor"), P("tensor", None), P(), P(),
    )
    out_specs = (
        P("dp", "tensor", None), P("dp", "tensor", None), P(), P(), P(None, None, "tensor"),
        P("tensor", None), P(), P(), P(), P(), P(None, "tensor"), P("tensor", None), P(), P(),
    )
    run = functools.partial(shards, mesh.shape["dp"], mesh.shape["tensor"])
    return jax.shard_map(run, mesh=mesh, in_specs=in_specs, out_specs=out_specs, check_vma=False)
```
